32 devices in a mesh: seq: 8 (over y, x, core), fsdp: 4 (over z).
Axes of the slice: x: 2, y: 2, z: 4, core: 2. Of those that a mesh axis runs over, the one named last changes fastest.
Arguments:
- stream_in: bfloat16 [4, 1024, 1536], P('fsdp', 'seq'), may hold values from -6 to 6
- cotangent: bfloat16 [4, 1024, 1536], P('fsdp', 'seq'), may hold values from -6 to 6
- starts: int32 [4, 4], P('fsdp'), may hold values from 1 to 1023
- params: float32 [31214592], P(('seq', 'fsdp'))
- momentum: float32 [31214592], P(('seq', 'fsdp')), may hold values from -300 to 300
- average: float32 [31214592], P(('seq', 'fsdp'))
Outputs:
- output: bfloat16 [4, 1024, 1536], P('fsdp', 'seq')
- input_grad: float32 [4, 1024, 1536], P('fsdp', 'seq')
- new_params: float32 [31214592], P(('seq', 'fsdp'))
- new_momentum: float32 [31214592], P(('seq', 'fsdp'))
- new_average: float32 [31214592], P(('seq', 'fsdp'))
The draws below stay inside these ranges and needn't reach their ends.
All inputs are finite; a program needn't handle non-finite values.
Results may differ from the reference program's by a relative error of at most 0.013.
The reference program's roundings to bfloat16 on the way count: a program that leaves them out, or rounds other values in their place, can miss the bound.
Values may be sent and summed in bfloat16 or wider, within the bound.
No kernel may reach another device: no remote copies, remote signals or barrier semaphores. Data moves between devices by JAX's collectives and lax.ppermute only.
A program may use at most 576 MiB of HBM per device.

```python
import math
import jax
import jax.numpy as jnp
from jax import lax

D = 1536
LRU = 2048
FF = 4608
HB = 128
KW = 4
TOK_DEV = 128
DOCS = 4
STREAMS = 4
STREAM = 1024
PARAMS = 31214592
N_SEQ = 8


def layout_drawn():
    return [('gain_one', (D,)), ('gain_two', (D,)), ('conv_bias', (LRU,)), ('bias_a', (LRU,)), ('bias_i', (LRU,)), ('lambda_raw', (LRU,)), ('conv_weight', (KW, LRU)), ('gate_a', (LRU // HB, HB, HB)), ('gate_i', (LRU // HB, HB, HB)), ('w_y', (D, LRU)), ('w_x', (D, LRU)), ('w_out', (LRU, D)), ('w_gate', (D, FF)), ('w_up', (D, FF)), ('w_down', (FF, D))]


def entry_values(key, entry_name, entry_shape):
    unit = jax.random.uniform(jax.random.fold_in(key, 1), entry_shape, jnp.float32)
    spread = jax.random.normal(jax.random.fold_in(key, 2), entry_shape, jnp.float32)
    if entry_name in ('gain_one', 'gain_two'):
        return 0.6 + 0.8 * unit
    if entry_name == 'conv_bias':
        return unit - 0.5
    if entry_name in ('bias_a', 'bias_i'):
        return 2.0 * unit - 1.0
    if entry_name == 'lambda_raw':
        other = jax.random.uniform(jax.random.fold_in(key, 3), entry_shape, jnp.float32)
        slow = jax.random.bernoulli(jax.random.fold_in(key, 4), 0.5, entry_shape)
        return jnp.where(slow, -11.5 + 1.7 * unit, -7.0 + 3.0 * other)
    if entry_name == 'conv_weight':
        return 0.5 * spread
    if entry_name in ('gate_a', 'gate_i'):
        return spread / math.sqrt(HB)
    if entry_name == 'w_out':
        return 2.0 * spread / math.sqrt(LRU)
    if entry_name == 'w_down':
        return 2.0 * spread / math.sqrt(FF)
    return spread / math.sqrt(D)


def draw_flat(key, salt):
    pieces = []
    for entry_index, entry in enumerate(layout_drawn()):
        subkey = jax.random.fold_in(key, salt + entry_index)
        pieces.append(entry_values(subkey, entry[0], entry[1]).reshape(-1))
    return jnp.concatenate(pieces)


def draw_params(key, part):
    return draw_flat(key, 0)


def draw_average(key, part):
    return draw_flat(key, 100)


def set_ends(values, own_key, low, high):
    index_at = [jax.random.randint(jax.random.fold_in(own_key, axis), (), 0, length) for axis, length in enumerate(values.shape)]
    main_axis = values.shape.index(max(values.shape))
    beside = index_at[:main_axis] + [(index_at[main_axis] + 1) % values.shape[main_axis]] + index_at[main_axis + 1:]
    return values.at[tuple(index_at)].set(low).at[tuple(beside)].set(high)


def block_scale(own_key, shape, cuts, low, largest):
    def one(axis_at, shards_of):
        heights = jax.random.uniform(jax.random.fold_in(jax.random.fold_in(own_key, 6), axis_at), (shards_of,), jnp.float32, low / len(cuts), largest / len(cuts))
        return jnp.repeat(jnp.exp(heights), shape[axis_at] // shards_of).reshape((-1,) + (1,) * (len(shape) - axis_at - 1))

    loudness = one(*cuts[0])
    for cut in cuts[1:]:
        loudness = loudness * one(*cut)
    return loudness


def gaussian(own_key, dims, width, most, shards=(), held_as=jnp.bfloat16):
    level = block_scale(own_key, dims, shards, -0.22, 0.18) if shards else 1.0
    array = jax.random.normal(own_key, dims, jnp.float32) * width * level
    return jnp.minimum(jnp.maximum(array, -most), most).astype(held_as)


def setup_inputs(seed: int = 0) -> dict:
    splits = jax.random.split(jax.random.key(seed), 7)
    return {
        "stream_in": gaussian(splits[0], (STREAMS, STREAM, D), 1.0, 6.0, ((0, 4), (1, 8))),
        "cotangent": gaussian(splits[1], (STREAMS, STREAM, D), 1.0, 6.0, ((0, 4), (1, 8))),
        "starts": set_ends(jax.random.randint(splits[2], (STREAMS, DOCS), 1, TOK_DEV * N_SEQ), jax.random.fold_in(splits[2], 1), 1, (TOK_DEV * N_SEQ) - 1).astype(jnp.int32),
        "params": draw_params(jax.random.fold_in(splits[6], 71), 0),
        "momentum": gaussian(splits[4], (PARAMS,), 50.0, 300.0, ((0, 32),), jnp.float32),
        "average": draw_average(jax.random.fold_in(splits[6], 71), 0),
    }


EPS = 1e-06
RATE = 3e-05
MOMENT = 0.9
BLEND = 0.9
DECAY_SCALE = 8.0
HIGH = lax.Precision.HIGHEST

@jax.custom_vjp
def low(v):
    return lax.optimization_barrier(v.astype(jnp.bfloat16)).astype(jnp.float32)

@jax.custom_vjp
def low_back(v):
    return v

def low_keep(v):
    return (low(v), None)

def low_pass(kept, grad):
    return (grad,)

def back_keep(v):
    return (v, None)

def back_low(kept, grad):
    return (low(grad),)
low.defvjp(low_keep, low_pass)
low_back.defvjp(back_keep, back_low)

def layout():
    return [('gain_one', (D,)), ('gain_two', (D,)), ('conv_bias', (LRU,)), ('bias_a', (LRU,)), ('bias_i', (LRU,)), ('lambda_raw', (LRU,)), ('conv_weight', (KW, LRU)), ('gate_a', (LRU // HB, HB, HB)), ('gate_i', (LRU // HB, HB, HB)), ('w_y', (D, LRU)), ('w_x', (D, LRU)), ('w_out', (LRU, D)), ('w_gate', (D, FF)), ('w_up', (D, FF)), ('w_down', (FF, D))]

def unpack(packed):
    result = {}
    offset = 0
    for entry_name, entry_shape in layout():
        amount = math.prod(entry_shape)
        result[entry_name] = packed[offset:offset + amount].reshape(entry_shape)
        offset += amount
    return result

def matmul(left, right):
    return jnp.dot(left, right, precision=HIGH, preferred_element_type=jnp.float32)

def rms_norm(values, gain):
    return values * lax.rsqrt(lax.optimization_barrier(jnp.mean(values * values, axis=-1, keepdims=True)) + EPS) * gain

def blocked(values, weight):
    shaped = values.reshape(values.shape[0], LRU // HB, HB)
    return jnp.einsum('tnh,nhk->tnk', shaped, weight, precision=HIGH).reshape(values.shape[0], LRU)

def combine(earlier, later):
    return (earlier[0] * later[0], later[0] * earlier[1] + later[1])

def gate_terms(pre_a, pre_i, conv_val, lambda_raw, starting):
    recall = jax.nn.sigmoid(pre_a)
    admit = jax.nn.sigmoid(pre_i)
    rate = DECAY_SCALE * jax.nn.softplus(lambda_raw) * recall
    decay = (1.0 - starting) * jnp.exp(-rate)
    scale_in = starting + (1.0 - starting) * jnp.sqrt(-jnp.expm1(-2.0 * rate))
    return (decay, scale_in * admit * conv_val)

def convolve(extended, weight, bias, segment_ext, rows):
    total = jnp.zeros((rows, LRU), jnp.float32) + bias
    for lag in range(KW):
        source = extended[KW - 1 - lag:KW - 1 - lag + rows]
        same = (segment_ext[KW - 1 - lag:KW - 1 - lag + rows] == segment_ext[KW - 1:]).astype(jnp.float32)
        total = total + weight[lag] * source * same[:, None]
    return total

def segment_ids(positions, doc_starts):
    return lax.optimization_barrier(jnp.sum((doc_starts[None, :] <= positions[:, None]).astype(jnp.int32), axis=1))

def start_flags(positions, doc_starts):
    return lax.optimization_barrier(jnp.max((doc_starts[None, :] == positions[:, None]).astype(jnp.float32), axis=1))

def stream_forward(weights, stream, doc_starts):
    rows = stream.shape[0]
    positions = jnp.arange(rows, dtype=jnp.int32)
    ext_pos = jnp.arange(rows + KW - 1, dtype=jnp.int32) - (KW - 1)
    segment_ext = segment_ids(ext_pos, doc_starts)
    starting = start_flags(positions, doc_starts)[:, None]
    normed = low(rms_norm(stream, weights['gain_one']))
    branch_y = low_back(matmul(normed, weights['w_y']))
    branch_x = low_back(low(matmul(normed, weights['w_x'])))
    extended = jnp.concatenate([jnp.zeros((KW - 1, LRU), jnp.float32), branch_x], axis=0)
    conv_out = low(convolve(extended, weights['conv_weight'], weights['conv_bias'], segment_ext, rows))
    pre_a = low_back(blocked(conv_out, weights['gate_a']) + weights['bias_a'])
    pre_i = low_back(blocked(conv_out, weights['gate_i']) + weights['bias_i'])
    decay, drive = gate_terms(pre_a, pre_i, conv_out, weights['lambda_raw'], starting)
    state = lax.associative_scan(combine, (decay, drive), axis=0)[1]
    mixed = low(state * jax.nn.gelu(branch_y, approximate=True))
    middle = stream + low_back(matmul(mixed, weights['w_out']))
    normed_two = low(rms_norm(middle, weights['gain_two']))
    gate = low_back(matmul(normed_two, weights['w_gate']))
    upward = low_back(matmul(normed_two, weights['w_up']))
    hidden = low(jax.nn.gelu(gate, approximate=True) * upward)
    return middle + low_back(matmul(hidden, weights['w_down']))

def reference(stream_in, cotangent, starts, params, momentum, average):

    def forward(packed, streams):
        weights = unpack(low(packed))

        def one_stream(pair):
            return stream_forward(weights, pair[0], pair[1])
        return lax.map(jax.checkpoint(one_stream), (streams, starts))
    streams = stream_in.astype(jnp.float32)
    result, back = jax.vjp(forward, params, streams)
    grad_params, grad_stream = back(cotangent.astype(jnp.float32))
    new_moment = MOMENT * momentum + grad_params
    new_params = params - RATE * (grad_params + MOMENT * new_moment)
    new_average = BLEND * average + (1.0 - BLEND) * new_params
    return (result.astype(jnp.bfloat16), grad_stream, new_params, new_moment, new_average)
```

```python
from functools import partial
import math

import jax
import jax.numpy as jnp
import numpy as np
from jax import lax
from jax.experimental import pallas as pl
from jax.experimental.pallas import tpu as pltpu
from jax.sharding import PartitionSpec as P


D = 1536
LRU = 2048
FF = 4608
HB = 128
KW = 4


EPS = 1e-06
RATE = 3e-05
MOMENT = 0.9
BLEND = 0.9
DECAY_SCALE = 8.0


def shifted(block, axis, distance):
    devices = range(lax.axis_size(axis))
    route = [(i - distance, i) for i in devices if i - distance in devices]
    return lax.ppermute(block, axis, route)


def carried_in(value, axis, join, neutral, backward):
    count, mine = (lax.axis_size(axis), lax.axis_index(axis))
    pieces = jax.tree.map(lambda part: lax.all_gather(part, axis), value)
    if backward:
        pieces = jax.tree.map(lambda part: part[::-1], pieces)
        mine = count - 1 - mine
    so_far = jax.tree.map(
        lambda part, zero: jnp.full_like(part, 0) + jnp.asarray(zero, part.dtype), value, neutral
    )

    def lap(position, so_far):
        longer = join(so_far, jax.tree.map(lambda part: part[position], pieces))
        return jax.tree.map(lambda new, old: jnp.where(position < mine, new, old), longer, so_far)

    return lax.fori_loop(0, count - 1, lap, so_far)


def layout():
    return [
        ("gain_one", (D,)),
        ("gain_two", (D,)),
        ("conv_bias", (LRU,)),
        ("bias_a", (LRU,)),
        ("bias_i", (LRU,)),
        ("lambda_raw", (LRU,)),
        ("conv_weight", (KW, LRU)),
        ("gate_a", (LRU // HB, HB, HB)),
        ("gate_i", (LRU // HB, HB, HB)),
        ("w_y", (D, LRU)),
        ("w_x", (D, LRU)),
        ("w_out", (LRU, D)),
        ("w_gate", (D, FF)),
        ("w_up", (D, FF)),
        ("w_down", (FF, D)),
    ]


def unpack(packed):
    result = {}
    offset = 0
    for entry_name, entry_shape in layout():
        amount = math.prod(entry_shape)
        result[entry_name] = packed[offset : offset + amount].reshape(entry_shape)
        offset += amount
    return result


def matmul(left, right):
    return jnp.dot(left, right, preferred_element_type=jnp.float32)


def matmul_t(left, right):
    return lax.dot_general(
        left, right, (((1,), (1,)), ((), ())), preferred_element_type=jnp.float32
    )


def t_matmul(left, right):
    return lax.dot_general(
        left, right, (((0,), (0,)), ((), ())), preferred_element_type=jnp.float32
    )


def blocked(values, weight):
    shaped = values.reshape(values.shape[0], LRU // HB, HB)
    return jnp.einsum("tnh,nhk->tnk", shaped, weight, preferred_element_type=jnp.float32).reshape(
        values.shape[0], LRU
    )


def blocked_t(values, weight):
    shaped = values.reshape(values.shape[0], LRU // HB, HB)
    return jnp.einsum("tnk,nhk->tnh", shaped, weight, preferred_element_type=jnp.float32).reshape(
        values.shape[0], LRU
    )


def blocked_grad(inputs, grads):
    left = inputs.reshape(inputs.shape[0], LRU // HB, HB)
    right = grads.reshape(grads.shape[0], LRU // HB, HB)
    return jnp.einsum("tnh,tnk->nhk", left, right, preferred_element_type=jnp.float32)


def rms_norm(values, gain):
    return values * lax.rsqrt(jnp.mean(values * values, axis=-1, keepdims=True) + EPS) * gain


def combine(earlier, later):
    return (earlier[0] * later[0], later[0] * earlier[1] + later[1])


def gate_terms(pre_a, pre_i, conv_val, lambda_raw, starting):
    recall = jax.nn.sigmoid(pre_a)
    admit = jax.nn.sigmoid(pre_i)
    rate = DECAY_SCALE * jax.nn.softplus(lambda_raw) * recall
    decay = (1.0 - starting) * jnp.exp(-rate)
    scale_in = starting + (1.0 - starting) * jnp.sqrt(-jnp.expm1(-2.0 * rate))
    return (decay, scale_in * admit * conv_val)


def convolve(extended, weight, bias, segment_ext, rows):
    total = jnp.zeros((rows, LRU), jnp.float32) + bias
    for lag in range(KW):
        source = extended[KW - 1 - lag : KW - 1 - lag + rows]
        same = (segment_ext[KW - 1 - lag : KW - 1 - lag + rows] == segment_ext[KW - 1 :]).astype(
            jnp.float32
        )
        total = total + weight[lag] * source * same[:, None]
    return total


def segment_ids(positions, doc_starts):
    return jnp.sum((doc_starts[None, :] <= positions[:, None]).astype(jnp.int32), axis=1)


def start_flags(positions, doc_starts):
    return jnp.max((doc_starts[None, :] == positions[:, None]).astype(jnp.float32), axis=1)


def gelu_product(left, right):
    return jax.nn.gelu(left, approximate=True) * right


def local(stream_in, cotangent, starts, params, momentum, average):
    weights = unpack(
        lax.all_gather(params.astype(jnp.bfloat16), ("seq", "fsdp"), axis=0, tiled=True)
    )
    stream = stream_in[0].astype(jnp.float32)
    incoming = cotangent[0].astype(jnp.float32)
    doc_starts = starts[0]
    rows = stream.shape[0]
    positions = lax.axis_index("seq") * rows + jnp.arange(rows, dtype=jnp.int32)
    ext_pos = positions[0] - (KW - 1) + jnp.arange(rows + KW - 1, dtype=jnp.int32)
    segment_ext = segment_ids(ext_pos, doc_starts)
    starting = start_flags(positions, doc_starts)[:, None]
    gain_one = weights["gain_one"].astype(jnp.float32)
    gain_two = weights["gain_two"].astype(jnp.float32)
    conv_weight = weights["conv_weight"].astype(jnp.float32)
    conv_bias = weights["conv_bias"].astype(jnp.float32)
    lambda_raw = weights["lambda_raw"].astype(jnp.float32)
    normed = rms_norm(stream, gain_one).astype(jnp.bfloat16)
    branch_y = matmul(normed, weights["w_y"])
    branch_x = matmul(normed, weights["w_x"]).astype(jnp.bfloat16)
    edge = shifted(branch_x[rows - (KW - 1) :], "seq", 1)
    extended = jnp.concatenate([edge, branch_x], axis=0).astype(jnp.float32)
    conv_out = convolve(extended, conv_weight, conv_bias, segment_ext, rows).astype(jnp.bfloat16)
    conv_val = conv_out.astype(jnp.float32)
    pre_a = blocked(conv_out, weights["gate_a"]) + weights["bias_a"].astype(jnp.float32)
    pre_i = blocked(conv_out, weights["gate_i"]) + weights["bias_i"].astype(jnp.float32)
    decay, drive = gate_terms(pre_a, pre_i, conv_val, lambda_raw, starting)
    prod_local, state_local = lax.associative_scan(combine, (decay, drive), axis=0)
    neutral = (jnp.ones((LRU,), jnp.float32), jnp.zeros((LRU,), jnp.float32))
    carried = carried_in((prod_local[-1], state_local[-1]), "seq", combine, neutral, False)
    carry_in = carried[1]
    state = lax.associative_scan(combine, (decay, drive.at[0].add(decay[0] * carry_in)), axis=0)[1]
    gelu_y = jax.nn.gelu(branch_y, approximate=True)
    mixed = (state * gelu_y).astype(jnp.bfloat16)
    middle = stream + matmul(mixed, weights["w_out"])
    normed_two = rms_norm(middle, gain_two).astype(jnp.bfloat16)
    gate = matmul(normed_two, weights["w_gate"])
    upward = matmul(normed_two, weights["w_up"])
    hidden = gelu_product(gate, upward).astype(jnp.bfloat16)
    output = (middle + matmul(hidden, weights["w_down"])).astype(jnp.bfloat16)
    grads = {}
    grad_out = incoming.astype(jnp.bfloat16)
    grads["w_down"] = t_matmul(hidden, grad_out)
    grad_hidden = matmul_t(grad_out, weights["w_down"])
    _, product_back = jax.vjp(gelu_product, gate, upward)
    grad_gate, grad_up = product_back(grad_hidden)
    grad_gate = grad_gate.astype(jnp.bfloat16)
    grad_up = grad_up.astype(jnp.bfloat16)
    grads["w_gate"] = t_matmul(normed_two, grad_gate)
    grads["w_up"] = t_matmul(normed_two, grad_up)
    grad_normed_two = matmul_t(grad_gate, weights["w_gate"]) + matmul_t(grad_up, weights["w_up"])
    _, norm_back_two = jax.vjp(rms_norm, middle, gain_two)
    grad_middle_part, grads["gain_two"] = norm_back_two(grad_normed_two)
    grad_middle = incoming + grad_middle_part
    grad_first = grad_middle.astype(jnp.bfloat16)
    grads["w_out"] = t_matmul(mixed, grad_first)
    grad_mixed = matmul_t(grad_first, weights["w_out"])
    _, gelu_back = jax.vjp(partial(jax.nn.gelu, approximate=True), branch_y)
    grad_y = gelu_back(grad_mixed * state)[0].astype(jnp.bfloat16)
    grad_state = grad_mixed * gelu_y
    next_decay = jnp.concatenate([decay[1:], jnp.ones((1, LRU), jnp.float32)], axis=0)
    suffix, adjoint_local = lax.associative_scan(
        combine, (next_decay, grad_state), axis=0, reverse=True
    )
    returned = carried_in(
        (prod_local[-1], decay[0] * adjoint_local[0]), "seq", combine, neutral, True
    )
    adjoint = adjoint_local + suffix * returned[1]
    previous = jnp.concatenate([carry_in[None, :], state[:-1]], axis=0)
    _, gates_back = jax.vjp(gate_terms, pre_a, pre_i, conv_val, lambda_raw, starting)
    grad_pre_a, grad_pre_i, grad_direct, grads["lambda_raw"], _ = gates_back(
        (adjoint * previous, adjoint)
    )
    grad_pre_a = grad_pre_a.astype(jnp.bfloat16)
    grad_pre_i = grad_pre_i.astype(jnp.bfloat16)
    grads["gate_a"] = blocked_grad(conv_out, grad_pre_a)
    grads["gate_i"] = blocked_grad(conv_out, grad_pre_i)
    grads["bias_a"] = jnp.sum(grad_pre_a.astype(jnp.float32), axis=0)
    grads["bias_i"] = jnp.sum(grad_pre_i.astype(jnp.float32), axis=0)
    grad_conv = (
        grad_direct
        + blocked_t(grad_pre_a, weights["gate_a"])
        + blocked_t(grad_pre_i, weights["gate_i"])
    )
    _, conv_back = jax.vjp(
        partial(convolve, segment_ext=segment_ext, rows=rows), extended, conv_weight, conv_bias
    )
    grad_ext, grads["conv_weight"], grads["conv_bias"] = conv_back(grad_conv)
    edge_back = shifted(grad_ext[: KW - 1], "seq", -1)
    grad_x = grad_ext[KW - 1 :] + jnp.concatenate(
        [jnp.zeros((rows - (KW - 1), LRU), jnp.float32), edge_back], axis=0
    )
    grad_x = grad_x.astype(jnp.bfloat16)
    grads["w_x"] = t_matmul(normed, grad_x)
    grads["w_y"] = t_matmul(normed, grad_y)
    grad_normed = matmul_t(grad_y, weights["w_y"]) + matmul_t(grad_x, weights["w_x"])
    _, norm_back_one = jax.vjp(rms_norm, stream, gain_one)
    grad_stream_part, grads["gain_one"] = norm_back_one(grad_normed)
    input_grad = grad_middle + grad_stream_part
    packed_grad = jnp.concatenate([grads[entry[0]].reshape(-1) for entry in layout()])
    summed = lax.psum_scatter(packed_grad, ("seq", "fsdp"), scatter_dimension=0, tiled=True)
    new_moment = MOMENT * momentum + summed
    new_params = params - RATE * (summed + MOMENT * new_moment)
    new_average = BLEND * average + (1.0 - BLEND) * new_params
    return (output[None], input_grad[None], new_params, new_moment, new_average)


LANE = 128
TP = 8
HALO = 544
SMALL = 160
GATES = 512
REGIONS = {
    "A": (4248, 256, 192, 32),
    "B": (53400, 1536, 16, 192),
    "C": (77976, 1152, 96, 144),
    "D": (188568, 1536, 36, 192),
}
ROWS = 243864
EVEN_FIRST = (0, 2, 4, 6, 1, 3, 5, 7)
F32 = jnp.float32
BF16 = jnp.bfloat16


class Plan:
    def __init__(self, n_seq, n_fsdp):
        self.n_fsdp = n_fsdp
        shards = n_seq * n_fsdp
        per = ROWS * LANE // shards
        self.per = per
        self.part = per % LANE
        self.own_rows = -(-per // 1024) * 8
        self.last = per // LANE
        bounds = [0]
        for i in range(1, shards):
            at = per * i / LANE
            for first, unit, count, _ in REGIONS.values():
                if first <= at < first + unit * count:
                    bounds.append(first + unit * round((at - first) / unit))
        bounds.append(ROWS)
        self.segments = []
        self.sizes = []
        self.table = np.zeros((shards, 16), np.int32)
        for i in range(shards):
            base = per * i // LANE
            self.table[i, 0] = per * i % LANE
            offset = SMALL + GATES if i == 0 else 0
            found = {}
            for slot, (name, (first, unit, count, wide)) in enumerate(REGIONS.items()):
                low = max(bounds[i], first)
                high = min(bounds[i + 1], first + unit * count)
                if high > low:
                    units = (high - low) // unit
                    found[name] = ((low - first) // unit, units, offset)
                    self.table[i, 1 + 3 * slot : 4 + 3 * slot] = (
                        low - base + HALO,
                        units,
                        offset,
                    )
                    offset += units * wide
            self.segments.append(found)
            self.sizes.append(offset)
            self.table[i, 13] = int(i == 0)
        self.lengths = [
            max(self.sizes[s * n_fsdp : (s + 1) * n_fsdp]) for s in range(n_seq)
        ]
        self.offsets = np.concatenate([[0], np.cumsum(self.lengths)]).astype(np.int32)
        self.longest = max(self.lengths)
        self.groups = ((0, 1), (2,), (3, 4, 5, 6), (7,))
        self.starts = [int(self.offsets[group[0]]) for group in self.groups]
        self.rows = [sum(self.lengths[s] for s in group) for group in self.groups]

    def pieces(self, name, groups):
        out = []
        for i, found in enumerate(self.segments):
            s, f = divmod(i, self.n_fsdp)
            if name in found and s in groups:
                first, units, offset = found[name]
                row = int(self.offsets[s] - self.offsets[groups[0]]) + offset
                out.append((f, row, first, units))
        return out


VMEM = pl.BlockSpec(memory_space=pltpu.VMEM)
ANY = pl.BlockSpec(memory_space=pl.ANY)
SMEM = pl.BlockSpec(memory_space=pltpu.SMEM)
LIMIT = pltpu.CompilerParams(vmem_limit_bytes=60 * 1024 * 1024)


def shape(dims, dtype):
    return jax.ShapeDtypeStruct(dims, dtype)


def aligned(value, multiple):
    return pl.multiple_of(value, multiple)


def lanes(rows):
    return lax.broadcasted_iota(jnp.int32, (rows, LANE), 1)


def swap_lanes(blocks):
    blocks = list(blocks)
    at = lanes(blocks[0].shape[0]) // 16
    for step in (4, 2, 1):
        low_side = (at & step) == 0
        for one in range(TP):
            if one & step == 0:
                left, right = blocks[one], blocks[one + step]
                blocks[one] = jnp.where(low_side, left, pltpu.roll(right, 16 * step, 1))
                blocks[one + step] = jnp.where(
                    low_side, pltpu.roll(left, LANE - 16 * step, 1), right
                )
    return blocks


def shift_down(source, source_row, target, target_row, rows, block, amount, unroll):
    def step(j, tail):
        z = pltpu.roll(source[pl.ds(source_row + j * block, block), :], amount, 1)
        above = pltpu.roll(jnp.concatenate([tail, z], axis=0), 1, 0)[8:]
        target[pl.ds(target_row + j * block, block), :] = jnp.where(
            lanes(block) < amount, above, z
        )
        return z[block - 8 :]

    lax.fori_loop(0, rows // block, step, jnp.zeros((8, LANE), F32), unroll=unroll)


def pack_body(plan, tab, hd, own, hu, *rest):
    outs, (win, al, wire, sems) = rest[:TP], rest[TP:]
    s, f = lax.axis_index("seq"), lax.axis_index("fsdp")
    me = s * plan.n_fsdp + f
    total = win.shape[0]
    first = pltpu.make_async_copy(hd, win.at[pl.ds(0, HALO)], sems.at[0])
    second = pltpu.make_async_copy(own, win.at[pl.ds(HALO, plan.own_rows)], sems.at[1])
    first.start()
    second.start()
    first.wait()
    second.wait()
    seam = HALO + plan.last
    kept = win[pl.ds(seam, 8), :]
    shift_down(hu, 0, win, seam, HALO, 32, plan.part, True)
    edge = lax.broadcasted_iota(jnp.int32, (8, LANE), 0) == 0
    win[pl.ds(seam, 8), :] = jnp.where(
        edge & (lanes(8) < plan.part), kept, win[pl.ds(seam, 8), :]
    )
    shift_down(win, 0, al, 0, total, 48, tab[me, 0], 7)

    def columns(g, _):
        at = tab[me, 1] + g * 256
        to = tab[me, 3] + g * 16
        for block in range(16):
            row = to + 16 * tab[me, 2] * (block // TP)
            wire[block % TP, pl.ds(aligned(row, 16), 16), :] = al[
                pl.ds(at + block, 16, stride=16), :
            ].astype(BF16)
        return 0

    lax.fori_loop(0, tab[me, 2], columns, 0)
    for slot in (4, 10):

        def grouped(j, _):
            for owner in range(TP):
                at = tab[me, slot] + j * 1536 + owner * 192
                to = tab[me, slot + 2] + j * 16
                for block in range(12):
                    row = to + 16 * tab[me, slot + 1] * block
                    wire[owner, pl.ds(aligned(row, 16), 16), :] = al[
                        pl.ds(at + block, 16, stride=12), :
                    ].astype(BF16)
            return 0

        lax.fori_loop(0, tab[me, slot + 1], grouped, 0)

    def mixed_columns(g, _):
        at = tab[me, 7] + g * 1152
        to = tab[me, 9] + g * 32
        wide = 32 * tab[me, 8]
        last = tab[me, 9] + 4 * wide + g * 16
        for half in range(2):
            for a in range(4):
                parts = swap_lanes(
                    [
                        al[pl.ds(at + 576 * half + 8 * a + b, 16, stride=36), :]
                        for b in range(TP)
                    ]
                )
                for owner in range(TP):
                    row = to + a * wide + 16 * half
                    wire[owner, pl.ds(aligned(row, 16), 16), :] = parts[owner].astype(BF16)
        parts = swap_lanes(
            [
                al[pl.ds(at + 576 * half + 32 + b, 16, stride=36), :]
                for half in range(2)
                for b in range(4)
            ]
        )
        for owner in range(TP):
            wire[owner, pl.ds(aligned(last, 16), 16), :] = parts[owner].astype(BF16)
        return 0

    lax.fori_loop(0, tab[me, 8], mixed_columns, 0)

    @pl.when(me == 0)
    def _():
        for owner in range(TP):
            wire[owner, pl.ds(0, SMALL), :] = al[pl.ds(HALO, SMALL), :].astype(BF16)
        for kind in range(2):
            for n in range(16):
                wire[n % TP, pl.ds(SMALL + 128 * (2 * kind + n // TP), 128), :] = al[
                    pl.ds(HALO + 152 + 2048 * kind + 128 * n, 128), :
                ].astype(BF16)

    copies = [
        pltpu.make_async_copy(wire.at[s ^ k], outs[k], sems.at[2 + k]) for k in range(TP)
    ]
    for copy in copies:
        copy.start()
    for copy in copies:
        copy.wait()


def pack(plan, hd, own, hu):
    total = -(-(HALO * 2 + plan.own_rows) // 672) * 672
    return pl.pallas_call(
        partial(pack_body, plan),
        out_shape=[shape((plan.longest, LANE), BF16)] * TP,
        in_specs=[SMEM, ANY, ANY, VMEM],
        out_specs=[ANY] * TP,
        scratch_shapes=[
            pltpu.VMEM((total, LANE), F32),
            pltpu.VMEM((total, LANE), F32),
            pltpu.VMEM((TP, plan.longest, LANE), BF16),
            pltpu.SemaphoreType.DMA((2 + TP,)),
        ],
        compiler_params=LIMIT,
        name="pack",
    )(jnp.asarray(plan.table), hd, own, hu)


def order_body(plan, *refs):
    pieces, outs, sems = refs[:TP], refs[TP : TP + 4], refs[TP + 4]
    s = lax.axis_index("seq")
    for start in (True, False):
        for number, group in enumerate(plan.groups):
            for source in group:
                size = plan.lengths[source]
                at = int(plan.offsets[source]) - plan.starts[number]
                for k in range(TP):

                    @pl.when((s ^ source) == k)
                    def _():
                        copy = pltpu.make_async_copy(
                            pieces[k].at[pl.ds(0, size)],
                            outs[number].at[pl.ds(at, size)],
                            sems.at[source],
                        )
                        if start:
                            copy.start()
                        else:
                            copy.wait()


def order(plan, pieces):
    return pl.pallas_call(
        partial(order_body, plan),
        out_shape=[shape((rows, LANE), BF16) for rows in plan.rows],
        in_specs=[ANY] * TP,
        out_specs=[VMEM] * 4,
        scratch_shapes=[pltpu.SemaphoreType.DMA((TP,))],
        compiler_params=LIMIT,
        name="order",
    )(*pieces)


def weight_copies(plan, number, weights, halves, b_rows):
    out = []
    for f, row, first, units in plan.pieces("A", plan.groups[number]):
        for target, begin, end in weights.get("A", ()):
            low, high = max(first, begin), min(first + units, end)
            if high > low:
                for n in range(2):
                    out.append(
                        (
                            f,
                            row + 16 * (units * n + low - first),
                            16 * (high - low),
                            target.at[pl.ds(16 * (low - begin), 16 * (high - low)), pl.ds(128 * n, 128)],
                        )
                    )
    for f, row, first, units in plan.pieces("B", plan.groups[number]):
        if b_rows is not None:
            for block in range(12):
                out.append(
                    (
                        f,
                        row + 16 * units * block,
                        16 * units,
                        b_rows.at[block, pl.ds(16 * first, 16 * units)],
                    )
                )
    for f, row, first, units in plan.pieces("C", plan.groups[number]):
        for target, begin, end in weights.get("C", ()):
            low, high = max(first, begin), min(first + units, end)
            if high > low:
                for a in range(4):
                    out.append(
                        (
                            f,
                            row + 32 * (units * a + low - first),
                            32 * (high - low),
                            target.at[pl.ds(32 * (low - begin), 32 * (high - low)), pl.ds(128 * a, 128)],
                        )
                    )
        if halves is not None:
            out.append(
                (f, row + 128 * units, 16 * units, halves.at[pl.ds(16 * first, 16 * units)])
            )
    for f, row, first, units in plan.pieces("D", plan.groups[number]):
        for target, begin, end in weights.get("D", ()):
            for n in range(12):
                out.append(
                    (
                        f,
                        row + 16 * units * n,
                        16 * units,
                        target.at[pl.ds(16 * (first - begin), 16 * units), pl.ds(128 * n, 128)],
                    )
                )
    return out


def fetch_line(plan, line, copies, sems):
    f = lax.axis_index("fsdp")
    for start in (True, False):
        for source in range(plan.n_fsdp):
            for away in range(plan.n_fsdp):

                @pl.when((f ^ source) == away)
                def _():
                    for number, (holder, row, rows, target) in enumerate(copies):
                        if holder == source:
                            copy = pltpu.make_async_copy(
                                line[away].at[pl.ds(row, rows)], target, sems.at[number]
                            )
                            if start:
                                copy.start()
                            else:
                                copy.wait()


def first_copies(plan, small, gates, w_y, w_x, b_head):
    out = [(0, 0, SMALL, small), (0, SMALL, GATES, gates)]
    out += weight_copies(plan, 0, {"A": ((w_y, 0, 96), (w_x, 96, 192))}, None, None)
    for f, row, first, units in plan.pieces("B", plan.groups[0]):
        out.append((f, row, 192 * units, b_head.at[pl.ds(192 * first, 192 * units)]))
    return out


def first_body(plan, *refs):
    line, refs = refs[: plan.n_fsdp], refs[plan.n_fsdp :]
    *targets, sems = refs
    fetch_line(plan, line, first_copies(plan, *targets), sems)


def head_rows(plan):
    return sum(144 * p[3] for p in plan.pieces("C", plan.groups[1]))


def b_head_rows(plan):
    return sum(192 * p[3] for p in plan.pieces("B", plan.groups[0]))


class Nowhere:
    at = property(lambda self: self)

    def __getitem__(self, _):
        return self


def count_first(plan):
    return len(first_copies(plan, *[Nowhere()] * 5))


def unpack_first(plan, line):
    return pl.pallas_call(
        partial(first_body, plan),
        out_shape=[
            shape((SMALL, LANE), BF16),
            shape((GATES, LANE), BF16),
            shape((D, 256), BF16),
            shape((D, 256), BF16),
            shape((b_head_rows(plan), LANE), BF16),
        ],
        in_specs=[ANY] * len(line),
        out_specs=[VMEM] * 5,
        scratch_shapes=[pltpu.SemaphoreType.DMA((count_first(plan),))],
        compiler_params=LIMIT,
        name="unpack_first",
    )(*line)


def middle_copies(plan, b_rows, head):
    out = weight_copies(plan, 1, {}, None, b_rows)
    for f, row, first, units in plan.pieces("C", plan.groups[1]):
        out.append((f, row, 144 * units, head.at[pl.ds(144 * first, 144 * units)]))
    return out


def b_head_copies(plan, b_head, b_rows):
    out = []
    for _, _, first, units in plan.pieces("B", plan.groups[0]):
        for block in range(12):
            out.append(
                (
                    b_head.at[pl.ds(192 * first + 16 * units * block, 16 * units)],
                    b_rows.at[block, pl.ds(16 * first, 16 * units)],
                )
            )
    return out


def middle_body(plan, *refs):
    line, refs = refs[: plan.n_fsdp], refs[plan.n_fsdp :]
    b_head, outs, head, b_rows, sems, more = refs[0], refs[1 : 1 + TP], *refs[1 + TP :]
    local_copies = [
        pltpu.make_async_copy(source, target, more.at[number])
        for number, (source, target) in enumerate(b_head_copies(plan, b_head, b_rows))
    ]
    for copy in local_copies:
        copy.start()
    fetch_line(plan, line, middle_copies(plan, b_rows, head), sems)
    for copy in local_copies:
        copy.wait()
    s = lax.axis_index("seq")
    for k in range(TP):
        for n in range(2):
            unit = (s ^ k) + TP * n
            for block in range(12):
                outs[k][pl.ds(192 * n + 16 * block, 16), :] = b_rows[
                    block, pl.ds(aligned(16 * unit, 16), 16), :
                ]


def unpack_middle(plan, line, b_head):
    return pl.pallas_call(
        partial(middle_body, plan),
        out_shape=[shape((384, LANE), BF16)] * TP + [shape((head_rows(plan), LANE), BF16)],
        in_specs=[ANY] * (len(line) + 1),
        out_specs=[VMEM] * (TP + 1),
        scratch_shapes=[
            pltpu.VMEM((12, 256, LANE), BF16),
            pltpu.SemaphoreType.DMA((len(middle_copies(plan, *[Nowhere()] * 2)),)),
            pltpu.SemaphoreType.DMA((len(b_head_copies(plan, *[Nowhere()] * 2)),)),
        ],
        compiler_params=LIMIT,
        name="unpack_middle",
    )(*line, b_head)


def head_copies(plan, head, weight, halves):
    out = []
    for _, _, first, units in plan.pieces("C", plan.groups[1]):
        for a in range(4):
            out.append(
                (
                    head.at[pl.ds(144 * first + 32 * units * a, 32 * units)],
                    weight.at[pl.ds(32 * first, 32 * units), pl.ds(128 * a, 128)],
                )
            )
        out.append(
            (
                head.at[pl.ds(144 * first + 128 * units, 16 * units)],
                halves.at[pl.ds(16 * first, 16 * units)],
            )
        )
    return out


def second_copies(plan, w_gate, w_up, w_down, halves):
    return weight_copies(
        plan,
        2,
        {"C": ((w_gate, 0, 48), (w_up, 48, 96)), "D": ((w_down, 0, 16),)},
        halves,
        None,
    )


def second_body(plan, *refs):
    line, refs = refs[: plan.n_fsdp], refs[plan.n_fsdp :]
    head, w_gate, w_up, w_down, halves, sems, more = refs
    local_copies = [
        pltpu.make_async_copy(source, target, more.at[number])
        for number, (source, target) in enumerate(head_copies(plan, head, w_gate, halves))
    ]
    for copy in local_copies:
        copy.start()
    fetch_line(plan, line, second_copies(plan, w_gate, w_up, w_down, halves), sems)
    for copy in local_copies:
        copy.wait()
    for weight, begin in ((w_gate, 0), (w_up, 48)):

        def step(g, _):
            last = halves[pl.ds(aligned(16 * (begin + g), 16), 16), :]
            weight[pl.ds(aligned(32 * g, 16), 16), pl.ds(512, 64)] = last[:, :64]
            weight[pl.ds(aligned(32 * g + 16, 16), 16), pl.ds(512, 64)] = last[:, 64:]
            return 0

        lax.fori_loop(0, 48, step, 0, unroll=4)


def unpack_second(plan, line, head):
    many = len(second_copies(plan, *[Nowhere()] * 4))
    few = len(head_copies(plan, *[Nowhere()] * 3))
    return pl.pallas_call(
        partial(second_body, plan),
        out_shape=[
            shape((D, FF // TP), BF16),
            shape((D, FF // TP), BF16),
            shape((256, D), BF16),
        ],
        in_specs=[ANY] * (len(line) + 1),
        out_specs=[VMEM] * 3,
        scratch_shapes=[
            pltpu.VMEM((96 * 16, LANE), BF16),
            pltpu.SemaphoreType.DMA((many,)),
            pltpu.SemaphoreType.DMA((few,)),
        ],
        compiler_params=LIMIT,
        name="unpack_second",
    )(*line, head)


def third_copies(plan, w_down):
    return weight_copies(plan, 3, {"D": ((w_down, 0, 36),)}, None, None)


def third_body(plan, *refs):
    line, refs = refs[: plan.n_fsdp], refs[plan.n_fsdp :]
    before, w_down, sems, one = refs
    copy = pltpu.make_async_copy(before, w_down.at[pl.ds(0, 256)], one.at[0])
    copy.start()
    fetch_line(plan, line, third_copies(plan, w_down), sems)
    copy.wait()


def unpack_third(plan, line, before):
    many = len(third_copies(plan, Nowhere()))
    return pl.pallas_call(
        partial(third_body, plan),
        out_shape=shape((FF // TP, D), BF16),
        in_specs=[ANY] * (len(line) + 1),
        out_specs=VMEM,
        scratch_shapes=[
            pltpu.SemaphoreType.DMA((many,)),
            pltpu.SemaphoreType.DMA((1,)),
        ],
        compiler_params=LIMIT,
        name="unpack_third",
    )(*line, before)


def out_rows_body(*refs):
    pieces, w_out = refs[:TP], refs[TP]
    s = lax.axis_index("seq")
    for k in range(TP):
        for n in range(2):
            to = aligned(128 * n + 16 * (s ^ k), 16)
            for block in range(12):
                w_out[pl.ds(to, 16), pl.ds(128 * block, 128)] = pieces[k][
                    pl.ds(192 * n + 16 * block, 16), :
                ]


def join_out_rows(pieces):
    return pl.pallas_call(
        out_rows_body,
        out_shape=shape((256, D), BF16),
        in_specs=[VMEM] * TP,
        out_specs=VMEM,
        compiler_params=LIMIT,
        name="join_out_rows",
    )(*pieces)


def split_rows_body(grad, *pieces):
    s = lax.axis_index("seq")
    for k in range(TP):
        for n in range(2):
            at = aligned(128 * n + 16 * (s ^ k), 16)
            for block in range(12):
                pieces[k][pl.ds(192 * n + 16 * block, 16), :] = grad[
                    pl.ds(at, 16), pl.ds(128 * block, 128)
                ]


def split_out_rows(grad):
    return pl.pallas_call(
        split_rows_body,
        out_shape=[shape((384, LANE), F32)] * TP,
        in_specs=[VMEM],
        out_specs=[VMEM] * TP,
        compiler_params=LIMIT,
        name="split_out_rows",
    )(grad)


def run_copies(copies, sems):
    made = [
        pltpu.make_async_copy(source, target, sems.at[number])
        for number, (source, target) in enumerate(copies)
    ]
    for copy in made:
        copy.start()
    for copy in made:
        copy.wait()


def to_wire(copies, wire):
    return [(source, wire.at[f, pl.ds(row, rows)]) for f, row, rows, source in copies]


def wire_second_body(plan, g_gate, g_up, g_down, wire, head, halves, sems):
    for grad, begin in ((g_gate, 0), (g_up, 48)):

        def step(g, _):
            left = grad[pl.ds(aligned(32 * g, 16), 16), pl.ds(512, 64)]
            right = grad[pl.ds(aligned(32 * g + 16, 16), 16), pl.ds(512, 64)]
            halves[pl.ds(aligned(16 * (begin + g), 16), 16), :] = jnp.concatenate(
                [left, right], axis=1
            )
            return 0

        lax.fori_loop(0, 48, step, 0, unroll=4)
    copies = to_wire(second_copies(plan, g_gate, g_up, g_down, halves), wire)
    copies += [(b, a) for a, b in head_copies(plan, head, g_gate, halves)]
    run_copies(copies, sems)


def wire_second(plan, g_gate, g_up, g_down):
    many = len(second_copies(plan, *[Nowhere()] * 4)) + len(
        head_copies(plan, *[Nowhere()] * 3)
    )
    return pl.pallas_call(
        partial(wire_second_body, plan),
        out_shape=[
            shape((plan.n_fsdp, plan.rows[2], LANE), F32),
            shape((head_rows(plan), LANE), F32),
        ],
        in_specs=[VMEM] * 3,
        out_specs=[ANY] * 2,
        scratch_shapes=[
            pltpu.VMEM((96 * 16, LANE), F32),
            pltpu.SemaphoreType.DMA((many,)),
        ],
        compiler_params=LIMIT,
        name="wire_second",
    )(g_gate, g_up, g_down)


def wire_third_body(plan, g_down, wire, sems):
    run_copies(to_wire(third_copies(plan, g_down), wire), sems)


def wire_third(plan, g_down):
    many = len(third_copies(plan, Nowhere()))
    return pl.pallas_call(
        partial(wire_third_body, plan),
        out_shape=shape((plan.n_fsdp, plan.rows[3], LANE), F32),
        in_specs=[VMEM],
        out_specs=ANY,
        scratch_shapes=[pltpu.SemaphoreType.DMA((many,))],
        compiler_params=LIMIT,
        name="wire_third",
    )(g_down)


def wire_middle_body(plan, head, *refs):
    pieces, (wire, b_head, b_rows, sems) = refs[:TP], refs[TP:]
    s = lax.axis_index("seq")
    for k in range(TP):
        for n in range(2):
            unit = (s ^ k) + TP * n
            for block in range(12):
                b_rows[block, pl.ds(aligned(16 * unit, 16), 16), :] = pieces[k][
                    pl.ds(192 * n + 16 * block, 16), :
                ]
    copies = to_wire(middle_copies(plan, b_rows, head), wire)
    copies += [(b, a) for a, b in b_head_copies(plan, b_head, b_rows)]
    run_copies(copies, sems)


def wire_middle(plan, head, pieces):
    many = len(middle_copies(plan, *[Nowhere()] * 2)) + len(
        b_head_copies(plan, *[Nowhere()] * 2)
    )
    return pl.pallas_call(
        partial(wire_middle_body, plan),
        out_shape=[
            shape((plan.n_fsdp, plan.rows[1], LANE), F32),
            shape((b_head_rows(plan), LANE), F32),
        ],
        in_specs=[VMEM] * (1 + TP),
        out_specs=[ANY] * 2,
        scratch_shapes=[
            pltpu.VMEM((12, 256, LANE), F32),
            pltpu.SemaphoreType.DMA((many,)),
        ],
        compiler_params=LIMIT,
        name="wire_middle",
    )(head, *pieces)


def split_copies(plan, copies):
    border = int(plan.offsets[1])
    return (
        [copy for copy in copies if copy[1] < border],
        [(f, row - border, rows, at) for f, row, rows, at in copies if row >= border],
    )


def wire_x_body(plan, g_x, b_head, wire, sems):
    copies = first_copies(plan, Nowhere(), Nowhere(), Nowhere(), g_x, b_head)
    run_copies(to_wire(split_copies(plan, copies)[1], wire), sems)


def wire_x(plan, g_x, b_head):
    return pl.pallas_call(
        partial(wire_x_body, plan),
        out_shape=shape((plan.n_fsdp, plan.lengths[1], LANE), F32),
        in_specs=[VMEM] * 2,
        out_specs=ANY,
        scratch_shapes=[pltpu.SemaphoreType.DMA((count_first(plan),))],
        compiler_params=LIMIT,
        name="wire_x",
    )(g_x, b_head)


def wire_y_body(plan, gains, vectors, gates, g_y, g_x, wire, small, sems):
    s = lax.axis_index("seq")
    small[...] = jnp.zeros_like(small)
    small[pl.ds(0, 24), :] = gains[...]
    for n in range(8):
        for part in range(2):
            small[pl.ds(24 + 16 * n + s + TP * part, 1), :] = vectors[
                pl.ds(2 * n + part, 1), :
            ]
    copies = first_copies(plan, small, gates, g_y, g_x, Nowhere())
    run_copies(to_wire(split_copies(plan, copies)[0], wire), sems)


def wire_y(plan, gains, vectors, gates, g_y, g_x):
    return pl.pallas_call(
        partial(wire_y_body, plan),
        out_shape=shape((plan.n_fsdp, plan.lengths[0], LANE), F32),
        in_specs=[VMEM] * 5,
        out_specs=ANY,
        scratch_shapes=[
            pltpu.VMEM((SMALL, LANE), F32),
            pltpu.SemaphoreType.DMA((count_first(plan),)),
        ],
        compiler_params=LIMIT,
        name="wire_y",
    )(gains, vectors, gates, g_y, g_x)


def spread_body(plan, targets, *refs):
    count = len(targets)
    sums, outs, sems = refs[:count], refs[count : count + TP], refs[count + TP]
    s = lax.axis_index("seq")
    for start in (True, False):
        for summed, group in zip(sums, targets):
            for target in group:
                size = plan.lengths[target]
                at = int(plan.offsets[target] - plan.offsets[group[0]])
                for k in range(TP):

                    @pl.when((s ^ target) == k)
                    def _():
                        copy = pltpu.make_async_copy(
                            summed.at[pl.ds(at, size)],
                            outs[k].at[pl.ds(0, size)],
                            sems.at[target],
                        )
                        if start:
                            copy.start()
                        else:
                            copy.wait()


def spread(plan, targets, sums):
    rows = max(plan.lengths[s] for group in targets for s in group)
    return pl.pallas_call(
        partial(spread_body, plan, targets),
        out_shape=[shape((rows, LANE), F32)] * TP,
        in_specs=[VMEM] * len(sums),
        out_specs=[ANY] * TP,
        scratch_shapes=[pltpu.SemaphoreType.DMA((TP,))],
        compiler_params=LIMIT,
    )(*sums)


def shift_up(source, source_row, target, target_row, rows, block, amount):
    def step(j, _):
        both = pltpu.roll(source[pl.ds(source_row + j * block, block + 8), :], amount, 1)
        below = pltpu.roll(both, block + 7, 0)[:block]
        target[pl.ds(target_row + j * block, block), :] = jnp.where(
            lanes(block) < amount, both[:block], below
        )
        return 0

    lax.fori_loop(0, rows // block, step, 0, unroll=True)


def collect_body(plan, tab, *refs):
    pieces, (own, hd, hu, al, win, wire, sems) = refs[: 3 * TP], refs[3 * TP :]
    s, f = lax.axis_index("seq"), lax.axis_index("fsdp")
    me = s * plan.n_fsdp + f

    def bring(start):
        for number in range(3):

            @pl.when(jnp.minimum(s, 2) == number)
            def _():
                for k in range(TP):
                    piece = pieces[TP * number + k]
                    copy = pltpu.make_async_copy(
                        piece, wire.at[s ^ k, pl.ds(0, piece.shape[0])], sems.at[k]
                    )
                    if start:
                        copy.start()
                    else:
                        copy.wait()

    bring(True)
    total = win.shape[0]

    def clear(j, _):
        al[pl.ds(aligned(j * 96, 8), 96), :] = jnp.zeros((96, LANE), F32)
        return 0

    lax.fori_loop(0, al.shape[0] // 96, clear, 0, unroll=4)
    bring(False)

    def columns(g, _):
        at = tab[me, 1] + g * 256
        to = tab[me, 3] + g * 16
        for block in range(16):
            row = to + 16 * tab[me, 2] * (block // TP)
            al[pl.ds(at + block, 16, stride=16), :] = wire[
                block % TP, pl.ds(aligned(row, 16), 16), :
            ]
        return 0

    lax.fori_loop(0, tab[me, 2], columns, 0)
    for slot in (4, 10):

        def grouped(j, _):
            for owner in range(TP):
                at = tab[me, slot] + j * 1536 + owner * 192
                to = tab[me, slot + 2] + j * 16
                for block in range(12):
                    row = to + 16 * tab[me, slot + 1] * block
                    al[pl.ds(at + block, 16, stride=12), :] = wire[
                        owner, pl.ds(aligned(row, 16), 16), :
                    ]
            return 0

        lax.fori_loop(0, tab[me, slot + 1], grouped, 0)

    def mixed_columns(g, _):
        at = tab[me, 7] + g * 1152
        to = tab[me, 9] + g * 32
        wide = 32 * tab[me, 8]
        last = tab[me, 9] + 4 * wide + g * 16
        for half in range(2):
            for a in range(4):
                parts = swap_lanes(
                    [
                        wire[owner, pl.ds(aligned(to + a * wide + 16 * half, 16), 16), :]
                        for owner in range(TP)
                    ]
                )
                for b in range(TP):
                    al[pl.ds(at + 576 * half + 8 * a + b, 16, stride=36), :] = parts[b]
        parts = swap_lanes(
            [wire[owner, pl.ds(aligned(last, 16), 16), :] for owner in range(TP)]
        )
        for half in range(2):
            for b in range(4):
                al[pl.ds(at + 576 * half + 32 + b, 16, stride=36), :] = parts[4 * half + b]
        return 0

    lax.fori_loop(0, tab[me, 8], mixed_columns, 0)

    @pl.when(me == 0)
    def _():
        summed = wire[0, pl.ds(0, 152), :]
        for owner in range(1, TP):
            summed = summed + wire[owner, pl.ds(0, 152), :]
        al[pl.ds(HALO, 152), :] = summed
        for kind in range(2):
            for n in range(16):
                al[pl.ds(HALO + 152 + 2048 * kind + 128 * n, 128), :] = wire[
                    n % TP, pl.ds(SMALL + 128 * (2 * kind + n // TP), 128), :
                ]

    def back(j, _):
        both = pltpu.roll(
            al[pl.ds(aligned(j * 48, 8), 56), :], lax.rem(LANE - tab[me, 0], LANE), 1
        )
        below = pltpu.roll(both, 55, 0)[:48]
        win[pl.ds(aligned(j * 48, 8), 48), :] = jnp.where(
            lanes(48) < LANE - tab[me, 0], both[:48], below
        )
        return 0

    lax.fori_loop(0, total // 48, back, 0, unroll=7)
    hd[...] = win[pl.ds(0, HALO), :]
    own[...] = win[pl.ds(HALO, plan.own_rows), :]
    shift_up(win, HALO + plan.last, hu, 0, HALO, 32, LANE - plan.part)


def collect(plan, pieces):
    total = -(-(HALO * 2 + plan.own_rows) // 672) * 672
    cleared = total + 96
    return pl.pallas_call(
        partial(collect_body, plan),
        out_shape=[
            shape((plan.own_rows, LANE), F32),
            shape((HALO, LANE), F32),
            shape((HALO, LANE), F32),
        ],
        in_specs=[SMEM] + [ANY] * (3 * TP),
        out_specs=[VMEM] * 3,
        scratch_shapes=[
            pltpu.VMEM((cleared, LANE), F32),
            pltpu.VMEM((total, LANE), F32),
            pltpu.VMEM((TP, plan.longest, LANE), F32),
            pltpu.SemaphoreType.DMA((TP,)),
        ],
        compiler_params=LIMIT,
        name="collect",
    )(jnp.asarray(plan.table), *pieces)


def tail_body(plan, value, out):
    first = (plan.last - HALO) % 8
    out[...] = jnp.zeros_like(out)
    shift_down(value, 0, out, first, HALO, 32, plan.part, True)
    z = pltpu.roll(value[pl.ds(HALO - 8, 8), :], plan.part, 1)
    row = lax.broadcasted_iota(jnp.int32, (8, LANE), 0)
    out[pl.ds(first + HALO, 8), :] = jnp.where(
        (row == 0) & (lanes(8) < plan.part), pltpu.roll(z, 1, 0), 0.0
    )


def place_tail(plan, value):
    rows = plan.own_rows - (plan.last - HALO) // 8 * 8
    return pl.pallas_call(
        partial(tail_body, plan),
        out_shape=shape((max(rows, HALO + 16), LANE), F32),
        in_specs=[VMEM],
        out_specs=VMEM,
        compiler_params=LIMIT,
        name="place_tail",
    )(value)[:rows]


def scan_body(reverse, coefficient, addend, out):
    rows, width = coefficient.shape
    at = lax.broadcasted_iota(jnp.int32, (8, width), 0)
    if reverse:
        at = 7 - at
    steps = rows // 8

    def step(j, carry):
        block = steps - 1 - j if reverse else j
        here = pl.ds(aligned(block * 8, 8), 8)
        a, b = coefficient[here, :], addend[here, :]
        for reach in (1, 2, 4):
            turn = 8 - reach if reverse else reach
            inside = at >= reach
            b = b + jnp.where(inside, a * pltpu.roll(b, turn, 0), 0.0)
            a = jnp.where(inside, a * pltpu.roll(a, turn, 0), a)
        value = b + a * carry
        out[here, :] = value
        edge = value[0:1] if reverse else value[7:8]
        return jnp.broadcast_to(edge, (8, width))

    lax.fori_loop(0, steps, step, jnp.zeros((8, width), F32), unroll=4)


def linear_scan(coefficient, addend, reverse):
    return pl.pallas_call(
        partial(scan_body, reverse),
        out_shape=shape(coefficient.shape, F32),
        in_specs=[VMEM] * 2,
        out_specs=VMEM,
        compiler_params=LIMIT,
        name="scan_back" if reverse else "scan",
    )(coefficient, addend)


def swap(value, bit):
    return lax.ppermute(value, "seq", [(i, i ^ bit) for i in range(TP)])


def exchange(pieces, targets=range(TP)):
    return [pieces[0]] + [
        lax.ppermute(pieces[k], "seq", [(i ^ k, i) for i in targets]) for k in range(1, TP)
    ]


def gather_stream(mine):
    half = mine.shape[0] // 2
    over_x, over_y = swap(mine, 2), swap(mine, 4)
    over_xy = [swap(over_x[:half], 4), swap(over_y[half:], 2)]
    chip = [mine, over_x, over_y] + over_xy
    return jnp.concatenate(chip + [swap(part, 1) for part in chip], axis=0)


def scatter_stream(partial_sums):
    rows = partial_sums.shape[0] // TP
    half = rows // 2
    other = swap(partial_sums[TP // 2 * rows :].astype(BF16), 1)
    q = (partial_sums[: TP // 2 * rows] + other.astype(F32)).reshape(4, rows, -1)
    up = swap(jnp.concatenate([q[1, :half], q[3, :half]]).astype(BF16), 2).astype(F32)
    down = swap(jnp.concatenate([q[2, half:], q[3, half:]]).astype(BF16), 4).astype(F32)
    top = swap((q[2, :half] + up[half:]).astype(BF16), 4).astype(F32)
    low = swap((q[1, half:] + down[half:]).astype(BF16), 2).astype(F32)
    return jnp.concatenate(
        [q[0, :half] + up[:half] + top, q[0, half:] + down[:half] + low], axis=0
    )


def to_positions(values, s):
    rows = values.shape[0] // TP
    parts = []
    for j in range(TP):
        k = s ^ j
        at = (k // 2 + 4 * (k % 2)) * rows
        parts.append(lax.dynamic_slice_in_dim(values, at, rows, 0))
    return jnp.concatenate(parts, axis=0)


def to_relative(values, s):
    rows = values.shape[0] // TP
    return jnp.concatenate(
        [lax.dynamic_slice_in_dim(values, (s ^ k) * rows, rows, 0) for k in EVEN_FIRST], axis=0
    )


def gather_line(value, count):
    out = [value]
    for x in range(1, count):
        out.append(lax.ppermute(value, "fsdp", [(i, i ^ x) for i in range(count)]))
    return out


def scatter_line(blocks, f):
    def own(j):
        return lax.dynamic_index_in_dim(blocks, j, 0, keepdims=False)

    count = blocks.shape[0]
    far, near = own(f ^ 2), own(f ^ 1)
    far = lax.ppermute(far, "fsdp", [(i, i ^ 1) for i in range(count)])
    near = lax.ppermute(near, "fsdp", [(i, i ^ 1) for i in range(count)])
    crossed = lax.ppermute(own(f ^ 3) + far, "fsdp", [(i, i ^ 3) for i in range(count)])
    return own(f) + near + crossed


def sliced(plan, *arguments):
    return sliced_step(plan, *arguments)


def sliced_step(plan, stream_in, cotangent, starts, params, momentum, average):
    n_fsdp = plan.n_fsdp
    s, f = lax.axis_index("seq"), lax.axis_index("fsdp")
    shards = TP * n_fsdp
    onward = [(i, i + 1) for i in range(shards - 1)]
    backward = [(i + 1, i) for i in range(shards - 1)]
    both = ("seq", "fsdp")
    edge = HALO * LANE
    per = plan.per

    hd, hu = lax.optimization_barrier((params[per - edge :], params[:edge]))
    hd = lax.ppermute(hd.astype(BF16), both, onward)
    hu = lax.ppermute(hu.astype(BF16), both, backward)
    own = jnp.pad(params, (0, plan.own_rows * LANE - per)).reshape(-1, LANE)
    pieces = pack(
        plan, hd.astype(F32).reshape(-1, LANE), own, hu.astype(F32).reshape(-1, LANE)
    )
    first, middle_wire, second, third = order(plan, exchange(pieces))
    stream_bf, first = lax.optimization_barrier((stream_in[0], first))
    line = gather_line(first, n_fsdp)
    small, gates, w_y, w_x, b_head = unpack_first(plan, line)
    line = gather_line(middle_wire, n_fsdp)
    *out_rows, head = unpack_middle(plan, line, b_head)
    w_out = join_out_rows(exchange(out_rows))
    line = gather_line(second, n_fsdp)
    w_gate, w_up, w_down = unpack_second(plan, line, head)
    w_down = unpack_third(plan, gather_line(third, n_fsdp), w_down)

    mine = stream_in[0].astype(F32)
    stream = gather_stream(stream_bf)
    cotangent_bf, stream = lax.optimization_barrier((cotangent[0], stream))
    stream = stream.astype(F32)
    grad_out = gather_stream(cotangent_bf)
    rows = stream.shape[0]

    small = small.astype(F32)
    gain_one = small[0:12].reshape(-1)
    gain_two = small[12:24].reshape(-1)

    def channels(at):
        return jnp.concatenate(
            [
                lax.dynamic_slice_in_dim(small, at + s, 1, 0),
                lax.dynamic_slice_in_dim(small, at + s + TP, 1, 0),
            ],
            axis=1,
        )[0]

    conv_bias, bias_a, bias_i, lambda_raw = (channels(24 + 16 * j) for j in range(4))
    conv_weight = jnp.stack([channels(88 + 16 * j) for j in range(KW)])

    positions = jnp.arange(rows, dtype=jnp.int32)
    ext_pos = jnp.arange(rows + KW - 1, dtype=jnp.int32) - (KW - 1)
    segment_ext = segment_ids(ext_pos, starts[0])
    starting = start_flags(positions, starts[0])[:, None]

    def gate_product(values, at):
        return jnp.concatenate(
            [matmul(values[:, :HB], gates[at : at + HB]), matmul(values[:, HB:], gates[at + HB : at + 2 * HB])],
            axis=1,
        )

    def gate_product_t(values, at):
        return jnp.concatenate(
            [matmul_t(values[:, :HB], gates[at : at + HB]), matmul_t(values[:, HB:], gates[at + HB : at + 2 * HB])],
            axis=1,
        )

    normed = rms_norm(stream, gain_one).astype(BF16)
    branch_y = to_positions(matmul(normed, w_y), s)
    branch_x = to_positions(matmul(normed, w_x).astype(BF16), s)
    extended = jnp.pad(branch_x, ((KW - 1, 0), (0, 0))).astype(F32)

    def convolve_here(extended, weight, bias):
        total = jnp.zeros((rows, bias.shape[0]), F32) + bias
        for lag in range(KW):
            source = extended[KW - 1 - lag : KW - 1 - lag + rows]
            same = segment_ext[KW - 1 - lag : KW - 1 - lag + rows] == segment_ext[KW - 1 :]
            total = total + weight[lag] * source * same.astype(F32)[:, None]
        return total

    conv_out = convolve_here(extended, conv_weight, conv_bias).astype(BF16)
    conv_val = conv_out.astype(F32)
    pre_a = gate_product(conv_out, 0) + bias_a
    pre_i = gate_product(conv_out, 2 * HB) + bias_i
    decay, drive = gate_terms(pre_a, pre_i, conv_val, lambda_raw, starting)
    state = linear_scan(decay, drive, False)
    gelu_y = jax.nn.gelu(branch_y, approximate=True)
    mixed = to_relative((state * gelu_y).astype(BF16), s)
    middle = mine + scatter_stream(matmul(mixed, w_out))
    normed_two_mine = rms_norm(middle, gain_two).astype(BF16)
    normed_two = gather_stream(normed_two_mine)
    gate = matmul(normed_two, w_gate)
    upward = matmul(normed_two, w_up)
    hidden = gelu_product(gate, upward).astype(BF16)
    output = (middle + scatter_stream(matmul(hidden, w_down))).astype(BF16)

    g_down = t_matmul(hidden, grad_out)
    summed_three = scatter_line(wire_third(plan, g_down), f)
    grad_hidden = matmul_t(grad_out, w_down)
    _, product_back = jax.vjp(gelu_product, gate, upward)
    grad_gate, grad_up = product_back(grad_hidden)
    grad_gate, grad_up = grad_gate.astype(BF16), grad_up.astype(BF16)
    g_gate = t_matmul(normed_two, grad_gate)
    g_up = t_matmul(normed_two, grad_up)
    grad_normed_two = scatter_stream(matmul_t(grad_gate, w_gate) + matmul_t(grad_up, w_up))
    wire_two, wire_head = wire_second(plan, g_gate, g_up, g_down)
    summed_two = scatter_line(wire_two, f)

    _, norm_back_two = jax.vjp(rms_norm, middle, gain_two)
    grad_middle_part, g_gain_two = norm_back_two(grad_normed_two)
    grad_middle = cotangent[0].astype(F32) + grad_middle_part
    grad_first = gather_stream(grad_middle.astype(BF16))
    g_out = t_matmul(mixed, grad_first)
    wire_mid, b_head = wire_middle(plan, wire_head, exchange(split_out_rows(g_out)))
    summed_mid = scatter_line(wire_mid, f)
    grad_mixed = to_positions(matmul_t(grad_first, w_out), s)
    _, gelu_back = jax.vjp(partial(jax.nn.gelu, approximate=True), branch_y)
    grad_y = gelu_back(grad_mixed * state)[0].astype(BF16)
    next_decay = jnp.concatenate([decay[1:], jnp.ones((1, decay.shape[1]), F32)], axis=0)
    adjoint = linear_scan(next_decay, grad_mixed * gelu_y, True)
    previous = jnp.concatenate([jnp.zeros((1, decay.shape[1]), F32), state[:-1]], axis=0)
    _, gates_back = jax.vjp(gate_terms, pre_a, pre_i, conv_val, lambda_raw, starting)
    grad_pre_a, grad_pre_i, grad_direct, g_lambda, _ = gates_back((adjoint * previous, adjoint))
    grad_pre_a, grad_pre_i = grad_pre_a.astype(BF16), grad_pre_i.astype(BF16)
    g_gates = jnp.concatenate(
        [
            t_matmul(conv_out[:, n : n + HB], grad[:, n : n + HB])
            for grad in (grad_pre_a, grad_pre_i)
            for n in (0, HB)
        ],
        axis=0,
    )
    g_bias_a = jnp.sum(grad_pre_a.astype(F32), axis=0)
    g_bias_i = jnp.sum(grad_pre_i.astype(F32), axis=0)
    grad_conv = grad_direct + gate_product_t(grad_pre_a, 0) + gate_product_t(grad_pre_i, 2 * HB)
    _, conv_back = jax.vjp(convolve_here, extended, conv_weight, conv_bias)
    grad_ext, g_conv_weight, g_conv_bias = conv_back(grad_conv)
    grad_x = to_relative(grad_ext[KW - 1 :].astype(BF16), s)
    grad_y = to_relative(grad_y, s)
    g_x = t_matmul(normed, grad_x)
    g_y = t_matmul(normed, grad_y)
    grad_normed = scatter_stream(matmul_t(grad_y, w_y) + matmul_t(grad_x, w_x))
    _, norm_back_one = jax.vjp(rms_norm, mine, gain_one)
    grad_stream_part, g_gain_one = norm_back_one(grad_normed)
    input_grad = grad_middle + grad_stream_part

    summed_x = scatter_line(wire_x(plan, g_x, b_head), f)
    gains = jnp.concatenate([g_gain_one, g_gain_two]).reshape(-1, LANE)
    vectors = jnp.stack(
        [g_conv_bias, g_bias_a, g_bias_i, g_lambda] + [g_conv_weight[k] for k in range(KW)]
    ).reshape(-1, LANE)
    summed_y = scatter_line(wire_y(plan, gains, vectors, g_gates, g_y, g_x), f)
    early = spread(plan, plan.groups[1:], (summed_mid, summed_two, summed_three))
    got = exchange(spread(plan, ((0,),), (summed_y,)), (0,))
    got += exchange(spread(plan, ((1,),), (summed_x,)), (1,))
    got += exchange(early, range(2, TP))
    grad_own, grad_hd, grad_hu = collect(plan, got)
    from_next = lax.ppermute(grad_hd, both, backward)
    from_before = lax.ppermute(grad_hu, both, onward)
    tail = place_tail(plan, from_next).reshape(-1)
    whole = plan.own_rows * LANE
    summed = (
        grad_own.reshape(-1)
        + jnp.pad(from_before.reshape(-1), (0, whole - edge))
        + jnp.pad(tail, (whole - tail.shape[0], 0))
    )[:per]
    new_moment = MOMENT * momentum + summed
    new_params = params - RATE * (summed + MOMENT * new_moment)
    new_average = BLEND * average + (1.0 - BLEND) * new_params
    return (output[None], input_grad[None], new_params, new_moment, new_average)


def solution(mesh):
    n_seq, n_fsdp = mesh.shape["seq"], mesh.shape["fsdp"]
    fast = (n_seq, n_fsdp) == (TP, 4)
    body = partial(sliced, Plan(n_seq, n_fsdp)) if fast else local
    return jax.shard_map(
        body,
        mesh=mesh,
        in_specs=(
            P("fsdp", "seq", None),
            P("fsdp", "seq", None),
            P("fsdp", None),
            P(("seq", "fsdp")),
            P(("seq", "fsdp")),
            P(("seq", "fsdp")),
        ),
        out_specs=(
            P("fsdp", "seq", None),
            P("fsdp", "seq", None),
            P(("seq", "fsdp")),
            P(("seq", "fsdp")),
            P(("seq", "fsdp")),
        ),
        check_vma=False,
    )
```

```python
from functools import partial
import math

import jax
import jax.numpy as jnp
import numpy as np
from jax import lax
from jax.experimental import pallas as pl
from jax.experimental.pallas import tpu as pltpu
from jax.sharding import PartitionSpec as P


D = 1536
LRU = 2048
FF = 4608
HB = 128
KW = 4


EPS = 1e-06
RATE = 3e-05
MOMENT = 0.9
BLEND = 0.9
DECAY_SCALE = 8.0


def shifted(block, axis, distance):
    devices = range(lax.axis_size(axis))
    route = [(i - distance, i) for i in devices if i - distance in devices]
    return lax.ppermute(block, axis, route)


def carried_in(value, axis, join, neutral, backward):
    count, mine = (lax.axis_size(axis), lax.axis_index(axis))
    pieces = jax.tree.map(lambda part: lax.all_gather(part, axis), value)
    if backward:
        pieces = jax.tree.map(lambda part: part[::-1], pieces)
        mine = count - 1 - mine
    so_far = jax.tree.map(
        lambda part, zero: jnp.full_like(part, 0) + jnp.asarray(zero, part.dtype), value, neutral
    )

    def lap(position, so_far):
        longer = join(so_far, jax.tree.map(lambda part: part[position], pieces))
        return jax.tree.map(lambda new, old: jnp.where(position < mine, new, old), longer, so_far)

    return lax.fori_loop(0, count - 1, lap, so_far)


def layout():
    return [
        ("gain_one", (D,)),
        ("gain_two", (D,)),
        ("conv_bias", (LRU,)),
        ("bias_a", (LRU,)),
        ("bias_i", (LRU,)),
        ("lambda_raw", (LRU,)),
        ("conv_weight", (KW, LRU)),
        ("gate_a", (LRU // HB, HB, HB)),
        ("gate_i", (LRU // HB, HB, HB)),
        ("w_y", (D, LRU)),
        ("w_x", (D, LRU)),
        ("w_out", (LRU, D)),
        ("w_gate", (D, FF)),
        ("w_up", (D, FF)),
        ("w_down", (FF, D)),
    ]


def unpack(packed):
    result = {}
    offset = 0
    for entry_name, entry_shape in layout():
        amount = math.prod(entry_shape)
        result[entry_name] = packed[offset : offset + amount].reshape(entry_shape)
        offset += amount
    return result


def matmul(left, right):
    return jnp.dot(left, right, preferred_element_type=jnp.float32)


def matmul_t(left, right):
    return lax.dot_general(
        left, right, (((1,), (1,)), ((), ())), preferred_element_type=jnp.float32
    )


def t_matmul(left, right):
    return lax.dot_general(
        left, right, (((0,), (0,)), ((), ())), preferred_element_type=jnp.float32
    )


def blocked(values, weight):
    shaped = values.reshape(values.shape[0], LRU // HB, HB)
    return jnp.einsum("tnh,nhk->tnk", shaped, weight, preferred_element_type=jnp.float32).reshape(
        values.shape[0], LRU
    )


def blocked_t(values, weight):
    shaped = values.reshape(values.shape[0], LRU // HB, HB)
    return jnp.einsum("tnk,nhk->tnh", shaped, weight, preferred_element_type=jnp.float32).reshape(
        values.shape[0], LRU
    )


def blocked_grad(inputs, grads):
    left = inputs.reshape(inputs.shape[0], LRU // HB, HB)
    right = grads.reshape(grads.shape[0], LRU // HB, HB)
    return jnp.einsum("tnh,tnk->nhk", left, right, preferred_element_type=jnp.float32)


def rms_norm(values, gain):
    return values * lax.rsqrt(jnp.mean(values * values, axis=-1, keepdims=True) + EPS) * gain


def combine(earlier, later):
    return (earlier[0] * later[0], later[0] * earlier[1] + later[1])


def gate_terms(pre_a, pre_i, conv_val, lambda_raw, starting):
    recall = jax.nn.sigmoid(pre_a)
    admit = jax.nn.sigmoid(pre_i)
    rate = DECAY_SCALE * jax.nn.softplus(lambda_raw) * recall
    decay = (1.0 - starting) * jnp.exp(-rate)
    scale_in = starting + (1.0 - starting) * jnp.sqrt(-jnp.expm1(-2.0 * rate))
    return (decay, scale_in * admit * conv_val)


def convolve(extended, weight, bias, segment_ext, rows):
    total = jnp.zeros((rows, LRU), jnp.float32) + bias
    for lag in range(KW):
        source = extended[KW - 1 - lag : KW - 1 - lag + rows]
        same = (segment_ext[KW - 1 - lag : KW - 1 - lag + rows] == segment_ext[KW - 1 :]).astype(
            jnp.float32
        )
        total = total + weight[lag] * source * same[:, None]
    return total


def segment_ids(positions, doc_starts):
    return jnp.sum((doc_starts[None, :] <= positions[:, None]).astype(jnp.int32), axis=1)


def start_flags(positions, doc_starts):
    return jnp.max((doc_starts[None, :] == positions[:, None]).astype(jnp.float32), axis=1)


def gelu_product(left, right):
    return jax.nn.gelu(left, approximate=True) * right


def local(stream_in, cotangent, starts, params, momentum, average):
    weights = unpack(
        lax.all_gather(params.astype(jnp.bfloat16), ("seq", "fsdp"), axis=0, tiled=True)
    )
    stream = stream_in[0].astype(jnp.float32)
    incoming = cotangent[0].astype(jnp.float32)
    doc_starts = starts[0]
    rows = stream.shape[0]
    positions = lax.axis_index("seq") * rows + jnp.arange(rows, dtype=jnp.int32)
    ext_pos = positions[0] - (KW - 1) + jnp.arange(rows + KW - 1, dtype=jnp.int32)
    segment_ext = segment_ids(ext_pos, doc_starts)
    starting = start_flags(positions, doc_starts)[:, None]
    gain_one = weights["gain_one"].astype(jnp.float32)
    gain_two = weights["gain_two"].astype(jnp.float32)
    conv_weight = weights["conv_weight"].astype(jnp.float32)
    conv_bias = weights["conv_bias"].astype(jnp.float32)
    lambda_raw = weights["lambda_raw"].astype(jnp.float32)
    normed = rms_norm(stream, gain_one).astype(jnp.bfloat16)
    branch_y = matmul(normed, weights["w_y"])
    branch_x = matmul(normed, weights["w_x"]).astype(jnp.bfloat16)
    edge = shifted(branch_x[rows - (KW - 1) :], "seq", 1)
    extended = jnp.concatenate([edge, branch_x], axis=0).astype(jnp.float32)
    conv_out = convolve(extended, conv_weight, conv_bias, segment_ext, rows).astype(jnp.bfloat16)
    conv_val = conv_out.astype(jnp.float32)
    pre_a = blocked(conv_out, weights["gate_a"]) + weights["bias_a"].astype(jnp.float32)
    pre_i = blocked(conv_out, weights["gate_i"]) + weights["bias_i"].astype(jnp.float32)
    decay, drive = gate_terms(pre_a, pre_i, conv_val, lambda_raw, starting)
    prod_local, state_local = lax.associative_scan(combine, (decay, drive), axis=0)
    neutral = (jnp.ones((LRU,), jnp.float32), jnp.zeros((LRU,), jnp.float32))
    carried = carried_in((prod_local[-1], state_local[-1]), "seq", combine, neutral, False)
    carry_in = carried[1]
    state = lax.associative_scan(combine, (decay, drive.at[0].add(decay[0] * carry_in)), axis=0)[1]
    gelu_y = jax.nn.gelu(branch_y, approximate=True)
    mixed = (state * gelu_y).astype(jnp.bfloat16)
    middle = stream + matmul(mixed, weights["w_out"])
    normed_two = rms_norm(middle, gain_two).astype(jnp.bfloat16)
    gate = matmul(normed_two, weights["w_gate"])
    upward = matmul(normed_two, weights["w_up"])
    hidden = gelu_product(gate, upward).astype(jnp.bfloat16)
    output = (middle + matmul(hidden, weights["w_down"])).astype(jnp.bfloat16)
    grads = {}
    grad_out = incoming.astype(jnp.bfloat16)
    grads["w_down"] = t_matmul(hidden, grad_out)
    grad_hidden = matmul_t(grad_out, weights["w_down"])
    _, product_back = jax.vjp(gelu_product, gate, upward)
    grad_gate, grad_up = product_back(grad_hidden)
    grad_gate = grad_gate.astype(jnp.bfloat16)
    grad_up = grad_up.astype(jnp.bfloat16)
    grads["w_gate"] = t_matmul(normed_two, grad_gate)
    grads["w_up"] = t_matmul(normed_two, grad_up)
    grad_normed_two = matmul_t(grad_gate, weights["w_gate"]) + matmul_t(grad_up, weights["w_up"])
    _, norm_back_two = jax.vjp(rms_norm, middle, gain_two)
    grad_middle_part, grads["gain_two"] = norm_back_two(grad_normed_two)
    grad_middle = incoming + grad_middle_part
    grad_first = grad_middle.astype(jnp.bfloat16)
    grads["w_out"] = t_matmul(mixed, grad_first)
    grad_mixed = matmul_t(grad_first, weights["w_out"])
    _, gelu_back = jax.vjp(partial(jax.nn.gelu, approximate=True), branch_y)
    grad_y = gelu_back(grad_mixed * state)[0].astype(jnp.bfloat16)
    grad_state = grad_mixed * gelu_y
    next_decay = jnp.concatenate([decay[1:], jnp.ones((1, LRU), jnp.float32)], axis=0)
    suffix, adjoint_local = lax.associative_scan(
        combine, (next_decay, grad_state), axis=0, reverse=True
    )
    returned = carried_in(
        (prod_local[-1], decay[0] * adjoint_local[0]), "seq", combine, neutral, True
    )
    adjoint = adjoint_local + suffix * returned[1]
    previous = jnp.concatenate([carry_in[None, :], state[:-1]], axis=0)
    _, gates_back = jax.vjp(gate_terms, pre_a, pre_i, conv_val, lambda_raw, starting)
    grad_pre_a, grad_pre_i, grad_direct, grads["lambda_raw"], _ = gates_back(
        (adjoint * previous, adjoint)
    )
    grad_pre_a = grad_pre_a.astype(jnp.bfloat16)
    grad_pre_i = grad_pre_i.astype(jnp.bfloat16)
    grads["gate_a"] = blocked_grad(conv_out, grad_pre_a)
    grads["gate_i"] = blocked_grad(conv_out, grad_pre_i)
    grads["bias_a"] = jnp.sum(grad_pre_a.astype(jnp.float32), axis=0)
    grads["bias_i"] = jnp.sum(grad_pre_i.astype(jnp.float32), axis=0)
    grad_conv = (
        grad_direct
        + blocked_t(grad_pre_a, weights["gate_a"])
        + blocked_t(grad_pre_i, weights["gate_i"])
    )
    _, conv_back = jax.vjp(
        partial(convolve, segment_ext=segment_ext, rows=rows), extended, conv_weight, conv_bias
    )
    grad_ext, grads["conv_weight"], grads["conv_bias"] = conv_back(grad_conv)
    edge_back = shifted(grad_ext[: KW - 1], "seq", -1)
    grad_x = grad_ext[KW - 1 :] + jnp.concatenate(
        [jnp.zeros((rows - (KW - 1), LRU), jnp.float32), edge_back], axis=0
    )
    grad_x = grad_x.astype(jnp.bfloat16)
    grads["w_x"] = t_matmul(normed, grad_x)
    grads["w_y"] = t_matmul(normed, grad_y)
    grad_normed = matmul_t(grad_y, weights["w_y"]) + matmul_t(grad_x, weights["w_x"])
    _, norm_back_one = jax.vjp(rms_norm, stream, gain_one)
    grad_stream_part, grads["gain_one"] = norm_back_one(grad_normed)
    input_grad = grad_middle + grad_stream_part
    packed_grad = jnp.concatenate([grads[entry[0]].reshape(-1) for entry in layout()])
    summed = lax.psum_scatter(packed_grad, ("seq", "fsdp"), scatter_dimension=0, tiled=True)
    new_moment = MOMENT * momentum + summed
    new_params = params - RATE * (summed + MOMENT * new_moment)
    new_average = BLEND * average + (1.0 - BLEND) * new_params
    return (output[None], input_grad[None], new_params, new_moment, new_average)


LANE = 128
TP = 8
HALO = 544
SMALL = 160
GATES = 512
REGIONS = {
    "A": (4248, 256, 192, 32),
    "B": (53400, 1536, 16, 192),
    "C": (77976, 1152, 96, 144),
    "D": (188568, 1536, 36, 192),
}
ROWS = 243864
EVEN_FIRST = (0, 2, 4, 6, 1, 3, 5, 7)
F32 = jnp.float32
BF16 = jnp.bfloat16


class Plan:
    def __init__(self, n_seq, n_fsdp):
        self.n_fsdp = n_fsdp
        shards = n_seq * n_fsdp
        per = ROWS * LANE // shards
        self.per = per
        self.part = per % LANE
        self.own_rows = -(-per // 1024) * 8
        self.last = per // LANE
        bounds = [0]
        for i in range(1, shards):
            at = per * i / LANE
            for first, unit, count, _ in REGIONS.values():
                if first <= at < first + unit * count:
                    bounds.append(first + unit * round((at - first) / unit))
        bounds.append(ROWS)
        self.segments = []
        self.sizes = []
        self.table = np.zeros((shards, 16), np.int32)
        for i in range(shards):
            base = per * i // LANE
            self.table[i, 0] = per * i % LANE
            offset = SMALL + GATES if i == 0 else 0
            found = {}
            for slot, (name, (first, unit, count, wide)) in enumerate(REGIONS.items()):
                low = max(bounds[i], first)
                high = min(bounds[i + 1], first + unit * count)
                if high > low:
                    units = (high - low) // unit
                    found[name] = ((low - first) // unit, units, offset)
                    self.table[i, 1 + 3 * slot : 4 + 3 * slot] = (
                        low - base + HALO,
                        units,
                        offset,
                    )
                    offset += units * wide
            self.segments.append(found)
            self.sizes.append(offset)
            self.table[i, 13] = int(i == 0)
        self.lengths = [
            max(self.sizes[s * n_fsdp : (s + 1) * n_fsdp]) for s in range(n_seq)
        ]
        self.offsets = np.concatenate([[0], np.cumsum(self.lengths)]).astype(np.int32)
        self.longest = max(self.lengths)
        self.groups = ((0, 1), (2,), (3, 4, 5, 6), (7,))
        self.starts = [int(self.offsets[group[0]]) for group in self.groups]
        self.rows = [sum(self.lengths[s] for s in group) for group in self.groups]

    def pieces(self, name, groups):
        out = []
        for i, found in enumerate(self.segments):
            s, f = divmod(i, self.n_fsdp)
            if name in found and s in groups:
                first, units, offset = found[name]
                row = int(self.offsets[s] - self.offsets[groups[0]]) + offset
                out.append((f, row, first, units))
        return out


VMEM = pl.BlockSpec(memory_space=pltpu.VMEM)
ANY = pl.BlockSpec(memory_space=pl.ANY)
SMEM = pl.BlockSpec(memory_space=pltpu.SMEM)
LIMIT = pltpu.CompilerParams(vmem_limit_bytes=60 * 1024 * 1024)


def shape(dims, dtype):
    return jax.ShapeDtypeStruct(dims, dtype)


def aligned(value, multiple):
    return pl.multiple_of(value, multiple)


def lanes(rows):
    return lax.broadcasted_iota(jnp.int32, (rows, LANE), 1)


def swap_lanes(blocks):
    blocks = list(blocks)
    at = lanes(blocks[0].shape[0]) // 16
    for step in (4, 2, 1):
        low_side = (at & step) == 0
        for one in range(TP):
            if one & step == 0:
                left, right = blocks[one], blocks[one + step]
                blocks[one] = jnp.where(low_side, left, pltpu.roll(right, 16 * step, 1))
                blocks[one + step] = jnp.where(
                    low_side, pltpu.roll(left, LANE - 16 * step, 1), right
                )
    return blocks


def shift_down(source, source_row, target, target_row, rows, block, amount, unroll):
    def step(j, tail):
        z = pltpu.roll(source[pl.ds(source_row + j * block, block), :], amount, 1)
        above = pltpu.roll(jnp.concatenate([tail, z], axis=0), 1, 0)[8:]
        target[pl.ds(target_row + j * block, block), :] = jnp.where(
            lanes(block) < amount, above, z
        )
        return z[block - 8 :]

    lax.fori_loop(0, rows // block, step, jnp.zeros((8, LANE), F32), unroll=unroll)


def pack_body(plan, tab, hd, own, hu, *rest):
    outs, (win, al, wire, sems) = rest[:TP], rest[TP:]
    s, f = lax.axis_index("seq"), lax.axis_index("fsdp")
    me = s * plan.n_fsdp + f
    total = win.shape[0]
    first = pltpu.make_async_copy(hd, win.at[pl.ds(0, HALO)], sems.at[0])
    second = pltpu.make_async_copy(own, win.at[pl.ds(HALO, plan.own_rows)], sems.at[1])
    first.start()
    second.start()
    first.wait()
    second.wait()
    seam = HALO + plan.last
    kept = win[pl.ds(seam, 8), :]
    shift_down(hu, 0, win, seam, HALO, 32, plan.part, True)
    edge = lax.broadcasted_iota(jnp.int32, (8, LANE), 0) == 0
    win[pl.ds(seam, 8), :] = jnp.where(
        edge & (lanes(8) < plan.part), kept, win[pl.ds(seam, 8), :]
    )
    shift_down(win, 0, al, 0, total, 48, tab[me, 0], 7)

    def columns(g, _):
        at = tab[me, 1] + g * 256
        to = tab[me, 3] + g * 16
        for block in range(16):
            row = to + 16 * tab[me, 2] * (block // TP)
            wire[block % TP, pl.ds(aligned(row, 16), 16), :] = al[
                pl.ds(at + block, 16, stride=16), :
            ].astype(BF16)
        return 0

    lax.fori_loop(0, tab[me, 2], columns, 0)
    for slot in (4, 10):

        def grouped(j, _):
            for owner in range(TP):
                at = tab[me, slot] + j * 1536 + owner * 192
                to = tab[me, slot + 2] + j * 16
                for block in range(12):
                    row = to + 16 * tab[me, slot + 1] * block
                    wire[owner, pl.ds(aligned(row, 16), 16), :] = al[
                        pl.ds(at + block, 16, stride=12), :
                    ].astype(BF16)
            return 0

        lax.fori_loop(0, tab[me, slot + 1], grouped, 0)

    def mixed_columns(g, _):
        at = tab[me, 7] + g * 1152
        to = tab[me, 9] + g * 32
        wide = 32 * tab[me, 8]
        last = tab[me, 9] + 4 * wide + g * 16
        for half in range(2):
            for a in range(4):
                parts = swap_lanes(
                    [
                        al[pl.ds(at + 576 * half + 8 * a + b, 16, stride=36), :]
                        for b in range(TP)
                    ]
                )
                for owner in range(TP):
                    row = to + a * wide + 16 * half
                    wire[owner, pl.ds(aligned(row, 16), 16), :] = parts[owner].astype(BF16)
        parts = swap_lanes(
            [
                al[pl.ds(at + 576 * half + 32 + b, 16, stride=36), :]
                for half in range(2)
                for b in range(4)
            ]
        )
        for owner in range(TP):
            wire[owner, pl.ds(aligned(last, 16), 16), :] = parts[owner].astype(BF16)
        return 0

    lax.fori_loop(0, tab[me, 8], mixed_columns, 0)

    @pl.when(me == 0)
    def _():
        for owner in range(TP):
            wire[owner, pl.ds(0, SMALL), :] = al[pl.ds(HALO, SMALL), :].astype(BF16)
        for kind in range(2):
            for n in range(16):
                wire[n % TP, pl.ds(SMALL + 128 * (2 * kind + n // TP), 128), :] = al[
                    pl.ds(HALO + 152 + 2048 * kind + 128 * n, 128), :
                ].astype(BF16)

    copies = [
        pltpu.make_async_copy(wire.at[s ^ k], outs[k], sems.at[2 + k]) for k in range(TP)
    ]
    for copy in copies:
        copy.start()
    for copy in copies:
        copy.wait()


def pack(plan, hd, own, hu):
    total = -(-(HALO * 2 + plan.own_rows) // 672) * 672
    return pl.pallas_call(
        partial(pack_body, plan),
        out_shape=[shape((plan.longest, LANE), BF16)] * TP,
        in_specs=[SMEM, ANY, ANY, VMEM],
        out_specs=[ANY] * TP,
        scratch_shapes=[
            pltpu.VMEM((total, LANE), F32),
            pltpu.VMEM((total, LANE), F32),
            pltpu.VMEM((TP, plan.longest, LANE), BF16),
            pltpu.SemaphoreType.DMA((2 + TP,)),
        ],
        compiler_params=LIMIT,
        name="pack",
    )(jnp.asarray(plan.table), hd, own, hu)


def order_body(plan, *refs):
    pieces, outs, sems = refs[:TP], refs[TP : TP + 4], refs[TP + 4]
    s = lax.axis_index("seq")
    for start in (True, False):
        for number, group in enumerate(plan.groups):
            for source in group:
                size = plan.lengths[source]
                at = int(plan.offsets[source]) - plan.starts[number]
                for k in range(TP):

                    @pl.when((s ^ source) == k)
                    def _():
                        copy = pltpu.make_async_copy(
                            pieces[k].at[pl.ds(0, size)],
                            outs[number].at[pl.ds(at, size)],
                            sems.at[source],
                        )
                        if start:
                            copy.start()
                        else:
                            copy.wait()


def order(plan, pieces):
    return pl.pallas_call(
        partial(order_body, plan),
        out_shape=[shape((rows, LANE), BF16) for rows in plan.rows],
        in_specs=[ANY] * TP,
        out_specs=[VMEM] * 4,
        scratch_shapes=[pltpu.SemaphoreType.DMA((TP,))],
        compiler_params=LIMIT,
        name="order",
    )(*pieces)


def weight_copies(plan, number, weights, halves, b_rows):
    out = []
    for f, row, first, units in plan.pieces("A", plan.groups[number]):
        for target, begin, end in weights.get("A", ()):
            low, high = max(first, begin), min(first + units, end)
            if high > low:
                for n in range(2):
                    out.append(
                        (
                            f,
                            row + 16 * (units * n + low - first),
                            16 * (high - low),
                            target.at[pl.ds(16 * (low - begin), 16 * (high - low)), pl.ds(128 * n, 128)],
                        )
                    )
    for f, row, first, units in plan.pieces("B", plan.groups[number]):
        if b_rows is not None:
            for block in range(12):
                out.append(
                    (
                        f,
                        row + 16 * units * block,
                        16 * units,
                        b_rows.at[block, pl.ds(16 * first, 16 * units)],
                    )
                )
    for f, row, first, units in plan.pieces("C", plan.groups[number]):
        for target, begin, end in weights.get("C", ()):
            low, high = max(first, begin), min(first + units, end)
            if high > low:
                for a in range(4):
                    out.append(
                        (
                            f,
                            row + 32 * (units * a + low - first),
                            32 * (high - low),
                            target.at[pl.ds(32 * (low - begin), 32 * (high - low)), pl.ds(128 * a, 128)],
                        )
                    )
        if halves is not None:
            out.append(
                (f, row + 128 * units, 16 * units, halves.at[pl.ds(16 * first, 16 * units)])
            )
    for f, row, first, units in plan.pieces("D", plan.groups[number]):
        for target, begin, end in weights.get("D", ()):
            for n in range(12):
                out.append(
                    (
                        f,
                        row + 16 * units * n,
                        16 * units,
                        target.at[pl.ds(16 * (first - begin), 16 * units), pl.ds(128 * n, 128)],
                    )
                )
    return out


def fetch_line(plan, line, copies, sems):
    f = lax.axis_index("fsdp")
    for start in (True, False):
        for source in range(plan.n_fsdp):
            for away in range(plan.n_fsdp):

                @pl.when((f ^ source) == away)
                def _():
                    for number, (holder, row, rows, target) in enumerate(copies):
                        if holder == source:
                            copy = pltpu.make_async_copy(
                                line[away].at[pl.ds(row, rows)], target, sems.at[number]
                            )
                            if start:
                                copy.start()
                            else:
                                copy.wait()


def first_copies(plan, small, gates, w_y, w_x, b_head):
    out = [(0, 0, SMALL, small), (0, SMALL, GATES, gates)]
    out += weight_copies(plan, 0, {"A": ((w_y, 0, 96), (w_x, 96, 192))}, None, None)
    for f, row, first, units in plan.pieces("B", plan.groups[0]):
        out.append((f, row, 192 * units, b_head.at[pl.ds(192 * first, 192 * units)]))
    return out


def first_body(plan, *refs):
    line, refs = refs[: plan.n_fsdp], refs[plan.n_fsdp :]
    *targets, sems = refs
    fetch_line(plan, line, first_copies(plan, *targets), sems)


def head_rows(plan):
    return sum(144 * p[3] for p in plan.pieces("C", plan.groups[1]))


def b_head_rows(plan):
    return sum(192 * p[3] for p in plan.pieces("B", plan.groups[0]))


class Nowhere:
    at = property(lambda self: self)

    def __getitem__(self, _):
        return self


def count_first(plan):
    return len(first_copies(plan, *[Nowhere()] * 5))


def unpack_first(plan, line):
    return pl.pallas_call(
        partial(first_body, plan),
        out_shape=[
            shape((SMALL, LANE), BF16),
            shape((GATES, LANE), BF16),
            shape((D, 256), BF16),
            shape((D, 256), BF16),
            shape((b_head_rows(plan), LANE), BF16),
        ],
        in_specs=[ANY] * len(line),
        out_specs=[VMEM] * 5,
        scratch_shapes=[pltpu.SemaphoreType.DMA((count_first(plan),))],
        compiler_params=LIMIT,
        name="unpack_first",
    )(*line)


def middle_copies(plan, b_rows, head):
    out = weight_copies(plan, 1, {}, None, b_rows)
    for f, row, first, units in plan.pieces("C", plan.groups[1]):
        out.append((f, row, 144 * units, head.at[pl.ds(144 * first, 144 * units)]))
    return out


def b_head_copies(plan, b_head, b_rows):
    out = []
    for _, _, first, units in plan.pieces("B", plan.groups[0]):
        for block in range(12):
            out.append(
                (
                    b_head.at[pl.ds(192 * first + 16 * units * block, 16 * units)],
                    b_rows.at[block, pl.ds(16 * first, 16 * units)],
                )
            )
    return out


def middle_body(plan, *refs):
    line, refs = refs[: plan.n_fsdp], refs[plan.n_fsdp :]
    b_head, outs, head, b_rows, sems, more = refs[0], refs[1 : 1 + TP], *refs[1 + TP :]
    local_copies = [
        pltpu.make_async_copy(source, target, more.at[number])
        for number, (source, target) in enumerate(b_head_copies(plan, b_head, b_rows))
    ]
    for copy in local_copies:
        copy.start()
    fetch_line(plan, line, middle_copies(plan, b_rows, head), sems)
    for copy in local_copies:
        copy.wait()
    s = lax.axis_index("seq")
    for k in range(TP):
        for n in range(2):
            unit = (s ^ k) + TP * n
            for block in range(12):
                outs[k][pl.ds(192 * n + 16 * block, 16), :] = b_rows[
                    block, pl.ds(aligned(16 * unit, 16), 16), :
                ]


def unpack_middle(plan, line, b_head):
    return pl.pallas_call(
        partial(middle_body, plan),
        out_shape=[shape((384, LANE), BF16)] * TP + [shape((head_rows(plan), LANE), BF16)],
        in_specs=[ANY] * (len(line) + 1),
        out_specs=[VMEM] * (TP + 1),
        scratch_shapes=[
            pltpu.VMEM((12, 256, LANE), BF16),
            pltpu.SemaphoreType.DMA((len(middle_copies(plan, *[Nowhere()] * 2)),)),
            pltpu.SemaphoreType.DMA((len(b_head_copies(plan, *[Nowhere()] * 2)),)),
        ],
        compiler_params=LIMIT,
        name="unpack_middle",
    )(*line, b_head)


def head_copies(plan, head, weight, halves):
    out = []
    for _, _, first, units in plan.pieces("C", plan.groups[1]):
        for a in range(4):
            out.append(
                (
                    head.at[pl.ds(144 * first + 32 * units * a, 32 * units)],
                    weight.at[pl.ds(32 * first, 32 * units), pl.ds(128 * a, 128)],
                )
            )
        out.append(
            (
                head.at[pl.ds(144 * first + 128 * units, 16 * units)],
                halves.at[pl.ds(16 * first, 16 * units)],
            )
        )
    return out


def second_copies(plan, w_gate, w_up, w_down, halves):
    return weight_copies(
        plan,
        2,
        {"C": ((w_gate, 0, 48), (w_up, 48, 96)), "D": ((w_down, 0, 16),)},
        halves,
        None,
    )


def second_body(plan, *refs):
    line, refs = refs[: plan.n_fsdp], refs[plan.n_fsdp :]
    head, w_gate, w_up, w_down, halves, sems, more = refs
    local_copies = [
        pltpu.make_async_copy(source, target, more.at[number])
        for number, (source, target) in enumerate(head_copies(plan, head, w_gate, halves))
    ]
    for copy in local_copies:
        copy.start()
    fetch_line(plan, line, second_copies(plan, w_gate, w_up, w_down, halves), sems)
    for copy in local_copies:
        copy.wait()
    for weight, begin in ((w_gate, 0), (w_up, 48)):

        def step(g, _):
            last = halves[pl.ds(aligned(16 * (begin + g), 16), 16), :]
            weight[pl.ds(aligned(32 * g, 16), 16), pl.ds(512, 64)] = last[:, :64]
            weight[pl.ds(aligned(32 * g + 16, 16), 16), pl.ds(512, 64)] = last[:, 64:]
            return 0

        lax.fori_loop(0, 48, step, 0, unroll=4)


def unpack_second(plan, line, head):
    many = len(second_copies(plan, *[Nowhere()] * 4))
    few = len(head_copies(plan, *[Nowhere()] * 3))
    return pl.pallas_call(
        partial(second_body, plan),
        out_shape=[
            shape((D, FF // TP), BF16),
            shape((D, FF // TP), BF16),
            shape((256, D), BF16),
        ],
        in_specs=[ANY] * (len(line) + 1),
        out_specs=[VMEM] * 3,
        scratch_shapes=[
            pltpu.VMEM((96 * 16, LANE), BF16),
            pltpu.SemaphoreType.DMA((many,)),
            pltpu.SemaphoreType.DMA((few,)),
        ],
        compiler_params=LIMIT,
        name="unpack_second",
    )(*line, head)


def third_copies(plan, w_down):
    return weight_copies(plan, 3, {"D": ((w_down, 0, 36),)}, None, None)


def third_body(plan, *refs):
    line, refs = refs[: plan.n_fsdp], refs[plan.n_fsdp :]
    before, w_down, sems, one = refs
    copy = pltpu.make_async_copy(before, w_down.at[pl.ds(0, 256)], one.at[0])
    copy.start()
    fetch_line(plan, line, third_copies(plan, w_down), sems)
    copy.wait()


def unpack_third(plan, line, before):
    many = len(third_copies(plan, Nowhere()))
    return pl.pallas_call(
        partial(third_body, plan),
        out_shape=shape((FF // TP, D), BF16),
        in_specs=[ANY] * (len(line) + 1),
        out_specs=VMEM,
        scratch_shapes=[
            pltpu.SemaphoreType.DMA((many,)),
            pltpu.SemaphoreType.DMA((1,)),
        ],
        compiler_params=LIMIT,
        name="unpack_third",
    )(*line, before)


def out_rows_body(*refs):
    pieces, w_out = refs[:TP], refs[TP]
    s = lax.axis_index("seq")
    for k in range(TP):
        for n in range(2):
            to = aligned(128 * n + 16 * (s ^ k), 16)
            for block in range(12):
                w_out[pl.ds(to, 16), pl.ds(128 * block, 128)] = pieces[k][
                    pl.ds(192 * n + 16 * block, 16), :
                ]


def join_out_rows(pieces):
    return pl.pallas_call(
        out_rows_body,
        out_shape=shape((256, D), BF16),
        in_specs=[VMEM] * TP,
        out_specs=VMEM,
        compiler_params=LIMIT,
        name="join_out_rows",
    )(*pieces)


def split_rows_body(grad, *pieces):
    s = lax.axis_index("seq")
    for k in range(TP):
        for n in range(2):
            at = aligned(128 * n + 16 * (s ^ k), 16)
            for block in range(12):
                pieces[k][pl.ds(192 * n + 16 * block, 16), :] = grad[
                    pl.ds(at, 16), pl.ds(128 * block, 128)
                ]


def split_out_rows(grad):
    return pl.pallas_call(
        split_rows_body,
        out_shape=[shape((384, LANE), F32)] * TP,
        in_specs=[VMEM],
        out_specs=[VMEM] * TP,
        compiler_params=LIMIT,
        name="split_out_rows",
    )(grad)


def run_copies(copies, sems):
    made = [
        pltpu.make_async_copy(source, target, sems.at[number])
        for number, (source, target) in enumerate(copies)
    ]
    for copy in made:
        copy.start()
    for copy in made:
        copy.wait()


def to_wire(copies, wire):
    return [(source, wire.at[f, pl.ds(row, rows)]) for f, row, rows, source in copies]


def wire_second_body(plan, g_gate, g_up, g_down, wire, head, halves, sems):
    for grad, begin in ((g_gate, 0), (g_up, 48)):

        def step(g, _):
            left = grad[pl.ds(aligned(32 * g, 16), 16), pl.ds(512, 64)]
            right = grad[pl.ds(aligned(32 * g + 16, 16), 16), pl.ds(512, 64)]
            halves[pl.ds(aligned(16 * (begin + g), 16), 16), :] = jnp.concatenate(
                [left, right], axis=1
            )
            return 0

        lax.fori_loop(0, 48, step, 0, unroll=4)
    copies = to_wire(second_copies(plan, g_gate, g_up, g_down, halves), wire)
    copies += [(b, a) for a, b in head_copies(plan, head, g_gate, halves)]
    run_copies(copies, sems)


def wire_second(plan, g_gate, g_up, g_down):
    many = len(second_copies(plan, *[Nowhere()] * 4)) + len(
        head_copies(plan, *[Nowhere()] * 3)
    )
    return pl.pallas_call(
        partial(wire_second_body, plan),
        out_shape=[
            shape((plan.n_fsdp, plan.rows[2], LANE), F32),
            shape((head_rows(plan), LANE), F32),
        ],
        in_specs=[VMEM] * 3,
        out_specs=[ANY] * 2,
        scratch_shapes=[
            pltpu.VMEM((96 * 16, LANE), F32),
            pltpu.SemaphoreType.DMA((many,)),
        ],
        compiler_params=LIMIT,
        name="wire_second",
    )(g_gate, g_up, g_down)


def wire_third_body(plan, g_down, wire, sems):
    run_copies(to_wire(third_copies(plan, g_down), wire), sems)


def wire_third(plan, g_down):
    many = len(third_copies(plan, Nowhere()))
    return pl.pallas_call(
        partial(wire_third_body, plan),
        out_shape=shape((plan.n_fsdp, plan.rows[3], LANE), F32),
        in_specs=[VMEM],
        out_specs=ANY,
        scratch_shapes=[pltpu.SemaphoreType.DMA((many,))],
        compiler_params=LIMIT,
        name="wire_third",
    )(g_down)


def wire_middle_body(plan, head, *refs):
    pieces, (wire, b_head, b_rows, sems) = refs[:TP], refs[TP:]
    s = lax.axis_index("seq")
    for k in range(TP):
        for n in range(2):
            unit = (s ^ k) + TP * n
            for block in range(12):
                b_rows[block, pl.ds(aligned(16 * unit, 16), 16), :] = pieces[k][
                    pl.ds(192 * n + 16 * block, 16), :
                ]
    copies = to_wire(middle_copies(plan, b_rows, head), wire)
    copies += [(b, a) for a, b in b_head_copies(plan, b_head, b_rows)]
    run_copies(copies, sems)


def wire_middle(plan, head, pieces):
    many = len(middle_copies(plan, *[Nowhere()] * 2)) + len(
        b_head_copies(plan, *[Nowhere()] * 2)
    )
    return pl.pallas_call(
        partial(wire_middle_body, plan),
        out_shape=[
            shape((plan.n_fsdp, plan.rows[1], LANE), F32),
            shape((b_head_rows(plan), LANE), F32),
        ],
        in_specs=[VMEM] * (1 + TP),
        out_specs=[ANY] * 2,
        scratch_shapes=[
            pltpu.VMEM((12, 256, LANE), F32),
            pltpu.SemaphoreType.DMA((many,)),
        ],
        compiler_params=LIMIT,
        name="wire_middle",
    )(head, *pieces)


def split_copies(plan, copies):
    border = int(plan.offsets[1])
    return (
        [copy for copy in copies if copy[1] < border],
        [(f, row - border, rows, at) for f, row, rows, at in copies if row >= border],
    )


def wire_x_body(plan, g_x, b_head, wire, sems):
    copies = first_copies(plan, Nowhere(), Nowhere(), Nowhere(), g_x, b_head)
    run_copies(to_wire(split_copies(plan, copies)[1], wire), sems)


def wire_x(plan, g_x, b_head):
    return pl.pallas_call(
        partial(wire_x_body, plan),
        out_shape=shape((plan.n_fsdp, plan.lengths[1], LANE), F32),
        in_specs=[VMEM] * 2,
        out_specs=ANY,
        scratch_shapes=[pltpu.SemaphoreType.DMA((count_first(plan),))],
        compiler_params=LIMIT,
        name="wire_x",
    )(g_x, b_head)


def wire_y_body(plan, gains, vectors, gates, g_y, g_x, wire, small, sems):
    s = lax.axis_index("seq")
    small[...] = jnp.zeros_like(small)
    small[pl.ds(0, 24), :] = gains[...]
    for n in range(8):
        for part in range(2):
            small[pl.ds(24 + 16 * n + s + TP * part, 1), :] = vectors[
                pl.ds(2 * n + part, 1), :
            ]
    copies = first_copies(plan, small, gates, g_y, g_x, Nowhere())
    run_copies(to_wire(split_copies(plan, copies)[0], wire), sems)


def wire_y(plan, gains, vectors, gates, g_y, g_x):
    return pl.pallas_call(
        partial(wire_y_body, plan),
        out_shape=shape((plan.n_fsdp, plan.lengths[0], LANE), F32),
        in_specs=[VMEM] * 5,
        out_specs=ANY,
        scratch_shapes=[
            pltpu.VMEM((SMALL, LANE), F32),
            pltpu.SemaphoreType.DMA((count_first(plan),)),
        ],
        compiler_params=LIMIT,
        name="wire_y",
    )(gains, vectors, gates, g_y, g_x)


def spread_body(plan, targets, *refs):
    count = len(targets)
    sums, outs, sems = refs[:count], refs[count : count + TP], refs[count + TP]
    s = lax.axis_index("seq")
    for start in (True, False):
        for summed, group in zip(sums, targets):
            for target in group:
                size = plan.lengths[target]
                at = int(plan.offsets[target] - plan.offsets[group[0]])
                for k in range(TP):

                    @pl.when((s ^ target) == k)
                    def _():
                        copy = pltpu.make_async_copy(
                            summed.at[pl.ds(at, size)],
                            outs[k].at[pl.ds(0, size)],
                            sems.at[target],
                        )
                        if start:
                            copy.start()
                        else:
                            copy.wait()


def spread(plan, targets, sums):
    rows = max(plan.lengths[s] for group in targets for s in group)
    return pl.pallas_call(
        partial(spread_body, plan, targets),
        out_shape=[shape((rows, LANE), F32)] * TP,
        in_specs=[VMEM] * len(sums),
        out_specs=[ANY] * TP,
        scratch_shapes=[pltpu.SemaphoreType.DMA((TP,))],
        compiler_params=LIMIT,
    )(*sums)


def shift_up(source, source_row, target, target_row, rows, block, amount):
    def step(j, _):
        both = pltpu.roll(source[pl.ds(source_row + j * block, block + 8), :], amount, 1)
        below = pltpu.roll(both, block + 7, 0)[:block]
        target[pl.ds(target_row + j * block, block), :] = jnp.where(
            lanes(block) < amount, both[:block], below
        )
        return 0

    lax.fori_loop(0, rows // block, step, 0, unroll=True)


def collect_body(plan, tab, *refs):
    pieces, (own, hd, hu, al, win, wire, sems) = refs[: 3 * TP], refs[3 * TP :]
    s, f = lax.axis_index("seq"), lax.axis_index("fsdp")
    me = s * plan.n_fsdp + f

    def bring(start):
        for number in range(3):

            @pl.when(jnp.minimum(s, 2) == number)
            def _():
                for k in range(TP):
                    piece = pieces[TP * number + k]
                    copy = pltpu.make_async_copy(
                        piece, wire.at[s ^ k, pl.ds(0, piece.shape[0])], sems.at[k]
                    )
                    if start:
                        copy.start()
                    else:
                        copy.wait()

    bring(True)
    total = win.shape[0]

    def clear(j, _):
        al[pl.ds(aligned(j * 96, 8), 96), :] = jnp.zeros((96, LANE), F32)
        return 0

    lax.fori_loop(0, al.shape[0] // 96, clear, 0, unroll=4)
    bring(False)

    def columns(g, _):
        at = tab[me, 1] + g * 256
        to = tab[me, 3] + g * 16
        for block in range(16):
            row = to + 16 * tab[me, 2] * (block // TP)
            al[pl.ds(at + block, 16, stride=16), :] = wire[
                block % TP, pl.ds(aligned(row, 16), 16), :
            ]
        return 0

    lax.fori_loop(0, tab[me, 2], columns, 0)
    for slot in (4, 10):

        def grouped(j, _):
            for owner in range(TP):
                at = tab[me, slot] + j * 1536 + owner * 192
                to = tab[me, slot + 2] + j * 16
                for block in range(12):
                    row = to + 16 * tab[me, slot + 1] * block
                    al[pl.ds(at + block, 16, stride=12), :] = wire[
                        owner, pl.ds(aligned(row, 16), 16), :
                    ]
            return 0

        lax.fori_loop(0, tab[me, slot + 1], grouped, 0)

    def mixed_columns(g, _):
        at = tab[me, 7] + g * 1152
        to = tab[me, 9] + g * 32
        wide = 32 * tab[me, 8]
        last = tab[me, 9] + 4 * wide + g * 16
        for half in range(2):
            for a in range(4):
                parts = swap_lanes(
                    [
                        wire[owner, pl.ds(aligned(to + a * wide + 16 * half, 16), 16), :]
                        for owner in range(TP)
                    ]
                )
                for b in range(TP):
                    al[pl.ds(at + 576 * half + 8 * a + b, 16, stride=36), :] = parts[b]
        parts = swap_lanes(
            [wire[owner, pl.ds(aligned(last, 16), 16), :] for owner in range(TP)]
        )
        for half in range(2):
            for b in range(4):
                al[pl.ds(at + 576 * half + 32 + b, 16, stride=36), :] = parts[4 * half + b]
        return 0

    lax.fori_loop(0, tab[me, 8], mixed_columns, 0)

    @pl.when(me == 0)
    def _():
        summed = wire[0, pl.ds(0, 152), :]
        for owner in range(1, TP):
            summed = summed + wire[owner, pl.ds(0, 152), :]
        al[pl.ds(HALO, 152), :] = summed
        for kind in range(2):
            for n in range(16):
                al[pl.ds(HALO + 152 + 2048 * kind + 128 * n, 128), :] = wire[
                    n % TP, pl.ds(SMALL + 128 * (2 * kind + n // TP), 128), :
                ]

    def back(j, _):
        both = pltpu.roll(
            al[pl.ds(aligned(j * 48, 8), 56), :], lax.rem(LANE - tab[me, 0], LANE), 1
        )
        below = pltpu.roll(both, 55, 0)[:48]
        win[pl.ds(aligned(j * 48, 8), 48), :] = jnp.where(
            lanes(48) < LANE - tab[me, 0], both[:48], below
        )
        return 0

    lax.fori_loop(0, total // 48, back, 0, unroll=7)
    hd[...] = win[pl.ds(0, HALO), :]
    own[...] = win[pl.ds(HALO, plan.own_rows), :]
    shift_up(win, HALO + plan.last, hu, 0, HALO, 32, LANE - plan.part)


def collect(plan, pieces):
    total = -(-(HALO * 2 + plan.own_rows) // 672) * 672
    cleared = total + 96
    return pl.pallas_call(
        partial(collect_body, plan),
        out_shape=[
            shape((plan.own_rows, LANE), F32),
            shape((HALO, LANE), F32),
            shape((HALO, LANE), F32),
        ],
        in_specs=[SMEM] + [ANY] * (3 * TP),
        out_specs=[VMEM] * 3,
        scratch_shapes=[
            pltpu.VMEM((cleared, LANE), F32),
            pltpu.VMEM((total, LANE), F32),
            pltpu.VMEM((TP, plan.longest, LANE), F32),
            pltpu.SemaphoreType.DMA((TP,)),
        ],
        compiler_params=LIMIT,
        name="collect",
    )(jnp.asarray(plan.table), *pieces)


def tail_body(plan, value, out):
    first = (plan.last - HALO) % 8
    out[...] = jnp.zeros_like(out)
    shift_down(value, 0, out, first, HALO, 32, plan.part, True)
    z = pltpu.roll(value[pl.ds(HALO - 8, 8), :], plan.part, 1)
    row = lax.broadcasted_iota(jnp.int32, (8, LANE), 0)
    out[pl.ds(first + HALO, 8), :] = jnp.where(
        (row == 0) & (lanes(8) < plan.part), pltpu.roll(z, 1, 0), 0.0
    )


def place_tail(plan, value):
    rows = plan.own_rows - (plan.last - HALO) // 8 * 8
    return pl.pallas_call(
        partial(tail_body, plan),
        out_shape=shape((max(rows, HALO + 16), LANE), F32),
        in_specs=[VMEM],
        out_specs=VMEM,
        compiler_params=LIMIT,
        name="place_tail",
    )(value)[:rows]


def scan_body(reverse, coefficient, addend, out):
    rows, width = coefficient.shape
    at = lax.broadcasted_iota(jnp.int32, (8, width), 0)
    if reverse:
        at = 7 - at
    steps = rows // 8

    def step(j, carry):
        block = steps - 1 - j if reverse else j
        here = pl.ds(aligned(block * 8, 8), 8)
        a, b = coefficient[here, :], addend[here, :]
        for reach in (1, 2, 4):
            turn = 8 - reach if reverse else reach
            inside = at >= reach
            b = b + jnp.where(inside, a * pltpu.roll(b, turn, 0), 0.0)
            a = jnp.where(inside, a * pltpu.roll(a, turn, 0), a)
        value = b + a * carry
        out[here, :] = value
        edge = value[0:1] if reverse else value[7:8]
        return jnp.broadcast_to(edge, (8, width))

    lax.fori_loop(0, steps, step, jnp.zeros((8, width), F32), unroll=4)


def linear_scan(coefficient, addend, reverse):
    return pl.pallas_call(
        partial(scan_body, reverse),
        out_shape=shape(coefficient.shape, F32),
        in_specs=[VMEM] * 2,
        out_specs=VMEM,
        compiler_params=LIMIT,
        name="scan_back" if reverse else "scan",
    )(coefficient, addend)


def swap(value, bit):
    return lax.ppermute(value, "seq", [(i, i ^ bit) for i in range(TP)])


def exchange(pieces, targets=range(TP)):
    return [pieces[0]] + [
        lax.ppermute(pieces[k], "seq", [(i ^ k, i) for i in targets]) for k in range(1, TP)
    ]


def gather_stream(mine):
    half = mine.shape[0] // 2
    over_x, over_y = swap(mine, 2), swap(mine, 4)
    over_xy = [swap(over_x[:half], 4), swap(over_y[half:], 2)]
    chip = [mine, over_x, over_y] + over_xy
    return jnp.concatenate(chip + [swap(part, 1) for part in chip], axis=0)


def scatter_stream(partial_sums):
    rows = partial_sums.shape[0] // TP
    half = rows // 2

    def send(value, bit):
        return swap(value.astype(BF16), bit).astype(F32)

    other = send(partial_sums[TP // 2 * rows :], 1)
    q = (partial_sums[: TP // 2 * rows] + other).reshape(4, rows, -1)
    up = send(jnp.concatenate([q[1, :half], q[3, :half]]), 2)
    down = send(jnp.concatenate([q[2, half:], q[3, half:]]), 4)
    top = send(q[2, :half] + up[half:], 4)
    low = send(q[1, half:] + down[half:], 2)
    return jnp.concatenate(
        [q[0, :half] + up[:half] + top, q[0, half:] + down[:half] + low], axis=0
    )


def to_positions(values, s):
    rows = values.shape[0] // TP
    parts = []
    for j in range(TP):
        k = s ^ j
        at = (k // 2 + 4 * (k % 2)) * rows
        parts.append(lax.dynamic_slice_in_dim(values, at, rows, 0))
    return jnp.concatenate(parts, axis=0)


def to_relative(values, s):
    rows = values.shape[0] // TP
    return jnp.concatenate(
        [lax.dynamic_slice_in_dim(values, (s ^ k) * rows, rows, 0) for k in EVEN_FIRST], axis=0
    )


def gather_line(value, count):
    out = [value]
    for x in range(1, count):
        out.append(lax.ppermute(value, "fsdp", [(i, i ^ x) for i in range(count)]))
    return out


def scatter_line(blocks, f):
    def own(j):
        return lax.dynamic_index_in_dim(blocks, j, 0, keepdims=False)

    count = blocks.shape[0]
    far, near = own(f ^ 2), own(f ^ 1)
    far = lax.ppermute(far, "fsdp", [(i, i ^ 1) for i in range(count)])
    near = lax.ppermute(near, "fsdp", [(i, i ^ 1) for i in range(count)])
    crossed = lax.ppermute(own(f ^ 3) + far, "fsdp", [(i, i ^ 3) for i in range(count)])
    return own(f) + near + crossed


def sliced(plan, *arguments):
    return sliced_step(plan, *arguments)


def sliced_step(plan, stream_in, cotangent, starts, params, momentum, average):
    n_fsdp = plan.n_fsdp
    s, f = lax.axis_index("seq"), lax.axis_index("fsdp")
    shards = TP * n_fsdp
    onward = [(i, i + 1) for i in range(shards - 1)]
    backward = [(i + 1, i) for i in range(shards - 1)]
    both = ("seq", "fsdp")
    edge = HALO * LANE
    per = plan.per

    hd, hu = lax.optimization_barrier((params[per - edge :], params[:edge]))
    hd = lax.ppermute(hd.astype(BF16), both, onward)
    hu = lax.ppermute(hu.astype(BF16), both, backward)
    own = jnp.pad(params, (0, plan.own_rows * LANE - per)).reshape(-1, LANE)
    pieces = pack(
        plan, hd.astype(F32).reshape(-1, LANE), own, hu.astype(F32).reshape(-1, LANE)
    )
    first, middle_wire, second, third = order(plan, exchange(pieces))
    stream_bf, first = lax.optimization_barrier((stream_in[0], first))
    line = gather_line(first, n_fsdp)
    middle_wire, second, third, line = lax.optimization_barrier(
        (middle_wire, second, third, line)
    )
    small, gates, w_y, w_x, b_head = unpack_first(plan, line)
    line = gather_line(middle_wire, n_fsdp)
    *out_rows, head = unpack_middle(plan, line, b_head)
    w_out = join_out_rows(exchange(out_rows))
    line = gather_line(second, n_fsdp)
    w_gate, w_up, w_down = unpack_second(plan, line, head)
    w_down = unpack_third(plan, gather_line(third, n_fsdp), w_down)

    mine = stream_in[0].astype(F32)
    stream = gather_stream(stream_bf)
    cotangent_bf, stream = lax.optimization_barrier((cotangent[0], stream))
    stream = stream.astype(F32)
    grad_out = gather_stream(cotangent_bf)
    rows = stream.shape[0]

    small = small.astype(F32)
    gain_one = small[0:12].reshape(-1)
    gain_two = small[12:24].reshape(-1)

    def channels(at):
        return jnp.concatenate(
            [
                lax.dynamic_slice_in_dim(small, at + s, 1, 0),
                lax.dynamic_slice_in_dim(small, at + s + TP, 1, 0),
            ],
            axis=1,
        )[0]

    conv_bias, bias_a, bias_i, lambda_raw = (channels(24 + 16 * j) for j in range(4))
    conv_weight = jnp.stack([channels(88 + 16 * j) for j in range(KW)])

    positions = jnp.arange(rows, dtype=jnp.int32)
    ext_pos = jnp.arange(rows + KW - 1, dtype=jnp.int32) - (KW - 1)
    segment_ext = segment_ids(ext_pos, starts[0])
    starting = start_flags(positions, starts[0])[:, None]

    def gate_product(values, at):
        return jnp.concatenate(
            [matmul(values[:, :HB], gates[at : at + HB]), matmul(values[:, HB:], gates[at + HB : at + 2 * HB])],
            axis=1,
        )

    def gate_product_t(values, at):
        return jnp.concatenate(
            [matmul_t(values[:, :HB], gates[at : at + HB]), matmul_t(values[:, HB:], gates[at + HB : at + 2 * HB])],
            axis=1,
        )

    normed = rms_norm(stream, gain_one).astype(BF16)
    branch_y = to_positions(matmul(normed, w_y), s)
    branch_x = to_positions(matmul(normed, w_x).astype(BF16), s)
    extended = jnp.pad(branch_x, ((KW - 1, 0), (0, 0))).astype(F32)

    def convolve_here(extended, weight, bias):
        total = jnp.zeros((rows, bias.shape[0]), F32) + bias
        for lag in range(KW):
            source = extended[KW - 1 - lag : KW - 1 - lag + rows]
            same = segment_ext[KW - 1 - lag : KW - 1 - lag + rows] == segment_ext[KW - 1 :]
            total = total + weight[lag] * source * same.astype(F32)[:, None]
        return total

    conv_out = convolve_here(extended, conv_weight, conv_bias).astype(BF16)
    conv_val = conv_out.astype(F32)
    pre_a = gate_product(conv_out, 0) + bias_a
    pre_i = gate_product(conv_out, 2 * HB) + bias_i
    decay, drive = gate_terms(pre_a, pre_i, conv_val, lambda_raw, starting)
    state = linear_scan(decay, drive, False)
    gelu_y = jax.nn.gelu(branch_y, approximate=True)
    mixed = to_relative((state * gelu_y).astype(BF16), s)
    middle = mine + scatter_stream(matmul(mixed, w_out))
    normed_two_mine = rms_norm(middle, gain_two).astype(BF16)
    normed_two = gather_stream(normed_two_mine)
    gate = matmul(normed_two, w_gate)
    upward = matmul(normed_two, w_up)
    hidden = gelu_product(gate, upward).astype(BF16)
    g_down = t_matmul(hidden, grad_out)
    summed_three = scatter_line(wire_third(plan, g_down), f)
    out_sums = matmul(hidden, w_down)
    output = (middle + scatter_stream(out_sums)).astype(BF16)
    gate, upward, _ = lax.optimization_barrier((gate, upward, hidden))

    grad_hidden = matmul_t(grad_out, w_down)
    _, product_back = jax.vjp(gelu_product, gate, upward)
    grad_gate, grad_up = product_back(grad_hidden)
    grad_gate, grad_up = grad_gate.astype(BF16), grad_up.astype(BF16)
    g_gate = t_matmul(normed_two, grad_gate)
    g_up = t_matmul(normed_two, grad_up)
    grad_normed_two = scatter_stream(matmul_t(grad_gate, w_gate) + matmul_t(grad_up, w_up))
    wire_two, wire_head = wire_second(plan, g_gate, g_up, g_down)
    summed_two = scatter_line(wire_two, f)

    _, norm_back_two = jax.vjp(rms_norm, middle, gain_two)
    grad_middle_part, g_gain_two = norm_back_two(grad_normed_two)
    grad_middle = cotangent[0].astype(F32) + grad_middle_part
    grad_first = gather_stream(grad_middle.astype(BF16))
    g_out = t_matmul(mixed, grad_first)
    wire_mid, b_head = wire_middle(plan, wire_head, exchange(split_out_rows(g_out)))
    summed_mid = scatter_line(wire_mid, f)
    grad_mixed = to_positions(matmul_t(grad_first, w_out), s)
    _, gelu_back = jax.vjp(partial(jax.nn.gelu, approximate=True), branch_y)
    grad_y = gelu_back(grad_mixed * state)[0].astype(BF16)
    next_decay = jnp.concatenate([decay[1:], jnp.ones((1, decay.shape[1]), F32)], axis=0)
    adjoint = linear_scan(next_decay, grad_mixed * gelu_y, True)
    previous = jnp.concatenate([jnp.zeros((1, decay.shape[1]), F32), state[:-1]], axis=0)
    _, gates_back = jax.vjp(gate_terms, pre_a, pre_i, conv_val, lambda_raw, starting)
    grad_pre_a, grad_pre_i, grad_direct, g_lambda, _ = gates_back((adjoint * previous, adjoint))
    grad_pre_a, grad_pre_i = grad_pre_a.astype(BF16), grad_pre_i.astype(BF16)
    g_gates = jnp.concatenate(
        [
            t_matmul(conv_out[:, n : n + HB], grad[:, n : n + HB])
            for grad in (grad_pre_a, grad_pre_i)
            for n in (0, HB)
        ],
        axis=0,
    )
    g_bias_a = jnp.sum(grad_pre_a.astype(F32), axis=0)
    g_bias_i = jnp.sum(grad_pre_i.astype(F32), axis=0)
    grad_conv = grad_direct + gate_product_t(grad_pre_a, 0) + gate_product_t(grad_pre_i, 2 * HB)
    _, conv_back = jax.vjp(convolve_here, extended, conv_weight, conv_bias)
    grad_ext, g_conv_weight, g_conv_bias = conv_back(grad_conv)
    grad_x = to_relative(grad_ext[KW - 1 :].astype(BF16), s)
    grad_y = to_relative(grad_y, s)
    g_x = t_matmul(normed, grad_x)
    g_y = t_matmul(normed, grad_y)
    grad_normed = scatter_stream(matmul_t(grad_y, w_y) + matmul_t(grad_x, w_x))
    _, norm_back_one = jax.vjp(rms_norm, mine, gain_one)
    grad_stream_part, g_gain_one = norm_back_one(grad_normed)
    input_grad = grad_middle + grad_stream_part

    summed_x = scatter_line(wire_x(plan, g_x, b_head), f)
    gains = jnp.concatenate([g_gain_one, g_gain_two]).reshape(-1, LANE)
    vectors = jnp.stack(
        [g_conv_bias, g_bias_a, g_bias_i, g_lambda] + [g_conv_weight[k] for k in range(KW)]
    ).reshape(-1, LANE)
    summed_y = scatter_line(wire_y(plan, gains, vectors, g_gates, g_y, g_x), f)
    early = spread(plan, plan.groups[1:], (summed_mid, summed_two, summed_three))
    got = exchange(spread(plan, ((0,),), (summed_y,)), (0,))
    got += exchange(spread(plan, ((1,),), (summed_x,)), (1,))
    got += exchange(early)
    grad_own, grad_hd, grad_hu = collect(plan, got)
    from_next = lax.ppermute(grad_hd, both, backward)
    from_before = lax.ppermute(grad_hu, both, onward)
    tail = place_tail(plan, from_next).reshape(-1)
    whole = plan.own_rows * LANE
    summed = (
        grad_own.reshape(-1)
        + jnp.pad(from_before.reshape(-1), (0, whole - edge))
        + jnp.pad(tail, (whole - tail.shape[0], 0))
    )[:per]
    new_moment = MOMENT * momentum + summed
    new_params = params - RATE * (summed + MOMENT * new_moment)
    new_average = BLEND * average + (1.0 - BLEND) * new_params
    return (output[None], input_grad[None], new_params, new_moment, new_average)


def solution(mesh):
    n_seq, n_fsdp = mesh.shape["seq"], mesh.shape["fsdp"]
    fast = (n_seq, n_fsdp) == (TP, 4)
    body = partial(sliced, Plan(n_seq, n_fsdp)) if fast else local
    return jax.shard_map(
        body,
        mesh=mesh,
        in_specs=(
            P("fsdp", "seq", None),
            P("fsdp", "seq", None),
            P("fsdp", None),
            P(("seq", "fsdp")),
            P(("seq", "fsdp")),
            P(("seq", "fsdp")),
        ),
        out_specs=(
            P("fsdp", "seq", None),
            P("fsdp", "seq", None),
            P(("seq", "fsdp")),
            P(("seq", "fsdp")),
            P(("seq", "fsdp")),
        ),
        check_vma=False,
    )
```

```python
from functools import partial
import math

import jax
import jax.numpy as jnp
import numpy as np
from jax import lax
from jax.experimental import pallas as pl
from jax.experimental.pallas import tpu as pltpu
from jax.sharding import PartitionSpec as P


D = 1536
LRU = 2048
FF = 4608
HB = 128
KW = 4


EPS = 1e-06
RATE = 3e-05
MOMENT = 0.9
BLEND = 0.9
DECAY_SCALE = 8.0


def shifted(block, axis, distance):
    devices = range(lax.axis_size(axis))
    route = [(i - distance, i) for i in devices if i - distance in devices]
    return lax.ppermute(block, axis, route)


def carried_in(value, axis, join, neutral, backward):
    count, mine = (lax.axis_size(axis), lax.axis_index(axis))
    pieces = jax.tree.map(lambda part: lax.all_gather(part, axis), value)
    if backward:
        pieces = jax.tree.map(lambda part: part[::-1], pieces)
        mine = count - 1 - mine
    so_far = jax.tree.map(
        lambda part, zero: jnp.full_like(part, 0) + jnp.asarray(zero, part.dtype), value, neutral
    )

    def lap(position, so_far):
        longer = join(so_far, jax.tree.map(lambda part: part[position], pieces))
        return jax.tree.map(lambda new, old: jnp.where(position < mine, new, old), longer, so_far)

    return lax.fori_loop(0, count - 1, lap, so_far)


def layout():
    return [
        ("gain_one", (D,)),
        ("gain_two", (D,)),
        ("conv_bias", (LRU,)),
        ("bias_a", (LRU,)),
        ("bias_i", (LRU,)),
        ("lambda_raw", (LRU,)),
        ("conv_weight", (KW, LRU)),
        ("gate_a", (LRU // HB, HB, HB)),
        ("gate_i", (LRU // HB, HB, HB)),
        ("w_y", (D, LRU)),
        ("w_x", (D, LRU)),
        ("w_out", (LRU, D)),
        ("w_gate", (D, FF)),
        ("w_up", (D, FF)),
        ("w_down", (FF, D)),
    ]


def unpack(packed):
    result = {}
    offset = 0
    for entry_name, entry_shape in layout():
        amount = math.prod(entry_shape)
        result[entry_name] = packed[offset : offset + amount].reshape(entry_shape)
        offset += amount
    return result


def matmul(left, right):
    return jnp.dot(left, right, preferred_element_type=jnp.float32)


def matmul_t(left, right):
    return lax.dot_general(
        left, right, (((1,), (1,)), ((), ())), preferred_element_type=jnp.float32
    )


def t_matmul(left, right):
    return lax.dot_general(
        left, right, (((0,), (0,)), ((), ())), preferred_element_type=jnp.float32
    )


def blocked(values, weight):
    shaped = values.reshape(values.shape[0], LRU // HB, HB)
    return jnp.einsum("tnh,nhk->tnk", shaped, weight, preferred_element_type=jnp.float32).reshape(
        values.shape[0], LRU
    )


def blocked_t(values, weight):
    shaped = values.reshape(values.shape[0], LRU // HB, HB)
    return jnp.einsum("tnk,nhk->tnh", shaped, weight, preferred_element_type=jnp.float32).reshape(
        values.shape[0], LRU
    )


def blocked_grad(inputs, grads):
    left = inputs.reshape(inputs.shape[0], LRU // HB, HB)
    right = grads.reshape(grads.shape[0], LRU // HB, HB)
    return jnp.einsum("tnh,tnk->nhk", left, right, preferred_element_type=jnp.float32)


def rms_norm(values, gain):
    return values * lax.rsqrt(jnp.mean(values * values, axis=-1, keepdims=True) + EPS) * gain


def combine(earlier, later):
    return (earlier[0] * later[0], later[0] * earlier[1] + later[1])


def gate_terms(pre_a, pre_i, conv_val, lambda_raw, starting):
    recall = jax.nn.sigmoid(pre_a)
    admit = jax.nn.sigmoid(pre_i)
    rate = DECAY_SCALE * jax.nn.softplus(lambda_raw) * recall
    decay = (1.0 - starting) * jnp.exp(-rate)
    scale_in = starting + (1.0 - starting) * jnp.sqrt(-jnp.expm1(-2.0 * rate))
    return (decay, scale_in * admit * conv_val)


def convolve(extended, weight, bias, segment_ext, rows):
    total = jnp.zeros((rows, LRU), jnp.float32) + bias
    for lag in range(KW):
        source = extended[KW - 1 - lag : KW - 1 - lag + rows]
        same = (segment_ext[KW - 1 - lag : KW - 1 - lag + rows] == segment_ext[KW - 1 :]).astype(
            jnp.float32
        )
        total = total + weight[lag] * source * same[:, None]
    return total


def segment_ids(positions, doc_starts):
    return jnp.sum((doc_starts[None, :] <= positions[:, None]).astype(jnp.int32), axis=1)


def start_flags(positions, doc_starts):
    return jnp.max((doc_starts[None, :] == positions[:, None]).astype(jnp.float32), axis=1)


def gelu_product(left, right):
    return jax.nn.gelu(left, approximate=True) * right


def local(stream_in, cotangent, starts, params, momentum, average):
    weights = unpack(
        lax.all_gather(params.astype(jnp.bfloat16), ("seq", "fsdp"), axis=0, tiled=True)
    )
    stream = stream_in[0].astype(jnp.float32)
    incoming = cotangent[0].astype(jnp.float32)
    doc_starts = starts[0]
    rows = stream.shape[0]
    positions = lax.axis_index("seq") * rows + jnp.arange(rows, dtype=jnp.int32)
    ext_pos = positions[0] - (KW - 1) + jnp.arange(rows + KW - 1, dtype=jnp.int32)
    segment_ext = segment_ids(ext_pos, doc_starts)
    starting = start_flags(positions, doc_starts)[:, None]
    gain_one = weights["gain_one"].astype(jnp.float32)
    gain_two = weights["gain_two"].astype(jnp.float32)
    conv_weight = weights["conv_weight"].astype(jnp.float32)
    conv_bias = weights["conv_bias"].astype(jnp.float32)
    lambda_raw = weights["lambda_raw"].astype(jnp.float32)
    normed = rms_norm(stream, gain_one).astype(jnp.bfloat16)
    branch_y = matmul(normed, weights["w_y"])
    branch_x = matmul(normed, weights["w_x"]).astype(jnp.bfloat16)
    edge = shifted(branch_x[rows - (KW - 1) :], "seq", 1)
    extended = jnp.concatenate([edge, branch_x], axis=0).astype(jnp.float32)
    conv_out = convolve(extended, conv_weight, conv_bias, segment_ext, rows).astype(jnp.bfloat16)
    conv_val = conv_out.astype(jnp.float32)
    pre_a = blocked(conv_out, weights["gate_a"]) + weights["bias_a"].astype(jnp.float32)
    pre_i = blocked(conv_out, weights["gate_i"]) + weights["bias_i"].astype(jnp.float32)
    decay, drive = gate_terms(pre_a, pre_i, conv_val, lambda_raw, starting)
    prod_local, state_local = lax.associative_scan(combine, (decay, drive), axis=0)
    neutral = (jnp.ones((LRU,), jnp.float32), jnp.zeros((LRU,), jnp.float32))
    carried = carried_in((prod_local[-1], state_local[-1]), "seq", combine, neutral, False)
    carry_in = carried[1]
    state = lax.associative_scan(combine, (decay, drive.at[0].add(decay[0] * carry_in)), axis=0)[1]
    gelu_y = jax.nn.gelu(branch_y, approximate=True)
    mixed = (state * gelu_y).astype(jnp.bfloat16)
    middle = stream + matmul(mixed, weights["w_out"])
    normed_two = rms_norm(middle, gain_two).astype(jnp.bfloat16)
    gate = matmul(normed_two, weights["w_gate"])
    upward = matmul(normed_two, weights["w_up"])
    hidden = gelu_product(gate, upward).astype(jnp.bfloat16)
    output = (middle + matmul(hidden, weights["w_down"])).astype(jnp.bfloat16)
    grads = {}
    grad_out = incoming.astype(jnp.bfloat16)
    grads["w_down"] = t_matmul(hidden, grad_out)
    grad_hidden = matmul_t(grad_out, weights["w_down"])
    _, product_back = jax.vjp(gelu_product, gate, upward)
    grad_gate, grad_up = product_back(grad_hidden)
    grad_gate = grad_gate.astype(jnp.bfloat16)
    grad_up = grad_up.astype(jnp.bfloat16)
    grads["w_gate"] = t_matmul(normed_two, grad_gate)
    grads["w_up"] = t_matmul(normed_two, grad_up)
    grad_normed_two = matmul_t(grad_gate, weights["w_gate"]) + matmul_t(grad_up, weights["w_up"])
    _, norm_back_two = jax.vjp(rms_norm, middle, gain_two)
    grad_middle_part, grads["gain_two"] = norm_back_two(grad_normed_two)
    grad_middle = incoming + grad_middle_part
    grad_first = grad_middle.astype(jnp.bfloat16)
    grads["w_out"] = t_matmul(mixed, grad_first)
    grad_mixed = matmul_t(grad_first, weights["w_out"])
    _, gelu_back = jax.vjp(partial(jax.nn.gelu, approximate=True), branch_y)
    grad_y = gelu_back(grad_mixed * state)[0].astype(jnp.bfloat16)
    grad_state = grad_mixed * gelu_y
    next_decay = jnp.concatenate([decay[1:], jnp.ones((1, LRU), jnp.float32)], axis=0)
    suffix, adjoint_local = lax.associative_scan(
        combine, (next_decay, grad_state), axis=0, reverse=True
    )
    returned = carried_in(
        (prod_local[-1], decay[0] * adjoint_local[0]), "seq", combine, neutral, True
    )
    adjoint = adjoint_local + suffix * returned[1]
    previous = jnp.concatenate([carry_in[None, :], state[:-1]], axis=0)
    _, gates_back = jax.vjp(gate_terms, pre_a, pre_i, conv_val, lambda_raw, starting)
    grad_pre_a, grad_pre_i, grad_direct, grads["lambda_raw"], _ = gates_back(
        (adjoint * previous, adjoint)
    )
    grad_pre_a = grad_pre_a.astype(jnp.bfloat16)
    grad_pre_i = grad_pre_i.astype(jnp.bfloat16)
    grads["gate_a"] = blocked_grad(conv_out, grad_pre_a)
    grads["gate_i"] = blocked_grad(conv_out, grad_pre_i)
    grads["bias_a"] = jnp.sum(grad_pre_a.astype(jnp.float32), axis=0)
    grads["bias_i"] = jnp.sum(grad_pre_i.astype(jnp.float32), axis=0)
    grad_conv = (
        grad_direct
        + blocked_t(grad_pre_a, weights["gate_a"])
        + blocked_t(grad_pre_i, weights["gate_i"])
    )
    _, conv_back = jax.vjp(
        partial(convolve, segment_ext=segment_ext, rows=rows), extended, conv_weight, conv_bias
    )
    grad_ext, grads["conv_weight"], grads["conv_bias"] = conv_back(grad_conv)
    edge_back = shifted(grad_ext[: KW - 1], "seq", -1)
    grad_x = grad_ext[KW - 1 :] + jnp.concatenate(
        [jnp.zeros((rows - (KW - 1), LRU), jnp.float32), edge_back], axis=0
    )
    grad_x = grad_x.astype(jnp.bfloat16)
    grads["w_x"] = t_matmul(normed, grad_x)
    grads["w_y"] = t_matmul(normed, grad_y)
    grad_normed = matmul_t(grad_y, weights["w_y"]) + matmul_t(grad_x, weights["w_x"])
    _, norm_back_one = jax.vjp(rms_norm, stream, gain_one)
    grad_stream_part, grads["gain_one"] = norm_back_one(grad_normed)
    input_grad = grad_middle + grad_stream_part
    packed_grad = jnp.concatenate([grads[entry[0]].reshape(-1) for entry in layout()])
    summed = lax.psum_scatter(packed_grad, ("seq", "fsdp"), scatter_dimension=0, tiled=True)
    new_moment = MOMENT * momentum + summed
    new_params = params - RATE * (summed + MOMENT * new_moment)
    new_average = BLEND * average + (1.0 - BLEND) * new_params
    return (output[None], input_grad[None], new_params, new_moment, new_average)


LANE = 128
TP = 8
HALO = 544
SMALL = 160
GATES = 512
REGIONS = {
    "A": (4248, 256, 192, 32),
    "B": (53400, 1536, 16, 192),
    "C": (77976, 1152, 96, 144),
    "D": (188568, 1536, 36, 192),
}
ROWS = 243864
EVEN_FIRST = (0, 2, 4, 6, 1, 3, 5, 7)
F32 = jnp.float32
BF16 = jnp.bfloat16


class Plan:
    def __init__(self, n_seq, n_fsdp):
        self.n_fsdp = n_fsdp
        shards = n_seq * n_fsdp
        per = ROWS * LANE // shards
        self.per = per
        self.part = per % LANE
        self.own_rows = -(-per // 1024) * 8
        self.last = per // LANE
        bounds = [0]
        for i in range(1, shards):
            at = per * i / LANE
            for first, unit, count, _ in REGIONS.values():
                if first <= at < first + unit * count:
                    bounds.append(first + unit * round((at - first) / unit))
        bounds.append(ROWS)
        self.segments = []
        self.sizes = []
        self.table = np.zeros((shards, 16), np.int32)
        for i in range(shards):
            base = per * i // LANE
            self.table[i, 0] = per * i % LANE
            offset = SMALL + GATES if i == 0 else 0
            found = {}
            for slot, (name, (first, unit, count, wide)) in enumerate(REGIONS.items()):
                low = max(bounds[i], first)
                high = min(bounds[i + 1], first + unit * count)
                if high > low:
                    units = (high - low) // unit
                    found[name] = ((low - first) // unit, units, offset)
                    self.table[i, 1 + 3 * slot : 4 + 3 * slot] = (
                        low - base + HALO,
                        units,
                        offset,
                    )
                    offset += units * wide
            self.segments.append(found)
            self.sizes.append(offset)
            self.table[i, 13] = int(i == 0)
        self.lengths = [
            max(self.sizes[s * n_fsdp : (s + 1) * n_fsdp]) for s in range(n_seq)
        ]
        self.offsets = np.concatenate([[0], np.cumsum(self.lengths)]).astype(np.int32)
        self.longest = max(self.lengths)
        self.groups = ((0, 1), (2,), (3, 4, 5, 6), (7,))
        self.starts = [int(self.offsets[group[0]]) for group in self.groups]
        self.rows = [sum(self.lengths[s] for s in group) for group in self.groups]

    def pieces(self, name, groups):
        out = []
        for i, found in enumerate(self.segments):
            s, f = divmod(i, self.n_fsdp)
            if name in found and s in groups:
                first, units, offset = found[name]
                row = int(self.offsets[s] - self.offsets[groups[0]]) + offset
                out.append((f, row, first, units))
        return out


VMEM = pl.BlockSpec(memory_space=pltpu.VMEM)
ANY = pl.BlockSpec(memory_space=pl.ANY)
SMEM = pl.BlockSpec(memory_space=pltpu.SMEM)
LIMIT = pltpu.CompilerParams(vmem_limit_bytes=60 * 1024 * 1024)


def shape(dims, dtype):
    return jax.ShapeDtypeStruct(dims, dtype)


def aligned(value, multiple):
    return pl.multiple_of(value, multiple)


def lanes(rows):
    return lax.broadcasted_iota(jnp.int32, (rows, LANE), 1)


def swap_lanes(blocks):
    blocks = list(blocks)
    at = lanes(blocks[0].shape[0]) // 16
    for step in (4, 2, 1):
        low_side = (at & step) == 0
        for one in range(TP):
            if one & step == 0:
                left, right = blocks[one], blocks[one + step]
                blocks[one] = jnp.where(low_side, left, pltpu.roll(right, 16 * step, 1))
                blocks[one + step] = jnp.where(
                    low_side, pltpu.roll(left, LANE - 16 * step, 1), right
                )
    return blocks


def shift_down(source, source_row, target, target_row, rows, block, amount, unroll):
    def step(j, tail):
        z = pltpu.roll(source[pl.ds(source_row + j * block, block), :], amount, 1)
        above = pltpu.roll(jnp.concatenate([tail, z], axis=0), 1, 0)[8:]
        target[pl.ds(target_row + j * block, block), :] = jnp.where(
            lanes(block) < amount, above, z
        )
        return z[block - 8 :]

    lax.fori_loop(0, rows // block, step, jnp.zeros((8, LANE), F32), unroll=unroll)


def pack_body(plan, tab, hd, own, hu, *rest):
    outs, (win, al, wire, sems) = rest[:TP], rest[TP:]
    s, f = lax.axis_index("seq"), lax.axis_index("fsdp")
    me = s * plan.n_fsdp + f
    total = win.shape[0]
    first = pltpu.make_async_copy(hd, win.at[pl.ds(0, HALO)], sems.at[0])
    second = pltpu.make_async_copy(own, win.at[pl.ds(HALO, plan.own_rows)], sems.at[1])
    first.start()
    second.start()
    first.wait()
    second.wait()
    seam = HALO + plan.last
    kept = win[pl.ds(seam, 8), :]
    shift_down(hu, 0, win, seam, HALO, 32, plan.part, True)
    edge = lax.broadcasted_iota(jnp.int32, (8, LANE), 0) == 0
    win[pl.ds(seam, 8), :] = jnp.where(
        edge & (lanes(8) < plan.part), kept, win[pl.ds(seam, 8), :]
    )
    shift_down(win, 0, al, 0, total, 48, tab[me, 0], 7)

    def columns(g, _):
        at = tab[me, 1] + g * 256
        to = tab[me, 3] + g * 16
        for block in range(16):
            row = to + 16 * tab[me, 2] * (block // TP)
            wire[block % TP, pl.ds(aligned(row, 16), 16), :] = al[
                pl.ds(at + block, 16, stride=16), :
            ].astype(BF16)
        return 0

    lax.fori_loop(0, tab[me, 2], columns, 0)
    for slot in (4, 10):

        def grouped(j, _):
            for owner in range(TP):
                at = tab[me, slot] + j * 1536 + owner * 192
                to = tab[me, slot + 2] + j * 16
                for block in range(12):
                    row = to + 16 * tab[me, slot + 1] * block
                    wire[owner, pl.ds(aligned(row, 16), 16), :] = al[
                        pl.ds(at + block, 16, stride=12), :
                    ].astype(BF16)
            return 0

        lax.fori_loop(0, tab[me, slot + 1], grouped, 0)

    def mixed_columns(g, _):
        at = tab[me, 7] + g * 1152
        to = tab[me, 9] + g * 32
        wide = 32 * tab[me, 8]
        last = tab[me, 9] + 4 * wide + g * 16
        for half in range(2):
            for a in range(4):
                parts = swap_lanes(
                    [
                        al[pl.ds(at + 576 * half + 8 * a + b, 16, stride=36), :]
                        for b in range(TP)
                    ]
                )
                for owner in range(TP):
                    row = to + a * wide + 16 * half
                    wire[owner, pl.ds(aligned(row, 16), 16), :] = parts[owner].astype(BF16)
        parts = swap_lanes(
            [
                al[pl.ds(at + 576 * half + 32 + b, 16, stride=36), :]
                for half in range(2)
                for b in range(4)
            ]
        )
        for owner in range(TP):
            wire[owner, pl.ds(aligned(last, 16), 16), :] = parts[owner].astype(BF16)
        return 0

    lax.fori_loop(0, tab[me, 8], mixed_columns, 0)

    @pl.when(me == 0)
    def _():
        for owner in range(TP):
            wire[owner, pl.ds(0, SMALL), :] = al[pl.ds(HALO, SMALL), :].astype(BF16)
        for kind in range(2):
            for n in range(16):
                wire[n % TP, pl.ds(SMALL + 128 * (2 * kind + n // TP), 128), :] = al[
                    pl.ds(HALO + 152 + 2048 * kind + 128 * n, 128), :
                ].astype(BF16)

    copies = [
        pltpu.make_async_copy(wire.at[s ^ k], outs[k], sems.at[2 + k]) for k in range(TP)
    ]
    for copy in copies:
        copy.start()
    for copy in copies:
        copy.wait()


def pack(plan, hd, own, hu):
    total = -(-(HALO * 2 + plan.own_rows) // 672) * 672
    return pl.pallas_call(
        partial(pack_body, plan),
        out_shape=[shape((plan.longest, LANE), BF16)] * TP,
        in_specs=[SMEM, ANY, ANY, VMEM],
        out_specs=[ANY] * TP,
        scratch_shapes=[
            pltpu.VMEM((total, LANE), F32),
            pltpu.VMEM((total, LANE), F32),
            pltpu.VMEM((TP, plan.longest, LANE), BF16),
            pltpu.SemaphoreType.DMA((2 + TP,)),
        ],
        compiler_params=LIMIT,
        name="pack",
    )(jnp.asarray(plan.table), hd, own, hu)


def order_body(plan, *refs):
    pieces, outs, sems = refs[:TP], refs[TP : TP + 4], refs[TP + 4]
    s = lax.axis_index("seq")
    for start in (True, False):
        for number, group in enumerate(plan.groups):
            for source in group:
                size = plan.lengths[source]
                at = int(plan.offsets[source]) - plan.starts[number]
                for k in range(TP):

                    @pl.when((s ^ source) == k)
                    def _():
                        copy = pltpu.make_async_copy(
                            pieces[k].at[pl.ds(0, size)],
                            outs[number].at[pl.ds(at, size)],
                            sems.at[source],
                        )
                        if start:
                            copy.start()
                        else:
                            copy.wait()


def order(plan, pieces):
    return pl.pallas_call(
        partial(order_body, plan),
        out_shape=[shape((rows, LANE), BF16) for rows in plan.rows],
        in_specs=[ANY] * TP,
        out_specs=[VMEM] * 4,
        scratch_shapes=[pltpu.SemaphoreType.DMA((TP,))],
        compiler_params=LIMIT,
        name="order",
    )(*pieces)


def weight_copies(plan, number, weights, halves, b_rows):
    out = []
    for f, row, first, units in plan.pieces("A", plan.groups[number]):
        for target, begin, end in weights.get("A", ()):
            low, high = max(first, begin), min(first + units, end)
            if high > low:
                for n in range(2):
                    out.append(
                        (
                            f,
                            row + 16 * (units * n + low - first),
                            16 * (high - low),
                            target.at[pl.ds(16 * (low - begin), 16 * (high - low)), pl.ds(128 * n, 128)],
                        )
                    )
    for f, row, first, units in plan.pieces("B", plan.groups[number]):
        if b_rows is not None:
            for block in range(12):
                out.append(
                    (
                        f,
                        row + 16 * units * block,
                        16 * units,
                        b_rows.at[block, pl.ds(16 * first, 16 * units)],
                    )
                )
    for f, row, first, units in plan.pieces("C", plan.groups[number]):
        for target, begin, end in weights.get("C", ()):
            low, high = max(first, begin), min(first + units, end)
            if high > low:
                for a in range(4):
                    out.append(
                        (
                            f,
                            row + 32 * (units * a + low - first),
                            32 * (high - low),
                            target.at[pl.ds(32 * (low - begin), 32 * (high - low)), pl.ds(128 * a, 128)],
                        )
                    )
        if halves is not None:
            out.append(
                (f, row + 128 * units, 16 * units, halves.at[pl.ds(16 * first, 16 * units)])
            )
    for f, row, first, units in plan.pieces("D", plan.groups[number]):
        for target, begin, end in weights.get("D", ()):
            for n in range(12):
                out.append(
                    (
                        f,
                        row + 16 * units * n,
                        16 * units,
                        target.at[pl.ds(16 * (first - begin), 16 * units), pl.ds(128 * n, 128)],
                    )
                )
    return out


def fetch_line(plan, line, copies, sems, first=0, phases=(True, False)):
    f = lax.axis_index("fsdp")
    for start in phases:
        for source in range(plan.n_fsdp):
            for away in range(plan.n_fsdp):

                @pl.when((f ^ source) == away)
                def _():
                    for number, (holder, row, rows, target) in enumerate(copies):
                        if holder == source:
                            copy = pltpu.make_async_copy(
                                line[away].at[pl.ds(row, rows)], target, sems.at[first + number]
                            )
                            if start:
                                copy.start()
                            else:
                                copy.wait()


def first_copies(plan, small, gates, w_y, w_x, b_head):
    out = [(0, 0, SMALL, small), (0, SMALL, GATES, gates)]
    out += weight_copies(plan, 0, {"A": ((w_y, 0, 96), (w_x, 96, 192))}, None, None)
    for f, row, first, units in plan.pieces("B", plan.groups[0]):
        out.append((f, row, 192 * units, b_head.at[pl.ds(192 * first, 192 * units)]))
    return out


def first_body(plan, *refs):
    line, refs = refs[: plan.n_fsdp], refs[plan.n_fsdp :]
    *targets, sems = refs
    fetch_line(plan, line, first_copies(plan, *targets), sems)


def head_rows(plan):
    return sum(144 * p[3] for p in plan.pieces("C", plan.groups[1]))


def b_head_rows(plan):
    return sum(192 * p[3] for p in plan.pieces("B", plan.groups[0]))


class Nowhere:
    at = property(lambda self: self)

    def __getitem__(self, _):
        return self


def count_first(plan):
    return len(first_copies(plan, *[Nowhere()] * 5))


def unpack_first(plan, line):
    return pl.pallas_call(
        partial(first_body, plan),
        out_shape=[
            shape((SMALL, LANE), BF16),
            shape((GATES, LANE), BF16),
            shape((D, 256), BF16),
            shape((D, 256), BF16),
            shape((b_head_rows(plan), LANE), BF16),
        ],
        in_specs=[ANY] * len(line),
        out_specs=[VMEM] * 5,
        scratch_shapes=[pltpu.SemaphoreType.DMA((count_first(plan),))],
        compiler_params=LIMIT,
        name="unpack_first",
    )(*line)


def middle_copies(plan, b_rows, head):
    out = weight_copies(plan, 1, {}, None, b_rows)
    for f, row, first, units in plan.pieces("C", plan.groups[1]):
        out.append((f, row, 144 * units, head.at[pl.ds(144 * first, 144 * units)]))
    return out


def b_head_copies(plan, b_head, b_rows):
    out = []
    for _, _, first, units in plan.pieces("B", plan.groups[0]):
        for block in range(12):
            out.append(
                (
                    b_head.at[pl.ds(192 * first + 16 * units * block, 16 * units)],
                    b_rows.at[block, pl.ds(16 * first, 16 * units)],
                )
            )
    return out


def middle_body(plan, *refs):
    line, refs = refs[: plan.n_fsdp], refs[plan.n_fsdp :]
    b_head, outs, head, b_rows, sems, more = refs[0], refs[1 : 1 + TP], *refs[1 + TP :]
    local_copies = [
        pltpu.make_async_copy(source, target, more.at[number])
        for number, (source, target) in enumerate(b_head_copies(plan, b_head, b_rows))
    ]
    for copy in local_copies:
        copy.start()
    fetch_line(plan, line, middle_copies(plan, b_rows, head), sems)
    for copy in local_copies:
        copy.wait()
    s = lax.axis_index("seq")
    for k in range(TP):
        for n in range(2):
            unit = (s ^ k) + TP * n
            for block in range(12):
                outs[k][pl.ds(192 * n + 16 * block, 16), :] = b_rows[
                    block, pl.ds(aligned(16 * unit, 16), 16), :
                ]


def unpack_middle(plan, line, b_head):
    return pl.pallas_call(
        partial(middle_body, plan),
        out_shape=[shape((384, LANE), BF16)] * TP + [shape((head_rows(plan), LANE), BF16)],
        in_specs=[ANY] * (len(line) + 1),
        out_specs=[VMEM] * (TP + 1),
        scratch_shapes=[
            pltpu.VMEM((12, 256, LANE), BF16),
            pltpu.SemaphoreType.DMA((len(middle_copies(plan, *[Nowhere()] * 2)),)),
            pltpu.SemaphoreType.DMA((len(b_head_copies(plan, *[Nowhere()] * 2)),)),
        ],
        compiler_params=LIMIT,
        name="unpack_middle",
    )(*line, b_head)


def head_copies(plan, head, weight, halves):
    out = []
    for _, _, first, units in plan.pieces("C", plan.groups[1]):
        for a in range(4):
            out.append(
                (
                    head.at[pl.ds(144 * first + 32 * units * a, 32 * units)],
                    weight.at[pl.ds(32 * first, 32 * units), pl.ds(128 * a, 128)],
                )
            )
        out.append(
            (
                head.at[pl.ds(144 * first + 128 * units, 16 * units)],
                halves.at[pl.ds(16 * first, 16 * units)],
            )
        )
    return out


def second_copies(plan, w_gate, w_up, w_down, halves):
    return weight_copies(
        plan,
        2,
        {"C": ((w_gate, 0, 48), (w_up, 48, 96)), "D": ((w_down, 0, 16),)},
        halves,
        None,
    )


def halves_copies(plan, halves):
    return [
        (f, row + 128 * units, 16 * units, halves.at[pl.ds(16 * first, 16 * units)])
        for f, row, first, units in plan.pieces("C", plan.groups[2])
    ]


def second_body(plan, *refs):
    line, refs = refs[: plan.n_fsdp], refs[plan.n_fsdp :]
    head, w_gate, w_up, w_down, halves, sems, more = refs
    local_copies = [
        pltpu.make_async_copy(source, target, more.at[number])
        for number, (source, target) in enumerate(head_copies(plan, head, w_gate, halves))
    ]
    for copy in local_copies:
        copy.start()
    merged = halves_copies(plan, halves)
    whole = second_copies(plan, w_gate, w_up, w_down, None)
    fetch_line(plan, line, merged, sems, 0, (True,))
    fetch_line(plan, line, whole, sems, len(merged), (True,))
    fetch_line(plan, line, merged, sems, 0, (False,))
    for copy in local_copies:
        copy.wait()
    for weight, begin in ((w_gate, 0), (w_up, 48)):

        def step(g, _):
            last = halves[pl.ds(aligned(16 * (begin + g), 16), 16), :]
            weight[pl.ds(aligned(32 * g, 16), 16), pl.ds(512, 64)] = last[:, :64]
            weight[pl.ds(aligned(32 * g + 16, 16), 16), pl.ds(512, 64)] = last[:, 64:]
            return 0

        lax.fori_loop(0, 48, step, 0, unroll=8)
    fetch_line(plan, line, whole, sems, len(merged), (False,))


def unpack_second(plan, line, head):
    many = len(second_copies(plan, *[Nowhere()] * 4))
    few = len(head_copies(plan, *[Nowhere()] * 3))
    return pl.pallas_call(
        partial(second_body, plan),
        out_shape=[
            shape((D, FF // TP), BF16),
            shape((D, FF // TP), BF16),
            shape((256, D), BF16),
        ],
        in_specs=[ANY] * (len(line) + 1),
        out_specs=[VMEM] * 3,
        scratch_shapes=[
            pltpu.VMEM((96 * 16, LANE), BF16),
            pltpu.SemaphoreType.DMA((many,)),
            pltpu.SemaphoreType.DMA((few,)),
        ],
        compiler_params=LIMIT,
        name="unpack_second",
    )(*line, head)


def third_copies(plan, w_down):
    return weight_copies(plan, 3, {"D": ((w_down, 0, 36),)}, None, None)


def third_body(plan, *refs):
    line, refs = refs[: plan.n_fsdp], refs[plan.n_fsdp :]
    before, w_down, sems, one = refs
    copy = pltpu.make_async_copy(before, w_down.at[pl.ds(0, 256)], one.at[0])
    copy.start()
    fetch_line(plan, line, third_copies(plan, w_down), sems)
    copy.wait()


def unpack_third(plan, line, before):
    many = len(third_copies(plan, Nowhere()))
    return pl.pallas_call(
        partial(third_body, plan),
        out_shape=shape((FF // TP, D), BF16),
        in_specs=[ANY] * (len(line) + 1),
        out_specs=VMEM,
        scratch_shapes=[
            pltpu.SemaphoreType.DMA((many,)),
            pltpu.SemaphoreType.DMA((1,)),
        ],
        compiler_params=LIMIT,
        name="unpack_third",
    )(*line, before)


def out_rows_body(*refs):
    pieces, w_out = refs[:TP], refs[TP]
    s = lax.axis_index("seq")
    for k in range(TP):
        for n in range(2):
            to = aligned(128 * n + 16 * (s ^ k), 16)
            for block in range(12):
                w_out[pl.ds(to, 16), pl.ds(128 * block, 128)] = pieces[k][
                    pl.ds(192 * n + 16 * block, 16), :
                ]


def join_out_rows(pieces):
    return pl.pallas_call(
        out_rows_body,
        out_shape=shape((256, D), BF16),
        in_specs=[VMEM] * TP,
        out_specs=VMEM,
        compiler_params=LIMIT,
        name="join_out_rows",
    )(*pieces)


def split_rows_body(grad, *pieces):
    s = lax.axis_index("seq")
    for k in range(TP):
        for n in range(2):
            at = aligned(128 * n + 16 * (s ^ k), 16)
            for block in range(12):
                pieces[k][pl.ds(192 * n + 16 * block, 16), :] = grad[
                    pl.ds(at, 16), pl.ds(128 * block, 128)
                ]


def split_out_rows(grad):
    return pl.pallas_call(
        split_rows_body,
        out_shape=[shape((384, LANE), F32)] * TP,
        in_specs=[VMEM],
        out_specs=[VMEM] * TP,
        compiler_params=LIMIT,
        name="split_out_rows",
    )(grad)


def start_copies(copies, sems, first=0):
    made = [
        pltpu.make_async_copy(source, target, sems.at[first + number])
        for number, (source, target) in enumerate(copies)
    ]
    for copy in made:
        copy.start()
    return made


def to_wires(plan, copies, wires, sems, first, start):
    f = lax.axis_index("fsdp")
    for j in range(plan.n_fsdp):
        for x in range(plan.n_fsdp):

            @pl.when((f ^ j) == x)
            def _():
                for number, (holder, row, rows, source) in enumerate(copies):
                    if holder == j:
                        copy = pltpu.make_async_copy(
                            source, wires[x].at[pl.ds(row, rows)], sems.at[first + number]
                        )
                        if start:
                            copy.start()
                        else:
                            copy.wait()


def wire_second_body(plan, g_gate, g_up, g_down, *refs):
    wires, (head, halves, sems) = refs[: plan.n_fsdp], refs[plan.n_fsdp :]
    whole = second_copies(plan, g_gate, g_up, g_down, None)
    merged = halves_copies(plan, halves)
    more = [(b, a) for a, b in head_copies(plan, head, g_gate, halves)]
    to_wires(plan, whole, wires, sems, 0, True)
    for grad, begin in ((g_gate, 0), (g_up, 48)):

        def step(g, _):
            left = grad[pl.ds(aligned(32 * g, 16), 16), pl.ds(512, 64)]
            right = grad[pl.ds(aligned(32 * g + 16, 16), 16), pl.ds(512, 64)]
            halves[pl.ds(aligned(16 * (begin + g), 16), 16), :] = jnp.concatenate(
                [left, right], axis=1
            )
            return 0

        lax.fori_loop(0, 48, step, 0, unroll=8)
    to_wires(plan, merged, wires, sems, len(whole), True)
    made = start_copies(more, sems, len(whole) + len(merged))
    to_wires(plan, whole, wires, sems, 0, False)
    to_wires(plan, merged, wires, sems, len(whole), False)
    for copy in made:
        copy.wait()


def wire_second(plan, g_gate, g_up, g_down):
    many = len(second_copies(plan, *[Nowhere()] * 4)) + len(
        head_copies(plan, *[Nowhere()] * 3)
    )
    out = pl.pallas_call(
        partial(wire_second_body, plan),
        out_shape=[shape((plan.rows[2], LANE), F32)] * plan.n_fsdp
        + [shape((head_rows(plan), LANE), F32)],
        in_specs=[VMEM] * 3,
        out_specs=[ANY] * (plan.n_fsdp + 1),
        scratch_shapes=[
            pltpu.VMEM((96 * 16, LANE), F32),
            pltpu.SemaphoreType.DMA((many,)),
        ],
        compiler_params=LIMIT,
        name="wire_second",
    )(g_gate, g_up, g_down)
    return out[:-1], out[-1]


def wire_plain(plan, copies_of, rows, operands):
    many = len(copies_of(*[Nowhere()] * len(operands)))

    def body(*refs):
        *refs, sems = refs
        sources, wires = refs[: len(operands)], refs[len(operands) :]
        copies = copies_of(*sources)
        to_wires(plan, copies, wires, sems, 0, True)
        to_wires(plan, copies, wires, sems, 0, False)

    return pl.pallas_call(
        body,
        out_shape=[shape((rows, LANE), F32)] * plan.n_fsdp,
        in_specs=[VMEM] * len(operands),
        out_specs=[ANY] * plan.n_fsdp,
        scratch_shapes=[pltpu.SemaphoreType.DMA((many,))],
        compiler_params=LIMIT,
    )(*operands)


def wire_third(plan, g_down):
    return wire_plain(plan, partial(third_copies, plan), plan.rows[3], (g_down,))


def wire_middle_body(plan, head, *refs):
    pieces, refs = refs[:TP], refs[TP:]
    wires, (b_head, b_rows, sems) = refs[: plan.n_fsdp], refs[plan.n_fsdp :]
    s = lax.axis_index("seq")
    for k in range(TP):
        for n in range(2):
            unit = (s ^ k) + TP * n
            for block in range(12):
                b_rows[block, pl.ds(aligned(16 * unit, 16), 16), :] = pieces[k][
                    pl.ds(192 * n + 16 * block, 16), :
                ]
    copies = middle_copies(plan, b_rows, head)
    to_wires(plan, copies, wires, sems, 0, True)
    more = [(b, a) for a, b in b_head_copies(plan, b_head, b_rows)]
    made = start_copies(more, sems, len(copies))
    to_wires(plan, copies, wires, sems, 0, False)
    for copy in made:
        copy.wait()


def wire_middle(plan, head, pieces):
    many = len(middle_copies(plan, *[Nowhere()] * 2)) + len(
        b_head_copies(plan, *[Nowhere()] * 2)
    )
    out = pl.pallas_call(
        partial(wire_middle_body, plan),
        out_shape=[shape((plan.rows[1], LANE), F32)] * plan.n_fsdp
        + [shape((b_head_rows(plan), LANE), F32)],
        in_specs=[VMEM] * (1 + TP),
        out_specs=[ANY] * (plan.n_fsdp + 1),
        scratch_shapes=[
            pltpu.VMEM((12, 256, LANE), F32),
            pltpu.SemaphoreType.DMA((many,)),
        ],
        compiler_params=LIMIT,
        name="wire_middle",
    )(head, *pieces)
    return out[:-1], out[-1]


def split_copies(plan, copies):
    border = int(plan.offsets[1])
    return (
        [copy for copy in copies if copy[1] < border],
        [(f, row - border, rows, at) for f, row, rows, at in copies if row >= border],
    )


def wire_x(plan, g_x, b_head):
    def copies_of(g_x, b_head):
        nowhere = Nowhere()
        return split_copies(plan, first_copies(plan, nowhere, nowhere, nowhere, g_x, b_head))[1]

    return wire_plain(plan, copies_of, plan.lengths[1], (g_x, b_head))


def wire_y_body(plan, gains, vectors, gates, g_y, g_x, *refs):
    wires, (small, sems) = refs[: plan.n_fsdp], refs[plan.n_fsdp :]
    s = lax.axis_index("seq")
    small[...] = jnp.zeros_like(small)
    small[pl.ds(0, 24), :] = gains[...]
    for n in range(8):
        for part in range(2):
            small[pl.ds(24 + 16 * n + s + TP * part, 1), :] = vectors[
                pl.ds(2 * n + part, 1), :
            ]
    copies = split_copies(plan, first_copies(plan, small, gates, g_y, g_x, Nowhere()))[0]
    to_wires(plan, copies, wires, sems, 0, True)
    to_wires(plan, copies, wires, sems, 0, False)


def wire_y(plan, gains, vectors, gates, g_y, g_x):
    return pl.pallas_call(
        partial(wire_y_body, plan),
        out_shape=[shape((plan.lengths[0], LANE), F32)] * plan.n_fsdp,
        in_specs=[VMEM] * 5,
        out_specs=[ANY] * plan.n_fsdp,
        scratch_shapes=[
            pltpu.VMEM((SMALL, LANE), F32),
            pltpu.SemaphoreType.DMA((count_first(plan),)),
        ],
        compiler_params=LIMIT,
        name="wire_y",
    )(gains, vectors, gates, g_y, g_x)


def spread_body(plan, targets, *refs):
    count = len(targets)
    sums, outs, sems = refs[:count], refs[count : count + TP], refs[count + TP]
    s = lax.axis_index("seq")
    for start in (True, False):
        for summed, group in zip(sums, targets):
            for target in group:
                size = plan.lengths[target]
                at = int(plan.offsets[target] - plan.offsets[group[0]])
                for k in range(TP):

                    @pl.when((s ^ target) == k)
                    def _():
                        copy = pltpu.make_async_copy(
                            summed.at[pl.ds(at, size)],
                            outs[k].at[pl.ds(0, size)],
                            sems.at[target],
                        )
                        if start:
                            copy.start()
                        else:
                            copy.wait()


def spread(plan, targets, sums):
    rows = max(plan.lengths[s] for group in targets for s in group)
    return pl.pallas_call(
        partial(spread_body, plan, targets),
        out_shape=[shape((rows, LANE), F32)] * TP,
        in_specs=[VMEM] * len(sums),
        out_specs=[ANY] * TP,
        scratch_shapes=[pltpu.SemaphoreType.DMA((TP,))],
        compiler_params=LIMIT,
    )(*sums)


def shift_up(source, source_row, target, target_row, rows, block, amount):
    def step(j, _):
        both = pltpu.roll(source[pl.ds(source_row + j * block, block + 8), :], amount, 1)
        below = pltpu.roll(both, block + 7, 0)[:block]
        target[pl.ds(target_row + j * block, block), :] = jnp.where(
            lanes(block) < amount, both[:block], below
        )
        return 0

    lax.fori_loop(0, rows // block, step, 0, unroll=True)


def collect_body(plan, tab, *refs):
    pieces, (own, hd, hu, al, win, wire, sems) = refs[: 2 * TP], refs[2 * TP :]
    s, f = lax.axis_index("seq"), lax.axis_index("fsdp")
    me = s * plan.n_fsdp + f

    def bring(start):
        for number in range(2):

            @pl.when(jnp.minimum(s, 1) == number)
            def _():
                for k in range(TP):
                    piece = pieces[TP * number + k]
                    copy = pltpu.make_async_copy(
                        piece, wire.at[s ^ k, pl.ds(0, piece.shape[0])], sems.at[k]
                    )
                    if start:
                        copy.start()
                    else:
                        copy.wait()

    bring(True)
    total = win.shape[0]

    def clear(j, _):
        al[pl.ds(aligned(j * 96, 8), 96), :] = jnp.zeros((96, LANE), F32)
        return 0

    lax.fori_loop(0, al.shape[0] // 96, clear, 0, unroll=4)
    bring(False)

    def columns(g, _):
        at = tab[me, 1] + g * 256
        to = tab[me, 3] + g * 16
        for block in range(16):
            row = to + 16 * tab[me, 2] * (block // TP)
            al[pl.ds(at + block, 16, stride=16), :] = wire[
                block % TP, pl.ds(aligned(row, 16), 16), :
            ]
        return 0

    lax.fori_loop(0, tab[me, 2], columns, 0)
    for slot in (4, 10):

        def grouped(j, _):
            for owner in range(TP):
                at = tab[me, slot] + j * 1536 + owner * 192
                to = tab[me, slot + 2] + j * 16
                for block in range(12):
                    row = to + 16 * tab[me, slot + 1] * block
                    al[pl.ds(at + block, 16, stride=12), :] = wire[
                        owner, pl.ds(aligned(row, 16), 16), :
                    ]
            return 0

        lax.fori_loop(0, tab[me, slot + 1], grouped, 0)

    def mixed_columns(g, _):
        at = tab[me, 7] + g * 1152
        to = tab[me, 9] + g * 32
        wide = 32 * tab[me, 8]
        last = tab[me, 9] + 4 * wide + g * 16
        for half in range(2):
            for a in range(4):
                parts = swap_lanes(
                    [
                        wire[owner, pl.ds(aligned(to + a * wide + 16 * half, 16), 16), :]
                        for owner in range(TP)
                    ]
                )
                for b in range(TP):
                    al[pl.ds(at + 576 * half + 8 * a + b, 16, stride=36), :] = parts[b]
        parts = swap_lanes(
            [wire[owner, pl.ds(aligned(last, 16), 16), :] for owner in range(TP)]
        )
        for half in range(2):
            for b in range(4):
                al[pl.ds(at + 576 * half + 32 + b, 16, stride=36), :] = parts[4 * half + b]
        return 0

    lax.fori_loop(0, tab[me, 8], mixed_columns, 0)

    @pl.when(me == 0)
    def _():
        summed = wire[0, pl.ds(0, 152), :]
        for owner in range(1, TP):
            summed = summed + wire[owner, pl.ds(0, 152), :]
        al[pl.ds(HALO, 152), :] = summed
        for kind in range(2):
            for n in range(16):
                al[pl.ds(HALO + 152 + 2048 * kind + 128 * n, 128), :] = wire[
                    n % TP, pl.ds(SMALL + 128 * (2 * kind + n // TP), 128), :
                ]

    def back(j, _):
        both = pltpu.roll(
            al[pl.ds(aligned(j * 48, 8), 56), :], lax.rem(LANE - tab[me, 0], LANE), 1
        )
        below = pltpu.roll(both, 55, 0)[:48]
        win[pl.ds(aligned(j * 48, 8), 48), :] = jnp.where(
            lanes(48) < LANE - tab[me, 0], both[:48], below
        )
        return 0

    lax.fori_loop(0, total // 48, back, 0, unroll=7)
    hd[...] = win[pl.ds(0, HALO), :]
    own[...] = win[pl.ds(HALO, plan.own_rows), :]
    shift_up(win, HALO + plan.last, hu, 0, HALO, 32, LANE - plan.part)


def collect(plan, pieces):
    total = -(-(HALO * 2 + plan.own_rows) // 672) * 672
    cleared = total + 96
    return pl.pallas_call(
        partial(collect_body, plan),
        out_shape=[
            shape((plan.own_rows, LANE), F32),
            shape((HALO, LANE), F32),
            shape((HALO, LANE), F32),
        ],
        in_specs=[SMEM] + [ANY] * (2 * TP),
        out_specs=[VMEM] * 3,
        scratch_shapes=[
            pltpu.VMEM((cleared, LANE), F32),
            pltpu.VMEM((total, LANE), F32),
            pltpu.VMEM((TP, plan.longest, LANE), F32),
            pltpu.SemaphoreType.DMA((TP,)),
        ],
        compiler_params=LIMIT,
        name="collect",
    )(jnp.asarray(plan.table), *pieces)


def tail_body(plan, value, out):
    first = (plan.last - HALO) % 8
    out[...] = jnp.zeros_like(out)
    shift_down(value, 0, out, first, HALO, 32, plan.part, True)
    z = pltpu.roll(value[pl.ds(HALO - 8, 8), :], plan.part, 1)
    row = lax.broadcasted_iota(jnp.int32, (8, LANE), 0)
    out[pl.ds(first + HALO, 8), :] = jnp.where(
        (row == 0) & (lanes(8) < plan.part), pltpu.roll(z, 1, 0), 0.0
    )


def place_tail(plan, value):
    rows = plan.own_rows - (plan.last - HALO) // 8 * 8
    return pl.pallas_call(
        partial(tail_body, plan),
        out_shape=shape((max(rows, HALO + 16), LANE), F32),
        in_specs=[VMEM],
        out_specs=VMEM,
        compiler_params=LIMIT,
        name="place_tail",
    )(value)[:rows]


def scan_body(reverse, coefficient, addend, out):
    rows, width = coefficient.shape
    at = lax.broadcasted_iota(jnp.int32, (8, width), 0)
    if reverse:
        at = 7 - at
    steps = rows // 8

    def step(j, carry):
        block = steps - 1 - j if reverse else j
        here = pl.ds(aligned(block * 8, 8), 8)
        a, b = coefficient[here, :], addend[here, :]
        for reach in (1, 2, 4):
            turn = 8 - reach if reverse else reach
            inside = at >= reach
            b = b + jnp.where(inside, a * pltpu.roll(b, turn, 0), 0.0)
            a = jnp.where(inside, a * pltpu.roll(a, turn, 0), a)
        value = b + a * carry
        out[here, :] = value
        edge = value[0:1] if reverse else value[7:8]
        return jnp.broadcast_to(edge, (8, width))

    lax.fori_loop(0, steps, step, jnp.zeros((8, width), F32), unroll=4)


def linear_scan(coefficient, addend, reverse):
    return pl.pallas_call(
        partial(scan_body, reverse),
        out_shape=shape(coefficient.shape, F32),
        in_specs=[VMEM] * 2,
        out_specs=VMEM,
        compiler_params=LIMIT,
        name="scan_back" if reverse else "scan",
    )(coefficient, addend)


def swap(value, bit):
    return lax.ppermute(value, "seq", [(i, i ^ bit) for i in range(TP)])


def exchange(pieces, targets=range(TP)):
    return [pieces[0]] + [
        lax.ppermute(pieces[k], "seq", [(i ^ k, i) for i in targets]) for k in range(1, TP)
    ]


def gather_stream(mine):
    half = mine.shape[0] // 2

    over_x, over_y = swap(mine, 2), swap(mine, 4)
    over_xy = [swap(over_x[:half], 4), swap(over_y[half:], 2)]
    chip = [mine, over_x, over_y] + over_xy
    return jnp.concatenate(chip + [swap(part, 1) for part in chip], axis=0)


def scatter_stream(partial_sums):
    rows = partial_sums.shape[0] // TP
    half = rows // 2

    def send(value, bit):
        return swap(value.astype(BF16), bit).astype(F32)

    other = send(partial_sums[TP // 2 * rows :], 1)
    q = (partial_sums[: TP // 2 * rows] + other).reshape(4, rows, -1)
    up = send(jnp.concatenate([q[1, :half], q[3, :half]]), 2)
    down = send(jnp.concatenate([q[2, half:], q[3, half:]]), 4)
    top = send(q[2, :half] + up[half:], 4)
    low = send(q[1, half:] + down[half:], 2)
    return jnp.concatenate(
        [q[0, :half] + up[:half] + top, q[0, half:] + down[:half] + low], axis=0
    )


def to_positions(values, s):
    rows = values.shape[0] // TP
    parts = []
    for j in range(TP):
        k = s ^ j
        at = (k // 2 + 4 * (k % 2)) * rows
        parts.append(lax.dynamic_slice_in_dim(values, at, rows, 0))
    return jnp.concatenate(parts, axis=0)


def to_relative(values, s):
    rows = values.shape[0] // TP
    return jnp.concatenate(
        [lax.dynamic_slice_in_dim(values, (s ^ k) * rows, rows, 0) for k in EVEN_FIRST], axis=0
    )


def gather_line(value, count):
    out = [value]
    for x in range(1, count):
        out.append(lax.ppermute(value, "fsdp", [(i, i ^ x) for i in range(count)]))
    return out


def scatter_line(blocks):
    count = len(blocks)
    own, near, far, cross = blocks
    far = lax.ppermute(far, "fsdp", [(i, i ^ 1) for i in range(count)])
    near = lax.ppermute(near, "fsdp", [(i, i ^ 1) for i in range(count)])
    cross = lax.ppermute(cross + far, "fsdp", [(i, i ^ 3) for i in range(count)])
    return own + near + cross


def sliced(plan, *arguments):
    return sliced_step(plan, *arguments)


def sliced_step(plan, stream_in, cotangent, starts, params, momentum, average):
    n_fsdp = plan.n_fsdp
    s = lax.axis_index("seq")
    shards = TP * n_fsdp
    onward = [(i, i + 1) for i in range(shards - 1)]
    backward = [(i + 1, i) for i in range(shards - 1)]
    both = ("seq", "fsdp")
    edge = HALO * LANE
    per = plan.per

    hd, hu = lax.optimization_barrier((params[per - edge :], params[:edge]))
    hd = lax.ppermute(hd.astype(BF16), both, onward)
    hu = lax.ppermute(hu.astype(BF16), both, backward)
    own = jnp.pad(params, (0, plan.own_rows * LANE - per)).reshape(-1, LANE)
    pieces = pack(
        plan, hd.astype(F32).reshape(-1, LANE), own, hu.astype(F32).reshape(-1, LANE)
    )
    first, middle_wire, second, third = order(plan, exchange(pieces))
    stream_bf, cotangent_bf, first = lax.optimization_barrier(
        (stream_in[0], cotangent[0], first)
    )
    line = gather_line(first, n_fsdp)
    middle_wire, second, third, line = lax.optimization_barrier(
        (middle_wire, second, third, line)
    )
    small, gates, w_y, w_x, b_head = unpack_first(plan, line)
    line = gather_line(middle_wire, n_fsdp)
    *out_rows, head = unpack_middle(plan, line, b_head)
    w_out = join_out_rows(exchange(out_rows))
    line = gather_line(second, n_fsdp)
    w_gate, w_up, w_down = unpack_second(plan, line, head)
    w_down = unpack_third(plan, gather_line(third, n_fsdp), w_down)

    mine = stream_in[0].astype(F32)
    stream = gather_stream(stream_bf)
    stream = stream.astype(F32)
    grad_out = gather_stream(cotangent_bf)
    rows = stream.shape[0]

    small = small.astype(F32)
    gain_one = small[0:12].reshape(-1)
    gain_two = small[12:24].reshape(-1)

    def channels(at):
        return jnp.concatenate(
            [
                lax.dynamic_slice_in_dim(small, at + s, 1, 0),
                lax.dynamic_slice_in_dim(small, at + s + TP, 1, 0),
            ],
            axis=1,
        )[0]

    conv_bias, bias_a, bias_i, lambda_raw = (channels(24 + 16 * j) for j in range(4))
    conv_weight = jnp.stack([channels(88 + 16 * j) for j in range(KW)])

    positions = jnp.arange(rows, dtype=jnp.int32)
    ext_pos = jnp.arange(rows + KW - 1, dtype=jnp.int32) - (KW - 1)
    segment_ext = segment_ids(ext_pos, starts[0])
    starting = start_flags(positions, starts[0])[:, None]

    def gate_product(values, at):
        return jnp.concatenate(
            [matmul(values[:, :HB], gates[at : at + HB]), matmul(values[:, HB:], gates[at + HB : at + 2 * HB])],
            axis=1,
        )

    def gate_product_t(values, at):
        return jnp.concatenate(
            [matmul_t(values[:, :HB], gates[at : at + HB]), matmul_t(values[:, HB:], gates[at + HB : at + 2 * HB])],
            axis=1,
        )

    normed = rms_norm(stream, gain_one).astype(BF16)
    branch_y = to_positions(matmul(normed, w_y), s)
    branch_x = to_positions(matmul(normed, w_x).astype(BF16), s)
    extended = jnp.pad(branch_x, ((KW - 1, 0), (0, 0))).astype(F32)

    def convolve_here(extended, weight, bias):
        total = jnp.zeros((rows, bias.shape[0]), F32) + bias
        for lag in range(KW):
            source = extended[KW - 1 - lag : KW - 1 - lag + rows]
            same = segment_ext[KW - 1 - lag : KW - 1 - lag + rows] == segment_ext[KW - 1 :]
            total = total + weight[lag] * source * same.astype(F32)[:, None]
        return total

    conv_out = convolve_here(extended, conv_weight, conv_bias).astype(BF16)
    conv_val = conv_out.astype(F32)
    pre_a = gate_product(conv_out, 0) + bias_a
    pre_i = gate_product(conv_out, 2 * HB) + bias_i
    decay, drive = gate_terms(pre_a, pre_i, conv_val, lambda_raw, starting)
    state = linear_scan(decay, drive, False)
    gelu_y = jax.nn.gelu(branch_y, approximate=True)
    mixed = to_relative((state * gelu_y).astype(BF16), s)
    middle = mine + scatter_stream(matmul(mixed, w_out))
    normed_two_mine = rms_norm(middle, gain_two).astype(BF16)
    normed_two = gather_stream(normed_two_mine)
    gate = matmul(normed_two, w_gate)
    upward = matmul(normed_two, w_up)
    hidden = gelu_product(gate, upward).astype(BF16)
    g_down = t_matmul(hidden, grad_out)
    summed_three = scatter_line(wire_third(plan, g_down))
    out_sums = matmul(hidden, w_down)
    output = (middle + scatter_stream(out_sums)).astype(BF16)
    gate, upward, _ = lax.optimization_barrier((gate, upward, hidden))

    grad_hidden = matmul_t(grad_out, w_down)
    _, product_back = jax.vjp(gelu_product, gate, upward)
    grad_gate, grad_up = product_back(grad_hidden)
    grad_gate, grad_up = grad_gate.astype(BF16), grad_up.astype(BF16)
    g_gate = t_matmul(normed_two, grad_gate)
    g_up = t_matmul(normed_two, grad_up)
    grad_normed_two = scatter_stream(matmul_t(grad_gate, w_gate) + matmul_t(grad_up, w_up))
    wire_two, wire_head = wire_second(plan, g_gate, g_up, g_down)
    summed_two = scatter_line(wire_two)

    _, norm_back_two = jax.vjp(rms_norm, middle, gain_two)
    grad_middle_part, g_gain_two = norm_back_two(grad_normed_two)
    grad_middle = cotangent[0].astype(F32) + grad_middle_part
    grad_first = gather_stream(grad_middle.astype(BF16))
    g_out = t_matmul(mixed, grad_first)
    wire_mid, b_head = wire_middle(plan, wire_head, exchange(split_out_rows(g_out)))
    summed_mid = scatter_line(wire_mid)
    grad_mixed = to_positions(matmul_t(grad_first, w_out), s)
    _, gelu_back = jax.vjp(partial(jax.nn.gelu, approximate=True), branch_y)
    grad_y = gelu_back(grad_mixed * state)[0].astype(BF16)
    next_decay = jnp.concatenate([decay[1:], jnp.ones((1, decay.shape[1]), F32)], axis=0)
    adjoint = linear_scan(next_decay, grad_mixed * gelu_y, True)
    previous = jnp.concatenate([jnp.zeros((1, decay.shape[1]), F32), state[:-1]], axis=0)
    _, gates_back = jax.vjp(gate_terms, pre_a, pre_i, conv_val, lambda_raw, starting)
    grad_pre_a, grad_pre_i, grad_direct, g_lambda, _ = gates_back((adjoint * previous, adjoint))
    grad_pre_a, grad_pre_i = grad_pre_a.astype(BF16), grad_pre_i.astype(BF16)
    g_gates = jnp.concatenate(
        [
            t_matmul(conv_out[:, n : n + HB], grad[:, n : n + HB])
            for grad in (grad_pre_a, grad_pre_i)
            for n in (0, HB)
        ],
        axis=0,
    )
    g_bias_a = jnp.sum(grad_pre_a.astype(F32), axis=0)
    g_bias_i = jnp.sum(grad_pre_i.astype(F32), axis=0)
    grad_conv = grad_direct + gate_product_t(grad_pre_a, 0) + gate_product_t(grad_pre_i, 2 * HB)
    _, conv_back = jax.vjp(convolve_here, extended, conv_weight, conv_bias)
    grad_ext, g_conv_weight, g_conv_bias = conv_back(grad_conv)
    grad_x = to_relative(grad_ext[KW - 1 :].astype(BF16), s)
    grad_y = to_relative(grad_y, s)
    g_x = t_matmul(normed, grad_x)
    g_y = t_matmul(normed, grad_y)
    grad_normed = scatter_stream(matmul_t(grad_y, w_y) + matmul_t(grad_x, w_x))
    _, norm_back_one = jax.vjp(rms_norm, mine, gain_one)
    grad_stream_part, g_gain_one = norm_back_one(grad_normed)
    input_grad = grad_middle + grad_stream_part

    summed_x = scatter_line(wire_x(plan, g_x, b_head))
    gains = jnp.concatenate([g_gain_one, g_gain_two]).reshape(-1, LANE)
    vectors = jnp.stack(
        [g_conv_bias, g_bias_a, g_bias_i, g_lambda] + [g_conv_weight[k] for k in range(KW)]
    ).reshape(-1, LANE)
    summed_y = scatter_line(wire_y(plan, gains, vectors, g_gates, g_y, g_x))
    early = spread(
        plan, ((1,),) + plan.groups[1:], (summed_x, summed_mid, summed_two, summed_three)
    )
    got = exchange(spread(plan, ((0,),), (summed_y,)), (0,))
    got += exchange(early)
    grad_own, grad_hd, grad_hu = collect(plan, got)
    from_next = lax.ppermute(grad_hd, both, backward)
    from_before = lax.ppermute(grad_hu, both, onward)
    tail = place_tail(plan, from_next).reshape(-1)
    whole = plan.own_rows * LANE
    summed = (
        grad_own.reshape(-1)
        + jnp.pad(from_before.reshape(-1), (0, whole - edge))
        + jnp.pad(tail, (whole - tail.shape[0], 0))
    )[:per]
    new_moment = MOMENT * momentum + summed
    new_params = params - RATE * (summed + MOMENT * new_moment)
    new_average = BLEND * average + (1.0 - BLEND) * new_params
    return (output[None], input_grad[None], new_params, new_moment, new_average)


def solution(mesh):
    n_seq, n_fsdp = mesh.shape["seq"], mesh.shape["fsdp"]
    fast = (n_seq, n_fsdp) == (TP, 4)
    body = partial(sliced, Plan(n_seq, n_fsdp)) if fast else local
    return jax.shard_map(
        body,
        mesh=mesh,
        in_specs=(
            P("fsdp", "seq", None),
            P("fsdp", "seq", None),
            P("fsdp", None),
            P(("seq", "fsdp")),
            P(("seq", "fsdp")),
            P(("seq", "fsdp")),
        ),
        out_specs=(
            P("fsdp", "seq", None),
            P("fsdp", "seq", None),
            P(("seq", "fsdp")),
            P(("seq", "fsdp")),
            P(("seq", "fsdp")),
        ),
        check_vma=False,
    )
```

```python
from functools import partial
import math

import jax
import jax.numpy as jnp
import numpy as np
from jax import lax
from jax.experimental import pallas as pl
from jax.experimental.pallas import tpu as pltpu
from jax.sharding import PartitionSpec as P


D = 1536
LRU = 2048
FF = 4608
HB = 128
KW = 4


EPS = 1e-06
RATE = 3e-05
MOMENT = 0.9
BLEND = 0.9
DECAY_SCALE = 8.0


def shifted(block, axis, distance):
    devices = range(lax.axis_size(axis))
    route = [(i - distance, i) for i in devices if i - distance in devices]
    return lax.ppermute(block, axis, route)


def carried_in(value, axis, join, neutral, backward):
    count, mine = (lax.axis_size(axis), lax.axis_index(axis))
    pieces = jax.tree.map(lambda part: lax.all_gather(part, axis), value)
    if backward:
        pieces = jax.tree.map(lambda part: part[::-1], pieces)
        mine = count - 1 - mine
    so_far = jax.tree.map(
        lambda part, zero: jnp.full_like(part, 0) + jnp.asarray(zero, part.dtype), value, neutral
    )

    def lap(position, so_far):
        longer = join(so_far, jax.tree.map(lambda part: part[position], pieces))
        return jax.tree.map(lambda new, old: jnp.where(position < mine, new, old), longer, so_far)

    return lax.fori_loop(0, count - 1, lap, so_far)


def layout():
    return [
        ("gain_one", (D,)),
        ("gain_two", (D,)),
        ("conv_bias", (LRU,)),
        ("bias_a", (LRU,)),
        ("bias_i", (LRU,)),
        ("lambda_raw", (LRU,)),
        ("conv_weight", (KW, LRU)),
        ("gate_a", (LRU // HB, HB, HB)),
        ("gate_i", (LRU // HB, HB, HB)),
        ("w_y", (D, LRU)),
        ("w_x", (D, LRU)),
        ("w_out", (LRU, D)),
        ("w_gate", (D, FF)),
        ("w_up", (D, FF)),
        ("w_down", (FF, D)),
    ]


def unpack(packed):
    result = {}
    offset = 0
    for entry_name, entry_shape in layout():
        amount = math.prod(entry_shape)
        result[entry_name] = packed[offset : offset + amount].reshape(entry_shape)
        offset += amount
    return result


def matmul(left, right):
    return jnp.dot(left, right, preferred_element_type=jnp.float32)


def matmul_t(left, right):
    return lax.dot_general(
        left, right, (((1,), (1,)), ((), ())), preferred_element_type=jnp.float32
    )


def t_matmul(left, right):
    return lax.dot_general(
        left, right, (((0,), (0,)), ((), ())), preferred_element_type=jnp.float32
    )


def blocked(values, weight):
    shaped = values.reshape(values.shape[0], LRU // HB, HB)
    return jnp.einsum("tnh,nhk->tnk", shaped, weight, preferred_element_type=jnp.float32).reshape(
        values.shape[0], LRU
    )


def blocked_t(values, weight):
    shaped = values.reshape(values.shape[0], LRU // HB, HB)
    return jnp.einsum("tnk,nhk->tnh", shaped, weight, preferred_element_type=jnp.float32).reshape(
        values.shape[0], LRU
    )


def blocked_grad(inputs, grads):
    left = inputs.reshape(inputs.shape[0], LRU // HB, HB)
    right = grads.reshape(grads.shape[0], LRU // HB, HB)
    return jnp.einsum("tnh,tnk->nhk", left, right, preferred_element_type=jnp.float32)


def rms_norm(values, gain):
    return values * lax.rsqrt(jnp.mean(values * values, axis=-1, keepdims=True) + EPS) * gain


def combine(earlier, later):
    return (earlier[0] * later[0], later[0] * earlier[1] + later[1])


def gate_terms(pre_a, pre_i, conv_val, lambda_raw, starting):
    recall = jax.nn.sigmoid(pre_a)
    admit = jax.nn.sigmoid(pre_i)
    rate = DECAY_SCALE * jax.nn.softplus(lambda_raw) * recall
    decay = (1.0 - starting) * jnp.exp(-rate)
    scale_in = starting + (1.0 - starting) * jnp.sqrt(-jnp.expm1(-2.0 * rate))
    return (decay, scale_in * admit * conv_val)


def convolve(extended, weight, bias, segment_ext, rows):
    total = jnp.zeros((rows, LRU), jnp.float32) + bias
    for lag in range(KW):
        source = extended[KW - 1 - lag : KW - 1 - lag + rows]
        same = (segment_ext[KW - 1 - lag : KW - 1 - lag + rows] == segment_ext[KW - 1 :]).astype(
            jnp.float32
        )
        total = total + weight[lag] * source * same[:, None]
    return total


def segment_ids(positions, doc_starts):
    return jnp.sum((doc_starts[None, :] <= positions[:, None]).astype(jnp.int32), axis=1)


def start_flags(positions, doc_starts):
    return jnp.max((doc_starts[None, :] == positions[:, None]).astype(jnp.float32), axis=1)


def gelu_product(left, right):
    return jax.nn.gelu(left, approximate=True) * right


def local(stream_in, cotangent, starts, params, momentum, average):
    weights = unpack(
        lax.all_gather(params.astype(jnp.bfloat16), ("seq", "fsdp"), axis=0, tiled=True)
    )
    stream = stream_in[0].astype(jnp.float32)
    incoming = cotangent[0].astype(jnp.float32)
    doc_starts = starts[0]
    rows = stream.shape[0]
    positions = lax.axis_index("seq") * rows + jnp.arange(rows, dtype=jnp.int32)
    ext_pos = positions[0] - (KW - 1) + jnp.arange(rows + KW - 1, dtype=jnp.int32)
    segment_ext = segment_ids(ext_pos, doc_starts)
    starting = start_flags(positions, doc_starts)[:, None]
    gain_one = weights["gain_one"].astype(jnp.float32)
    gain_two = weights["gain_two"].astype(jnp.float32)
    conv_weight = weights["conv_weight"].astype(jnp.float32)
    conv_bias = weights["conv_bias"].astype(jnp.float32)
    lambda_raw = weights["lambda_raw"].astype(jnp.float32)
    normed = rms_norm(stream, gain_one).astype(jnp.bfloat16)
    branch_y = matmul(normed, weights["w_y"])
    branch_x = matmul(normed, weights["w_x"]).astype(jnp.bfloat16)
    edge = shifted(branch_x[rows - (KW - 1) :], "seq", 1)
    extended = jnp.concatenate([edge, branch_x], axis=0).astype(jnp.float32)
    conv_out = convolve(extended, conv_weight, conv_bias, segment_ext, rows).astype(jnp.bfloat16)
    conv_val = conv_out.astype(jnp.float32)
    pre_a = blocked(conv_out, weights["gate_a"]) + weights["bias_a"].astype(jnp.float32)
    pre_i = blocked(conv_out, weights["gate_i"]) + weights["bias_i"].astype(jnp.float32)
    decay, drive = gate_terms(pre_a, pre_i, conv_val, lambda_raw, starting)
    prod_local, state_local = lax.associative_scan(combine, (decay, drive), axis=0)
    neutral = (jnp.ones((LRU,), jnp.float32), jnp.zeros((LRU,), jnp.float32))
    carried = carried_in((prod_local[-1], state_local[-1]), "seq", combine, neutral, False)
    carry_in = carried[1]
    state = lax.associative_scan(combine, (decay, drive.at[0].add(decay[0] * carry_in)), axis=0)[1]
    gelu_y = jax.nn.gelu(branch_y, approximate=True)
    mixed = (state * gelu_y).astype(jnp.bfloat16)
    middle = stream + matmul(mixed, weights["w_out"])
    normed_two = rms_norm(middle, gain_two).astype(jnp.bfloat16)
    gate = matmul(normed_two, weights["w_gate"])
    upward = matmul(normed_two, weights["w_up"])
    hidden = gelu_product(gate, upward).astype(jnp.bfloat16)
    output = (middle + matmul(hidden, weights["w_down"])).astype(jnp.bfloat16)
    grads = {}
    grad_out = incoming.astype(jnp.bfloat16)
    grads["w_down"] = t_matmul(hidden, grad_out)
    grad_hidden = matmul_t(grad_out, weights["w_down"])
    _, product_back = jax.vjp(gelu_product, gate, upward)
    grad_gate, grad_up = product_back(grad_hidden)
    grad_gate = grad_gate.astype(jnp.bfloat16)
    grad_up = grad_up.astype(jnp.bfloat16)
    grads["w_gate"] = t_matmul(normed_two, grad_gate)
    grads["w_up"] = t_matmul(normed_two, grad_up)
    grad_normed_two = matmul_t(grad_gate, weights["w_gate"]) + matmul_t(grad_up, weights["w_up"])
    _, norm_back_two = jax.vjp(rms_norm, middle, gain_two)
    grad_middle_part, grads["gain_two"] = norm_back_two(grad_normed_two)
    grad_middle = incoming + grad_middle_part
    grad_first = grad_middle.astype(jnp.bfloat16)
    grads["w_out"] = t_matmul(mixed, grad_first)
    grad_mixed = matmul_t(grad_first, weights["w_out"])
    _, gelu_back = jax.vjp(partial(jax.nn.gelu, approximate=True), branch_y)
    grad_y = gelu_back(grad_mixed * state)[0].astype(jnp.bfloat16)
    grad_state = grad_mixed * gelu_y
    next_decay = jnp.concatenate([decay[1:], jnp.ones((1, LRU), jnp.float32)], axis=0)
    suffix, adjoint_local = lax.associative_scan(
        combine, (next_decay, grad_state), axis=0, reverse=True
    )
    returned = carried_in(
        (prod_local[-1], decay[0] * adjoint_local[0]), "seq", combine, neutral, True
    )
    adjoint = adjoint_local + suffix * returned[1]
    previous = jnp.concatenate([carry_in[None, :], state[:-1]], axis=0)
    _, gates_back = jax.vjp(gate_terms, pre_a, pre_i, conv_val, lambda_raw, starting)
    grad_pre_a, grad_pre_i, grad_direct, grads["lambda_raw"], _ = gates_back(
        (adjoint * previous, adjoint)
    )
    grad_pre_a = grad_pre_a.astype(jnp.bfloat16)
    grad_pre_i = grad_pre_i.astype(jnp.bfloat16)
    grads["gate_a"] = blocked_grad(conv_out, grad_pre_a)
    grads["gate_i"] = blocked_grad(conv_out, grad_pre_i)
    grads["bias_a"] = jnp.sum(grad_pre_a.astype(jnp.float32), axis=0)
    grads["bias_i"] = jnp.sum(grad_pre_i.astype(jnp.float32), axis=0)
    grad_conv = (
        grad_direct
        + blocked_t(grad_pre_a, weights["gate_a"])
        + blocked_t(grad_pre_i, weights["gate_i"])
    )
    _, conv_back = jax.vjp(
        partial(convolve, segment_ext=segment_ext, rows=rows), extended, conv_weight, conv_bias
    )
    grad_ext, grads["conv_weight"], grads["conv_bias"] = conv_back(grad_conv)
    edge_back = shifted(grad_ext[: KW - 1], "seq", -1)
    grad_x = grad_ext[KW - 1 :] + jnp.concatenate(
        [jnp.zeros((rows - (KW - 1), LRU), jnp.float32), edge_back], axis=0
    )
    grad_x = grad_x.astype(jnp.bfloat16)
    grads["w_x"] = t_matmul(normed, grad_x)
    grads["w_y"] = t_matmul(normed, grad_y)
    grad_normed = matmul_t(grad_y, weights["w_y"]) + matmul_t(grad_x, weights["w_x"])
    _, norm_back_one = jax.vjp(rms_norm, stream, gain_one)
    grad_stream_part, grads["gain_one"] = norm_back_one(grad_normed)
    input_grad = grad_middle + grad_stream_part
    packed_grad = jnp.concatenate([grads[entry[0]].reshape(-1) for entry in layout()])
    summed = lax.psum_scatter(packed_grad, ("seq", "fsdp"), scatter_dimension=0, tiled=True)
    new_moment = MOMENT * momentum + summed
    new_params = params - RATE * (summed + MOMENT * new_moment)
    new_average = BLEND * average + (1.0 - BLEND) * new_params
    return (output[None], input_grad[None], new_params, new_moment, new_average)


LANE = 128
TP = 8
HALO = 544
SMALL = 160
GATES = 512
REGIONS = {
    "A": (4248, 256, 192, 32),
    "B": (53400, 1536, 16, 192),
    "C": (77976, 1152, 96, 144),
    "D": (188568, 1536, 36, 192),
}
ROWS = 243864
EVEN_FIRST = (0, 2, 4, 6, 1, 3, 5, 7)
F32 = jnp.float32
BF16 = jnp.bfloat16


class Plan:
    def __init__(self, n_seq, n_fsdp):
        self.n_fsdp = n_fsdp
        shards = n_seq * n_fsdp
        per = ROWS * LANE // shards
        self.per = per
        self.part = per % LANE
        self.own_rows = -(-per // 1024) * 8
        self.last = per // LANE
        bounds = [0]
        for i in range(1, shards):
            at = per * i / LANE
            for first, unit, count, _ in REGIONS.values():
                if first <= at < first + unit * count:
                    bounds.append(first + unit * round((at - first) / unit))
        bounds.append(ROWS)
        self.segments = []
        self.sizes = []
        self.table = np.zeros((shards, 16), np.int32)
        for i in range(shards):
            base = per * i // LANE
            self.table[i, 0] = per * i % LANE
            offset = SMALL + GATES if i == 0 else 0
            found = {}
            for slot, (name, (first, unit, count, wide)) in enumerate(REGIONS.items()):
                low = max(bounds[i], first)
                high = min(bounds[i + 1], first + unit * count)
                if high > low:
                    units = (high - low) // unit
                    found[name] = ((low - first) // unit, units, offset)
                    self.table[i, 1 + 3 * slot : 4 + 3 * slot] = (
                        low - base + HALO,
                        units,
                        offset,
                    )
                    offset += units * wide
            self.segments.append(found)
            self.sizes.append(offset)
            self.table[i, 13] = int(i == 0)
        self.lengths = [
            max(self.sizes[s * n_fsdp : (s + 1) * n_fsdp]) for s in range(n_seq)
        ]
        self.offsets = np.concatenate([[0], np.cumsum(self.lengths)]).astype(np.int32)
        self.longest = max(self.lengths)
        self.groups = ((0, 1), (2,), (3, 4, 5, 6), (7,))
        self.starts = [int(self.offsets[group[0]]) for group in self.groups]
        self.rows = [sum(self.lengths[s] for s in group) for group in self.groups]

    def pieces(self, name, groups):
        out = []
        for i, found in enumerate(self.segments):
            s, f = divmod(i, self.n_fsdp)
            if name in found and s in groups:
                first, units, offset = found[name]
                row = int(self.offsets[s] - self.offsets[groups[0]]) + offset
                out.append((f, row, first, units))
        return out


VMEM = pl.BlockSpec(memory_space=pltpu.VMEM)
ANY = pl.BlockSpec(memory_space=pl.ANY)
SMEM = pl.BlockSpec(memory_space=pltpu.SMEM)
LIMIT = pltpu.CompilerParams(vmem_limit_bytes=60 * 1024 * 1024)


def shape(dims, dtype):
    return jax.ShapeDtypeStruct(dims, dtype)


def aligned(value, multiple):
    return pl.multiple_of(value, multiple)


def lanes(rows):
    return lax.broadcasted_iota(jnp.int32, (rows, LANE), 1)


def swap_lanes(blocks):
    blocks = list(blocks)
    at = lanes(blocks[0].shape[0]) // 16
    for step in (4, 2, 1):
        low_side = (at & step) == 0
        for one in range(TP):
            if one & step == 0:
                left, right = blocks[one], blocks[one + step]
                blocks[one] = jnp.where(low_side, left, pltpu.roll(right, 16 * step, 1))
                blocks[one + step] = jnp.where(
                    low_side, pltpu.roll(left, LANE - 16 * step, 1), right
                )
    return blocks


def shift_down(source, source_row, target, target_row, rows, block, amount, unroll):
    def step(j, tail):
        z = pltpu.roll(source[pl.ds(source_row + j * block, block), :], amount, 1)
        above = pltpu.roll(jnp.concatenate([tail, z], axis=0), 1, 0)[8:]
        target[pl.ds(target_row + j * block, block), :] = jnp.where(
            lanes(block) < amount, above, z
        )
        return z[block - 8 :]

    lax.fori_loop(0, rows // block, step, jnp.zeros((8, LANE), F32), unroll=unroll)


def pack_body(plan, tab, hd, own, hu, *rest):
    outs, (win, al, wire, sems) = rest[:TP], rest[TP:]
    s, f = lax.axis_index("seq"), lax.axis_index("fsdp")
    me = s * plan.n_fsdp + f
    total = win.shape[0]
    first = pltpu.make_async_copy(hd, win.at[pl.ds(0, HALO)], sems.at[0])
    second = pltpu.make_async_copy(own, win.at[pl.ds(HALO, plan.own_rows)], sems.at[1])
    first.start()
    second.start()
    first.wait()
    second.wait()
    seam = HALO + plan.last
    kept = win[pl.ds(seam, 8), :]
    shift_down(hu, 0, win, seam, HALO, 32, plan.part, True)
    edge = lax.broadcasted_iota(jnp.int32, (8, LANE), 0) == 0
    win[pl.ds(seam, 8), :] = jnp.where(
        edge & (lanes(8) < plan.part), kept, win[pl.ds(seam, 8), :]
    )
    shift_down(win, 0, al, 0, total, 48, tab[me, 0], 7)

    def columns(g, _):
        at = tab[me, 1] + g * 256
        to = tab[me, 3] + g * 16
        for block in range(16):
            row = to + 16 * tab[me, 2] * (block // TP)
            wire[block % TP, pl.ds(aligned(row, 16), 16), :] = al[
                pl.ds(at + block, 16, stride=16), :
            ].astype(BF16)
        return 0

    lax.fori_loop(0, tab[me, 2], columns, 0)
    for slot in (4, 10):

        def grouped(j, _):
            for owner in range(TP):
                at = tab[me, slot] + j * 1536 + owner * 192
                to = tab[me, slot + 2] + j * 16
                for block in range(12):
                    row = to + 16 * tab[me, slot + 1] * block
                    wire[owner, pl.ds(aligned(row, 16), 16), :] = al[
                        pl.ds(at + block, 16, stride=12), :
                    ].astype(BF16)
            return 0

        lax.fori_loop(0, tab[me, slot + 1], grouped, 0)

    def mixed_columns(g, _):
        at = tab[me, 7] + g * 1152
        to = tab[me, 9] + g * 32
        wide = 32 * tab[me, 8]
        last = tab[me, 9] + 4 * wide + g * 16
        for half in range(2):
            for a in range(4):
                parts = swap_lanes(
                    [
                        al[pl.ds(at + 576 * half + 8 * a + b, 16, stride=36), :]
                        for b in range(TP)
                    ]
                )
                for owner in range(TP):
                    row = to + a * wide + 16 * half
                    wire[owner, pl.ds(aligned(row, 16), 16), :] = parts[owner].astype(BF16)
        parts = swap_lanes(
            [
                al[pl.ds(at + 576 * half + 32 + b, 16, stride=36), :]
                for half in range(2)
                for b in range(4)
            ]
        )
        for owner in range(TP):
            wire[owner, pl.ds(aligned(last, 16), 16), :] = parts[owner].astype(BF16)
        return 0

    lax.fori_loop(0, tab[me, 8], mixed_columns, 0)

    @pl.when(me == 0)
    def _():
        for owner in range(TP):
            wire[owner, pl.ds(0, SMALL), :] = al[pl.ds(HALO, SMALL), :].astype(BF16)
        for kind in range(2):
            for n in range(16):
                wire[n % TP, pl.ds(SMALL + 128 * (2 * kind + n // TP), 128), :] = al[
                    pl.ds(HALO + 152 + 2048 * kind + 128 * n, 128), :
                ].astype(BF16)

    copies = [
        pltpu.make_async_copy(wire.at[s ^ k], outs[k], sems.at[2 + k]) for k in range(TP)
    ]
    for copy in copies:
        copy.start()
    for copy in copies:
        copy.wait()


def pack(plan, hd, own, hu):
    total = -(-(HALO * 2 + plan.own_rows) // 672) * 672
    return pl.pallas_call(
        partial(pack_body, plan),
        out_shape=[shape((plan.longest, LANE), BF16)] * TP,
        in_specs=[SMEM, ANY, ANY, VMEM],
        out_specs=[ANY] * TP,
        scratch_shapes=[
            pltpu.VMEM((total, LANE), F32),
            pltpu.VMEM((total, LANE), F32),
            pltpu.VMEM((TP, plan.longest, LANE), BF16),
            pltpu.SemaphoreType.DMA((2 + TP,)),
        ],
        compiler_params=LIMIT,
        name="pack",
    )(jnp.asarray(plan.table), hd, own, hu)


def order_body(plan, *refs):
    pieces, outs, sems = refs[:TP], refs[TP : TP + 4], refs[TP + 4]
    s = lax.axis_index("seq")
    for start in (True, False):
        for number, group in enumerate(plan.groups):
            for source in group:
                size = plan.lengths[source]
                at = int(plan.offsets[source]) - plan.starts[number]
                for k in range(TP):

                    @pl.when((s ^ source) == k)
                    def _():
                        copy = pltpu.make_async_copy(
                            pieces[k].at[pl.ds(0, size)],
                            outs[number].at[pl.ds(at, size)],
                            sems.at[source],
                        )
                        if start:
                            copy.start()
                        else:
                            copy.wait()


def order(plan, pieces):
    return pl.pallas_call(
        partial(order_body, plan),
        out_shape=[shape((rows, LANE), BF16) for rows in plan.rows],
        in_specs=[ANY] * TP,
        out_specs=[VMEM] * 4,
        scratch_shapes=[pltpu.SemaphoreType.DMA((TP,))],
        compiler_params=LIMIT,
        name="order",
    )(*pieces)


def weight_copies(plan, number, weights, halves, b_rows):
    out = []
    for f, row, first, units in plan.pieces("A", plan.groups[number]):
        for target, begin, end in weights.get("A", ()):
            low, high = max(first, begin), min(first + units, end)
            if high > low:
                for n in range(2):
                    out.append(
                        (
                            f,
                            row + 16 * (units * n + low - first),
                            16 * (high - low),
                            target.at[pl.ds(16 * (low - begin), 16 * (high - low)), pl.ds(128 * n, 128)],
                        )
                    )
    for f, row, first, units in plan.pieces("B", plan.groups[number]):
        if b_rows is not None:
            for block in range(12):
                out.append(
                    (
                        f,
                        row + 16 * units * block,
                        16 * units,
                        b_rows.at[block, pl.ds(16 * first, 16 * units)],
                    )
                )
    for f, row, first, units in plan.pieces("C", plan.groups[number]):
        for target, begin, end in weights.get("C", ()):
            low, high = max(first, begin), min(first + units, end)
            if high > low:
                for a in range(4):
                    out.append(
                        (
                            f,
                            row + 32 * (units * a + low - first),
                            32 * (high - low),
                            target.at[pl.ds(32 * (low - begin), 32 * (high - low)), pl.ds(128 * a, 128)],
                        )
                    )
        if halves is not None:
            out.append(
                (f, row + 128 * units, 16 * units, halves.at[pl.ds(16 * first, 16 * units)])
            )
    for f, row, first, units in plan.pieces("D", plan.groups[number]):
        for target, begin, end in weights.get("D", ()):
            for n in range(12):
                out.append(
                    (
                        f,
                        row + 16 * units * n,
                        16 * units,
                        target.at[pl.ds(16 * (first - begin), 16 * units), pl.ds(128 * n, 128)],
                    )
                )
    return out


def fetch_line(plan, line, copies, sems, first=0, phases=(True, False)):
    f = lax.axis_index("fsdp")
    for start in phases:
        for source in range(plan.n_fsdp):
            for away in range(plan.n_fsdp):

                @pl.when((f ^ source) == away)
                def _():
                    for number, (holder, row, rows, target) in enumerate(copies):
                        if holder == source:
                            copy = pltpu.make_async_copy(
                                line[away].at[pl.ds(row, rows)], target, sems.at[first + number]
                            )
                            if start:
                                copy.start()
                            else:
                                copy.wait()


def first_copies(plan, small, gates, w_y, w_x, b_head):
    out = [(0, 0, SMALL, small), (0, SMALL, GATES, gates)]
    out += weight_copies(plan, 0, {"A": ((w_y, 0, 96), (w_x, 96, 192))}, None, None)
    for f, row, first, units in plan.pieces("B", plan.groups[0]):
        out.append((f, row, 192 * units, b_head.at[pl.ds(192 * first, 192 * units)]))
    return out


def first_body(plan, *refs):
    line, refs = refs[: plan.n_fsdp], refs[plan.n_fsdp :]
    *targets, sems = refs
    fetch_line(plan, line, first_copies(plan, *targets), sems)


def head_rows(plan):
    return sum(144 * p[3] for p in plan.pieces("C", plan.groups[1]))


def b_head_rows(plan):
    return sum(192 * p[3] for p in plan.pieces("B", plan.groups[0]))


class Nowhere:
    at = property(lambda self: self)

    def __getitem__(self, _):
        return self


def count_first(plan):
    return len(first_copies(plan, *[Nowhere()] * 5))


def unpack_first(plan, line):
    return pl.pallas_call(
        partial(first_body, plan),
        out_shape=[
            shape((SMALL, LANE), BF16),
            shape((GATES, LANE), BF16),
            shape((D, 256), BF16),
            shape((D, 256), BF16),
            shape((b_head_rows(plan), LANE), BF16),
        ],
        in_specs=[ANY] * len(line),
        out_specs=[VMEM] * 5,
        scratch_shapes=[pltpu.SemaphoreType.DMA((count_first(plan),))],
        compiler_params=LIMIT,
        name="unpack_first",
    )(*line)


def middle_copies(plan, b_rows, head):
    out = weight_copies(plan, 1, {}, None, b_rows)
    for f, row, first, units in plan.pieces("C", plan.groups[1]):
        out.append((f, row, 144 * units, head.at[pl.ds(144 * first, 144 * units)]))
    return out


def b_head_copies(plan, b_head, b_rows):
    out = []
    for _, _, first, units in plan.pieces("B", plan.groups[0]):
        for block in range(12):
            out.append(
                (
                    b_head.at[pl.ds(192 * first + 16 * units * block, 16 * units)],
                    b_rows.at[block, pl.ds(16 * first, 16 * units)],
                )
            )
    return out


def middle_body(plan, *refs):
    line, refs = refs[: plan.n_fsdp], refs[plan.n_fsdp :]
    b_head, outs, head, b_rows, sems, more = refs[0], refs[1 : 1 + TP], *refs[1 + TP :]
    local_copies = [
        pltpu.make_async_copy(source, target, more.at[number])
        for number, (source, target) in enumerate(b_head_copies(plan, b_head, b_rows))
    ]
    for copy in local_copies:
        copy.start()
    fetch_line(plan, line, middle_copies(plan, b_rows, head), sems)
    for copy in local_copies:
        copy.wait()
    s = lax.axis_index("seq")
    for k in range(TP):
        for n in range(2):
            unit = (s ^ k) + TP * n
            for block in range(12):
                outs[k][pl.ds(192 * n + 16 * block, 16), :] = b_rows[
                    block, pl.ds(aligned(16 * unit, 16), 16), :
                ]


def unpack_middle(plan, line, b_head):
    return pl.pallas_call(
        partial(middle_body, plan),
        out_shape=[shape((384, LANE), BF16)] * TP + [shape((head_rows(plan), LANE), BF16)],
        in_specs=[ANY] * (len(line) + 1),
        out_specs=[VMEM] * (TP + 1),
        scratch_shapes=[
            pltpu.VMEM((12, 256, LANE), BF16),
            pltpu.SemaphoreType.DMA((len(middle_copies(plan, *[Nowhere()] * 2)),)),
            pltpu.SemaphoreType.DMA((len(b_head_copies(plan, *[Nowhere()] * 2)),)),
        ],
        compiler_params=LIMIT,
        name="unpack_middle",
    )(*line, b_head)


def head_copies(plan, head, weight, halves):
    out = []
    for _, _, first, units in plan.pieces("C", plan.groups[1]):
        for a in range(4):
            out.append(
                (
                    head.at[pl.ds(144 * first + 32 * units * a, 32 * units)],
                    weight.at[pl.ds(32 * first, 32 * units), pl.ds(128 * a, 128)],
                )
            )
        out.append(
            (
                head.at[pl.ds(144 * first + 128 * units, 16 * units)],
                halves.at[pl.ds(16 * first, 16 * units)],
            )
        )
    return out


def second_copies(plan, w_gate, w_up, w_down, halves):
    return weight_copies(
        plan,
        2,
        {"C": ((w_gate, 0, 48), (w_up, 48, 96)), "D": ((w_down, 0, 16),)},
        halves,
        None,
    )


def halves_copies(plan, halves):
    return [
        (f, row + 128 * units, 16 * units, halves.at[pl.ds(16 * first, 16 * units)])
        for f, row, first, units in plan.pieces("C", plan.groups[2])
    ]


def second_body(plan, *refs):
    line, refs = refs[: plan.n_fsdp], refs[plan.n_fsdp :]
    head, w_gate, w_up, w_down, halves, sems, more = refs
    local_copies = [
        pltpu.make_async_copy(source, target, more.at[number])
        for number, (source, target) in enumerate(head_copies(plan, head, w_gate, halves))
    ]
    for copy in local_copies:
        copy.start()
    merged = halves_copies(plan, halves)
    whole = second_copies(plan, w_gate, w_up, w_down, None)
    fetch_line(plan, line, merged, sems, 0, (True,))
    fetch_line(plan, line, whole, sems, len(merged), (True,))
    fetch_line(plan, line, merged, sems, 0, (False,))
    for copy in local_copies:
        copy.wait()
    for weight, begin in ((w_gate, 0), (w_up, 48)):

        def step(g, _):
            last = halves[pl.ds(aligned(16 * (begin + g), 16), 16), :]
            weight[pl.ds(aligned(32 * g, 16), 16), pl.ds(512, 64)] = last[:, :64]
            weight[pl.ds(aligned(32 * g + 16, 16), 16), pl.ds(512, 64)] = last[:, 64:]
            return 0

        lax.fori_loop(0, 48, step, 0, unroll=8)
    fetch_line(plan, line, whole, sems, len(merged), (False,))


def unpack_second(plan, line, head):
    many = len(second_copies(plan, *[Nowhere()] * 4))
    few = len(head_copies(plan, *[Nowhere()] * 3))
    return pl.pallas_call(
        partial(second_body, plan),
        out_shape=[
            shape((D, FF // TP), BF16),
            shape((D, FF // TP), BF16),
            shape((256, D), BF16),
        ],
        in_specs=[ANY] * (len(line) + 1),
        out_specs=[VMEM] * 3,
        scratch_shapes=[
            pltpu.VMEM((96 * 16, LANE), BF16),
            pltpu.SemaphoreType.DMA((many,)),
            pltpu.SemaphoreType.DMA((few,)),
        ],
        compiler_params=LIMIT,
        name="unpack_second",
    )(*line, head)


def third_copies(plan, w_down):
    return weight_copies(plan, 3, {"D": ((w_down, 0, 36),)}, None, None)


def third_body(plan, *refs):
    line, refs = refs[: plan.n_fsdp], refs[plan.n_fsdp :]
    before, w_down, sems, one = refs
    copy = pltpu.make_async_copy(before, w_down.at[pl.ds(0, 256)], one.at[0])
    copy.start()
    fetch_line(plan, line, third_copies(plan, w_down), sems)
    copy.wait()


def unpack_third(plan, line, before):
    many = len(third_copies(plan, Nowhere()))
    return pl.pallas_call(
        partial(third_body, plan),
        out_shape=shape((FF // TP, D), BF16),
        in_specs=[ANY] * (len(line) + 1),
        out_specs=VMEM,
        scratch_shapes=[
            pltpu.SemaphoreType.DMA((many,)),
            pltpu.SemaphoreType.DMA((1,)),
        ],
        compiler_params=LIMIT,
        name="unpack_third",
    )(*line, before)


def out_rows_body(*refs):
    pieces, w_out = refs[:TP], refs[TP]
    s = lax.axis_index("seq")
    for k in range(TP):
        for n in range(2):
            to = aligned(128 * n + 16 * (s ^ k), 16)
            for block in range(12):
                w_out[pl.ds(to, 16), pl.ds(128 * block, 128)] = pieces[k][
                    pl.ds(192 * n + 16 * block, 16), :
                ]


def join_out_rows(pieces):
    return pl.pallas_call(
        out_rows_body,
        out_shape=shape((256, D), BF16),
        in_specs=[VMEM] * TP,
        out_specs=VMEM,
        compiler_params=LIMIT,
        name="join_out_rows",
    )(*pieces)


def split_rows_body(grad, *pieces):
    s = lax.axis_index("seq")
    for k in range(TP):
        for n in range(2):
            at = aligned(128 * n + 16 * (s ^ k), 16)
            for block in range(12):
                pieces[k][pl.ds(192 * n + 16 * block, 16), :] = grad[
                    pl.ds(at, 16), pl.ds(128 * block, 128)
                ]


def split_out_rows(grad):
    return pl.pallas_call(
        split_rows_body,
        out_shape=[shape((384, LANE), F32)] * TP,
        in_specs=[VMEM],
        out_specs=[VMEM] * TP,
        compiler_params=LIMIT,
        name="split_out_rows",
    )(grad)


def start_copies(copies, sems, first=0):
    made = [
        pltpu.make_async_copy(source, target, sems.at[first + number])
        for number, (source, target) in enumerate(copies)
    ]
    for copy in made:
        copy.start()
    return made


def to_wires(plan, copies, wires, sems, first, start):
    f = lax.axis_index("fsdp")
    for j in range(plan.n_fsdp):
        for x in range(plan.n_fsdp):

            @pl.when((f ^ j) == x)
            def _():
                for number, (holder, row, rows, source) in enumerate(copies):
                    if holder == j:
                        copy = pltpu.make_async_copy(
                            source, wires[x].at[pl.ds(row, rows)], sems.at[first + number]
                        )
                        if start:
                            copy.start()
                        else:
                            copy.wait()


def wire_second_body(plan, g_gate, g_up, g_down, *refs):
    wires, (head, halves, sems) = refs[: plan.n_fsdp], refs[plan.n_fsdp :]
    whole = second_copies(plan, g_gate, g_up, g_down, None)
    merged = halves_copies(plan, halves)
    more = [(b, a) for a, b in head_copies(plan, head, g_gate, halves)]
    to_wires(plan, whole, wires, sems, 0, True)
    for grad, begin in ((g_gate, 0), (g_up, 48)):

        def step(g, _):
            left = grad[pl.ds(aligned(32 * g, 16), 16), pl.ds(512, 64)]
            right = grad[pl.ds(aligned(32 * g + 16, 16), 16), pl.ds(512, 64)]
            halves[pl.ds(aligned(16 * (begin + g), 16), 16), :] = jnp.concatenate(
                [left, right], axis=1
            )
            return 0

        lax.fori_loop(0, 48, step, 0, unroll=8)
    to_wires(plan, merged, wires, sems, len(whole), True)
    made = start_copies(more, sems, len(whole) + len(merged))
    to_wires(plan, whole, wires, sems, 0, False)
    to_wires(plan, merged, wires, sems, len(whole), False)
    for copy in made:
        copy.wait()


def wire_second(plan, g_gate, g_up, g_down):
    many = len(second_copies(plan, *[Nowhere()] * 4)) + len(
        head_copies(plan, *[Nowhere()] * 3)
    )
    out = pl.pallas_call(
        partial(wire_second_body, plan),
        out_shape=[shape((plan.rows[2], LANE), F32)] * plan.n_fsdp
        + [shape((head_rows(plan), LANE), F32)],
        in_specs=[VMEM] * 3,
        out_specs=[ANY] * (plan.n_fsdp + 1),
        scratch_shapes=[
            pltpu.VMEM((96 * 16, LANE), F32),
            pltpu.SemaphoreType.DMA((many,)),
        ],
        compiler_params=LIMIT,
        name="wire_second",
    )(g_gate, g_up, g_down)
    return out[:-1], out[-1]


def wire_plain(plan, copies_of, rows, operands):
    many = len(copies_of(*[Nowhere()] * len(operands)))

    def body(*refs):
        *refs, sems = refs
        sources, wires = refs[: len(operands)], refs[len(operands) :]
        copies = copies_of(*sources)
        to_wires(plan, copies, wires, sems, 0, True)
        to_wires(plan, copies, wires, sems, 0, False)

    return pl.pallas_call(
        body,
        out_shape=[shape((rows, LANE), F32)] * plan.n_fsdp,
        in_specs=[VMEM] * len(operands),
        out_specs=[ANY] * plan.n_fsdp,
        scratch_shapes=[pltpu.SemaphoreType.DMA((many,))],
        compiler_params=LIMIT,
    )(*operands)


def wire_third(plan, g_down):
    return wire_plain(plan, partial(third_copies, plan), plan.rows[3], (g_down,))


def wire_middle_body(plan, head, *refs):
    pieces, refs = refs[:TP], refs[TP:]
    wires, (b_head, b_rows, sems) = refs[: plan.n_fsdp], refs[plan.n_fsdp :]
    s = lax.axis_index("seq")
    for k in range(TP):
        for n in range(2):
            unit = (s ^ k) + TP * n
            for block in range(12):
                b_rows[block, pl.ds(aligned(16 * unit, 16), 16), :] = pieces[k][
                    pl.ds(192 * n + 16 * block, 16), :
                ]
    copies = middle_copies(plan, b_rows, head)
    to_wires(plan, copies, wires, sems, 0, True)
    more = [(b, a) for a, b in b_head_copies(plan, b_head, b_rows)]
    made = start_copies(more, sems, len(copies))
    to_wires(plan, copies, wires, sems, 0, False)
    for copy in made:
        copy.wait()


def wire_middle(plan, head, pieces):
    many = len(middle_copies(plan, *[Nowhere()] * 2)) + len(
        b_head_copies(plan, *[Nowhere()] * 2)
    )
    out = pl.pallas_call(
        partial(wire_middle_body, plan),
        out_shape=[shape((plan.rows[1], LANE), F32)] * plan.n_fsdp
        + [shape((b_head_rows(plan), LANE), F32)],
        in_specs=[VMEM] * (1 + TP),
        out_specs=[ANY] * (plan.n_fsdp + 1),
        scratch_shapes=[
            pltpu.VMEM((12, 256, LANE), F32),
            pltpu.SemaphoreType.DMA((many,)),
        ],
        compiler_params=LIMIT,
        name="wire_middle",
    )(head, *pieces)
    return out[:-1], out[-1]


def split_copies(plan, copies):
    border = int(plan.offsets[1])
    return (
        [copy for copy in copies if copy[1] < border],
        [(f, row - border, rows, at) for f, row, rows, at in copies if row >= border],
    )


def wire_x(plan, g_x, b_head):
    def copies_of(g_x, b_head):
        nowhere = Nowhere()
        return split_copies(plan, first_copies(plan, nowhere, nowhere, nowhere, g_x, b_head))[1]

    return wire_plain(plan, copies_of, plan.lengths[1], (g_x, b_head))


def wire_y_body(plan, gains, vectors, gates, g_y, g_x, *refs):
    wires, (small, sems) = refs[: plan.n_fsdp], refs[plan.n_fsdp :]
    s = lax.axis_index("seq")
    small[...] = jnp.zeros_like(small)
    small[pl.ds(0, 24), :] = gains[...]
    for n in range(8):
        for part in range(2):
            small[pl.ds(24 + 16 * n + s + TP * part, 1), :] = vectors[
                pl.ds(2 * n + part, 1), :
            ]
    copies = split_copies(plan, first_copies(plan, small, gates, g_y, g_x, Nowhere()))[0]
    to_wires(plan, copies, wires, sems, 0, True)
    to_wires(plan, copies, wires, sems, 0, False)


def wire_y(plan, gains, vectors, gates, g_y, g_x):
    return pl.pallas_call(
        partial(wire_y_body, plan),
        out_shape=[shape((plan.lengths[0], LANE), F32)] * plan.n_fsdp,
        in_specs=[VMEM] * 5,
        out_specs=[ANY] * plan.n_fsdp,
        scratch_shapes=[
            pltpu.VMEM((SMALL, LANE), F32),
            pltpu.SemaphoreType.DMA((count_first(plan),)),
        ],
        compiler_params=LIMIT,
        name="wire_y",
    )(gains, vectors, gates, g_y, g_x)


def spread_body(plan, targets, *refs):
    count = len(targets)
    sums, outs, sems = refs[:count], refs[count : count + TP], refs[count + TP]
    s = lax.axis_index("seq")
    for start in (True, False):
        for summed, group in zip(sums, targets):
            for target in group:
                size = plan.lengths[target]
                at = int(plan.offsets[target] - plan.offsets[group[0]])
                for k in range(TP):

                    @pl.when((s ^ target) == k)
                    def _():
                        copy = pltpu.make_async_copy(
                            summed.at[pl.ds(at, size)],
                            outs[k].at[pl.ds(0, size)],
                            sems.at[target],
                        )
                        if start:
                            copy.start()
                        else:
                            copy.wait()


def spread(plan, targets, sums):
    rows = max(plan.lengths[s] for group in targets for s in group)
    return pl.pallas_call(
        partial(spread_body, plan, targets),
        out_shape=[shape((rows, LANE), F32)] * TP,
        in_specs=[VMEM] * len(sums),
        out_specs=[ANY] * TP,
        scratch_shapes=[pltpu.SemaphoreType.DMA((TP,))],
        compiler_params=LIMIT,
    )(*sums)


def shift_up(source, source_row, target, target_row, rows, block, amount):
    def step(j, _):
        both = pltpu.roll(source[pl.ds(source_row + j * block, block + 8), :], amount, 1)
        below = pltpu.roll(both, block + 7, 0)[:block]
        target[pl.ds(target_row + j * block, block), :] = jnp.where(
            lanes(block) < amount, both[:block], below
        )
        return 0

    lax.fori_loop(0, rows // block, step, 0, unroll=True)


def collect_body(plan, tab, *refs):
    pieces, (own, hd, hu, al, win, wire, sems) = refs[: 2 * TP], refs[2 * TP :]
    s, f = lax.axis_index("seq"), lax.axis_index("fsdp")
    me = s * plan.n_fsdp + f

    def bring(start):
        for number in range(2):

            @pl.when(jnp.minimum(s, 1) == number)
            def _():
                for k in range(TP):
                    piece = pieces[TP * number + k]
                    copy = pltpu.make_async_copy(
                        piece, wire.at[s ^ k, pl.ds(0, piece.shape[0])], sems.at[k]
                    )
                    if start:
                        copy.start()
                    else:
                        copy.wait()

    bring(True)
    total = win.shape[0]

    def clear(j, _):
        al[pl.ds(aligned(j * 96, 8), 96), :] = jnp.zeros((96, LANE), F32)
        return 0

    lax.fori_loop(0, al.shape[0] // 96, clear, 0, unroll=4)
    bring(False)

    def columns(g, _):
        at = tab[me, 1] + g * 256
        to = tab[me, 3] + g * 16
        for block in range(16):
            row = to + 16 * tab[me, 2] * (block // TP)
            al[pl.ds(at + block, 16, stride=16), :] = wire[
                block % TP, pl.ds(aligned(row, 16), 16), :
            ]
        return 0

    lax.fori_loop(0, tab[me, 2], columns, 0)
    for slot in (4, 10):

        def grouped(j, _):
            for owner in range(TP):
                at = tab[me, slot] + j * 1536 + owner * 192
                to = tab[me, slot + 2] + j * 16
                for block in range(12):
                    row = to + 16 * tab[me, slot + 1] * block
                    al[pl.ds(at + block, 16, stride=12), :] = wire[
                        owner, pl.ds(aligned(row, 16), 16), :
                    ]
            return 0

        lax.fori_loop(0, tab[me, slot + 1], grouped, 0)

    def mixed_columns(g, _):
        at = tab[me, 7] + g * 1152
        to = tab[me, 9] + g * 32
        wide = 32 * tab[me, 8]
        last = tab[me, 9] + 4 * wide + g * 16
        for half in range(2):
            for a in range(4):
                parts = swap_lanes(
                    [
                        wire[owner, pl.ds(aligned(to + a * wide + 16 * half, 16), 16), :]
                        for owner in range(TP)
                    ]
                )
                for b in range(TP):
                    al[pl.ds(at + 576 * half + 8 * a + b, 16, stride=36), :] = parts[b]
        parts = swap_lanes(
            [wire[owner, pl.ds(aligned(last, 16), 16), :] for owner in range(TP)]
        )
        for half in range(2):
            for b in range(4):
                al[pl.ds(at + 576 * half + 32 + b, 16, stride=36), :] = parts[4 * half + b]
        return 0

    lax.fori_loop(0, tab[me, 8], mixed_columns, 0)

    @pl.when(me == 0)
    def _():
        summed = wire[0, pl.ds(0, 152), :]
        for owner in range(1, TP):
            summed = summed + wire[owner, pl.ds(0, 152), :]
        al[pl.ds(HALO, 152), :] = summed
        for kind in range(2):
            for n in range(16):
                al[pl.ds(HALO + 152 + 2048 * kind + 128 * n, 128), :] = wire[
                    n % TP, pl.ds(SMALL + 128 * (2 * kind + n // TP), 128), :
                ]

    def back(j, _):
        both = pltpu.roll(
            al[pl.ds(aligned(j * 48, 8), 56), :], lax.rem(LANE - tab[me, 0], LANE), 1
        )
        below = pltpu.roll(both, 55, 0)[:48]
        win[pl.ds(aligned(j * 48, 8), 48), :] = jnp.where(
            lanes(48) < LANE - tab[me, 0], both[:48], below
        )
        return 0

    lax.fori_loop(0, total // 48, back, 0, unroll=7)
    hd[...] = win[pl.ds(0, HALO), :]
    own[...] = win[pl.ds(HALO, plan.own_rows), :]
    shift_up(win, HALO + plan.last, hu, 0, HALO, 32, LANE - plan.part)


def collect(plan, pieces):
    total = -(-(HALO * 2 + plan.own_rows) // 672) * 672
    cleared = total + 96
    return pl.pallas_call(
        partial(collect_body, plan),
        out_shape=[
            shape((plan.own_rows, LANE), F32),
            shape((HALO, LANE), F32),
            shape((HALO, LANE), F32),
        ],
        in_specs=[SMEM] + [ANY] * (2 * TP),
        out_specs=[VMEM] * 3,
        scratch_shapes=[
            pltpu.VMEM((cleared, LANE), F32),
            pltpu.VMEM((total, LANE), F32),
            pltpu.VMEM((TP, plan.longest, LANE), F32),
            pltpu.SemaphoreType.DMA((TP,)),
        ],
        compiler_params=LIMIT,
        name="collect",
    )(jnp.asarray(plan.table), *pieces)


def tail_body(plan, value, out):
    first = (plan.last - HALO) % 8
    out[...] = jnp.zeros_like(out)
    shift_down(value, 0, out, first, HALO, 32, plan.part, True)
    z = pltpu.roll(value[pl.ds(HALO - 8, 8), :], plan.part, 1)
    row = lax.broadcasted_iota(jnp.int32, (8, LANE), 0)
    out[pl.ds(first + HALO, 8), :] = jnp.where(
        (row == 0) & (lanes(8) < plan.part), pltpu.roll(z, 1, 0), 0.0
    )


def place_tail(plan, value):
    rows = plan.own_rows - (plan.last - HALO) // 8 * 8
    return pl.pallas_call(
        partial(tail_body, plan),
        out_shape=shape((max(rows, HALO + 16), LANE), F32),
        in_specs=[VMEM],
        out_specs=VMEM,
        compiler_params=LIMIT,
        name="place_tail",
    )(value)[:rows]


def scan_body(reverse, coefficient, addend, out):
    rows, width = coefficient.shape
    at = lax.broadcasted_iota(jnp.int32, (8, width), 0)
    if reverse:
        at = 7 - at
    steps = rows // 8

    def step(j, carry):
        block = steps - 1 - j if reverse else j
        here = pl.ds(aligned(block * 8, 8), 8)
        a, b = coefficient[here, :], addend[here, :]
        for reach in (1, 2, 4):
            turn = 8 - reach if reverse else reach
            inside = at >= reach
            b = b + jnp.where(inside, a * pltpu.roll(b, turn, 0), 0.0)
            a = jnp.where(inside, a * pltpu.roll(a, turn, 0), a)
        value = b + a * carry
        out[here, :] = value
        edge = value[0:1] if reverse else value[7:8]
        return jnp.broadcast_to(edge, (8, width))

    lax.fori_loop(0, steps, step, jnp.zeros((8, width), F32), unroll=4)


def linear_scan(coefficient, addend, reverse):
    return pl.pallas_call(
        partial(scan_body, reverse),
        out_shape=shape(coefficient.shape, F32),
        in_specs=[VMEM] * 2,
        out_specs=VMEM,
        compiler_params=LIMIT,
        name="scan_back" if reverse else "scan",
    )(coefficient, addend)


def swap(value, bit):
    return lax.ppermute(value, "seq", [(i, i ^ bit) for i in range(TP)])


def exchange(pieces, targets=range(TP)):
    return [pieces[0]] + [
        lax.ppermute(pieces[k], "seq", [(i ^ k, i) for i in targets]) for k in range(1, TP)
    ]


def gather_stream(mine):
    half = mine.shape[0] // 2

    over_x, over_y = swap(mine, 2), swap(mine, 4)
    over_xy = [swap(over_x[:half], 4), swap(over_y[half:], 2)]
    chip = [mine, over_x, over_y] + over_xy
    return jnp.concatenate(chip + [swap(part, 1) for part in chip], axis=0)


def scatter_stream(partial_sums):
    rows = partial_sums.shape[0] // TP
    half = rows // 2

    def send(value, bit):
        return swap(value.astype(BF16), bit).astype(F32)

    other = send(partial_sums[TP // 2 * rows :], 1)
    q = (partial_sums[: TP // 2 * rows] + other).reshape(4, rows, -1)
    up = send(jnp.concatenate([q[1, :half], q[3, :half]]), 2)
    down = send(jnp.concatenate([q[2, half:], q[3, half:]]), 4)
    top = send(q[2, :half] + up[half:], 4)
    low = send(q[1, half:] + down[half:], 2)
    return jnp.concatenate(
        [q[0, :half] + up[:half] + top, q[0, half:] + down[:half] + low], axis=0
    )


def to_positions(values, s):
    rows = values.shape[0] // TP
    parts = []
    for j in range(TP):
        k = s ^ j
        at = (k // 2 + 4 * (k % 2)) * rows
        parts.append(lax.dynamic_slice_in_dim(values, at, rows, 0))
    return jnp.concatenate(parts, axis=0)


def to_relative(values, s):
    rows = values.shape[0] // TP
    return jnp.concatenate(
        [lax.dynamic_slice_in_dim(values, (s ^ k) * rows, rows, 0) for k in EVEN_FIRST], axis=0
    )


def gather_line(value, count):
    def send(value, bit):
        return lax.ppermute(value, "fsdp", [(i, i ^ bit) for i in range(count)])

    opposite, near = send(value, 3), send(value, 1)
    return [value, near, send(opposite, 1), opposite]


def scatter_line(blocks):
    count = len(blocks)
    own, near, far, cross = blocks
    far = lax.ppermute(far, "fsdp", [(i, i ^ 1) for i in range(count)])
    near = lax.ppermute(near, "fsdp", [(i, i ^ 1) for i in range(count)])
    cross = lax.ppermute(cross + far, "fsdp", [(i, i ^ 3) for i in range(count)])
    return own + near + cross


def sliced(plan, *arguments):
    return sliced_step(plan, *arguments)


def sliced_step(plan, stream_in, cotangent, starts, params, momentum, average):
    n_fsdp = plan.n_fsdp
    s = lax.axis_index("seq")
    shards = TP * n_fsdp
    onward = [(i, i + 1) for i in range(shards - 1)]
    backward = [(i + 1, i) for i in range(shards - 1)]
    both = ("seq", "fsdp")
    edge = HALO * LANE
    per = plan.per

    hd, hu = lax.optimization_barrier((params[per - edge :], params[:edge]))
    hd = lax.ppermute(hd.astype(BF16), both, onward)
    hu = lax.ppermute(hu.astype(BF16), both, backward)
    own = jnp.pad(params, (0, plan.own_rows * LANE - per)).reshape(-1, LANE)
    pieces = pack(
        plan, hd.astype(F32).reshape(-1, LANE), own, hu.astype(F32).reshape(-1, LANE)
    )
    first, middle_wire, second, third = order(plan, exchange(pieces))
    stream_bf, cotangent_bf, first = lax.optimization_barrier(
        (stream_in[0], cotangent[0], first)
    )
    line = gather_line(first, n_fsdp)
    middle_wire, second, third, line = lax.optimization_barrier(
        (middle_wire, second, third, line)
    )
    small, gates, w_y, w_x, b_head = unpack_first(plan, line)
    line = gather_line(middle_wire, n_fsdp)
    *out_rows, head = unpack_middle(plan, line, b_head)
    w_out = join_out_rows(exchange(out_rows))
    line = gather_line(second, n_fsdp)
    w_gate, w_up, w_down = unpack_second(plan, line, head)
    w_down = unpack_third(plan, gather_line(third, n_fsdp), w_down)

    mine = stream_in[0].astype(F32)
    stream = gather_stream(stream_bf)
    stream = stream.astype(F32)
    grad_out = gather_stream(cotangent_bf)
    rows = stream.shape[0]

    small = small.astype(F32)
    gain_one = small[0:12].reshape(-1)
    gain_two = small[12:24].reshape(-1)

    def channels(at):
        return jnp.concatenate(
            [
                lax.dynamic_slice_in_dim(small, at + s, 1, 0),
                lax.dynamic_slice_in_dim(small, at + s + TP, 1, 0),
            ],
            axis=1,
        )[0]

    conv_bias, bias_a, bias_i, lambda_raw = (channels(24 + 16 * j) for j in range(4))
    conv_weight = jnp.stack([channels(88 + 16 * j) for j in range(KW)])

    positions = jnp.arange(rows, dtype=jnp.int32)
    ext_pos = jnp.arange(rows + KW - 1, dtype=jnp.int32) - (KW - 1)
    segment_ext = segment_ids(ext_pos, starts[0])
    starting = start_flags(positions, starts[0])[:, None]

    def gate_product(values, at):
        return jnp.concatenate(
            [matmul(values[:, :HB], gates[at : at + HB]), matmul(values[:, HB:], gates[at + HB : at + 2 * HB])],
            axis=1,
        )

    def gate_product_t(values, at):
        return jnp.concatenate(
            [matmul_t(values[:, :HB], gates[at : at + HB]), matmul_t(values[:, HB:], gates[at + HB : at + 2 * HB])],
            axis=1,
        )

    normed = rms_norm(stream, gain_one).astype(BF16)
    branch_y = matmul(normed, w_y)
    branch_x = matmul(normed, w_x).astype(BF16)
    branch_y = to_positions(branch_y, s)
    branch_x = to_positions(branch_x, s)
    extended = jnp.pad(branch_x, ((KW - 1, 0), (0, 0))).astype(F32)

    def convolve_here(extended, weight, bias):
        total = jnp.zeros((rows, bias.shape[0]), F32) + bias
        for lag in range(KW):
            source = extended[KW - 1 - lag : KW - 1 - lag + rows]
            same = segment_ext[KW - 1 - lag : KW - 1 - lag + rows] == segment_ext[KW - 1 :]
            total = total + weight[lag] * source * same.astype(F32)[:, None]
        return total

    conv_out = convolve_here(extended, conv_weight, conv_bias).astype(BF16)
    conv_val = conv_out.astype(F32)
    pre_a = gate_product(conv_out, 0) + bias_a
    pre_i = gate_product(conv_out, 2 * HB) + bias_i
    decay, drive = gate_terms(pre_a, pre_i, conv_val, lambda_raw, starting)
    state = linear_scan(decay, drive, False)
    gelu_y = jax.nn.gelu(branch_y, approximate=True)
    mixed = to_relative((state * gelu_y).astype(BF16), s)
    middle = mine + scatter_stream(matmul(mixed, w_out))
    normed_two_mine = rms_norm(middle, gain_two).astype(BF16)
    normed_two = gather_stream(normed_two_mine)
    gate = matmul(normed_two, w_gate)
    upward = matmul(normed_two, w_up)
    hidden = gelu_product(gate, upward).astype(BF16)
    g_down = t_matmul(hidden, grad_out)
    summed_three = scatter_line(wire_third(plan, g_down))
    out_sums = matmul(hidden, w_down)
    output = (middle + scatter_stream(out_sums)).astype(BF16)
    gate, upward, _ = lax.optimization_barrier((gate, upward, hidden))

    grad_hidden = matmul_t(grad_out, w_down)
    _, product_back = jax.vjp(gelu_product, gate, upward)
    grad_gate, grad_up = product_back(grad_hidden)
    grad_gate, grad_up = grad_gate.astype(BF16), grad_up.astype(BF16)
    g_gate = t_matmul(normed_two, grad_gate)
    g_up = t_matmul(normed_two, grad_up)
    grad_normed_two = scatter_stream(matmul_t(grad_gate, w_gate) + matmul_t(grad_up, w_up))
    wire_two, wire_head = wire_second(plan, g_gate, g_up, g_down)
    summed_two = scatter_line(wire_two)

    _, norm_back_two = jax.vjp(rms_norm, middle, gain_two)
    grad_middle_part, g_gain_two = norm_back_two(grad_normed_two)
    grad_middle = cotangent[0].astype(F32) + grad_middle_part
    grad_first = gather_stream(grad_middle.astype(BF16))
    g_out = t_matmul(mixed, grad_first)
    wire_mid, b_head = wire_middle(plan, wire_head, exchange(split_out_rows(g_out)))
    summed_mid = scatter_line(wire_mid)
    grad_mixed = to_positions(matmul_t(grad_first, w_out), s)
    _, gelu_back = jax.vjp(partial(jax.nn.gelu, approximate=True), branch_y)
    grad_y = gelu_back(grad_mixed * state)[0].astype(BF16)
    next_decay = jnp.concatenate([decay[1:], jnp.ones((1, decay.shape[1]), F32)], axis=0)
    adjoint = linear_scan(next_decay, grad_mixed * gelu_y, True)
    previous = jnp.concatenate([jnp.zeros((1, decay.shape[1]), F32), state[:-1]], axis=0)
    _, gates_back = jax.vjp(gate_terms, pre_a, pre_i, conv_val, lambda_raw, starting)
    grad_pre_a, grad_pre_i, grad_direct, g_lambda, _ = gates_back((adjoint * previous, adjoint))
    grad_pre_a, grad_pre_i = grad_pre_a.astype(BF16), grad_pre_i.astype(BF16)
    g_gates = jnp.concatenate(
        [
            t_matmul(conv_out[:, n : n + HB], grad[:, n : n + HB])
            for grad in (grad_pre_a, grad_pre_i)
            for n in (0, HB)
        ],
        axis=0,
    )
    g_bias_a = jnp.sum(grad_pre_a.astype(F32), axis=0)
    g_bias_i = jnp.sum(grad_pre_i.astype(F32), axis=0)
    grad_conv = grad_direct + gate_product_t(grad_pre_a, 0) + gate_product_t(grad_pre_i, 2 * HB)
    _, conv_back = jax.vjp(convolve_here, extended, conv_weight, conv_bias)
    grad_ext, g_conv_weight, g_conv_bias = conv_back(grad_conv)
    grad_x = to_relative(grad_ext[KW - 1 :].astype(BF16), s)
    grad_y = to_relative(grad_y, s)
    g_x = t_matmul(normed, grad_x)
    g_y = t_matmul(normed, grad_y)
    grad_normed = scatter_stream(matmul_t(grad_y, w_y) + matmul_t(grad_x, w_x))
    _, norm_back_one = jax.vjp(rms_norm, mine, gain_one)
    grad_stream_part, g_gain_one = norm_back_one(grad_normed)
    input_grad = grad_middle + grad_stream_part

    summed_x = scatter_line(wire_x(plan, g_x, b_head))
    gains = jnp.concatenate([g_gain_one, g_gain_two]).reshape(-1, LANE)
    vectors = jnp.stack(
        [g_conv_bias, g_bias_a, g_bias_i, g_lambda] + [g_conv_weight[k] for k in range(KW)]
    ).reshape(-1, LANE)
    summed_y = scatter_line(wire_y(plan, gains, vectors, g_gates, g_y, g_x))
    early = spread(
        plan, ((1,),) + plan.groups[1:], (summed_x, summed_mid, summed_two, summed_three)
    )
    got = exchange(spread(plan, ((0,),), (summed_y,)), (0,))
    got += exchange(early)
    grad_own, grad_hd, grad_hu = collect(plan, got)
    from_next = lax.ppermute(grad_hd, both, backward)
    from_before = lax.ppermute(grad_hu, both, onward)
    tail = place_tail(plan, from_next).reshape(-1)
    whole = plan.own_rows * LANE
    summed = (
        grad_own.reshape(-1)
        + jnp.pad(from_before.reshape(-1), (0, whole - edge))
        + jnp.pad(tail, (whole - tail.shape[0], 0))
    )[:per]
    new_moment = MOMENT * momentum + summed
    new_params = params - RATE * (summed + MOMENT * new_moment)
    new_average = BLEND * average + (1.0 - BLEND) * new_params
    return (output[None], input_grad[None], new_params, new_moment, new_average)


def solution(mesh):
    n_seq, n_fsdp = mesh.shape["seq"], mesh.shape["fsdp"]
    fast = (n_seq, n_fsdp) == (TP, 4)
    body = partial(sliced, Plan(n_seq, n_fsdp)) if fast else local
    return jax.shard_map(
        body,
        mesh=mesh,
        in_specs=(
            P("fsdp", "seq", None),
            P("fsdp", "seq", None),
            P("fsdp", None),
            P(("seq", "fsdp")),
            P(("seq", "fsdp")),
            P(("seq", "fsdp")),
        ),
        out_specs=(
            P("fsdp", "seq", None),
            P("fsdp", "seq", None),
            P(("seq", "fsdp")),
            P(("seq", "fsdp")),
            P(("seq", "fsdp")),
        ),
        check_vma=False,
    )
```

```python
from functools import partial
import math

import jax
import jax.numpy as jnp
import numpy as np
from jax import lax
from jax.experimental import pallas as pl
from jax.experimental.pallas import tpu as pltpu
from jax.sharding import PartitionSpec as P


D = 1536
LRU = 2048
FF = 4608
HB = 128
KW = 4


EPS = 1e-06
RATE = 3e-05
MOMENT = 0.9
BLEND = 0.9
DECAY_SCALE = 8.0


def shifted(block, axis, distance):
    devices = range(lax.axis_size(axis))
    route = [(i - distance, i) for i in devices if i - distance in devices]
    return lax.ppermute(block, axis, route)


def carried_in(value, axis, join, neutral, backward):
    count, mine = (lax.axis_size(axis), lax.axis_index(axis))
    pieces = jax.tree.map(lambda part: lax.all_gather(part, axis), value)
    if backward:
        pieces = jax.tree.map(lambda part: part[::-1], pieces)
        mine = count - 1 - mine
    so_far = jax.tree.map(
        lambda part, zero: jnp.full_like(part, 0) + jnp.asarray(zero, part.dtype), value, neutral
    )

    def lap(position, so_far):
        longer = join(so_far, jax.tree.map(lambda part: part[position], pieces))
        return jax.tree.map(lambda new, old: jnp.where(position < mine, new, old), longer, so_far)

    return lax.fori_loop(0, count - 1, lap, so_far)


def layout():
    return [
        ("gain_one", (D,)),
        ("gain_two", (D,)),
        ("conv_bias", (LRU,)),
        ("bias_a", (LRU,)),
        ("bias_i", (LRU,)),
        ("lambda_raw", (LRU,)),
        ("conv_weight", (KW, LRU)),
        ("gate_a", (LRU // HB, HB, HB)),
        ("gate_i", (LRU // HB, HB, HB)),
        ("w_y", (D, LRU)),
        ("w_x", (D, LRU)),
        ("w_out", (LRU, D)),
        ("w_gate", (D, FF)),
        ("w_up", (D, FF)),
        ("w_down", (FF, D)),
    ]


def unpack(packed):
    result = {}
    offset = 0
    for entry_name, entry_shape in layout():
        amount = math.prod(entry_shape)
        result[entry_name] = packed[offset : offset + amount].reshape(entry_shape)
        offset += amount
    return result


def matmul(left, right):
    return jnp.dot(left, right, preferred_element_type=jnp.float32)


def matmul_t(left, right):
    return lax.dot_general(
        left, right, (((1,), (1,)), ((), ())), preferred_element_type=jnp.float32
    )


def t_matmul(left, right):
    return lax.dot_general(
        left, right, (((0,), (0,)), ((), ())), preferred_element_type=jnp.float32
    )


def blocked(values, weight):
    shaped = values.reshape(values.shape[0], LRU // HB, HB)
    return jnp.einsum("tnh,nhk->tnk", shaped, weight, preferred_element_type=jnp.float32).reshape(
        values.shape[0], LRU
    )


def blocked_t(values, weight):
    shaped = values.reshape(values.shape[0], LRU // HB, HB)
    return jnp.einsum("tnk,nhk->tnh", shaped, weight, preferred_element_type=jnp.float32).reshape(
        values.shape[0], LRU
    )


def blocked_grad(inputs, grads):
    left = inputs.reshape(inputs.shape[0], LRU // HB, HB)
    right = grads.reshape(grads.shape[0], LRU // HB, HB)
    return jnp.einsum("tnh,tnk->nhk", left, right, preferred_element_type=jnp.float32)


def rms_norm(values, gain):
    return values * lax.rsqrt(jnp.mean(values * values, axis=-1, keepdims=True) + EPS) * gain


def combine(earlier, later):
    return (earlier[0] * later[0], later[0] * earlier[1] + later[1])


def gate_terms(pre_a, pre_i, conv_val, lambda_raw, starting):
    recall = jax.nn.sigmoid(pre_a)
    admit = jax.nn.sigmoid(pre_i)
    rate = DECAY_SCALE * jax.nn.softplus(lambda_raw) * recall
    decay = (1.0 - starting) * jnp.exp(-rate)
    scale_in = starting + (1.0 - starting) * jnp.sqrt(-jnp.expm1(-2.0 * rate))
    return (decay, scale_in * admit * conv_val)


def convolve(extended, weight, bias, segment_ext, rows):
    total = jnp.zeros((rows, LRU), jnp.float32) + bias
    for lag in range(KW):
        source = extended[KW - 1 - lag : KW - 1 - lag + rows]
        same = (segment_ext[KW - 1 - lag : KW - 1 - lag + rows] == segment_ext[KW - 1 :]).astype(
            jnp.float32
        )
        total = total + weight[lag] * source * same[:, None]
    return total


def segment_ids(positions, doc_starts):
    return jnp.sum((doc_starts[None, :] <= positions[:, None]).astype(jnp.int32), axis=1)


def start_flags(positions, doc_starts):
    return jnp.max((doc_starts[None, :] == positions[:, None]).astype(jnp.float32), axis=1)


def gelu_product(left, right):
    return jax.nn.gelu(left, approximate=True) * right


def local(stream_in, cotangent, starts, params, momentum, average):
    weights = unpack(
        lax.all_gather(params.astype(jnp.bfloat16), ("seq", "fsdp"), axis=0, tiled=True)
    )
    stream = stream_in[0].astype(jnp.float32)
    incoming = cotangent[0].astype(jnp.float32)
    doc_starts = starts[0]
    rows = stream.shape[0]
    positions = lax.axis_index("seq") * rows + jnp.arange(rows, dtype=jnp.int32)
    ext_pos = positions[0] - (KW - 1) + jnp.arange(rows + KW - 1, dtype=jnp.int32)
    segment_ext = segment_ids(ext_pos, doc_starts)
    starting = start_flags(positions, doc_starts)[:, None]
    gain_one = weights["gain_one"].astype(jnp.float32)
    gain_two = weights["gain_two"].astype(jnp.float32)
    conv_weight = weights["conv_weight"].astype(jnp.float32)
    conv_bias = weights["conv_bias"].astype(jnp.float32)
    lambda_raw = weights["lambda_raw"].astype(jnp.float32)
    normed = rms_norm(stream, gain_one).astype(jnp.bfloat16)
    branch_y = matmul(normed, weights["w_y"])
    branch_x = matmul(normed, weights["w_x"]).astype(jnp.bfloat16)
    edge = shifted(branch_x[rows - (KW - 1) :], "seq", 1)
    extended = jnp.concatenate([edge, branch_x], axis=0).astype(jnp.float32)
    conv_out = convolve(extended, conv_weight, conv_bias, segment_ext, rows).astype(jnp.bfloat16)
    conv_val = conv_out.astype(jnp.float32)
    pre_a = blocked(conv_out, weights["gate_a"]) + weights["bias_a"].astype(jnp.float32)
    pre_i = blocked(conv_out, weights["gate_i"]) + weights["bias_i"].astype(jnp.float32)
    decay, drive = gate_terms(pre_a, pre_i, conv_val, lambda_raw, starting)
    prod_local, state_local = lax.associative_scan(combine, (decay, drive), axis=0)
    neutral = (jnp.ones((LRU,), jnp.float32), jnp.zeros((LRU,), jnp.float32))
    carried = carried_in((prod_local[-1], state_local[-1]), "seq", combine, neutral, False)
    carry_in = carried[1]
    state = lax.associative_scan(combine, (decay, drive.at[0].add(decay[0] * carry_in)), axis=0)[1]
    gelu_y = jax.nn.gelu(branch_y, approximate=True)
    mixed = (state * gelu_y).astype(jnp.bfloat16)
    middle = stream + matmul(mixed, weights["w_out"])
    normed_two = rms_norm(middle, gain_two).astype(jnp.bfloat16)
    gate = matmul(normed_two, weights["w_gate"])
    upward = matmul(normed_two, weights["w_up"])
    hidden = gelu_product(gate, upward).astype(jnp.bfloat16)
    output = (middle + matmul(hidden, weights["w_down"])).astype(jnp.bfloat16)
    grads = {}
    grad_out = incoming.astype(jnp.bfloat16)
    grads["w_down"] = t_matmul(hidden, grad_out)
    grad_hidden = matmul_t(grad_out, weights["w_down"])
    _, product_back = jax.vjp(gelu_product, gate, upward)
    grad_gate, grad_up = product_back(grad_hidden)
    grad_gate = grad_gate.astype(jnp.bfloat16)
    grad_up = grad_up.astype(jnp.bfloat16)
    grads["w_gate"] = t_matmul(normed_two, grad_gate)
    grads["w_up"] = t_matmul(normed_two, grad_up)
    grad_normed_two = matmul_t(grad_gate, weights["w_gate"]) + matmul_t(grad_up, weights["w_up"])
    _, norm_back_two = jax.vjp(rms_norm, middle, gain_two)
    grad_middle_part, grads["gain_two"] = norm_back_two(grad_normed_two)
    grad_middle = incoming + grad_middle_part
    grad_first = grad_middle.astype(jnp.bfloat16)
    grads["w_out"] = t_matmul(mixed, grad_first)
    grad_mixed = matmul_t(grad_first, weights["w_out"])
    _, gelu_back = jax.vjp(partial(jax.nn.gelu, approximate=True), branch_y)
    grad_y = gelu_back(grad_mixed * state)[0].astype(jnp.bfloat16)
    grad_state = grad_mixed * gelu_y
    next_decay = jnp.concatenate([decay[1:], jnp.ones((1, LRU), jnp.float32)], axis=0)
    suffix, adjoint_local = lax.associative_scan(
        combine, (next_decay, grad_state), axis=0, reverse=True
    )
    returned = carried_in(
        (prod_local[-1], decay[0] * adjoint_local[0]), "seq", combine, neutral, True
    )
    adjoint = adjoint_local + suffix * returned[1]
    previous = jnp.concatenate([carry_in[None, :], state[:-1]], axis=0)
    _, gates_back = jax.vjp(gate_terms, pre_a, pre_i, conv_val, lambda_raw, starting)
    grad_pre_a, grad_pre_i, grad_direct, grads["lambda_raw"], _ = gates_back(
        (adjoint * previous, adjoint)
    )
    grad_pre_a = grad_pre_a.astype(jnp.bfloat16)
    grad_pre_i = grad_pre_i.astype(jnp.bfloat16)
    grads["gate_a"] = blocked_grad(conv_out, grad_pre_a)
    grads["gate_i"] = blocked_grad(conv_out, grad_pre_i)
    grads["bias_a"] = jnp.sum(grad_pre_a.astype(jnp.float32), axis=0)
    grads["bias_i"] = jnp.sum(grad_pre_i.astype(jnp.float32), axis=0)
    grad_conv = (
        grad_direct
        + blocked_t(grad_pre_a, weights["gate_a"])
        + blocked_t(grad_pre_i, weights["gate_i"])
    )
    _, conv_back = jax.vjp(
        partial(convolve, segment_ext=segment_ext, rows=rows), extended, conv_weight, conv_bias
    )
    grad_ext, grads["conv_weight"], grads["conv_bias"] = conv_back(grad_conv)
    edge_back = shifted(grad_ext[: KW - 1], "seq", -1)
    grad_x = grad_ext[KW - 1 :] + jnp.concatenate(
        [jnp.zeros((rows - (KW - 1), LRU), jnp.float32), edge_back], axis=0
    )
    grad_x = grad_x.astype(jnp.bfloat16)
    grads["w_x"] = t_matmul(normed, grad_x)
    grads["w_y"] = t_matmul(normed, grad_y)
    grad_normed = matmul_t(grad_y, weights["w_y"]) + matmul_t(grad_x, weights["w_x"])
    _, norm_back_one = jax.vjp(rms_norm, stream, gain_one)
    grad_stream_part, grads["gain_one"] = norm_back_one(grad_normed)
    input_grad = grad_middle + grad_stream_part
    packed_grad = jnp.concatenate([grads[entry[0]].reshape(-1) for entry in layout()])
    summed = lax.psum_scatter(packed_grad, ("seq", "fsdp"), scatter_dimension=0, tiled=True)
    new_moment = MOMENT * momentum + summed
    new_params = params - RATE * (summed + MOMENT * new_moment)
    new_average = BLEND * average + (1.0 - BLEND) * new_params
    return (output[None], input_grad[None], new_params, new_moment, new_average)


LANE = 128
TP = 8
HALO = 544
SMALL = 160
GATES = 512
REGIONS = {
    "A": (4248, 256, 192, 32),
    "B": (53400, 1536, 16, 192),
    "C": (77976, 1152, 96, 144),
    "D": (188568, 1536, 36, 192),
}
ROWS = 243864
EVEN_FIRST = (0, 2, 4, 6, 1, 3, 5, 7)
F32 = jnp.float32
BF16 = jnp.bfloat16


class Plan:
    def __init__(self, n_seq, n_fsdp):
        self.n_fsdp = n_fsdp
        shards = n_seq * n_fsdp
        per = ROWS * LANE // shards
        self.per = per
        self.part = per % LANE
        self.own_rows = -(-per // 1024) * 8
        self.last = per // LANE
        bounds = [0]
        for i in range(1, shards):
            at = per * i / LANE
            for first, unit, count, _ in REGIONS.values():
                if first <= at < first + unit * count:
                    bounds.append(first + unit * round((at - first) / unit))
        bounds.append(ROWS)
        self.segments = []
        self.sizes = []
        self.table = np.zeros((shards, 16), np.int32)
        for i in range(shards):
            base = per * i // LANE
            self.table[i, 0] = per * i % LANE
            offset = SMALL + GATES if i == 0 else 0
            found = {}
            for slot, (name, (first, unit, count, wide)) in enumerate(REGIONS.items()):
                low = max(bounds[i], first)
                high = min(bounds[i + 1], first + unit * count)
                if high > low:
                    units = (high - low) // unit
                    found[name] = ((low - first) // unit, units, offset)
                    self.table[i, 1 + 3 * slot : 4 + 3 * slot] = (
                        low - base + HALO,
                        units,
                        offset,
                    )
                    offset += units * wide
            self.segments.append(found)
            self.sizes.append(offset)
            self.table[i, 13] = int(i == 0)
        self.lengths = [
            max(self.sizes[s * n_fsdp : (s + 1) * n_fsdp]) for s in range(n_seq)
        ]
        self.offsets = np.concatenate([[0], np.cumsum(self.lengths)]).astype(np.int32)
        self.longest = max(self.lengths)
        self.groups = ((0, 1), (2,), (3, 4, 5, 6), (7,))
        self.starts = [int(self.offsets[group[0]]) for group in self.groups]
        self.rows = [sum(self.lengths[s] for s in group) for group in self.groups]

    def pieces(self, name, groups):
        out = []
        for i, found in enumerate(self.segments):
            s, f = divmod(i, self.n_fsdp)
            if name in found and s in groups:
                first, units, offset = found[name]
                row = int(self.offsets[s] - self.offsets[groups[0]]) + offset
                out.append((f, row, first, units))
        return out


VMEM = pl.BlockSpec(memory_space=pltpu.VMEM)
ANY = pl.BlockSpec(memory_space=pl.ANY)
SMEM = pl.BlockSpec(memory_space=pltpu.SMEM)
LIMIT = pltpu.CompilerParams(vmem_limit_bytes=60 * 1024 * 1024)


def shape(dims, dtype):
    return jax.ShapeDtypeStruct(dims, dtype)


def aligned(value, multiple):
    return pl.multiple_of(value, multiple)


def lanes(rows):
    return lax.broadcasted_iota(jnp.int32, (rows, LANE), 1)


def swap_lanes(blocks):
    blocks = list(blocks)
    at = lanes(blocks[0].shape[0]) // 16
    for step in (4, 2, 1):
        low_side = (at & step) == 0
        for one in range(TP):
            if one & step == 0:
                left, right = blocks[one], blocks[one + step]
                blocks[one] = jnp.where(low_side, left, pltpu.roll(right, 16 * step, 1))
                blocks[one + step] = jnp.where(
                    low_side, pltpu.roll(left, LANE - 16 * step, 1), right
                )
    return blocks


def shift_down(source, source_row, target, target_row, rows, block, amount, unroll):
    def step(j, tail):
        z = pltpu.roll(source[pl.ds(source_row + j * block, block), :], amount, 1)
        above = pltpu.roll(jnp.concatenate([tail, z], axis=0), 1, 0)[8:]
        target[pl.ds(target_row + j * block, block), :] = jnp.where(
            lanes(block) < amount, above, z
        )
        return z[block - 8 :]

    lax.fori_loop(0, rows // block, step, jnp.zeros((8, LANE), F32), unroll=unroll)


def pack_body(plan, tab, hd, own, hu, *rest):
    outs, (win, al, wire, sems) = rest[:TP], rest[TP:]
    s, f = lax.axis_index("seq"), lax.axis_index("fsdp")
    me = s * plan.n_fsdp + f
    total = win.shape[0]
    first = pltpu.make_async_copy(hd, win.at[pl.ds(0, HALO)], sems.at[0])
    second = pltpu.make_async_copy(own, win.at[pl.ds(HALO, plan.own_rows)], sems.at[1])
    first.start()
    second.start()
    first.wait()
    second.wait()
    seam = HALO + plan.last
    kept = win[pl.ds(seam, 8), :]
    shift_down(hu, 0, win, seam, HALO, 32, plan.part, True)
    edge = lax.broadcasted_iota(jnp.int32, (8, LANE), 0) == 0
    win[pl.ds(seam, 8), :] = jnp.where(
        edge & (lanes(8) < plan.part), kept, win[pl.ds(seam, 8), :]
    )
    shift_down(win, 0, al, 0, total, 48, tab[me, 0], 7)

    def columns(g, _):
        at = tab[me, 1] + g * 256
        to = tab[me, 3] + g * 16
        for block in range(16):
            row = to + 16 * tab[me, 2] * (block // TP)
            wire[block % TP, pl.ds(aligned(row, 16), 16), :] = al[
                pl.ds(at + block, 16, stride=16), :
            ].astype(BF16)
        return 0

    lax.fori_loop(0, tab[me, 2], columns, 0)
    for slot in (4, 10):

        def grouped(j, _):
            for owner in range(TP):
                at = tab[me, slot] + j * 1536 + owner * 192
                to = tab[me, slot + 2] + j * 16
                for block in range(12):
                    row = to + 16 * tab[me, slot + 1] * block
                    wire[owner, pl.ds(aligned(row, 16), 16), :] = al[
                        pl.ds(at + block, 16, stride=12), :
                    ].astype(BF16)
            return 0

        lax.fori_loop(0, tab[me, slot + 1], grouped, 0)

    def mixed_columns(g, _):
        at = tab[me, 7] + g * 1152
        to = tab[me, 9] + g * 32
        wide = 32 * tab[me, 8]
        last = tab[me, 9] + 4 * wide + g * 16
        for half in range(2):
            for a in range(4):
                parts = swap_lanes(
                    [
                        al[pl.ds(at + 576 * half + 8 * a + b, 16, stride=36), :]
                        for b in range(TP)
                    ]
                )
                for owner in range(TP):
                    row = to + a * wide + 16 * half
                    wire[owner, pl.ds(aligned(row, 16), 16), :] = parts[owner].astype(BF16)
        parts = swap_lanes(
            [
                al[pl.ds(at + 576 * half + 32 + b, 16, stride=36), :]
                for half in range(2)
                for b in range(4)
            ]
        )
        for owner in range(TP):
            wire[owner, pl.ds(aligned(last, 16), 16), :] = parts[owner].astype(BF16)
        return 0

    lax.fori_loop(0, tab[me, 8], mixed_columns, 0)

    @pl.when(me == 0)
    def _():
        for owner in range(TP):
            wire[owner, pl.ds(0, SMALL), :] = al[pl.ds(HALO, SMALL), :].astype(BF16)
        for kind in range(2):
            for n in range(16):
                wire[n % TP, pl.ds(SMALL + 128 * (2 * kind + n // TP), 128), :] = al[
                    pl.ds(HALO + 152 + 2048 * kind + 128 * n, 128), :
                ].astype(BF16)

    copies = [
        pltpu.make_async_copy(wire.at[s ^ k], outs[k], sems.at[2 + k]) for k in range(TP)
    ]
    for copy in copies:
        copy.start()
    for copy in copies:
        copy.wait()


def pack(plan, hd, own, hu):
    total = -(-(HALO * 2 + plan.own_rows) // 672) * 672
    return pl.pallas_call(
        partial(pack_body, plan),
        out_shape=[shape((plan.longest, LANE), BF16)] * TP,
        in_specs=[SMEM, ANY, ANY, VMEM],
        out_specs=[ANY] * TP,
        scratch_shapes=[
            pltpu.VMEM((total, LANE), F32),
            pltpu.VMEM((total, LANE), F32),
            pltpu.VMEM((TP, plan.longest, LANE), BF16),
            pltpu.SemaphoreType.DMA((2 + TP,)),
        ],
        compiler_params=LIMIT,
        name="pack",
    )(jnp.asarray(plan.table), hd, own, hu)


def order_body(plan, *refs):
    pieces, outs, sems = refs[:TP], refs[TP : TP + 4], refs[TP + 4]
    s = lax.axis_index("seq")
    for start in (True, False):
        for number, group in enumerate(plan.groups):
            for source in group:
                size = plan.lengths[source]
                at = int(plan.offsets[source]) - plan.starts[number]
                for k in range(TP):

                    @pl.when((s ^ source) == k)
                    def _():
                        copy = pltpu.make_async_copy(
                            pieces[k].at[pl.ds(0, size)],
                            outs[number].at[pl.ds(at, size)],
                            sems.at[source],
                        )
                        if start:
                            copy.start()
                        else:
                            copy.wait()


def order(plan, pieces):
    return pl.pallas_call(
        partial(order_body, plan),
        out_shape=[shape((rows, LANE), BF16) for rows in plan.rows],
        in_specs=[ANY] * TP,
        out_specs=[VMEM] * 4,
        scratch_shapes=[pltpu.SemaphoreType.DMA((TP,))],
        compiler_params=LIMIT,
        name="order",
    )(*pieces)


def weight_copies(plan, number, weights, halves, b_rows):
    out = []
    for f, row, first, units in plan.pieces("A", plan.groups[number]):
        for target, begin, end in weights.get("A", ()):
            low, high = max(first, begin), min(first + units, end)
            if high > low:
                for n in range(2):
                    out.append(
                        (
                            f,
                            row + 16 * (units * n + low - first),
                            16 * (high - low),
                            target.at[pl.ds(16 * (low - begin), 16 * (high - low)), pl.ds(128 * n, 128)],
                        )
                    )
    for f, row, first, units in plan.pieces("B", plan.groups[number]):
        if b_rows is not None:
            for block in range(12):
                out.append(
                    (
                        f,
                        row + 16 * units * block,
                        16 * units,
                        b_rows.at[block, pl.ds(16 * first, 16 * units)],
                    )
                )
    for f, row, first, units in plan.pieces("C", plan.groups[number]):
        for target, begin, end in weights.get("C", ()):
            low, high = max(first, begin), min(first + units, end)
            if high > low:
                for a in range(4):
                    out.append(
                        (
                            f,
                            row + 32 * (units * a + low - first),
                            32 * (high - low),
                            target.at[pl.ds(32 * (low - begin), 32 * (high - low)), pl.ds(128 * a, 128)],
                        )
                    )
        if halves is not None:
            out.append(
                (f, row + 128 * units, 16 * units, halves.at[pl.ds(16 * first, 16 * units)])
            )
    for f, row, first, units in plan.pieces("D", plan.groups[number]):
        for target, begin, end in weights.get("D", ()):
            for n in range(12):
                out.append(
                    (
                        f,
                        row + 16 * units * n,
                        16 * units,
                        target.at[pl.ds(16 * (first - begin), 16 * units), pl.ds(128 * n, 128)],
                    )
                )
    return out


def fetch_line(plan, line, copies, sems, first=0, phases=(True, False)):
    f = lax.axis_index("fsdp")
    for start in phases:
        for source in range(plan.n_fsdp):
            for away in range(plan.n_fsdp):

                @pl.when((f ^ source) == away)
                def _():
                    for number, (holder, row, rows, target) in enumerate(copies):
                        if holder == source:
                            copy = pltpu.make_async_copy(
                                line[away].at[pl.ds(row, rows)], target, sems.at[first + number]
                            )
                            if start:
                                copy.start()
                            else:
                                copy.wait()


def first_copies(plan, small, gates, w_y, w_x, b_head):
    out = [(0, 0, SMALL, small), (0, SMALL, GATES, gates)]
    out += weight_copies(plan, 0, {"A": ((w_y, 0, 96), (w_x, 96, 192))}, None, None)
    for f, row, first, units in plan.pieces("B", plan.groups[0]):
        out.append((f, row, 192 * units, b_head.at[pl.ds(192 * first, 192 * units)]))
    return out


def first_body(plan, *refs):
    line, refs = refs[: plan.n_fsdp], refs[plan.n_fsdp :]
    *targets, sems = refs
    fetch_line(plan, line, first_copies(plan, *targets), sems)


def head_rows(plan):
    return sum(144 * p[3] for p in plan.pieces("C", plan.groups[1]))


def b_head_rows(plan):
    return sum(192 * p[3] for p in plan.pieces("B", plan.groups[0]))


class Nowhere:
    at = property(lambda self: self)

    def __getitem__(self, _):
        return self


def count_first(plan):
    return len(first_copies(plan, *[Nowhere()] * 5))


def unpack_first(plan, line):
    return pl.pallas_call(
        partial(first_body, plan),
        out_shape=[
            shape((SMALL, LANE), BF16),
            shape((GATES, LANE), BF16),
            shape((D, 256), BF16),
            shape((D, 256), BF16),
            shape((b_head_rows(plan), LANE), BF16),
        ],
        in_specs=[ANY] * len(line),
        out_specs=[VMEM] * 5,
        scratch_shapes=[pltpu.SemaphoreType.DMA((count_first(plan),))],
        compiler_params=LIMIT,
        name="unpack_first",
    )(*line)


def middle_copies(plan, b_rows, head):
    out = weight_copies(plan, 1, {}, None, b_rows)
    for f, row, first, units in plan.pieces("C", plan.groups[1]):
        out.append((f, row, 144 * units, head.at[pl.ds(144 * first, 144 * units)]))
    return out


def b_head_copies(plan, b_head, b_rows):
    out = []
    for _, _, first, units in plan.pieces("B", plan.groups[0]):
        for block in range(12):
            out.append(
                (
                    b_head.at[pl.ds(192 * first + 16 * units * block, 16 * units)],
                    b_rows.at[block, pl.ds(16 * first, 16 * units)],
                )
            )
    return out


def middle_body(plan, *refs):
    line, refs = refs[: plan.n_fsdp], refs[plan.n_fsdp :]
    b_head, outs, head, b_rows, sems, more = refs[0], refs[1 : 1 + TP], *refs[1 + TP :]
    local_copies = [
        pltpu.make_async_copy(source, target, more.at[number])
        for number, (source, target) in enumerate(b_head_copies(plan, b_head, b_rows))
    ]
    for copy in local_copies:
        copy.start()
    fetch_line(plan, line, middle_copies(plan, b_rows, head), sems)
    for copy in local_copies:
        copy.wait()
    s = lax.axis_index("seq")
    for k in range(TP):
        for n in range(2):
            unit = (s ^ k) + TP * n
            for block in range(12):
                outs[k][pl.ds(192 * n + 16 * block, 16), :] = b_rows[
                    block, pl.ds(aligned(16 * unit, 16), 16), :
                ]


def unpack_middle(plan, line, b_head):
    return pl.pallas_call(
        partial(middle_body, plan),
        out_shape=[shape((384, LANE), BF16)] * TP + [shape((head_rows(plan), LANE), BF16)],
        in_specs=[ANY] * (len(line) + 1),
        out_specs=[VMEM] * (TP + 1),
        scratch_shapes=[
            pltpu.VMEM((12, 256, LANE), BF16),
            pltpu.SemaphoreType.DMA((len(middle_copies(plan, *[Nowhere()] * 2)),)),
            pltpu.SemaphoreType.DMA((len(b_head_copies(plan, *[Nowhere()] * 2)),)),
        ],
        compiler_params=LIMIT,
        name="unpack_middle",
    )(*line, b_head)


def head_copies(plan, head, weight, halves):
    out = []
    for _, _, first, units in plan.pieces("C", plan.groups[1]):
        for a in range(4):
            out.append(
                (
                    head.at[pl.ds(144 * first + 32 * units * a, 32 * units)],
                    weight.at[pl.ds(32 * first, 32 * units), pl.ds(128 * a, 128)],
                )
            )
        out.append(
            (
                head.at[pl.ds(144 * first + 128 * units, 16 * units)],
                halves.at[pl.ds(16 * first, 16 * units)],
            )
        )
    return out


def second_copies(plan, w_gate, w_up, w_down, halves):
    return weight_copies(
        plan,
        2,
        {"C": ((w_gate, 0, 48), (w_up, 48, 96)), "D": ((w_down, 0, 16),)},
        halves,
        None,
    )


def halves_copies(plan, halves):
    return [
        (f, row + 128 * units, 16 * units, halves.at[pl.ds(16 * first, 16 * units)])
        for f, row, first, units in plan.pieces("C", plan.groups[2])
    ]


def second_body(plan, *refs):
    line, refs = refs[: plan.n_fsdp], refs[plan.n_fsdp :]
    head, w_gate, w_up, w_down, halves, sems, more = refs
    local_copies = [
        pltpu.make_async_copy(source, target, more.at[number])
        for number, (source, target) in enumerate(head_copies(plan, head, w_gate, halves))
    ]
    for copy in local_copies:
        copy.start()
    merged = halves_copies(plan, halves)
    whole = second_copies(plan, w_gate, w_up, w_down, None)
    fetch_line(plan, line, merged, sems, 0, (True,))
    fetch_line(plan, line, whole, sems, len(merged), (True,))
    fetch_line(plan, line, merged, sems, 0, (False,))
    for copy in local_copies:
        copy.wait()
    for weight, begin in ((w_gate, 0), (w_up, 48)):

        def step(g, _):
            last = halves[pl.ds(aligned(16 * (begin + g), 16), 16), :]
            weight[pl.ds(aligned(32 * g, 16), 16), pl.ds(512, 64)] = last[:, :64]
            weight[pl.ds(aligned(32 * g + 16, 16), 16), pl.ds(512, 64)] = last[:, 64:]
            return 0

        lax.fori_loop(0, 48, step, 0, unroll=8)
    fetch_line(plan, line, whole, sems, len(merged), (False,))


def unpack_second(plan, line, head):
    many = len(second_copies(plan, *[Nowhere()] * 4))
    few = len(head_copies(plan, *[Nowhere()] * 3))
    return pl.pallas_call(
        partial(second_body, plan),
        out_shape=[
            shape((D, FF // TP), BF16),
            shape((D, FF // TP), BF16),
            shape((256, D), BF16),
        ],
        in_specs=[ANY] * (len(line) + 1),
        out_specs=[VMEM] * 3,
        scratch_shapes=[
            pltpu.VMEM((96 * 16, LANE), BF16),
            pltpu.SemaphoreType.DMA((many,)),
            pltpu.SemaphoreType.DMA((few,)),
        ],
        compiler_params=LIMIT,
        name="unpack_second",
    )(*line, head)


def third_copies(plan, w_down):
    return weight_copies(plan, 3, {"D": ((w_down, 0, 36),)}, None, None)


def third_body(plan, *refs):
    line, refs = refs[: plan.n_fsdp], refs[plan.n_fsdp :]
    before, w_down, sems, one = refs
    copy = pltpu.make_async_copy(before, w_down.at[pl.ds(0, 256)], one.at[0])
    copy.start()
    fetch_line(plan, line, third_copies(plan, w_down), sems)
    copy.wait()


def unpack_third(plan, line, before):
    many = len(third_copies(plan, Nowhere()))
    return pl.pallas_call(
        partial(third_body, plan),
        out_shape=shape((FF // TP, D), BF16),
        in_specs=[ANY] * (len(line) + 1),
        out_specs=VMEM,
        scratch_shapes=[
            pltpu.SemaphoreType.DMA((many,)),
            pltpu.SemaphoreType.DMA((1,)),
        ],
        compiler_params=LIMIT,
        name="unpack_third",
    )(*line, before)


def out_rows_body(*refs):
    pieces, w_out = refs[:TP], refs[TP]
    s = lax.axis_index("seq")
    for k in range(TP):
        for n in range(2):
            to = aligned(128 * n + 16 * (s ^ k), 16)
            for block in range(12):
                w_out[pl.ds(to, 16), pl.ds(128 * block, 128)] = pieces[k][
                    pl.ds(192 * n + 16 * block, 16), :
                ]


def join_out_rows(pieces):
    return pl.pallas_call(
        out_rows_body,
        out_shape=shape((256, D), BF16),
        in_specs=[VMEM] * TP,
        out_specs=VMEM,
        compiler_params=LIMIT,
        name="join_out_rows",
    )(*pieces)


def split_rows_body(grad, *pieces):
    s = lax.axis_index("seq")
    for k in range(TP):
        for n in range(2):
            at = aligned(128 * n + 16 * (s ^ k), 16)
            for block in range(12):
                pieces[k][pl.ds(192 * n + 16 * block, 16), :] = grad[
                    pl.ds(at, 16), pl.ds(128 * block, 128)
                ]


def split_out_rows(grad):
    return pl.pallas_call(
        split_rows_body,
        out_shape=[shape((384, LANE), F32)] * TP,
        in_specs=[VMEM],
        out_specs=[VMEM] * TP,
        compiler_params=LIMIT,
        name="split_out_rows",
    )(grad)


def start_copies(copies, sems, first=0):
    made = [
        pltpu.make_async_copy(source, target, sems.at[first + number])
        for number, (source, target) in enumerate(copies)
    ]
    for copy in made:
        copy.start()
    return made


def to_wires(plan, copies, wires, sems, first, start):
    f = lax.axis_index("fsdp")
    for j in range(plan.n_fsdp):
        for x in range(plan.n_fsdp):

            @pl.when((f ^ j) == x)
            def _():
                for number, (holder, row, rows, source) in enumerate(copies):
                    if holder == j:
                        copy = pltpu.make_async_copy(
                            source, wires[x].at[pl.ds(row, rows)], sems.at[first + number]
                        )
                        if start:
                            copy.start()
                        else:
                            copy.wait()


def wire_second_body(plan, g_gate, g_up, g_down, *refs):
    wires, (head, halves, sems) = refs[: plan.n_fsdp], refs[plan.n_fsdp :]
    whole = second_copies(plan, g_gate, g_up, g_down, None)
    merged = halves_copies(plan, halves)
    more = [(b, a) for a, b in head_copies(plan, head, g_gate, halves)]
    to_wires(plan, whole, wires, sems, 0, True)
    for grad, begin in ((g_gate, 0), (g_up, 48)):

        def step(g, _):
            left = grad[pl.ds(aligned(32 * g, 16), 16), pl.ds(512, 64)]
            right = grad[pl.ds(aligned(32 * g + 16, 16), 16), pl.ds(512, 64)]
            halves[pl.ds(aligned(16 * (begin + g), 16), 16), :] = jnp.concatenate(
                [left, right], axis=1
            )
            return 0

        lax.fori_loop(0, 48, step, 0, unroll=8)
    to_wires(plan, merged, wires, sems, len(whole), True)
    made = start_copies(more, sems, len(whole) + len(merged))
    to_wires(plan, whole, wires, sems, 0, False)
    to_wires(plan, merged, wires, sems, len(whole), False)
    for copy in made:
        copy.wait()


def wire_second(plan, g_gate, g_up, g_down):
    many = len(second_copies(plan, *[Nowhere()] * 4)) + len(
        head_copies(plan, *[Nowhere()] * 3)
    )
    out = pl.pallas_call(
        partial(wire_second_body, plan),
        out_shape=[shape((plan.rows[2], LANE), F32)] * plan.n_fsdp
        + [shape((head_rows(plan), LANE), F32)],
        in_specs=[VMEM] * 3,
        out_specs=[ANY] * (plan.n_fsdp + 1),
        scratch_shapes=[
            pltpu.VMEM((96 * 16, LANE), F32),
            pltpu.SemaphoreType.DMA((many,)),
        ],
        compiler_params=LIMIT,
        name="wire_second",
    )(g_gate, g_up, g_down)
    return out[:-1], out[-1]


def wire_plain(plan, copies_of, rows, operands):
    many = len(copies_of(*[Nowhere()] * len(operands)))

    def body(*refs):
        *refs, sems = refs
        sources, wires = refs[: len(operands)], refs[len(operands) :]
        copies = copies_of(*sources)
        to_wires(plan, copies, wires, sems, 0, True)
        to_wires(plan, copies, wires, sems, 0, False)

    return pl.pallas_call(
        body,
        out_shape=[shape((rows, LANE), F32)] * plan.n_fsdp,
        in_specs=[VMEM] * len(operands),
        out_specs=[ANY] * plan.n_fsdp,
        scratch_shapes=[pltpu.SemaphoreType.DMA((many,))],
        compiler_params=LIMIT,
    )(*operands)


def wire_third(plan, g_down):
    return wire_plain(plan, partial(third_copies, plan), plan.rows[3], (g_down,))


def wire_middle_body(plan, head, *refs):
    pieces, refs = refs[:TP], refs[TP:]
    wires, (b_head, b_rows, sems) = refs[: plan.n_fsdp], refs[plan.n_fsdp :]
    s = lax.axis_index("seq")
    for k in range(TP):
        for n in range(2):
            unit = (s ^ k) + TP * n
            for block in range(12):
                b_rows[block, pl.ds(aligned(16 * unit, 16), 16), :] = pieces[k][
                    pl.ds(192 * n + 16 * block, 16), :
                ]
    copies = middle_copies(plan, b_rows, head)
    to_wires(plan, copies, wires, sems, 0, True)
    more = [(b, a) for a, b in b_head_copies(plan, b_head, b_rows)]
    made = start_copies(more, sems, len(copies))
    to_wires(plan, copies, wires, sems, 0, False)
    for copy in made:
        copy.wait()


def wire_middle(plan, head, pieces):
    many = len(middle_copies(plan, *[Nowhere()] * 2)) + len(
        b_head_copies(plan, *[Nowhere()] * 2)
    )
    out = pl.pallas_call(
        partial(wire_middle_body, plan),
        out_shape=[shape((plan.rows[1], LANE), F32)] * plan.n_fsdp
        + [shape((b_head_rows(plan), LANE), F32)],
        in_specs=[VMEM] * (1 + TP),
        out_specs=[ANY] * (plan.n_fsdp + 1),
        scratch_shapes=[
            pltpu.VMEM((12, 256, LANE), F32),
            pltpu.SemaphoreType.DMA((many,)),
        ],
        compiler_params=LIMIT,
        name="wire_middle",
    )(head, *pieces)
    return out[:-1], out[-1]


def split_copies(plan, copies):
    border = int(plan.offsets[1])
    return (
        [copy for copy in copies if copy[1] < border],
        [(f, row - border, rows, at) for f, row, rows, at in copies if row >= border],
    )


def wire_x(plan, g_x, b_head):
    def copies_of(g_x, b_head):
        nowhere = Nowhere()
        return split_copies(plan, first_copies(plan, nowhere, nowhere, nowhere, g_x, b_head))[1]

    return wire_plain(plan, copies_of, plan.lengths[1], (g_x, b_head))


def wire_y_body(plan, gains, vectors, gates, g_y, g_x, *refs):
    wires, (small, sems) = refs[: plan.n_fsdp], refs[plan.n_fsdp :]
    s = lax.axis_index("seq")
    small[...] = jnp.zeros_like(small)
    small[pl.ds(0, 24), :] = gains[...]
    for n in range(8):
        for part in range(2):
            small[pl.ds(24 + 16 * n + s + TP * part, 1), :] = vectors[
                pl.ds(2 * n + part, 1), :
            ]
    copies = split_copies(plan, first_copies(plan, small, gates, g_y, g_x, Nowhere()))[0]
    to_wires(plan, copies, wires, sems, 0, True)
    to_wires(plan, copies, wires, sems, 0, False)


def wire_y(plan, gains, vectors, gates, g_y, g_x):
    return pl.pallas_call(
        partial(wire_y_body, plan),
        out_shape=[shape((plan.lengths[0], LANE), F32)] * plan.n_fsdp,
        in_specs=[VMEM] * 5,
        out_specs=[ANY] * plan.n_fsdp,
        scratch_shapes=[
            pltpu.VMEM((SMALL, LANE), F32),
            pltpu.SemaphoreType.DMA((count_first(plan),)),
        ],
        compiler_params=LIMIT,
        name="wire_y",
    )(gains, vectors, gates, g_y, g_x)


def spread_body(plan, targets, *refs):
    count = len(targets)
    sums, outs, sems = refs[:count], refs[count : count + TP], refs[count + TP]
    s = lax.axis_index("seq")
    for start in (True, False):
        for summed, group in zip(sums, targets):
            for target in group:
                size = plan.lengths[target]
                at = int(plan.offsets[target] - plan.offsets[group[0]])
                for k in range(TP):

                    @pl.when((s ^ target) == k)
                    def _():
                        copy = pltpu.make_async_copy(
                            summed.at[pl.ds(at, size)],
                            outs[k].at[pl.ds(0, size)],
                            sems.at[target],
                        )
                        if start:
                            copy.start()
                        else:
                            copy.wait()


def spread(plan, targets, sums):
    rows = max(plan.lengths[s] for group in targets for s in group)
    return pl.pallas_call(
        partial(spread_body, plan, targets),
        out_shape=[shape((rows, LANE), F32)] * TP,
        in_specs=[VMEM] * len(sums),
        out_specs=[ANY] * TP,
        scratch_shapes=[pltpu.SemaphoreType.DMA((TP,))],
        compiler_params=LIMIT,
    )(*sums)


def shift_up(source, source_row, target, target_row, rows, block, amount):
    def step(j, _):
        both = pltpu.roll(source[pl.ds(source_row + j * block, block + 8), :], amount, 1)
        below = pltpu.roll(both, block + 7, 0)[:block]
        target[pl.ds(target_row + j * block, block), :] = jnp.where(
            lanes(block) < amount, both[:block], below
        )
        return 0

    lax.fori_loop(0, rows // block, step, 0, unroll=True)


def collect_body(plan, tab, *refs):
    pieces, (own, hd, hu, al, win, wire, sems) = refs[: 3 * TP], refs[3 * TP :]
    s, f = lax.axis_index("seq"), lax.axis_index("fsdp")
    me = s * plan.n_fsdp + f

    def bring(start):
        for number, (low, high) in enumerate(((0, 0), (1, 2), (3, TP - 1))):

            @pl.when((s >= low) & (s <= high))
            def _():
                for k in range(TP):
                    piece = pieces[TP * number + k]
                    copy = pltpu.make_async_copy(
                        piece, wire.at[s ^ k, pl.ds(0, piece.shape[0])], sems.at[k]
                    )
                    if start:
                        copy.start()
                    else:
                        copy.wait()

    bring(True)
    total = win.shape[0]

    def clear(j, _):
        al[pl.ds(aligned(j * 96, 8), 96), :] = jnp.zeros((96, LANE), F32)
        return 0

    lax.fori_loop(0, al.shape[0] // 96, clear, 0, unroll=4)
    bring(False)

    def columns(g, _):
        at = tab[me, 1] + g * 256
        to = tab[me, 3] + g * 16
        for block in range(16):
            row = to + 16 * tab[me, 2] * (block // TP)
            al[pl.ds(at + block, 16, stride=16), :] = wire[
                block % TP, pl.ds(aligned(row, 16), 16), :
            ]
        return 0

    lax.fori_loop(0, tab[me, 2], columns, 0)
    for slot in (4, 10):

        def grouped(j, _):
            for owner in range(TP):
                at = tab[me, slot] + j * 1536 + owner * 192
                to = tab[me, slot + 2] + j * 16
                for block in range(12):
                    row = to + 16 * tab[me, slot + 1] * block
                    al[pl.ds(at + block, 16, stride=12), :] = wire[
                        owner, pl.ds(aligned(row, 16), 16), :
                    ]
            return 0

        lax.fori_loop(0, tab[me, slot + 1], grouped, 0)

    def mixed_columns(g, _):
        at = tab[me, 7] + g * 1152
        to = tab[me, 9] + g * 32
        wide = 32 * tab[me, 8]
        last = tab[me, 9] + 4 * wide + g * 16
        for half in range(2):
            for a in range(4):
                parts = swap_lanes(
                    [
                        wire[owner, pl.ds(aligned(to + a * wide + 16 * half, 16), 16), :]
                        for owner in range(TP)
                    ]
                )
                for b in range(TP):
                    al[pl.ds(at + 576 * half + 8 * a + b, 16, stride=36), :] = parts[b]
        parts = swap_lanes(
            [wire[owner, pl.ds(aligned(last, 16), 16), :] for owner in range(TP)]
        )
        for half in range(2):
            for b in range(4):
                al[pl.ds(at + 576 * half + 32 + b, 16, stride=36), :] = parts[4 * half + b]
        return 0

    lax.fori_loop(0, tab[me, 8], mixed_columns, 0)

    @pl.when(me == 0)
    def _():
        summed = wire[0, pl.ds(0, 152), :]
        for owner in range(1, TP):
            summed = summed + wire[owner, pl.ds(0, 152), :]
        al[pl.ds(HALO, 152), :] = summed
        for kind in range(2):
            for n in range(16):
                al[pl.ds(HALO + 152 + 2048 * kind + 128 * n, 128), :] = wire[
                    n % TP, pl.ds(SMALL + 128 * (2 * kind + n // TP), 128), :
                ]

    def back(j, _):
        both = pltpu.roll(
            al[pl.ds(aligned(j * 48, 8), 56), :], lax.rem(LANE - tab[me, 0], LANE), 1
        )
        below = pltpu.roll(both, 55, 0)[:48]
        win[pl.ds(aligned(j * 48, 8), 48), :] = jnp.where(
            lanes(48) < LANE - tab[me, 0], both[:48], below
        )
        return 0

    lax.fori_loop(0, total // 48, back, 0, unroll=7)
    hd[...] = win[pl.ds(0, HALO), :]
    own[...] = win[pl.ds(HALO, plan.own_rows), :]
    shift_up(win, HALO + plan.last, hu, 0, HALO, 32, LANE - plan.part)


def collect(plan, pieces):
    total = -(-(HALO * 2 + plan.own_rows) // 672) * 672
    cleared = total + 96
    return pl.pallas_call(
        partial(collect_body, plan),
        out_shape=[
            shape((plan.own_rows, LANE), F32),
            shape((HALO, LANE), F32),
            shape((HALO, LANE), F32),
        ],
        in_specs=[SMEM] + [ANY] * (3 * TP),
        out_specs=[VMEM] * 3,
        scratch_shapes=[
            pltpu.VMEM((cleared, LANE), F32),
            pltpu.VMEM((total, LANE), F32),
            pltpu.VMEM((TP, plan.longest, LANE), F32),
            pltpu.SemaphoreType.DMA((TP,)),
        ],
        compiler_params=LIMIT,
        name="collect",
    )(jnp.asarray(plan.table), *pieces)


def tail_body(plan, value, out):
    first = (plan.last - HALO) % 8
    out[...] = jnp.zeros_like(out)
    shift_down(value, 0, out, first, HALO, 32, plan.part, True)
    z = pltpu.roll(value[pl.ds(HALO - 8, 8), :], plan.part, 1)
    row = lax.broadcasted_iota(jnp.int32, (8, LANE), 0)
    out[pl.ds(first + HALO, 8), :] = jnp.where(
        (row == 0) & (lanes(8) < plan.part), pltpu.roll(z, 1, 0), 0.0
    )


def place_tail(plan, value):
    rows = plan.own_rows - (plan.last - HALO) // 8 * 8
    return pl.pallas_call(
        partial(tail_body, plan),
        out_shape=shape((max(rows, HALO + 16), LANE), F32),
        in_specs=[VMEM],
        out_specs=VMEM,
        compiler_params=LIMIT,
        name="place_tail",
    )(value)[:rows]


def scan_body(reverse, coefficient, addend, out):
    rows, width = coefficient.shape
    at = lax.broadcasted_iota(jnp.int32, (8, width), 0)
    if reverse:
        at = 7 - at
    steps = rows // 8

    def step(j, carry):
        block = steps - 1 - j if reverse else j
        here = pl.ds(aligned(block * 8, 8), 8)
        a, b = coefficient[here, :], addend[here, :]
        for reach in (1, 2, 4):
            turn = 8 - reach if reverse else reach
            inside = at >= reach
            b = b + jnp.where(inside, a * pltpu.roll(b, turn, 0), 0.0)
            a = jnp.where(inside, a * pltpu.roll(a, turn, 0), a)
        value = b + a * carry
        out[here, :] = value
        edge = value[0:1] if reverse else value[7:8]
        return jnp.broadcast_to(edge, (8, width))

    lax.fori_loop(0, steps, step, jnp.zeros((8, width), F32), unroll=4)


def linear_scan(coefficient, addend, reverse):
    return pl.pallas_call(
        partial(scan_body, reverse),
        out_shape=shape(coefficient.shape, F32),
        in_specs=[VMEM] * 2,
        out_specs=VMEM,
        compiler_params=LIMIT,
        name="scan_back" if reverse else "scan",
    )(coefficient, addend)


def swap(value, bit):
    return lax.ppermute(value, "seq", [(i, i ^ bit) for i in range(TP)])


def exchange(pieces, targets=range(TP)):
    return [pieces[0]] + [
        lax.ppermute(pieces[k], "seq", [(i ^ k, i) for i in targets]) for k in range(1, TP)
    ]


def gather_stream(mine):
    half = mine.shape[0] // 2

    over_x, over_y = swap(mine, 2), swap(mine, 4)
    over_xy = [swap(over_x[:half], 4), swap(over_y[half:], 2)]
    chip = [mine, over_x, over_y] + over_xy
    return jnp.concatenate(chip + [swap(part, 1) for part in chip], axis=0)


def scatter_stream(partial_sums):
    rows = partial_sums.shape[0] // TP
    half = rows // 2

    def send(value, bit):
        return swap(value.astype(BF16), bit).astype(F32)

    other = send(partial_sums[TP // 2 * rows :], 1)
    q = (partial_sums[: TP // 2 * rows] + other).reshape(4, rows, -1)
    up = send(jnp.concatenate([q[1, :half], q[3, :half]]), 2)
    down = send(jnp.concatenate([q[2, half:], q[3, half:]]), 4)
    top = send(q[2, :half] + up[half:], 4)
    low = send(q[1, half:] + down[half:], 2)
    return jnp.concatenate(
        [q[0, :half] + up[:half] + top, q[0, half:] + down[:half] + low], axis=0
    )


def to_positions(values, s):
    rows = values.shape[0] // TP
    parts = []
    for j in range(TP):
        k = s ^ j
        at = (k // 2 + 4 * (k % 2)) * rows
        parts.append(lax.dynamic_slice_in_dim(values, at, rows, 0))
    return jnp.concatenate(parts, axis=0)


def to_relative(values, s):
    rows = values.shape[0] // TP
    return jnp.concatenate(
        [lax.dynamic_slice_in_dim(values, (s ^ k) * rows, rows, 0) for k in EVEN_FIRST], axis=0
    )


def gather_line(value, count):
    def send(value, bit):
        return lax.ppermute(value, "fsdp", [(i, i ^ bit) for i in range(count)])

    opposite, near = send(value, 3), send(value, 1)
    return [value, near, send(opposite, 1), opposite]


def scatter_line(blocks):
    count = len(blocks)
    own, near, far, cross = blocks
    far = lax.ppermute(far, "fsdp", [(i, i ^ 1) for i in range(count)])
    near = lax.ppermute(near, "fsdp", [(i, i ^ 1) for i in range(count)])
    cross = lax.ppermute(cross + far, "fsdp", [(i, i ^ 3) for i in range(count)])
    return own + near + cross


def sliced(plan, *arguments):
    return sliced_step(plan, *arguments)


def sliced_step(plan, stream_in, cotangent, starts, params, momentum, average):
    n_fsdp = plan.n_fsdp
    s = lax.axis_index("seq")
    shards = TP * n_fsdp
    onward = [(i, i + 1) for i in range(shards - 1)]
    backward = [(i + 1, i) for i in range(shards - 1)]
    both = ("seq", "fsdp")
    edge = HALO * LANE
    per = plan.per

    hd, hu = lax.optimization_barrier((params[per - edge :], params[:edge]))
    hd = lax.ppermute(hd.astype(BF16), both, onward)
    hu = lax.ppermute(hu.astype(BF16), both, backward)
    own = jnp.pad(params, (0, plan.own_rows * LANE - per)).reshape(-1, LANE)
    pieces = pack(
        plan, hd.astype(F32).reshape(-1, LANE), own, hu.astype(F32).reshape(-1, LANE)
    )
    first, middle_wire, second, third = order(plan, exchange(pieces))
    stream_bf, cotangent_bf, first = lax.optimization_barrier(
        (stream_in[0], cotangent[0], first)
    )
    line = gather_line(first, n_fsdp)
    middle_wire, second, third, line = lax.optimization_barrier(
        (middle_wire, second, third, line)
    )
    small, gates, w_y, w_x, b_head = unpack_first(plan, line)
    line = gather_line(middle_wire, n_fsdp)
    *out_rows, head = unpack_middle(plan, line, b_head)
    w_out = join_out_rows(exchange(out_rows))
    line = gather_line(second, n_fsdp)
    w_gate, w_up, w_down = unpack_second(plan, line, head)
    w_down = unpack_third(plan, gather_line(third, n_fsdp), w_down)

    mine = stream_in[0].astype(F32)
    stream = gather_stream(stream_bf)
    stream = stream.astype(F32)
    grad_out = gather_stream(cotangent_bf)
    rows = stream.shape[0]

    small = small.astype(F32)
    gain_one = small[0:12].reshape(-1)
    gain_two = small[12:24].reshape(-1)

    def channels(at):
        return jnp.concatenate(
            [
                lax.dynamic_slice_in_dim(small, at + s, 1, 0),
                lax.dynamic_slice_in_dim(small, at + s + TP, 1, 0),
            ],
            axis=1,
        )[0]

    conv_bias, bias_a, bias_i, lambda_raw = (channels(24 + 16 * j) for j in range(4))
    conv_weight = jnp.stack([channels(88 + 16 * j) for j in range(KW)])

    positions = jnp.arange(rows, dtype=jnp.int32)
    ext_pos = jnp.arange(rows + KW - 1, dtype=jnp.int32) - (KW - 1)
    segment_ext = segment_ids(ext_pos, starts[0])
    starting = start_flags(positions, starts[0])[:, None]

    def gate_product(values, at):
        return jnp.concatenate(
            [matmul(values[:, :HB], gates[at : at + HB]), matmul(values[:, HB:], gates[at + HB : at + 2 * HB])],
            axis=1,
        )

    def gate_product_t(values, at):
        return jnp.concatenate(
            [matmul_t(values[:, :HB], gates[at : at + HB]), matmul_t(values[:, HB:], gates[at + HB : at + 2 * HB])],
            axis=1,
        )

    normed = rms_norm(stream, gain_one).astype(BF16)
    branch_y = matmul(normed, w_y)
    branch_x = matmul(normed, w_x).astype(BF16)
    branch_y = to_positions(branch_y, s)
    branch_x = to_positions(branch_x, s)
    extended = jnp.pad(branch_x, ((KW - 1, 0), (0, 0))).astype(F32)

    def convolve_here(extended, weight, bias):
        total = jnp.zeros((rows, bias.shape[0]), F32) + bias
        for lag in range(KW):
            source = extended[KW - 1 - lag : KW - 1 - lag + rows]
            same = segment_ext[KW - 1 - lag : KW - 1 - lag + rows] == segment_ext[KW - 1 :]
            total = total + weight[lag] * source * same.astype(F32)[:, None]
        return total

    conv_out = convolve_here(extended, conv_weight, conv_bias).astype(BF16)
    conv_val = conv_out.astype(F32)
    pre_a = gate_product(conv_out, 0) + bias_a
    pre_i = gate_product(conv_out, 2 * HB) + bias_i
    decay, drive = gate_terms(pre_a, pre_i, conv_val, lambda_raw, starting)
    state = linear_scan(decay, drive, False)
    gelu_y = jax.nn.gelu(branch_y, approximate=True)
    mixed = to_relative((state * gelu_y).astype(BF16), s)
    middle = mine + scatter_stream(matmul(mixed, w_out))
    normed_two_mine = rms_norm(middle, gain_two).astype(BF16)
    normed_two = gather_stream(normed_two_mine)
    gate = matmul(normed_two, w_gate)
    upward = matmul(normed_two, w_up)
    hidden = gelu_product(gate, upward).astype(BF16)
    g_down = t_matmul(hidden, grad_out)
    summed_three = scatter_line(wire_third(plan, g_down))
    out_sums = matmul(hidden, w_down)
    output = (middle + scatter_stream(out_sums)).astype(BF16)
    gate, upward, _ = lax.optimization_barrier((gate, upward, hidden))

    grad_hidden = matmul_t(grad_out, w_down)
    _, product_back = jax.vjp(gelu_product, gate, upward)
    grad_gate, grad_up = product_back(grad_hidden)
    grad_gate, grad_up = grad_gate.astype(BF16), grad_up.astype(BF16)
    g_gate = t_matmul(normed_two, grad_gate)
    g_up = t_matmul(normed_two, grad_up)
    grad_normed_two = scatter_stream(matmul_t(grad_gate, w_gate) + matmul_t(grad_up, w_up))
    wire_two, wire_head = wire_second(plan, g_gate, g_up, g_down)
    summed_two = scatter_line(wire_two)

    _, norm_back_two = jax.vjp(rms_norm, middle, gain_two)
    grad_middle_part, g_gain_two = norm_back_two(grad_normed_two)
    grad_middle = cotangent[0].astype(F32) + grad_middle_part
    grad_first = gather_stream(grad_middle.astype(BF16))
    g_out = t_matmul(mixed, grad_first)
    wire_mid, b_head = wire_middle(plan, wire_head, exchange(split_out_rows(g_out)))
    summed_mid = scatter_line(wire_mid)
    grad_mixed = to_positions(matmul_t(grad_first, w_out), s)
    _, gelu_back = jax.vjp(partial(jax.nn.gelu, approximate=True), branch_y)
    grad_y = gelu_back(grad_mixed * state)[0].astype(BF16)
    next_decay = jnp.concatenate([decay[1:], jnp.ones((1, decay.shape[1]), F32)], axis=0)
    adjoint = linear_scan(next_decay, grad_mixed * gelu_y, True)
    previous = jnp.concatenate([jnp.zeros((1, decay.shape[1]), F32), state[:-1]], axis=0)
    _, gates_back = jax.vjp(gate_terms, pre_a, pre_i, conv_val, lambda_raw, starting)
    grad_pre_a, grad_pre_i, grad_direct, g_lambda, _ = gates_back((adjoint * previous, adjoint))
    grad_pre_a, grad_pre_i = grad_pre_a.astype(BF16), grad_pre_i.astype(BF16)
    g_gates = jnp.concatenate(
        [
            t_matmul(conv_out[:, n : n + HB], grad[:, n : n + HB])
            for grad in (grad_pre_a, grad_pre_i)
            for n in (0, HB)
        ],
        axis=0,
    )
    g_bias_a = jnp.sum(grad_pre_a.astype(F32), axis=0)
    g_bias_i = jnp.sum(grad_pre_i.astype(F32), axis=0)
    grad_conv = grad_direct + gate_product_t(grad_pre_a, 0) + gate_product_t(grad_pre_i, 2 * HB)
    _, conv_back = jax.vjp(convolve_here, extended, conv_weight, conv_bias)
    grad_ext, g_conv_weight, g_conv_bias = conv_back(grad_conv)
    grad_x = to_relative(grad_ext[KW - 1 :].astype(BF16), s)
    grad_y = to_relative(grad_y, s)
    g_x = t_matmul(normed, grad_x)
    g_y = t_matmul(normed, grad_y)
    grad_normed = scatter_stream(matmul_t(grad_y, w_y) + matmul_t(grad_x, w_x))
    _, norm_back_one = jax.vjp(rms_norm, mine, gain_one)
    grad_stream_part, g_gain_one = norm_back_one(grad_normed)
    input_grad = grad_middle + grad_stream_part

    summed_x = scatter_line(wire_x(plan, g_x, b_head))
    gains = jnp.concatenate([g_gain_one, g_gain_two]).reshape(-1, LANE)
    vectors = jnp.stack(
        [g_conv_bias, g_bias_a, g_bias_i, g_lambda] + [g_conv_weight[k] for k in range(KW)]
    ).reshape(-1, LANE)
    summed_y = scatter_line(wire_y(plan, gains, vectors, g_gates, g_y, g_x))
    early = spread(plan, plan.groups[2:], (summed_two, summed_three))
    middle_set = spread(plan, ((1,), (2,)), (summed_x, summed_mid))
    got = exchange(spread(plan, ((0,),), (summed_y,)), (0,))
    got += exchange(middle_set, (1, 2))
    got += exchange(early)
    grad_own, grad_hd, grad_hu = collect(plan, got)
    from_next = lax.ppermute(grad_hd, both, backward)
    from_before = lax.ppermute(grad_hu, both, onward)
    tail = place_tail(plan, from_next).reshape(-1)
    whole = plan.own_rows * LANE
    summed = (
        grad_own.reshape(-1)
        + jnp.pad(from_before.reshape(-1), (0, whole - edge))
        + jnp.pad(tail, (whole - tail.shape[0], 0))
    )[:per]
    new_moment = MOMENT * momentum + summed
    new_params = params - RATE * (summed + MOMENT * new_moment)
    new_average = BLEND * average + (1.0 - BLEND) * new_params
    return (output[None], input_grad[None], new_params, new_moment, new_average)


def solution(mesh):
    n_seq, n_fsdp = mesh.shape["seq"], mesh.shape["fsdp"]
    fast = (n_seq, n_fsdp) == (TP, 4)
    body = partial(sliced, Plan(n_seq, n_fsdp)) if fast else local
    return jax.shard_map(
        body,
        mesh=mesh,
        in_specs=(
            P("fsdp", "seq", None),
            P("fsdp", "seq", None),
            P("fsdp", None),
            P(("seq", "fsdp")),
            P(("seq", "fsdp")),
            P(("seq", "fsdp")),
        ),
        out_specs=(
            P("fsdp", "seq", None),
            P("fsdp", "seq", None),
            P(("seq", "fsdp")),
            P(("seq", "fsdp")),
            P(("seq", "fsdp")),
        ),
        check_vma=False,
    )
```

```python
from functools import partial
import math

import jax
import jax.numpy as jnp
import numpy as np
from jax import lax
from jax.experimental import pallas as pl
from jax.experimental.pallas import tpu as pltpu
from jax.sharding import PartitionSpec as P


D = 1536
LRU = 2048
FF = 4608
HB = 128
KW = 4


EPS = 1e-06
RATE = 3e-05
MOMENT = 0.9
BLEND = 0.9
DECAY_SCALE = 8.0


def shifted(block, axis, distance):
    devices = range(lax.axis_size(axis))
    route = [(i - distance, i) for i in devices if i - distance in devices]
    return lax.ppermute(block, axis, route)


def carried_in(value, axis, join, neutral, backward):
    count, mine = (lax.axis_size(axis), lax.axis_index(axis))
    pieces = jax.tree.map(lambda part: lax.all_gather(part, axis), value)
    if backward:
        pieces = jax.tree.map(lambda part: part[::-1], pieces)
        mine = count - 1 - mine
    so_far = jax.tree.map(
        lambda part, zero: jnp.full_like(part, 0) + jnp.asarray(zero, part.dtype), value, neutral
    )

    def lap(position, so_far):
        longer = join(so_far, jax.tree.map(lambda part: part[position], pieces))
        return jax.tree.map(lambda new, old: jnp.where(position < mine, new, old), longer, so_far)

    return lax.fori_loop(0, count - 1, lap, so_far)


def layout():
    return [
        ("gain_one", (D,)),
        ("gain_two", (D,)),
        ("conv_bias", (LRU,)),
        ("bias_a", (LRU,)),
        ("bias_i", (LRU,)),
        ("lambda_raw", (LRU,)),
        ("conv_weight", (KW, LRU)),
        ("gate_a", (LRU // HB, HB, HB)),
        ("gate_i", (LRU // HB, HB, HB)),
        ("w_y", (D, LRU)),
        ("w_x", (D, LRU)),
        ("w_out", (LRU, D)),
        ("w_gate", (D, FF)),
        ("w_up", (D, FF)),
        ("w_down", (FF, D)),
    ]


def unpack(packed):
    result = {}
    offset = 0
    for entry_name, entry_shape in layout():
        amount = math.prod(entry_shape)
        result[entry_name] = packed[offset : offset + amount].reshape(entry_shape)
        offset += amount
    return result


def matmul(left, right):
    return jnp.dot(left, right, preferred_element_type=jnp.float32)


def matmul_t(left, right):
    return lax.dot_general(
        left, right, (((1,), (1,)), ((), ())), preferred_element_type=jnp.float32
    )


def t_matmul(left, right):
    return lax.dot_general(
        left, right, (((0,), (0,)), ((), ())), preferred_element_type=jnp.float32
    )


def blocked(values, weight):
    shaped = values.reshape(values.shape[0], LRU // HB, HB)
    return jnp.einsum("tnh,nhk->tnk", shaped, weight, preferred_element_type=jnp.float32).reshape(
        values.shape[0], LRU
    )


def blocked_t(values, weight):
    shaped = values.reshape(values.shape[0], LRU // HB, HB)
    return jnp.einsum("tnk,nhk->tnh", shaped, weight, preferred_element_type=jnp.float32).reshape(
        values.shape[0], LRU
    )


def blocked_grad(inputs, grads):
    left = inputs.reshape(inputs.shape[0], LRU // HB, HB)
    right = grads.reshape(grads.shape[0], LRU // HB, HB)
    return jnp.einsum("tnh,tnk->nhk", left, right, preferred_element_type=jnp.float32)


def rms_norm(values, gain):
    return values * lax.rsqrt(jnp.mean(values * values, axis=-1, keepdims=True) + EPS) * gain


def combine(earlier, later):
    return (earlier[0] * later[0], later[0] * earlier[1] + later[1])


def gate_terms(pre_a, pre_i, conv_val, lambda_raw, starting):
    recall = jax.nn.sigmoid(pre_a)
    admit = jax.nn.sigmoid(pre_i)
    rate = DECAY_SCALE * jax.nn.softplus(lambda_raw) * recall
    decay = (1.0 - starting) * jnp.exp(-rate)
    scale_in = starting + (1.0 - starting) * jnp.sqrt(-jnp.expm1(-2.0 * rate))
    return (decay, scale_in * admit * conv_val)


def convolve(extended, weight, bias, segment_ext, rows):
    total = jnp.zeros((rows, LRU), jnp.float32) + bias
    for lag in range(KW):
        source = extended[KW - 1 - lag : KW - 1 - lag + rows]
        same = (segment_ext[KW - 1 - lag : KW - 1 - lag + rows] == segment_ext[KW - 1 :]).astype(
            jnp.float32
        )
        total = total + weight[lag] * source * same[:, None]
    return total


def segment_ids(positions, doc_starts):
    return jnp.sum((doc_starts[None, :] <= positions[:, None]).astype(jnp.int32), axis=1)


def start_flags(positions, doc_starts):
    return jnp.max((doc_starts[None, :] == positions[:, None]).astype(jnp.float32), axis=1)


def gelu_product(left, right):
    return jax.nn.gelu(left, approximate=True) * right


def local(stream_in, cotangent, starts, params, momentum, average):
    weights = unpack(
        lax.all_gather(params.astype(jnp.bfloat16), ("seq", "fsdp"), axis=0, tiled=True)
    )
    stream = stream_in[0].astype(jnp.float32)
    incoming = cotangent[0].astype(jnp.float32)
    doc_starts = starts[0]
    rows = stream.shape[0]
    positions = lax.axis_index("seq") * rows + jnp.arange(rows, dtype=jnp.int32)
    ext_pos = positions[0] - (KW - 1) + jnp.arange(rows + KW - 1, dtype=jnp.int32)
    segment_ext = segment_ids(ext_pos, doc_starts)
    starting = start_flags(positions, doc_starts)[:, None]
    gain_one = weights["gain_one"].astype(jnp.float32)
    gain_two = weights["gain_two"].astype(jnp.float32)
    conv_weight = weights["conv_weight"].astype(jnp.float32)
    conv_bias = weights["conv_bias"].astype(jnp.float32)
    lambda_raw = weights["lambda_raw"].astype(jnp.float32)
    normed = rms_norm(stream, gain_one).astype(jnp.bfloat16)
    branch_y = matmul(normed, weights["w_y"])
    branch_x = matmul(normed, weights["w_x"]).astype(jnp.bfloat16)
    edge = shifted(branch_x[rows - (KW - 1) :], "seq", 1)
    extended = jnp.concatenate([edge, branch_x], axis=0).astype(jnp.float32)
    conv_out = convolve(extended, conv_weight, conv_bias, segment_ext, rows).astype(jnp.bfloat16)
    conv_val = conv_out.astype(jnp.float32)
    pre_a = blocked(conv_out, weights["gate_a"]) + weights["bias_a"].astype(jnp.float32)
    pre_i = blocked(conv_out, weights["gate_i"]) + weights["bias_i"].astype(jnp.float32)
    decay, drive = gate_terms(pre_a, pre_i, conv_val, lambda_raw, starting)
    prod_local, state_local = lax.associative_scan(combine, (decay, drive), axis=0)
    neutral = (jnp.ones((LRU,), jnp.float32), jnp.zeros((LRU,), jnp.float32))
    carried = carried_in((prod_local[-1], state_local[-1]), "seq", combine, neutral, False)
    carry_in = carried[1]
    state = lax.associative_scan(combine, (decay, drive.at[0].add(decay[0] * carry_in)), axis=0)[1]
    gelu_y = jax.nn.gelu(branch_y, approximate=True)
    mixed = (state * gelu_y).astype(jnp.bfloat16)
    middle = stream + matmul(mixed, weights["w_out"])
    normed_two = rms_norm(middle, gain_two).astype(jnp.bfloat16)
    gate = matmul(normed_two, weights["w_gate"])
    upward = matmul(normed_two, weights["w_up"])
    hidden = gelu_product(gate, upward).astype(jnp.bfloat16)
    output = (middle + matmul(hidden, weights["w_down"])).astype(jnp.bfloat16)
    grads = {}
    grad_out = incoming.astype(jnp.bfloat16)
    grads["w_down"] = t_matmul(hidden, grad_out)
    grad_hidden = matmul_t(grad_out, weights["w_down"])
    _, product_back = jax.vjp(gelu_product, gate, upward)
    grad_gate, grad_up = product_back(grad_hidden)
    grad_gate = grad_gate.astype(jnp.bfloat16)
    grad_up = grad_up.astype(jnp.bfloat16)
    grads["w_gate"] = t_matmul(normed_two, grad_gate)
    grads["w_up"] = t_matmul(normed_two, grad_up)
    grad_normed_two = matmul_t(grad_gate, weights["w_gate"]) + matmul_t(grad_up, weights["w_up"])
    _, norm_back_two = jax.vjp(rms_norm, middle, gain_two)
    grad_middle_part, grads["gain_two"] = norm_back_two(grad_normed_two)
    grad_middle = incoming + grad_middle_part
    grad_first = grad_middle.astype(jnp.bfloat16)
    grads["w_out"] = t_matmul(mixed, grad_first)
    grad_mixed = matmul_t(grad_first, weights["w_out"])
    _, gelu_back = jax.vjp(partial(jax.nn.gelu, approximate=True), branch_y)
    grad_y = gelu_back(grad_mixed * state)[0].astype(jnp.bfloat16)
    grad_state = grad_mixed * gelu_y
    next_decay = jnp.concatenate([decay[1:], jnp.ones((1, LRU), jnp.float32)], axis=0)
    suffix, adjoint_local = lax.associative_scan(
        combine, (next_decay, grad_state), axis=0, reverse=True
    )
    returned = carried_in(
        (prod_local[-1], decay[0] * adjoint_local[0]), "seq", combine, neutral, True
    )
    adjoint = adjoint_local + suffix * returned[1]
    previous = jnp.concatenate([carry_in[None, :], state[:-1]], axis=0)
    _, gates_back = jax.vjp(gate_terms, pre_a, pre_i, conv_val, lambda_raw, starting)
    grad_pre_a, grad_pre_i, grad_direct, grads["lambda_raw"], _ = gates_back(
        (adjoint * previous, adjoint)
    )
    grad_pre_a = grad_pre_a.astype(jnp.bfloat16)
    grad_pre_i = grad_pre_i.astype(jnp.bfloat16)
    grads["gate_a"] = blocked_grad(conv_out, grad_pre_a)
    grads["gate_i"] = blocked_grad(conv_out, grad_pre_i)
    grads["bias_a"] = jnp.sum(grad_pre_a.astype(jnp.float32), axis=0)
    grads["bias_i"] = jnp.sum(grad_pre_i.astype(jnp.float32), axis=0)
    grad_conv = (
        grad_direct
        + blocked_t(grad_pre_a, weights["gate_a"])
        + blocked_t(grad_pre_i, weights["gate_i"])
    )
    _, conv_back = jax.vjp(
        partial(convolve, segment_ext=segment_ext, rows=rows), extended, conv_weight, conv_bias
    )
    grad_ext, grads["conv_weight"], grads["conv_bias"] = conv_back(grad_conv)
    edge_back = shifted(grad_ext[: KW - 1], "seq", -1)
    grad_x = grad_ext[KW - 1 :] + jnp.concatenate(
        [jnp.zeros((rows - (KW - 1), LRU), jnp.float32), edge_back], axis=0
    )
    grad_x = grad_x.astype(jnp.bfloat16)
    grads["w_x"] = t_matmul(normed, grad_x)
    grads["w_y"] = t_matmul(normed, grad_y)
    grad_normed = matmul_t(grad_y, weights["w_y"]) + matmul_t(grad_x, weights["w_x"])
    _, norm_back_one = jax.vjp(rms_norm, stream, gain_one)
    grad_stream_part, grads["gain_one"] = norm_back_one(grad_normed)
    input_grad = grad_middle + grad_stream_part
    packed_grad = jnp.concatenate([grads[entry[0]].reshape(-1) for entry in layout()])
    summed = lax.psum_scatter(packed_grad, ("seq", "fsdp"), scatter_dimension=0, tiled=True)
    new_moment = MOMENT * momentum + summed
    new_params = params - RATE * (summed + MOMENT * new_moment)
    new_average = BLEND * average + (1.0 - BLEND) * new_params
    return (output[None], input_grad[None], new_params, new_moment, new_average)


LANE = 128
TP = 8
HALO = 544
SMALL = 160
GATES = 512
REGIONS = {
    "A": (4248, 256, 192, 32),
    "B": (53400, 1536, 16, 192),
    "C": (77976, 1152, 96, 144),
    "D": (188568, 1536, 36, 192),
}
ROWS = 243864
EVEN_FIRST = (0, 2, 4, 6, 1, 3, 5, 7)
F32 = jnp.float32
BF16 = jnp.bfloat16


class Plan:
    def __init__(self, n_seq, n_fsdp):
        self.n_fsdp = n_fsdp
        shards = n_seq * n_fsdp
        per = ROWS * LANE // shards
        self.per = per
        self.part = per % LANE
        self.own_rows = -(-per // 1024) * 8
        self.last = per // LANE
        bounds = [0]
        for i in range(1, shards):
            at = per * i / LANE
            for first, unit, count, _ in REGIONS.values():
                if first <= at < first + unit * count:
                    bounds.append(first + unit * round((at - first) / unit))
        bounds.append(ROWS)
        self.segments = []
        self.sizes = []
        self.table = np.zeros((shards, 16), np.int32)
        for i in range(shards):
            base = per * i // LANE
            self.table[i, 0] = per * i % LANE
            offset = SMALL + GATES if i == 0 else 0
            found = {}
            for slot, (name, (first, unit, count, wide)) in enumerate(REGIONS.items()):
                low = max(bounds[i], first)
                high = min(bounds[i + 1], first + unit * count)
                if high > low:
                    units = (high - low) // unit
                    found[name] = ((low - first) // unit, units, offset)
                    self.table[i, 1 + 3 * slot : 4 + 3 * slot] = (
                        low - base + HALO,
                        units,
                        offset,
                    )
                    offset += units * wide
            self.segments.append(found)
            self.sizes.append(offset)
            self.table[i, 13] = int(i == 0)
        self.lengths = [
            max(self.sizes[s * n_fsdp : (s + 1) * n_fsdp]) for s in range(n_seq)
        ]
        self.offsets = np.concatenate([[0], np.cumsum(self.lengths)]).astype(np.int32)
        self.longest = max(self.lengths)
        self.groups = ((0, 1), (2,), (3, 4, 5, 6), (7,))
        self.starts = [int(self.offsets[group[0]]) for group in self.groups]
        self.rows = [sum(self.lengths[s] for s in group) for group in self.groups]

    def pieces(self, name, groups):
        out = []
        for i, found in enumerate(self.segments):
            s, f = divmod(i, self.n_fsdp)
            if name in found and s in groups:
                first, units, offset = found[name]
                row = int(self.offsets[s] - self.offsets[groups[0]]) + offset
                out.append((f, row, first, units))
        return out


VMEM = pl.BlockSpec(memory_space=pltpu.VMEM)
ANY = pl.BlockSpec(memory_space=pl.ANY)
SMEM = pl.BlockSpec(memory_space=pltpu.SMEM)
LIMIT = pltpu.CompilerParams(vmem_limit_bytes=60 * 1024 * 1024)


def shape(dims, dtype):
    return jax.ShapeDtypeStruct(dims, dtype)


def aligned(value, multiple):
    return pl.multiple_of(value, multiple)


def lanes(rows):
    return lax.broadcasted_iota(jnp.int32, (rows, LANE), 1)


def swap_lanes(blocks):
    blocks = list(blocks)
    at = lanes(blocks[0].shape[0]) // 16
    for step in (4, 2, 1):
        low_side = (at & step) == 0
        for one in range(TP):
            if one & step == 0:
                left, right = blocks[one], blocks[one + step]
                blocks[one] = jnp.where(low_side, left, pltpu.roll(right, 16 * step, 1))
                blocks[one + step] = jnp.where(
                    low_side, pltpu.roll(left, LANE - 16 * step, 1), right
                )
    return blocks


def shift_down(source, source_row, target, target_row, rows, block, amount, unroll):
    def step(j, tail):
        z = pltpu.roll(source[pl.ds(source_row + j * block, block), :], amount, 1)
        above = pltpu.roll(jnp.concatenate([tail, z], axis=0), 1, 0)[8:]
        target[pl.ds(target_row + j * block, block), :] = jnp.where(
            lanes(block) < amount, above, z
        )
        return z[block - 8 :]

    lax.fori_loop(0, rows // block, step, jnp.zeros((8, LANE), F32), unroll=unroll)


def pack_body(plan, tab, hd, own, hu, *rest):
    outs, (win, al, wire, sems) = rest[:TP], rest[TP:]
    s, f = lax.axis_index("seq"), lax.axis_index("fsdp")
    me = s * plan.n_fsdp + f
    total = win.shape[0]
    first = pltpu.make_async_copy(hd, win.at[pl.ds(0, HALO)], sems.at[0])
    second = pltpu.make_async_copy(own, win.at[pl.ds(HALO, plan.own_rows)], sems.at[1])
    first.start()
    second.start()
    first.wait()
    second.wait()
    seam = HALO + plan.last
    kept = win[pl.ds(seam, 8), :]
    shift_down(hu, 0, win, seam, HALO, 32, plan.part, True)
    edge = lax.broadcasted_iota(jnp.int32, (8, LANE), 0) == 0
    win[pl.ds(seam, 8), :] = jnp.where(
        edge & (lanes(8) < plan.part), kept, win[pl.ds(seam, 8), :]
    )
    shift_down(win, 0, al, 0, total, 48, tab[me, 0], 7)

    def columns(g, _):
        at = tab[me, 1] + g * 256
        to = tab[me, 3] + g * 16
        for block in range(16):
            row = to + 16 * tab[me, 2] * (block // TP)
            wire[block % TP, pl.ds(aligned(row, 16), 16), :] = al[
                pl.ds(at + block, 16, stride=16), :
            ].astype(BF16)
        return 0

    lax.fori_loop(0, tab[me, 2], columns, 0)
    for slot in (4, 10):

        def grouped(j, _):
            for owner in range(TP):
                at = tab[me, slot] + j * 1536 + owner * 192
                to = tab[me, slot + 2] + j * 16
                for block in range(12):
                    row = to + 16 * tab[me, slot + 1] * block
                    wire[owner, pl.ds(aligned(row, 16), 16), :] = al[
                        pl.ds(at + block, 16, stride=12), :
                    ].astype(BF16)
            return 0

        lax.fori_loop(0, tab[me, slot + 1], grouped, 0)

    def mixed_columns(g, _):
        at = tab[me, 7] + g * 1152
        to = tab[me, 9] + g * 32
        wide = 32 * tab[me, 8]
        last = tab[me, 9] + 4 * wide + g * 16
        for half in range(2):
            for a in range(4):
                parts = swap_lanes(
                    [
                        al[pl.ds(at + 576 * half + 8 * a + b, 16, stride=36), :]
                        for b in range(TP)
                    ]
                )
                for owner in range(TP):
                    row = to + a * wide + 16 * half
                    wire[owner, pl.ds(aligned(row, 16), 16), :] = parts[owner].astype(BF16)
        parts = swap_lanes(
            [
                al[pl.ds(at + 576 * half + 32 + b, 16, stride=36), :]
                for half in range(2)
                for b in range(4)
            ]
        )
        for owner in range(TP):
            wire[owner, pl.ds(aligned(last, 16), 16), :] = parts[owner].astype(BF16)
        return 0

    lax.fori_loop(0, tab[me, 8], mixed_columns, 0)

    @pl.when(me == 0)
    def _():
        for owner in range(TP):
            wire[owner, pl.ds(0, SMALL), :] = al[pl.ds(HALO, SMALL), :].astype(BF16)
        for kind in range(2):
            for n in range(16):
                wire[n % TP, pl.ds(SMALL + 128 * (2 * kind + n // TP), 128), :] = al[
                    pl.ds(HALO + 152 + 2048 * kind + 128 * n, 128), :
                ].astype(BF16)

    copies = [
        pltpu.make_async_copy(wire.at[s ^ k], outs[k], sems.at[2 + k]) for k in range(TP)
    ]
    for copy in copies:
        copy.start()
    for copy in copies:
        copy.wait()


def pack(plan, hd, own, hu):
    total = -(-(HALO * 2 + plan.own_rows) // 672) * 672
    return pl.pallas_call(
        partial(pack_body, plan),
        out_shape=[shape((plan.longest, LANE), BF16)] * TP,
        in_specs=[SMEM, ANY, ANY, VMEM],
        out_specs=[ANY] * TP,
        scratch_shapes=[
            pltpu.VMEM((total, LANE), F32),
            pltpu.VMEM((total, LANE), F32),
            pltpu.VMEM((TP, plan.longest, LANE), BF16),
            pltpu.SemaphoreType.DMA((2 + TP,)),
        ],
        compiler_params=LIMIT,
        name="pack",
    )(jnp.asarray(plan.table), hd, own, hu)


def order_body(plan, *refs):
    pieces, outs, sems = refs[:TP], refs[TP : TP + 4], refs[TP + 4]
    s = lax.axis_index("seq")
    for start in (True, False):
        for number, group in enumerate(plan.groups):
            for source in group:
                size = plan.lengths[source]
                at = int(plan.offsets[source]) - plan.starts[number]
                for k in range(TP):

                    @pl.when((s ^ source) == k)
                    def _():
                        copy = pltpu.make_async_copy(
                            pieces[k].at[pl.ds(0, size)],
                            outs[number].at[pl.ds(at, size)],
                            sems.at[source],
                        )
                        if start:
                            copy.start()
                        else:
                            copy.wait()


def order(plan, pieces):
    return pl.pallas_call(
        partial(order_body, plan),
        out_shape=[shape((rows, LANE), BF16) for rows in plan.rows],
        in_specs=[ANY] * TP,
        out_specs=[VMEM] * 4,
        scratch_shapes=[pltpu.SemaphoreType.DMA((TP,))],
        compiler_params=LIMIT,
        name="order",
    )(*pieces)


def weight_copies(plan, number, weights, halves, b_rows):
    out = []
    for f, row, first, units in plan.pieces("A", plan.groups[number]):
        for target, begin, end in weights.get("A", ()):
            low, high = max(first, begin), min(first + units, end)
            if high > low:
                for n in range(2):
                    out.append(
                        (
                            f,
                            row + 16 * (units * n + low - first),
                            16 * (high - low),
                            target.at[pl.ds(16 * (low - begin), 16 * (high - low)), pl.ds(128 * n, 128)],
                        )
                    )
    for f, row, first, units in plan.pieces("B", plan.groups[number]):
        if b_rows is not None:
            for block in range(12):
                out.append(
                    (
                        f,
                        row + 16 * units * block,
                        16 * units,
                        b_rows.at[block, pl.ds(16 * first, 16 * units)],
                    )
                )
    for f, row, first, units in plan.pieces("C", plan.groups[number]):
        for target, begin, end in weights.get("C", ()):
            low, high = max(first, begin), min(first + units, end)
            if high > low:
                for a in range(4):
                    out.append(
                        (
                            f,
                            row + 32 * (units * a + low - first),
                            32 * (high - low),
                            target.at[pl.ds(32 * (low - begin), 32 * (high - low)), pl.ds(128 * a, 128)],
                        )
                    )
        if halves is not None:
            out.append(
                (f, row + 128 * units, 16 * units, halves.at[pl.ds(16 * first, 16 * units)])
            )
    for f, row, first, units in plan.pieces("D", plan.groups[number]):
        for target, begin, end in weights.get("D", ()):
            for n in range(12):
                out.append(
                    (
                        f,
                        row + 16 * units * n,
                        16 * units,
                        target.at[pl.ds(16 * (first - begin), 16 * units), pl.ds(128 * n, 128)],
                    )
                )
    return out


def fetch_line(plan, line, copies, sems, first=0, phases=(True, False)):
    f = lax.axis_index("fsdp")
    for start in phases:
        for source in range(plan.n_fsdp):
            for away in range(plan.n_fsdp):

                @pl.when((f ^ source) == away)
                def _():
                    for number, (holder, row, rows, target) in enumerate(copies):
                        if holder == source:
                            copy = pltpu.make_async_copy(
                                line[away].at[pl.ds(row, rows)], target, sems.at[first + number]
                            )
                            if start:
                                copy.start()
                            else:
                                copy.wait()


def first_copies(plan, small, gates, w_y, w_x, b_head):
    out = [(0, 0, SMALL, small), (0, SMALL, GATES, gates)]
    out += weight_copies(plan, 0, {"A": ((w_y, 0, 96), (w_x, 96, 192))}, None, None)
    for f, row, first, units in plan.pieces("B", plan.groups[0]):
        out.append((f, row, 192 * units, b_head.at[pl.ds(192 * first, 192 * units)]))
    return out


def first_body(plan, *refs):
    line, refs = refs[: plan.n_fsdp], refs[plan.n_fsdp :]
    *targets, sems = refs
    fetch_line(plan, line, first_copies(plan, *targets), sems)


def head_rows(plan):
    return sum(144 * p[3] for p in plan.pieces("C", plan.groups[1]))


def b_head_rows(plan):
    return sum(192 * p[3] for p in plan.pieces("B", plan.groups[0]))


class Nowhere:
    at = property(lambda self: self)

    def __getitem__(self, _):
        return self


def count_first(plan):
    return len(first_copies(plan, *[Nowhere()] * 5))


def unpack_first(plan, line):
    return pl.pallas_call(
        partial(first_body, plan),
        out_shape=[
            shape((SMALL, LANE), BF16),
            shape((GATES, LANE), BF16),
            shape((D, 256), BF16),
            shape((D, 256), BF16),
            shape((b_head_rows(plan), LANE), BF16),
        ],
        in_specs=[ANY] * len(line),
        out_specs=[VMEM] * 5,
        scratch_shapes=[pltpu.SemaphoreType.DMA((count_first(plan),))],
        compiler_params=LIMIT,
        name="unpack_first",
    )(*line)


def middle_copies(plan, b_rows, head):
    out = weight_copies(plan, 1, {}, None, b_rows)
    for f, row, first, units in plan.pieces("C", plan.groups[1]):
        out.append((f, row, 144 * units, head.at[pl.ds(144 * first, 144 * units)]))
    return out


def b_head_copies(plan, b_head, b_rows):
    out = []
    for _, _, first, units in plan.pieces("B", plan.groups[0]):
        for block in range(12):
            out.append(
                (
                    b_head.at[pl.ds(192 * first + 16 * units * block, 16 * units)],
                    b_rows.at[block, pl.ds(16 * first, 16 * units)],
                )
            )
    return out


def middle_body(plan, *refs):
    line, refs = refs[: plan.n_fsdp], refs[plan.n_fsdp :]
    b_head, outs, head, b_rows, sems, more = refs[0], refs[1 : 1 + TP], *refs[1 + TP :]
    local_copies = [
        pltpu.make_async_copy(source, target, more.at[number])
        for number, (source, target) in enumerate(b_head_copies(plan, b_head, b_rows))
    ]
    for copy in local_copies:
        copy.start()
    fetch_line(plan, line, middle_copies(plan, b_rows, head), sems)
    for copy in local_copies:
        copy.wait()
    s = lax.axis_index("seq")
    for k in range(TP):
        for n in range(2):
            unit = (s ^ k) + TP * n
            for block in range(12):
                outs[k][pl.ds(192 * n + 16 * block, 16), :] = b_rows[
                    block, pl.ds(aligned(16 * unit, 16), 16), :
                ]


def unpack_middle(plan, line, b_head):
    return pl.pallas_call(
        partial(middle_body, plan),
        out_shape=[shape((384, LANE), BF16)] * TP + [shape((head_rows(plan), LANE), BF16)],
        in_specs=[ANY] * (len(line) + 1),
        out_specs=[VMEM] * (TP + 1),
        scratch_shapes=[
            pltpu.VMEM((12, 256, LANE), BF16),
            pltpu.SemaphoreType.DMA((len(middle_copies(plan, *[Nowhere()] * 2)),)),
            pltpu.SemaphoreType.DMA((len(b_head_copies(plan, *[Nowhere()] * 2)),)),
        ],
        compiler_params=LIMIT,
        name="unpack_middle",
    )(*line, b_head)


def head_copies(plan, head, weight, halves):
    out = []
    for _, _, first, units in plan.pieces("C", plan.groups[1]):
        for a in range(4):
            out.append(
                (
                    head.at[pl.ds(144 * first + 32 * units * a, 32 * units)],
                    weight.at[pl.ds(32 * first, 32 * units), pl.ds(128 * a, 128)],
                )
            )
        out.append(
            (
                head.at[pl.ds(144 * first + 128 * units, 16 * units)],
                halves.at[pl.ds(16 * first, 16 * units)],
            )
        )
    return out


def second_copies(plan, w_gate, w_up, w_down, halves):
    return weight_copies(
        plan,
        2,
        {"C": ((w_gate, 0, 48), (w_up, 48, 96)), "D": ((w_down, 0, 16),)},
        halves,
        None,
    )


def halves_copies(plan, halves):
    return [
        (f, row + 128 * units, 16 * units, halves.at[pl.ds(16 * first, 16 * units)])
        for f, row, first, units in plan.pieces("C", plan.groups[2])
    ]


def second_body(plan, *refs):
    line, refs = refs[: plan.n_fsdp], refs[plan.n_fsdp :]
    head, w_gate, w_up, w_down, halves, sems, more = refs
    local_copies = [
        pltpu.make_async_copy(source, target, more.at[number])
        for number, (source, target) in enumerate(head_copies(plan, head, w_gate, halves))
    ]
    for copy in local_copies:
        copy.start()
    merged = halves_copies(plan, halves)
    whole = second_copies(plan, w_gate, w_up, w_down, None)
    fetch_line(plan, line, merged, sems, 0, (True,))
    fetch_line(plan, line, whole, sems, len(merged), (True,))
    fetch_line(plan, line, merged, sems, 0, (False,))
    for copy in local_copies:
        copy.wait()
    for weight, begin in ((w_gate, 0), (w_up, 48)):

        def step(g, _):
            last = halves[pl.ds(aligned(16 * (begin + g), 16), 16), :]
            weight[pl.ds(aligned(32 * g, 16), 16), pl.ds(512, 64)] = last[:, :64]
            weight[pl.ds(aligned(32 * g + 16, 16), 16), pl.ds(512, 64)] = last[:, 64:]
            return 0

        lax.fori_loop(0, 48, step, 0, unroll=8)
    fetch_line(plan, line, whole, sems, len(merged), (False,))


def unpack_second(plan, line, head):
    many = len(second_copies(plan, *[Nowhere()] * 4))
    few = len(head_copies(plan, *[Nowhere()] * 3))
    return pl.pallas_call(
        partial(second_body, plan),
        out_shape=[
            shape((D, FF // TP), BF16),
            shape((D, FF // TP), BF16),
            shape((256, D), BF16),
        ],
        in_specs=[ANY] * (len(line) + 1),
        out_specs=[VMEM] * 3,
        scratch_shapes=[
            pltpu.VMEM((96 * 16, LANE), BF16),
            pltpu.SemaphoreType.DMA((many,)),
            pltpu.SemaphoreType.DMA((few,)),
        ],
        compiler_params=LIMIT,
        name="unpack_second",
    )(*line, head)


def third_copies(plan, w_down):
    return weight_copies(plan, 3, {"D": ((w_down, 0, 36),)}, None, None)


def third_body(plan, *refs):
    line, refs = refs[: plan.n_fsdp], refs[plan.n_fsdp :]
    before, w_down, sems, one = refs
    copy = pltpu.make_async_copy(before, w_down.at[pl.ds(0, 256)], one.at[0])
    copy.start()
    fetch_line(plan, line, third_copies(plan, w_down), sems)
    copy.wait()


def unpack_third(plan, line, before):
    many = len(third_copies(plan, Nowhere()))
    return pl.pallas_call(
        partial(third_body, plan),
        out_shape=shape((FF // TP, D), BF16),
        in_specs=[ANY] * (len(line) + 1),
        out_specs=VMEM,
        scratch_shapes=[
            pltpu.SemaphoreType.DMA((many,)),
            pltpu.SemaphoreType.DMA((1,)),
        ],
        compiler_params=LIMIT,
        name="unpack_third",
    )(*line, before)


def out_rows_body(*refs):
    pieces, w_out = refs[:TP], refs[TP]
    s = lax.axis_index("seq")
    for k in range(TP):
        for n in range(2):
            to = aligned(128 * n + 16 * (s ^ k), 16)
            for block in range(12):
                w_out[pl.ds(to, 16), pl.ds(128 * block, 128)] = pieces[k][
                    pl.ds(192 * n + 16 * block, 16), :
                ]


def join_out_rows(pieces):
    return pl.pallas_call(
        out_rows_body,
        out_shape=shape((256, D), BF16),
        in_specs=[VMEM] * TP,
        out_specs=VMEM,
        compiler_params=LIMIT,
        name="join_out_rows",
    )(*pieces)


def split_rows_body(grad, *pieces):
    s = lax.axis_index("seq")
    for k in range(TP):
        for n in range(2):
            at = aligned(128 * n + 16 * (s ^ k), 16)
            for block in range(12):
                pieces[k][pl.ds(192 * n + 16 * block, 16), :] = grad[
                    pl.ds(at, 16), pl.ds(128 * block, 128)
                ]


def split_out_rows(grad):
    return pl.pallas_call(
        split_rows_body,
        out_shape=[shape((384, LANE), F32)] * TP,
        in_specs=[VMEM],
        out_specs=[VMEM] * TP,
        compiler_params=LIMIT,
        name="split_out_rows",
    )(grad)


def start_copies(copies, sems, first=0):
    made = [
        pltpu.make_async_copy(source, target, sems.at[first + number])
        for number, (source, target) in enumerate(copies)
    ]
    for copy in made:
        copy.start()
    return made


def to_wires(plan, copies, wires, sems, first, start):
    f = lax.axis_index("fsdp")
    for j in range(plan.n_fsdp):
        for x in range(plan.n_fsdp):

            @pl.when((f ^ j) == x)
            def _():
                for number, (holder, row, rows, source) in enumerate(copies):
                    if holder == j:
                        copy = pltpu.make_async_copy(
                            source, wires[x].at[pl.ds(row, rows)], sems.at[first + number]
                        )
                        if start:
                            copy.start()
                        else:
                            copy.wait()


def wire_second_body(plan, g_gate, g_up, g_down, *refs):
    wires, (head, halves, sems) = refs[: plan.n_fsdp], refs[plan.n_fsdp :]
    whole = second_copies(plan, g_gate, g_up, g_down, None)
    merged = halves_copies(plan, halves)
    more = [(b, a) for a, b in head_copies(plan, head, g_gate, halves)]
    to_wires(plan, whole, wires, sems, 0, True)
    for grad, begin in ((g_gate, 0), (g_up, 48)):

        def step(g, _):
            left = grad[pl.ds(aligned(32 * g, 16), 16), pl.ds(512, 64)]
            right = grad[pl.ds(aligned(32 * g + 16, 16), 16), pl.ds(512, 64)]
            halves[pl.ds(aligned(16 * (begin + g), 16), 16), :] = jnp.concatenate(
                [left, right], axis=1
            )
            return 0

        lax.fori_loop(0, 48, step, 0, unroll=8)
    to_wires(plan, merged, wires, sems, len(whole), True)
    made = start_copies(more, sems, len(whole) + len(merged))
    to_wires(plan, whole, wires, sems, 0, False)
    to_wires(plan, merged, wires, sems, len(whole), False)
    for copy in made:
        copy.wait()


def wire_second(plan, g_gate, g_up, g_down):
    many = len(second_copies(plan, *[Nowhere()] * 4)) + len(
        head_copies(plan, *[Nowhere()] * 3)
    )
    out = pl.pallas_call(
        partial(wire_second_body, plan),
        out_shape=[shape((plan.rows[2], LANE), F32)] * plan.n_fsdp
        + [shape((head_rows(plan), LANE), F32)],
        in_specs=[VMEM] * 3,
        out_specs=[ANY] * (plan.n_fsdp + 1),
        scratch_shapes=[
            pltpu.VMEM((96 * 16, LANE), F32),
            pltpu.SemaphoreType.DMA((many,)),
        ],
        compiler_params=LIMIT,
        name="wire_second",
    )(g_gate, g_up, g_down)
    return out[:-1], out[-1]


def wire_plain(plan, copies_of, rows, operands):
    many = len(copies_of(*[Nowhere()] * len(operands)))

    def body(*refs):
        *refs, sems = refs
        sources, wires = refs[: len(operands)], refs[len(operands) :]
        copies = copies_of(*sources)
        to_wires(plan, copies, wires, sems, 0, True)
        to_wires(plan, copies, wires, sems, 0, False)

    return pl.pallas_call(
        body,
        out_shape=[shape((rows, LANE), F32)] * plan.n_fsdp,
        in_specs=[VMEM] * len(operands),
        out_specs=[ANY] * plan.n_fsdp,
        scratch_shapes=[pltpu.SemaphoreType.DMA((many,))],
        compiler_params=LIMIT,
    )(*operands)


def wire_third(plan, g_down):
    return wire_plain(plan, partial(third_copies, plan), plan.rows[3], (g_down,))


def wire_middle_body(plan, head, *refs):
    pieces, refs = refs[:TP], refs[TP:]
    wires, (b_head, b_rows, sems) = refs[: plan.n_fsdp], refs[plan.n_fsdp :]
    s = lax.axis_index("seq")
    for k in range(TP):
        for n in range(2):
            unit = (s ^ k) + TP * n
            for block in range(12):
                b_rows[block, pl.ds(aligned(16 * unit, 16), 16), :] = pieces[k][
                    pl.ds(192 * n + 16 * block, 16), :
                ]
    copies = middle_copies(plan, b_rows, head)
    to_wires(plan, copies, wires, sems, 0, True)
    more = [(b, a) for a, b in b_head_copies(plan, b_head, b_rows)]
    made = start_copies(more, sems, len(copies))
    to_wires(plan, copies, wires, sems, 0, False)
    for copy in made:
        copy.wait()


def wire_middle(plan, head, pieces):
    many = len(middle_copies(plan, *[Nowhere()] * 2)) + len(
        b_head_copies(plan, *[Nowhere()] * 2)
    )
    out = pl.pallas_call(
        partial(wire_middle_body, plan),
        out_shape=[shape((plan.rows[1], LANE), F32)] * plan.n_fsdp
        + [shape((b_head_rows(plan), LANE), F32)],
        in_specs=[VMEM] * (1 + TP),
        out_specs=[ANY] * (plan.n_fsdp + 1),
        scratch_shapes=[
            pltpu.VMEM((12, 256, LANE), F32),
            pltpu.SemaphoreType.DMA((many,)),
        ],
        compiler_params=LIMIT,
        name="wire_middle",
    )(head, *pieces)
    return out[:-1], out[-1]


def split_copies(plan, copies):
    border = int(plan.offsets[1])
    return (
        [copy for copy in copies if copy[1] < border],
        [(f, row - border, rows, at) for f, row, rows, at in copies if row >= border],
    )


def wire_x(plan, g_x, b_head):
    def copies_of(g_x, b_head):
        nowhere = Nowhere()
        return split_copies(plan, first_copies(plan, nowhere, nowhere, nowhere, g_x, b_head))[1]

    return wire_plain(plan, copies_of, plan.lengths[1], (g_x, b_head))


def wire_y_body(plan, gains, vectors, gates, g_y, g_x, *refs):
    wires, (small, sems) = refs[: plan.n_fsdp], refs[plan.n_fsdp :]
    s = lax.axis_index("seq")
    small[...] = jnp.zeros_like(small)
    small[pl.ds(0, 24), :] = gains[...]
    for n in range(8):
        for part in range(2):
            small[pl.ds(24 + 16 * n + s + TP * part, 1), :] = vectors[
                pl.ds(2 * n + part, 1), :
            ]
    copies = split_copies(plan, first_copies(plan, small, gates, g_y, g_x, Nowhere()))[0]
    to_wires(plan, copies, wires, sems, 0, True)
    to_wires(plan, copies, wires, sems, 0, False)


def wire_y(plan, gains, vectors, gates, g_y, g_x):
    return pl.pallas_call(
        partial(wire_y_body, plan),
        out_shape=[shape((plan.lengths[0], LANE), F32)] * plan.n_fsdp,
        in_specs=[VMEM] * 5,
        out_specs=[ANY] * plan.n_fsdp,
        scratch_shapes=[
            pltpu.VMEM((SMALL, LANE), F32),
            pltpu.SemaphoreType.DMA((count_first(plan),)),
        ],
        compiler_params=LIMIT,
        name="wire_y",
    )(gains, vectors, gates, g_y, g_x)


def spread_body(plan, targets, *refs):
    count = len(targets)
    sums, outs, sems = refs[:count], refs[count : count + TP], refs[count + TP]
    s = lax.axis_index("seq")
    for start in (True, False):
        for summed, group in zip(sums, targets):
            for target in group:
                size = plan.lengths[target]
                at = int(plan.offsets[target] - plan.offsets[group[0]])
                for k in range(TP):

                    @pl.when((s ^ target) == k)
                    def _():
                        copy = pltpu.make_async_copy(
                            summed.at[pl.ds(at, size)],
                            outs[k].at[pl.ds(0, size)],
                            sems.at[target],
                        )
                        if start:
                            copy.start()
                        else:
                            copy.wait()


def spread(plan, targets, sums):
    rows = max(plan.lengths[s] for group in targets for s in group)
    return pl.pallas_call(
        partial(spread_body, plan, targets),
        out_shape=[shape((rows, LANE), F32)] * TP,
        in_specs=[VMEM] * len(sums),
        out_specs=[ANY] * TP,
        scratch_shapes=[pltpu.SemaphoreType.DMA((TP,))],
        compiler_params=LIMIT,
    )(*sums)


def shift_up(source, source_row, target, target_row, rows, block, amount):
    def step(j, _):
        both = pltpu.roll(source[pl.ds(source_row + j * block, block + 8), :], amount, 1)
        below = pltpu.roll(both, block + 7, 0)[:block]
        target[pl.ds(target_row + j * block, block), :] = jnp.where(
            lanes(block) < amount, both[:block], below
        )
        return 0

    lax.fori_loop(0, rows // block, step, 0, unroll=True)


def collect_body(plan, tab, *refs):
    pieces, (own, hd, hu, al, win, wire, sems) = refs[: 3 * TP], refs[3 * TP :]
    s, f = lax.axis_index("seq"), lax.axis_index("fsdp")
    me = s * plan.n_fsdp + f

    def bring(start):
        for number, (low, high) in enumerate(((0, 0), (1, 2), (3, TP - 1))):

            @pl.when((s >= low) & (s <= high))
            def _():
                for k in range(TP):
                    piece = pieces[TP * number + k]
                    copy = pltpu.make_async_copy(
                        piece, wire.at[s ^ k, pl.ds(0, piece.shape[0])], sems.at[k]
                    )
                    if start:
                        copy.start()
                    else:
                        copy.wait()

    bring(True)
    total = win.shape[0]

    def clear(j, _):
        al[pl.ds(aligned(j * 96, 8), 96), :] = jnp.zeros((96, LANE), F32)
        return 0

    lax.fori_loop(0, al.shape[0] // 96, clear, 0, unroll=4)
    bring(False)

    def columns(g, _):
        at = tab[me, 1] + g * 256
        to = tab[me, 3] + g * 16
        for block in range(16):
            row = to + 16 * tab[me, 2] * (block // TP)
            al[pl.ds(at + block, 16, stride=16), :] = wire[
                block % TP, pl.ds(aligned(row, 16), 16), :
            ]
        return 0

    lax.fori_loop(0, tab[me, 2], columns, 0)
    for slot in (4, 10):

        def grouped(j, _):
            for owner in range(TP):
                at = tab[me, slot] + j * 1536 + owner * 192
                to = tab[me, slot + 2] + j * 16
                for block in range(12):
                    row = to + 16 * tab[me, slot + 1] * block
                    al[pl.ds(at + block, 16, stride=12), :] = wire[
                        owner, pl.ds(aligned(row, 16), 16), :
                    ]
            return 0

        lax.fori_loop(0, tab[me, slot + 1], grouped, 0)

    def mixed_columns(g, _):
        at = tab[me, 7] + g * 1152
        to = tab[me, 9] + g * 32
        wide = 32 * tab[me, 8]
        last = tab[me, 9] + 4 * wide + g * 16
        for half in range(2):
            for a in range(4):
                parts = swap_lanes(
                    [
                        wire[owner, pl.ds(aligned(to + a * wide + 16 * half, 16), 16), :]
                        for owner in range(TP)
                    ]
                )
                for b in range(TP):
                    al[pl.ds(at + 576 * half + 8 * a + b, 16, stride=36), :] = parts[b]
        parts = swap_lanes(
            [wire[owner, pl.ds(aligned(last, 16), 16), :] for owner in range(TP)]
        )
        for half in range(2):
            for b in range(4):
                al[pl.ds(at + 576 * half + 32 + b, 16, stride=36), :] = parts[4 * half + b]
        return 0

    lax.fori_loop(0, tab[me, 8], mixed_columns, 0)

    @pl.when(me == 0)
    def _():
        summed = wire[0, pl.ds(0, 152), :]
        for owner in range(1, TP):
            summed = summed + wire[owner, pl.ds(0, 152), :]
        al[pl.ds(HALO, 152), :] = summed
        for kind in range(2):
            for n in range(16):
                al[pl.ds(HALO + 152 + 2048 * kind + 128 * n, 128), :] = wire[
                    n % TP, pl.ds(SMALL + 128 * (2 * kind + n // TP), 128), :
                ]

    def back(j, _):
        both = pltpu.roll(
            al[pl.ds(aligned(j * 48, 8), 56), :], lax.rem(LANE - tab[me, 0], LANE), 1
        )
        below = pltpu.roll(both, 55, 0)[:48]
        win[pl.ds(aligned(j * 48, 8), 48), :] = jnp.where(
            lanes(48) < LANE - tab[me, 0], both[:48], below
        )
        return 0

    lax.fori_loop(0, total // 48, back, 0, unroll=7)
    hd[...] = win[pl.ds(0, HALO), :]
    own[...] = win[pl.ds(HALO, plan.own_rows), :]
    shift_up(win, HALO + plan.last, hu, 0, HALO, 32, LANE - plan.part)


def collect(plan, pieces):
    total = -(-(HALO * 2 + plan.own_rows) // 672) * 672
    cleared = total + 96
    return pl.pallas_call(
        partial(collect_body, plan),
        out_shape=[
            shape((plan.own_rows, LANE), F32),
            shape((HALO, LANE), F32),
            shape((HALO, LANE), F32),
        ],
        in_specs=[SMEM] + [ANY] * (3 * TP),
        out_specs=[VMEM] * 3,
        scratch_shapes=[
            pltpu.VMEM((cleared, LANE), F32),
            pltpu.VMEM((total, LANE), F32),
            pltpu.VMEM((TP, plan.longest, LANE), F32),
            pltpu.SemaphoreType.DMA((TP,)),
        ],
        compiler_params=LIMIT,
        name="collect",
    )(jnp.asarray(plan.table), *pieces)


def tail_body(plan, value, out):
    first = (plan.last - HALO) % 8
    out[...] = jnp.zeros_like(out)
    shift_down(value, 0, out, first, HALO, 32, plan.part, True)
    z = pltpu.roll(value[pl.ds(HALO - 8, 8), :], plan.part, 1)
    row = lax.broadcasted_iota(jnp.int32, (8, LANE), 0)
    out[pl.ds(first + HALO, 8), :] = jnp.where(
        (row == 0) & (lanes(8) < plan.part), pltpu.roll(z, 1, 0), 0.0
    )


def place_tail(plan, value):
    rows = plan.own_rows - (plan.last - HALO) // 8 * 8
    return pl.pallas_call(
        partial(tail_body, plan),
        out_shape=shape((max(rows, HALO + 16), LANE), F32),
        in_specs=[VMEM],
        out_specs=VMEM,
        compiler_params=LIMIT,
        name="place_tail",
    )(value)[:rows]


def scan_body(reverse, coefficient, addend, out):
    rows, width = coefficient.shape
    at = lax.broadcasted_iota(jnp.int32, (8, width), 0)
    if reverse:
        at = 7 - at
    steps = rows // 8

    def step(j, carry):
        block = steps - 1 - j if reverse else j
        here = pl.ds(aligned(block * 8, 8), 8)
        a, b = coefficient[here, :], addend[here, :]
        for reach in (1, 2, 4):
            turn = 8 - reach if reverse else reach
            inside = at >= reach
            b = b + jnp.where(inside, a * pltpu.roll(b, turn, 0), 0.0)
            a = jnp.where(inside, a * pltpu.roll(a, turn, 0), a)
        value = b + a * carry
        out[here, :] = value
        edge = value[0:1] if reverse else value[7:8]
        return jnp.broadcast_to(edge, (8, width))

    lax.fori_loop(0, steps, step, jnp.zeros((8, width), F32), unroll=4)


def linear_scan(coefficient, addend, reverse):
    return pl.pallas_call(
        partial(scan_body, reverse),
        out_shape=shape(coefficient.shape, F32),
        in_specs=[VMEM] * 2,
        out_specs=VMEM,
        compiler_params=LIMIT,
        name="scan_back" if reverse else "scan",
    )(coefficient, addend)


def swap(value, bit):
    return lax.ppermute(value, "seq", [(i, i ^ bit) for i in range(TP)])


def exchange(pieces, targets=range(TP)):
    return [pieces[0]] + [
        lax.ppermute(pieces[k], "seq", [(i ^ k, i) for i in targets]) for k in range(1, TP)
    ]


def gather_stream(mine):
    half = mine.shape[0] // 2

    over_x, over_y = swap(mine, 2), swap(mine, 4)
    over_xy = [swap(over_x[:half], 4), swap(over_y[half:], 2)]
    chip = [mine, over_x, over_y] + over_xy
    return jnp.concatenate(chip + [swap(part, 1) for part in chip], axis=0)


def scatter_stream(partial_sums):
    rows = partial_sums.shape[0] // TP
    half = rows // 2

    def send(value, bit):
        return swap(value.astype(BF16), bit).astype(F32)

    other = send(partial_sums[TP // 2 * rows :], 1)
    q = (partial_sums[: TP // 2 * rows] + other).reshape(4, rows, -1)
    up = send(jnp.concatenate([q[1, :half], q[3, :half]]), 2)
    down = send(jnp.concatenate([q[2, half:], q[3, half:]]), 4)
    top, low, up, down = lax.optimization_barrier(
        (
            (q[2, :half] + up[half:]).astype(BF16),
            (q[1, half:] + down[half:]).astype(BF16),
            up[:half],
            down[:half],
        )
    )
    top, low = send(top, 4), send(low, 2)
    return jnp.concatenate(
        [q[0, :half] + up + top, q[0, half:] + down + low], axis=0
    )


def to_positions(values, s):
    rows = values.shape[0] // TP
    parts = []
    for j in range(TP):
        k = s ^ j
        at = (k // 2 + 4 * (k % 2)) * rows
        parts.append(lax.dynamic_slice_in_dim(values, at, rows, 0))
    return jnp.concatenate(parts, axis=0)


def to_relative(values, s):
    rows = values.shape[0] // TP
    return jnp.concatenate(
        [lax.dynamic_slice_in_dim(values, (s ^ k) * rows, rows, 0) for k in EVEN_FIRST], axis=0
    )


def gather_line(value, count):
    def send(value, bit):
        return lax.ppermute(value, "fsdp", [(i, i ^ bit) for i in range(count)])

    opposite, near = send(value, 3), send(value, 1)
    return [value, near, send(opposite, 1), opposite]


def scatter_line(blocks):
    count = len(blocks)
    own, near, far, cross = blocks
    far = lax.ppermute(far, "fsdp", [(i, i ^ 1) for i in range(count)])
    near = lax.ppermute(near, "fsdp", [(i, i ^ 1) for i in range(count)])
    cross = lax.ppermute(cross + far, "fsdp", [(i, i ^ 3) for i in range(count)])
    return own + near + cross


def sliced(plan, *arguments):
    return sliced_step(plan, *arguments)


def sliced_step(plan, stream_in, cotangent, starts, params, momentum, average):
    n_fsdp = plan.n_fsdp
    s = lax.axis_index("seq")
    shards = TP * n_fsdp
    onward = [(i, i + 1) for i in range(shards - 1)]
    backward = [(i + 1, i) for i in range(shards - 1)]
    both = ("seq", "fsdp")
    edge = HALO * LANE
    per = plan.per

    hd, hu = lax.optimization_barrier((params[per - edge :], params[:edge]))
    hd = lax.ppermute(hd.astype(BF16), both, onward)
    hu = lax.ppermute(hu.astype(BF16), both, backward)
    own = jnp.pad(params, (0, plan.own_rows * LANE - per)).reshape(-1, LANE)
    pieces = pack(
        plan, hd.astype(F32).reshape(-1, LANE), own, hu.astype(F32).reshape(-1, LANE)
    )
    first, middle_wire, second, third = order(plan, exchange(pieces))
    stream_bf, cotangent_bf, first = lax.optimization_barrier(
        (stream_in[0], cotangent[0], first)
    )
    line = gather_line(first, n_fsdp)
    middle_wire, second, third, line = lax.optimization_barrier(
        (middle_wire, second, third, line)
    )
    small, gates, w_y, w_x, b_head = unpack_first(plan, line)
    line = gather_line(middle_wire, n_fsdp)
    *out_rows, head = unpack_middle(plan, line, b_head)
    w_out = join_out_rows(exchange(out_rows))
    line = gather_line(second, n_fsdp)
    w_gate, w_up, w_down = unpack_second(plan, line, head)
    w_down = unpack_third(plan, gather_line(third, n_fsdp), w_down)

    mine = stream_in[0].astype(F32)
    stream = gather_stream(stream_bf)
    stream = stream.astype(F32)
    grad_out = gather_stream(cotangent_bf)
    rows = stream.shape[0]

    small = small.astype(F32)
    gain_one = small[0:12].reshape(-1)
    gain_two = small[12:24].reshape(-1)

    def channels(at):
        return jnp.concatenate(
            [
                lax.dynamic_slice_in_dim(small, at + s, 1, 0),
                lax.dynamic_slice_in_dim(small, at + s + TP, 1, 0),
            ],
            axis=1,
        )[0]

    conv_bias, bias_a, bias_i, lambda_raw = (channels(24 + 16 * j) for j in range(4))
    conv_weight = jnp.stack([channels(88 + 16 * j) for j in range(KW)])

    positions = jnp.arange(rows, dtype=jnp.int32)
    ext_pos = jnp.arange(rows + KW - 1, dtype=jnp.int32) - (KW - 1)
    segment_ext = segment_ids(ext_pos, starts[0])
    starting = start_flags(positions, starts[0])[:, None]

    def gate_product(values, at):
        return jnp.concatenate(
            [matmul(values[:, :HB], gates[at : at + HB]), matmul(values[:, HB:], gates[at + HB : at + 2 * HB])],
            axis=1,
        )

    def gate_product_t(values, at):
        return jnp.concatenate(
            [matmul_t(values[:, :HB], gates[at : at + HB]), matmul_t(values[:, HB:], gates[at + HB : at + 2 * HB])],
            axis=1,
        )

    normed = rms_norm(stream, gain_one).astype(BF16)
    branch_y = matmul(normed, w_y)
    branch_x = matmul(normed, w_x).astype(BF16)
    branch_y = to_positions(branch_y, s)
    branch_x = to_positions(branch_x, s)
    extended = jnp.pad(branch_x, ((KW - 1, 0), (0, 0))).astype(F32)

    def convolve_here(extended, weight, bias):
        total = jnp.zeros((rows, bias.shape[0]), F32) + bias
        for lag in range(KW):
            source = extended[KW - 1 - lag : KW - 1 - lag + rows]
            same = segment_ext[KW - 1 - lag : KW - 1 - lag + rows] == segment_ext[KW - 1 :]
            total = total + weight[lag] * source * same.astype(F32)[:, None]
        return total

    conv_out = convolve_here(extended, conv_weight, conv_bias).astype(BF16)
    conv_val = conv_out.astype(F32)
    pre_a = gate_product(conv_out, 0) + bias_a
    pre_i = gate_product(conv_out, 2 * HB) + bias_i
    decay, drive = gate_terms(pre_a, pre_i, conv_val, lambda_raw, starting)
    state = linear_scan(decay, drive, False)
    gelu_y = jax.nn.gelu(branch_y, approximate=True)
    mixed = to_relative((state * gelu_y).astype(BF16), s)
    middle = mine + scatter_stream(matmul(mixed, w_out))
    normed_two_mine = rms_norm(middle, gain_two).astype(BF16)
    normed_two = gather_stream(normed_two_mine)
    gate = matmul(normed_two, w_gate)
    upward = matmul(normed_two, w_up)
    hidden = gelu_product(gate, upward).astype(BF16)
    g_down = t_matmul(hidden, grad_out)
    summed_three = scatter_line(wire_third(plan, g_down))
    out_sums = matmul(hidden, w_down)
    output = (middle + scatter_stream(out_sums)).astype(BF16)
    gate, upward, _ = lax.optimization_barrier((gate, upward, hidden))

    grad_hidden = matmul_t(grad_out, w_down)
    _, product_back = jax.vjp(gelu_product, gate, upward)
    grad_gate, grad_up = product_back(grad_hidden)
    grad_gate, grad_up = grad_gate.astype(BF16), grad_up.astype(BF16)
    g_gate = t_matmul(normed_two, grad_gate)
    g_up = t_matmul(normed_two, grad_up)
    grad_normed_two = scatter_stream(matmul_t(grad_gate, w_gate) + matmul_t(grad_up, w_up))
    wire_two, wire_head = wire_second(plan, g_gate, g_up, g_down)
    summed_two = scatter_line(wire_two)

    _, norm_back_two = jax.vjp(rms_norm, middle, gain_two)
    grad_middle_part, g_gain_two = norm_back_two(grad_normed_two)
    grad_middle = cotangent[0].astype(F32) + grad_middle_part
    grad_first = gather_stream(grad_middle.astype(BF16))
    g_out = t_matmul(mixed, grad_first)
    wire_mid, b_head = wire_middle(plan, wire_head, exchange(split_out_rows(g_out)))
    summed_mid = scatter_line(wire_mid)
    grad_mixed = to_positions(matmul_t(grad_first, w_out), s)
    _, gelu_back = jax.vjp(partial(jax.nn.gelu, approximate=True), branch_y)
    grad_y = gelu_back(grad_mixed * state)[0].astype(BF16)
    next_decay = jnp.concatenate([decay[1:], jnp.ones((1, decay.shape[1]), F32)], axis=0)
    adjoint = linear_scan(next_decay, grad_mixed * gelu_y, True)
    previous = jnp.concatenate([jnp.zeros((1, decay.shape[1]), F32), state[:-1]], axis=0)
    _, gates_back = jax.vjp(gate_terms, pre_a, pre_i, conv_val, lambda_raw, starting)
    grad_pre_a, grad_pre_i, grad_direct, g_lambda, _ = gates_back((adjoint * previous, adjoint))
    grad_pre_a, grad_pre_i = grad_pre_a.astype(BF16), grad_pre_i.astype(BF16)
    g_gates = jnp.concatenate(
        [
            t_matmul(conv_out[:, n : n + HB], grad[:, n : n + HB])
            for grad in (grad_pre_a, grad_pre_i)
            for n in (0, HB)
        ],
        axis=0,
    )
    g_bias_a = jnp.sum(grad_pre_a.astype(F32), axis=0)
    g_bias_i = jnp.sum(grad_pre_i.astype(F32), axis=0)
    grad_conv = grad_direct + gate_product_t(grad_pre_a, 0) + gate_product_t(grad_pre_i, 2 * HB)
    _, conv_back = jax.vjp(convolve_here, extended, conv_weight, conv_bias)
    grad_ext, g_conv_weight, g_conv_bias = conv_back(grad_conv)
    grad_x = to_relative(grad_ext[KW - 1 :].astype(BF16), s)
    grad_y = to_relative(grad_y, s)
    g_x = t_matmul(normed, grad_x)
    g_y = t_matmul(normed, grad_y)
    grad_normed = scatter_stream(matmul_t(grad_y, w_y) + matmul_t(grad_x, w_x))
    _, norm_back_one = jax.vjp(rms_norm, mine, gain_one)
    grad_stream_part, g_gain_one = norm_back_one(grad_normed)
    input_grad = grad_middle + grad_stream_part

    summed_x = scatter_line(wire_x(plan, g_x, b_head))
    gains = jnp.concatenate([g_gain_one, g_gain_two]).reshape(-1, LANE)
    vectors = jnp.stack(
        [g_conv_bias, g_bias_a, g_bias_i, g_lambda] + [g_conv_weight[k] for k in range(KW)]
    ).reshape(-1, LANE)
    summed_y = scatter_line(wire_y(plan, gains, vectors, g_gates, g_y, g_x))
    early = spread(plan, plan.groups[2:], (summed_two, summed_three))
    middle_set = spread(plan, ((1,), (2,)), (summed_x, summed_mid))
    got = exchange(spread(plan, ((0,),), (summed_y,)), (0,))
    got += exchange(middle_set, (1, 2))
    got += exchange(early)
    grad_own, grad_hd, grad_hu = collect(plan, got)
    from_next = lax.ppermute(grad_hd, both, backward)
    from_before = lax.ppermute(grad_hu, both, onward)
    tail = place_tail(plan, from_next).reshape(-1)
    whole = plan.own_rows * LANE
    summed = (
        grad_own.reshape(-1)
        + jnp.pad(from_before.reshape(-1), (0, whole - edge))
        + jnp.pad(tail, (whole - tail.shape[0], 0))
    )[:per]
    new_moment = MOMENT * momentum + summed
    new_params = params - RATE * (summed + MOMENT * new_moment)
    new_average = BLEND * average + (1.0 - BLEND) * new_params
    return (output[None], input_grad[None], new_params, new_moment, new_average)


def solution(mesh):
    n_seq, n_fsdp = mesh.shape["seq"], mesh.shape["fsdp"]
    fast = (n_seq, n_fsdp) == (TP, 4)
    body = partial(sliced, Plan(n_seq, n_fsdp)) if fast else local
    return jax.shard_map(
        body,
        mesh=mesh,
        in_specs=(
            P("fsdp", "seq", None),
            P("fsdp", "seq", None),
            P("fsdp", None),
            P(("seq", "fsdp")),
            P(("seq", "fsdp")),
            P(("seq", "fsdp")),
        ),
        out_specs=(
            P("fsdp", "seq", None),
            P("fsdp", "seq", None),
            P(("seq", "fsdp")),
            P(("seq", "fsdp")),
            P(("seq", "fsdp")),
        ),
        check_vma=False,
    )
```

```python
from functools import partial
import math

import jax
import jax.numpy as jnp
import numpy as np
from jax import lax
from jax.experimental import pallas as pl
from jax.experimental.pallas import tpu as pltpu
from jax.sharding import PartitionSpec as P


D = 1536
LRU = 2048
FF = 4608
HB = 128
KW = 4


EPS = 1e-06
RATE = 3e-05
MOMENT = 0.9
BLEND = 0.9
DECAY_SCALE = 8.0


def shifted(block, axis, distance):
    devices = range(lax.axis_size(axis))
    route = [(i - distance, i) for i in devices if i - distance in devices]
    return lax.ppermute(block, axis, route)


def carried_in(value, axis, join, neutral, backward):
    count, mine = (lax.axis_size(axis), lax.axis_index(axis))
    pieces = jax.tree.map(lambda part: lax.all_gather(part, axis), value)
    if backward:
        pieces = jax.tree.map(lambda part: part[::-1], pieces)
        mine = count - 1 - mine
    so_far = jax.tree.map(
        lambda part, zero: jnp.full_like(part, 0) + jnp.asarray(zero, part.dtype), value, neutral
    )

    def lap(position, so_far):
        longer = join(so_far, jax.tree.map(lambda part: part[position], pieces))
        return jax.tree.map(lambda new, old: jnp.where(position < mine, new, old), longer, so_far)

    return lax.fori_loop(0, count - 1, lap, so_far)


def layout():
    return [
        ("gain_one", (D,)),
        ("gain_two", (D,)),
        ("conv_bias", (LRU,)),
        ("bias_a", (LRU,)),
        ("bias_i", (LRU,)),
        ("lambda_raw", (LRU,)),
        ("conv_weight", (KW, LRU)),
        ("gate_a", (LRU // HB, HB, HB)),
        ("gate_i", (LRU // HB, HB, HB)),
        ("w_y", (D, LRU)),
        ("w_x", (D, LRU)),
        ("w_out", (LRU, D)),
        ("w_gate", (D, FF)),
        ("w_up", (D, FF)),
        ("w_down", (FF, D)),
    ]


def unpack(packed):
    result = {}
    offset = 0
    for entry_name, entry_shape in layout():
        amount = math.prod(entry_shape)
        result[entry_name] = packed[offset : offset + amount].reshape(entry_shape)
        offset += amount
    return result


def matmul(left, right):
    return jnp.dot(left, right, preferred_element_type=jnp.float32)


def matmul_t(left, right):
    return lax.dot_general(
        left, right, (((1,), (1,)), ((), ())), preferred_element_type=jnp.float32
    )


def t_matmul(left, right):
    return lax.dot_general(
        left, right, (((0,), (0,)), ((), ())), preferred_element_type=jnp.float32
    )


def blocked(values, weight):
    shaped = values.reshape(values.shape[0], LRU // HB, HB)
    return jnp.einsum("tnh,nhk->tnk", shaped, weight, preferred_element_type=jnp.float32).reshape(
        values.shape[0], LRU
    )


def blocked_t(values, weight):
    shaped = values.reshape(values.shape[0], LRU // HB, HB)
    return jnp.einsum("tnk,nhk->tnh", shaped, weight, preferred_element_type=jnp.float32).reshape(
        values.shape[0], LRU
    )


def blocked_grad(inputs, grads):
    left = inputs.reshape(inputs.shape[0], LRU // HB, HB)
    right = grads.reshape(grads.shape[0], LRU // HB, HB)
    return jnp.einsum("tnh,tnk->nhk", left, right, preferred_element_type=jnp.float32)


def rms_norm(values, gain):
    return values * lax.rsqrt(jnp.mean(values * values, axis=-1, keepdims=True) + EPS) * gain


def combine(earlier, later):
    return (earlier[0] * later[0], later[0] * earlier[1] + later[1])


def gate_terms(pre_a, pre_i, conv_val, lambda_raw, starting):
    recall = jax.nn.sigmoid(pre_a)
    admit = jax.nn.sigmoid(pre_i)
    rate = DECAY_SCALE * jax.nn.softplus(lambda_raw) * recall
    decay = (1.0 - starting) * jnp.exp(-rate)
    scale_in = starting + (1.0 - starting) * jnp.sqrt(-jnp.expm1(-2.0 * rate))
    return (decay, scale_in * admit * conv_val)


def convolve(extended, weight, bias, segment_ext, rows):
    total = jnp.zeros((rows, LRU), jnp.float32) + bias
    for lag in range(KW):
        source = extended[KW - 1 - lag : KW - 1 - lag + rows]
        same = (segment_ext[KW - 1 - lag : KW - 1 - lag + rows] == segment_ext[KW - 1 :]).astype(
            jnp.float32
        )
        total = total + weight[lag] * source * same[:, None]
    return total


def segment_ids(positions, doc_starts):
    return jnp.sum((doc_starts[None, :] <= positions[:, None]).astype(jnp.int32), axis=1)


def start_flags(positions, doc_starts):
    return jnp.max((doc_starts[None, :] == positions[:, None]).astype(jnp.float32), axis=1)


def gelu_product(left, right):
    return jax.nn.gelu(left, approximate=True) * right


def local(stream_in, cotangent, starts, params, momentum, average):
    weights = unpack(
        lax.all_gather(params.astype(jnp.bfloat16), ("seq", "fsdp"), axis=0, tiled=True)
    )
    stream = stream_in[0].astype(jnp.float32)
    incoming = cotangent[0].astype(jnp.float32)
    doc_starts = starts[0]
    rows = stream.shape[0]
    positions = lax.axis_index("seq") * rows + jnp.arange(rows, dtype=jnp.int32)
    ext_pos = positions[0] - (KW - 1) + jnp.arange(rows + KW - 1, dtype=jnp.int32)
    segment_ext = segment_ids(ext_pos, doc_starts)
    starting = start_flags(positions, doc_starts)[:, None]
    gain_one = weights["gain_one"].astype(jnp.float32)
    gain_two = weights["gain_two"].astype(jnp.float32)
    conv_weight = weights["conv_weight"].astype(jnp.float32)
    conv_bias = weights["conv_bias"].astype(jnp.float32)
    lambda_raw = weights["lambda_raw"].astype(jnp.float32)
    normed = rms_norm(stream, gain_one).astype(jnp.bfloat16)
    branch_y = matmul(normed, weights["w_y"])
    branch_x = matmul(normed, weights["w_x"]).astype(jnp.bfloat16)
    edge = shifted(branch_x[rows - (KW - 1) :], "seq", 1)
    extended = jnp.concatenate([edge, branch_x], axis=0).astype(jnp.float32)
    conv_out = convolve(extended, conv_weight, conv_bias, segment_ext, rows).astype(jnp.bfloat16)
    conv_val = conv_out.astype(jnp.float32)
    pre_a = blocked(conv_out, weights["gate_a"]) + weights["bias_a"].astype(jnp.float32)
    pre_i = blocked(conv_out, weights["gate_i"]) + weights["bias_i"].astype(jnp.float32)
    decay, drive = gate_terms(pre_a, pre_i, conv_val, lambda_raw, starting)
    prod_local, state_local = lax.associative_scan(combine, (decay, drive), axis=0)
    neutral = (jnp.ones((LRU,), jnp.float32), jnp.zeros((LRU,), jnp.float32))
    carried = carried_in((prod_local[-1], state_local[-1]), "seq", combine, neutral, False)
    carry_in = carried[1]
    state = lax.associative_scan(combine, (decay, drive.at[0].add(decay[0] * carry_in)), axis=0)[1]
    gelu_y = jax.nn.gelu(branch_y, approximate=True)
    mixed = (state * gelu_y).astype(jnp.bfloat16)
    middle = stream + matmul(mixed, weights["w_out"])
    normed_two = rms_norm(middle, gain_two).astype(jnp.bfloat16)
    gate = matmul(normed_two, weights["w_gate"])
    upward = matmul(normed_two, weights["w_up"])
    hidden = gelu_product(gate, upward).astype(jnp.bfloat16)
    output = (middle + matmul(hidden, weights["w_down"])).astype(jnp.bfloat16)
    grads = {}
    grad_out = incoming.astype(jnp.bfloat16)
    grads["w_down"] = t_matmul(hidden, grad_out)
    grad_hidden = matmul_t(grad_out, weights["w_down"])
    _, product_back = jax.vjp(gelu_product, gate, upward)
    grad_gate, grad_up = product_back(grad_hidden)
    grad_gate = grad_gate.astype(jnp.bfloat16)
    grad_up = grad_up.astype(jnp.bfloat16)
    grads["w_gate"] = t_matmul(normed_two, grad_gate)
    grads["w_up"] = t_matmul(normed_two, grad_up)
    grad_normed_two = matmul_t(grad_gate, weights["w_gate"]) + matmul_t(grad_up, weights["w_up"])
    _, norm_back_two = jax.vjp(rms_norm, middle, gain_two)
    grad_middle_part, grads["gain_two"] = norm_back_two(grad_normed_two)
    grad_middle = incoming + grad_middle_part
    grad_first = grad_middle.astype(jnp.bfloat16)
    grads["w_out"] = t_matmul(mixed, grad_first)
    grad_mixed = matmul_t(grad_first, weights["w_out"])
    _, gelu_back = jax.vjp(partial(jax.nn.gelu, approximate=True), branch_y)
    grad_y = gelu_back(grad_mixed * state)[0].astype(jnp.bfloat16)
    grad_state = grad_mixed * gelu_y
    next_decay = jnp.concatenate([decay[1:], jnp.ones((1, LRU), jnp.float32)], axis=0)
    suffix, adjoint_local = lax.associative_scan(
        combine, (next_decay, grad_state), axis=0, reverse=True
    )
    returned = carried_in(
        (prod_local[-1], decay[0] * adjoint_local[0]), "seq", combine, neutral, True
    )
    adjoint = adjoint_local + suffix * returned[1]
    previous = jnp.concatenate([carry_in[None, :], state[:-1]], axis=0)
    _, gates_back = jax.vjp(gate_terms, pre_a, pre_i, conv_val, lambda_raw, starting)
    grad_pre_a, grad_pre_i, grad_direct, grads["lambda_raw"], _ = gates_back(
        (adjoint * previous, adjoint)
    )
    grad_pre_a = grad_pre_a.astype(jnp.bfloat16)
    grad_pre_i = grad_pre_i.astype(jnp.bfloat16)
    grads["gate_a"] = blocked_grad(conv_out, grad_pre_a)
    grads["gate_i"] = blocked_grad(conv_out, grad_pre_i)
    grads["bias_a"] = jnp.sum(grad_pre_a.astype(jnp.float32), axis=0)
    grads["bias_i"] = jnp.sum(grad_pre_i.astype(jnp.float32), axis=0)
    grad_conv = (
        grad_direct
        + blocked_t(grad_pre_a, weights["gate_a"])
        + blocked_t(grad_pre_i, weights["gate_i"])
    )
    _, conv_back = jax.vjp(
        partial(convolve, segment_ext=segment_ext, rows=rows), extended, conv_weight, conv_bias
    )
    grad_ext, grads["conv_weight"], grads["conv_bias"] = conv_back(grad_conv)
    edge_back = shifted(grad_ext[: KW - 1], "seq", -1)
    grad_x = grad_ext[KW - 1 :] + jnp.concatenate(
        [jnp.zeros((rows - (KW - 1), LRU), jnp.float32), edge_back], axis=0
    )
    grad_x = grad_x.astype(jnp.bfloat16)
    grads["w_x"] = t_matmul(normed, grad_x)
    grads["w_y"] = t_matmul(normed, grad_y)
    grad_normed = matmul_t(grad_y, weights["w_y"]) + matmul_t(grad_x, weights["w_x"])
    _, norm_back_one = jax.vjp(rms_norm, stream, gain_one)
    grad_stream_part, grads["gain_one"] = norm_back_one(grad_normed)
    input_grad = grad_middle + grad_stream_part
    packed_grad = jnp.concatenate([grads[entry[0]].reshape(-1) for entry in layout()])
    summed = lax.psum_scatter(packed_grad, ("seq", "fsdp"), scatter_dimension=0, tiled=True)
    new_moment = MOMENT * momentum + summed
    new_params = params - RATE * (summed + MOMENT * new_moment)
    new_average = BLEND * average + (1.0 - BLEND) * new_params
    return (output[None], input_grad[None], new_params, new_moment, new_average)


LANE = 128
TP = 8
HALO = 544
SMALL = 160
GATES = 512
REGIONS = {
    "A": (4248, 256, 192, 32),
    "B": (53400, 1536, 16, 192),
    "C": (77976, 1152, 96, 144),
    "D": (188568, 1536, 36, 192),
}
ROWS = 243864
EVEN_FIRST = (0, 2, 4, 6, 1, 3, 5, 7)
F32 = jnp.float32
BF16 = jnp.bfloat16


class Plan:
    def __init__(self, n_seq, n_fsdp):
        self.n_fsdp = n_fsdp
        shards = n_seq * n_fsdp
        per = ROWS * LANE // shards
        self.per = per
        self.part = per % LANE
        self.own_rows = -(-per // 1024) * 8
        self.last = per // LANE
        bounds = [0]
        for i in range(1, shards):
            at = per * i / LANE
            for first, unit, count, _ in REGIONS.values():
                if first <= at < first + unit * count:
                    bounds.append(first + unit * round((at - first) / unit))
        bounds.append(ROWS)
        self.segments = []
        self.sizes = []
        self.table = np.zeros((shards, 16), np.int32)
        for i in range(shards):
            base = per * i // LANE
            self.table[i, 0] = per * i % LANE
            offset = SMALL + GATES if i == 0 else 0
            found = {}
            for slot, (name, (first, unit, count, wide)) in enumerate(REGIONS.items()):
                low = max(bounds[i], first)
                high = min(bounds[i + 1], first + unit * count)
                if high > low:
                    units = (high - low) // unit
                    found[name] = ((low - first) // unit, units, offset)
                    self.table[i, 1 + 3 * slot : 4 + 3 * slot] = (
                        low - base + HALO,
                        units,
                        offset,
                    )
                    offset += units * wide
            self.segments.append(found)
            self.sizes.append(offset)
            self.table[i, 13] = int(i == 0)
        self.lengths = [
            max(self.sizes[s * n_fsdp : (s + 1) * n_fsdp]) for s in range(n_seq)
        ]
        self.offsets = np.concatenate([[0], np.cumsum(self.lengths)]).astype(np.int32)
        self.longest = max(self.lengths)
        self.groups = ((0, 1), (2,), (3, 4, 5, 6), (7,))
        self.starts = [int(self.offsets[group[0]]) for group in self.groups]
        self.rows = [sum(self.lengths[s] for s in group) for group in self.groups]

    def pieces(self, name, groups):
        out = []
        for i, found in enumerate(self.segments):
            s, f = divmod(i, self.n_fsdp)
            if name in found and s in groups:
                first, units, offset = found[name]
                row = int(self.offsets[s] - self.offsets[groups[0]]) + offset
                out.append((f, row, first, units))
        return out


VMEM = pl.BlockSpec(memory_space=pltpu.VMEM)
ANY = pl.BlockSpec(memory_space=pl.ANY)
SMEM = pl.BlockSpec(memory_space=pltpu.SMEM)
LIMIT = pltpu.CompilerParams(vmem_limit_bytes=60 * 1024 * 1024)


def shape(dims, dtype):
    return jax.ShapeDtypeStruct(dims, dtype)


def aligned(value, multiple):
    return pl.multiple_of(value, multiple)


def lanes(rows):
    return lax.broadcasted_iota(jnp.int32, (rows, LANE), 1)


def swap_lanes(blocks):
    blocks = list(blocks)
    at = lanes(blocks[0].shape[0]) // 16
    for step in (4, 2, 1):
        low_side = (at & step) == 0
        for one in range(TP):
            if one & step == 0:
                left, right = blocks[one], blocks[one + step]
                blocks[one] = jnp.where(low_side, left, pltpu.roll(right, 16 * step, 1))
                blocks[one + step] = jnp.where(
                    low_side, pltpu.roll(left, LANE - 16 * step, 1), right
                )
    return blocks


def shift_down(source, source_row, target, target_row, rows, block, amount, unroll):
    def step(j, tail):
        z = pltpu.roll(source[pl.ds(source_row + j * block, block), :], amount, 1)
        above = pltpu.roll(jnp.concatenate([tail, z], axis=0), 1, 0)[8:]
        target[pl.ds(target_row + j * block, block), :] = jnp.where(
            lanes(block) < amount, above, z
        )
        return z[block - 8 :]

    lax.fori_loop(0, rows // block, step, jnp.zeros((8, LANE), F32), unroll=unroll)


def pack_body(plan, tab, hd, own, hu, *rest):
    outs, (win, al, wire, sems) = rest[:TP], rest[TP:]
    s, f = lax.axis_index("seq"), lax.axis_index("fsdp")
    me = s * plan.n_fsdp + f
    total = win.shape[0]
    first = pltpu.make_async_copy(hd, win.at[pl.ds(0, HALO)], sems.at[0])
    second = pltpu.make_async_copy(own, win.at[pl.ds(HALO, plan.own_rows)], sems.at[1])
    first.start()
    second.start()
    first.wait()
    second.wait()
    seam = HALO + plan.last
    kept = win[pl.ds(seam, 8), :]
    shift_down(hu, 0, win, seam, HALO, 32, plan.part, True)
    edge = lax.broadcasted_iota(jnp.int32, (8, LANE), 0) == 0
    win[pl.ds(seam, 8), :] = jnp.where(
        edge & (lanes(8) < plan.part), kept, win[pl.ds(seam, 8), :]
    )
    shift_down(win, 0, al, 0, total, 48, tab[me, 0], 7)

    def columns(g, _):
        at = tab[me, 1] + g * 256
        to = tab[me, 3] + g * 16
        for block in range(16):
            row = to + 16 * tab[me, 2] * (block // TP)
            wire[block % TP, pl.ds(aligned(row, 16), 16), :] = al[
                pl.ds(at + block, 16, stride=16), :
            ].astype(BF16)
        return 0

    lax.fori_loop(0, tab[me, 2], columns, 0)
    for slot in (4, 10):

        def grouped(j, _):
            for owner in range(TP):
                at = tab[me, slot] + j * 1536 + owner * 192
                to = tab[me, slot + 2] + j * 16
                for block in range(12):
                    row = to + 16 * tab[me, slot + 1] * block
                    wire[owner, pl.ds(aligned(row, 16), 16), :] = al[
                        pl.ds(at + block, 16, stride=12), :
                    ].astype(BF16)
            return 0

        lax.fori_loop(0, tab[me, slot + 1], grouped, 0)

    def mixed_columns(g, _):
        at = tab[me, 7] + g * 1152
        to = tab[me, 9] + g * 32
        wide = 32 * tab[me, 8]
        last = tab[me, 9] + 4 * wide + g * 16
        for half in range(2):
            for a in range(4):
                parts = swap_lanes(
                    [
                        al[pl.ds(at + 576 * half + 8 * a + b, 16, stride=36), :]
                        for b in range(TP)
                    ]
                )
                for owner in range(TP):
                    row = to + a * wide + 16 * half
                    wire[owner, pl.ds(aligned(row, 16), 16), :] = parts[owner].astype(BF16)
        parts = swap_lanes(
            [
                al[pl.ds(at + 576 * half + 32 + b, 16, stride=36), :]
                for half in range(2)
                for b in range(4)
            ]
        )
        for owner in range(TP):
            wire[owner, pl.ds(aligned(last, 16), 16), :] = parts[owner].astype(BF16)
        return 0

    lax.fori_loop(0, tab[me, 8], mixed_columns, 0)

    @pl.when(me == 0)
    def _():
        for owner in range(TP):
            wire[owner, pl.ds(0, SMALL), :] = al[pl.ds(HALO, SMALL), :].astype(BF16)
        for kind in range(2):
            for n in range(16):
                wire[n % TP, pl.ds(SMALL + 128 * (2 * kind + n // TP), 128), :] = al[
                    pl.ds(HALO + 152 + 2048 * kind + 128 * n, 128), :
                ].astype(BF16)

    copies = [
        pltpu.make_async_copy(wire.at[s ^ k], outs[k], sems.at[2 + k]) for k in range(TP)
    ]
    for copy in copies:
        copy.start()
    for copy in copies:
        copy.wait()


def pack(plan, hd, own, hu):
    total = -(-(HALO * 2 + plan.own_rows) // 672) * 672
    return pl.pallas_call(
        partial(pack_body, plan),
        out_shape=[shape((plan.longest, LANE), BF16)] * TP,
        in_specs=[SMEM, ANY, ANY, VMEM],
        out_specs=[ANY] * TP,
        scratch_shapes=[
            pltpu.VMEM((total, LANE), F32),
            pltpu.VMEM((total, LANE), F32),
            pltpu.VMEM((TP, plan.longest, LANE), BF16),
            pltpu.SemaphoreType.DMA((2 + TP,)),
        ],
        compiler_params=LIMIT,
        name="pack",
    )(jnp.asarray(plan.table), hd, own, hu)


def order_body(plan, *refs):
    pieces, outs, sems = refs[:TP], refs[TP : TP + 4], refs[TP + 4]
    s = lax.axis_index("seq")
    for start in (True, False):
        for number, group in enumerate(plan.groups):
            for source in group:
                size = plan.lengths[source]
                at = int(plan.offsets[source]) - plan.starts[number]
                for k in range(TP):

                    @pl.when((s ^ source) == k)
                    def _():
                        copy = pltpu.make_async_copy(
                            pieces[k].at[pl.ds(0, size)],
                            outs[number].at[pl.ds(at, size)],
                            sems.at[source],
                        )
                        if start:
                            copy.start()
                        else:
                            copy.wait()


def order(plan, pieces):
    return pl.pallas_call(
        partial(order_body, plan),
        out_shape=[shape((rows, LANE), BF16) for rows in plan.rows],
        in_specs=[ANY] * TP,
        out_specs=[VMEM] * 4,
        scratch_shapes=[pltpu.SemaphoreType.DMA((TP,))],
        compiler_params=LIMIT,
        name="order",
    )(*pieces)


def weight_copies(plan, number, weights, halves, b_rows):
    out = []
    for f, row, first, units in plan.pieces("A", plan.groups[number]):
        for target, begin, end in weights.get("A", ()):
            low, high = max(first, begin), min(first + units, end)
            if high > low:
                for n in range(2):
                    out.append(
                        (
                            f,
                            row + 16 * (units * n + low - first),
                            16 * (high - low),
                            target.at[pl.ds(16 * (low - begin), 16 * (high - low)), pl.ds(128 * n, 128)],
                        )
                    )
    for f, row, first, units in plan.pieces("B", plan.groups[number]):
        if b_rows is not None:
            for block in range(12):
                out.append(
                    (
                        f,
                        row + 16 * units * block,
                        16 * units,
                        b_rows.at[block, pl.ds(16 * first, 16 * units)],
                    )
                )
    for f, row, first, units in plan.pieces("C", plan.groups[number]):
        for target, begin, end in weights.get("C", ()):
            low, high = max(first, begin), min(first + units, end)
            if high > low:
                for a in range(4):
                    out.append(
                        (
                            f,
                            row + 32 * (units * a + low - first),
                            32 * (high - low),
                            target.at[pl.ds(32 * (low - begin), 32 * (high - low)), pl.ds(128 * a, 128)],
                        )
                    )
        if halves is not None:
            out.append(
                (f, row + 128 * units, 16 * units, halves.at[pl.ds(16 * first, 16 * units)])
            )
    for f, row, first, units in plan.pieces("D", plan.groups[number]):
        for target, begin, end in weights.get("D", ()):
            for n in range(12):
                out.append(
                    (
                        f,
                        row + 16 * units * n,
                        16 * units,
                        target.at[pl.ds(16 * (first - begin), 16 * units), pl.ds(128 * n, 128)],
                    )
                )
    return out


def fetch_line(plan, line, copies, sems, first=0, phases=(True, False)):
    f = lax.axis_index("fsdp")
    for start in phases:
        for source in range(plan.n_fsdp):
            for away in range(plan.n_fsdp):

                @pl.when((f ^ source) == away)
                def _():
                    for number, (holder, row, rows, target) in enumerate(copies):
                        if holder == source:
                            copy = pltpu.make_async_copy(
                                line[away].at[pl.ds(row, rows)], target, sems.at[first + number]
                            )
                            if start:
                                copy.start()
                            else:
                                copy.wait()


def first_copies(plan, small, gates, w_y, w_x, b_head):
    out = [(0, 0, SMALL, small), (0, SMALL, GATES, gates)]
    out += weight_copies(plan, 0, {"A": ((w_y, 0, 96), (w_x, 96, 192))}, None, None)
    for f, row, first, units in plan.pieces("B", plan.groups[0]):
        out.append((f, row, 192 * units, b_head.at[pl.ds(192 * first, 192 * units)]))
    return out


def first_body(plan, *refs):
    line, refs = refs[: plan.n_fsdp], refs[plan.n_fsdp :]
    *targets, sems = refs
    fetch_line(plan, line, first_copies(plan, *targets), sems)


def head_rows(plan):
    return sum(144 * p[3] for p in plan.pieces("C", plan.groups[1]))


def b_head_rows(plan):
    return sum(192 * p[3] for p in plan.pieces("B", plan.groups[0]))


class Nowhere:
    at = property(lambda self: self)

    def __getitem__(self, _):
        return self


def count_first(plan):
    return len(first_copies(plan, *[Nowhere()] * 5))


def unpack_first(plan, line):
    return pl.pallas_call(
        partial(first_body, plan),
        out_shape=[
            shape((SMALL, LANE), BF16),
            shape((GATES, LANE), BF16),
            shape((D, 256), BF16),
            shape((D, 256), BF16),
            shape((b_head_rows(plan), LANE), BF16),
        ],
        in_specs=[ANY] * len(line),
        out_specs=[VMEM] * 5,
        scratch_shapes=[pltpu.SemaphoreType.DMA((count_first(plan),))],
        compiler_params=LIMIT,
        name="unpack_first",
    )(*line)


def middle_copies(plan, b_rows, head):
    out = weight_copies(plan, 1, {}, None, b_rows)
    for f, row, first, units in plan.pieces("C", plan.groups[1]):
        out.append((f, row, 144 * units, head.at[pl.ds(144 * first, 144 * units)]))
    return out


def b_head_copies(plan, b_head, b_rows):
    out = []
    for _, _, first, units in plan.pieces("B", plan.groups[0]):
        for block in range(12):
            out.append(
                (
                    b_head.at[pl.ds(192 * first + 16 * units * block, 16 * units)],
                    b_rows.at[block, pl.ds(16 * first, 16 * units)],
                )
            )
    return out


def middle_body(plan, *refs):
    line, refs = refs[: plan.n_fsdp], refs[plan.n_fsdp :]
    b_head, outs, head, b_rows, sems, more = refs[0], refs[1 : 1 + TP], *refs[1 + TP :]
    local_copies = [
        pltpu.make_async_copy(source, target, more.at[number])
        for number, (source, target) in enumerate(b_head_copies(plan, b_head, b_rows))
    ]
    for copy in local_copies:
        copy.start()
    fetch_line(plan, line, middle_copies(plan, b_rows, head), sems)
    for copy in local_copies:
        copy.wait()
    s = lax.axis_index("seq")
    for k in range(TP):
        for n in range(2):
            unit = (s ^ k) + TP * n
            for block in range(12):
                outs[k][pl.ds(192 * n + 16 * block, 16), :] = b_rows[
                    block, pl.ds(aligned(16 * unit, 16), 16), :
                ]


def unpack_middle(plan, line, b_head):
    return pl.pallas_call(
        partial(middle_body, plan),
        out_shape=[shape((384, LANE), BF16)] * TP + [shape((head_rows(plan), LANE), BF16)],
        in_specs=[ANY] * (len(line) + 1),
        out_specs=[VMEM] * (TP + 1),
        scratch_shapes=[
            pltpu.VMEM((12, 256, LANE), BF16),
            pltpu.SemaphoreType.DMA((len(middle_copies(plan, *[Nowhere()] * 2)),)),
            pltpu.SemaphoreType.DMA((len(b_head_copies(plan, *[Nowhere()] * 2)),)),
        ],
        compiler_params=LIMIT,
        name="unpack_middle",
    )(*line, b_head)


def head_copies(plan, head, weight, halves):
    out = []
    for _, _, first, units in plan.pieces("C", plan.groups[1]):
        for a in range(4):
            out.append(
                (
                    head.at[pl.ds(144 * first + 32 * units * a, 32 * units)],
                    weight.at[pl.ds(32 * first, 32 * units), pl.ds(128 * a, 128)],
                )
            )
        out.append(
            (
                head.at[pl.ds(144 * first + 128 * units, 16 * units)],
                halves.at[pl.ds(16 * first, 16 * units)],
            )
        )
    return out


def second_copies(plan, w_gate, w_up, w_down, halves):
    return weight_copies(
        plan,
        2,
        {"C": ((w_gate, 0, 48), (w_up, 48, 96)), "D": ((w_down, 0, 16),)},
        halves,
        None,
    )


def halves_copies(plan, halves):
    return [
        (f, row + 128 * units, 16 * units, halves.at[pl.ds(16 * first, 16 * units)])
        for f, row, first, units in plan.pieces("C", plan.groups[2])
    ]


def second_body(plan, *refs):
    line, refs = refs[: plan.n_fsdp], refs[plan.n_fsdp :]
    head, w_gate, w_up, w_down, halves, sems, more = refs
    local_copies = [
        pltpu.make_async_copy(source, target, more.at[number])
        for number, (source, target) in enumerate(head_copies(plan, head, w_gate, halves))
    ]
    for copy in local_copies:
        copy.start()
    merged = halves_copies(plan, halves)
    whole = second_copies(plan, w_gate, w_up, w_down, None)
    fetch_line(plan, line, merged, sems, 0, (True,))
    fetch_line(plan, line, whole, sems, len(merged), (True,))
    fetch_line(plan, line, merged, sems, 0, (False,))
    for copy in local_copies:
        copy.wait()
    for weight, begin in ((w_gate, 0), (w_up, 48)):

        def step(g, _):
            last = halves[pl.ds(aligned(16 * (begin + g), 16), 16), :]
            weight[pl.ds(aligned(32 * g, 16), 16), pl.ds(512, 64)] = last[:, :64]
            weight[pl.ds(aligned(32 * g + 16, 16), 16), pl.ds(512, 64)] = last[:, 64:]
            return 0

        lax.fori_loop(0, 48, step, 0, unroll=8)
    fetch_line(plan, line, whole, sems, len(merged), (False,))


def unpack_second(plan, line, head):
    many = len(second_copies(plan, *[Nowhere()] * 4))
    few = len(head_copies(plan, *[Nowhere()] * 3))
    return pl.pallas_call(
        partial(second_body, plan),
        out_shape=[
            shape((D, FF // TP), BF16),
            shape((D, FF // TP), BF16),
            shape((256, D), BF16),
        ],
        in_specs=[ANY] * (len(line) + 1),
        out_specs=[VMEM] * 3,
        scratch_shapes=[
            pltpu.VMEM((96 * 16, LANE), BF16),
            pltpu.SemaphoreType.DMA((many,)),
            pltpu.SemaphoreType.DMA((few,)),
        ],
        compiler_params=LIMIT,
        name="unpack_second",
    )(*line, head)


def third_copies(plan, w_down):
    return weight_copies(plan, 3, {"D": ((w_down, 0, 36),)}, None, None)


def third_body(plan, *refs):
    line, refs = refs[: plan.n_fsdp], refs[plan.n_fsdp :]
    before, w_down, sems, one = refs
    copy = pltpu.make_async_copy(before, w_down.at[pl.ds(0, 256)], one.at[0])
    copy.start()
    fetch_line(plan, line, third_copies(plan, w_down), sems)
    copy.wait()


def unpack_third(plan, line, before):
    many = len(third_copies(plan, Nowhere()))
    return pl.pallas_call(
        partial(third_body, plan),
        out_shape=shape((FF // TP, D), BF16),
        in_specs=[ANY] * (len(line) + 1),
        out_specs=VMEM,
        scratch_shapes=[
            pltpu.SemaphoreType.DMA((many,)),
            pltpu.SemaphoreType.DMA((1,)),
        ],
        compiler_params=LIMIT,
        name="unpack_third",
    )(*line, before)


def out_rows_body(*refs):
    pieces, w_out = refs[:TP], refs[TP]
    s = lax.axis_index("seq")
    for k in range(TP):
        for n in range(2):
            to = aligned(128 * n + 16 * (s ^ k), 16)
            for block in range(12):
                w_out[pl.ds(to, 16), pl.ds(128 * block, 128)] = pieces[k][
                    pl.ds(192 * n + 16 * block, 16), :
                ]


def join_out_rows(pieces):
    return pl.pallas_call(
        out_rows_body,
        out_shape=shape((256, D), BF16),
        in_specs=[VMEM] * TP,
        out_specs=VMEM,
        compiler_params=LIMIT,
        name="join_out_rows",
    )(*pieces)


def split_rows_body(grad, *pieces):
    s = lax.axis_index("seq")
    for k in range(TP):
        for n in range(2):
            at = aligned(128 * n + 16 * (s ^ k), 16)
            for block in range(12):
                pieces[k][pl.ds(192 * n + 16 * block, 16), :] = grad[
                    pl.ds(at, 16), pl.ds(128 * block, 128)
                ]


def split_out_rows(grad):
    return pl.pallas_call(
        split_rows_body,
        out_shape=[shape((384, LANE), F32)] * TP,
        in_specs=[VMEM],
        out_specs=[VMEM] * TP,
        compiler_params=LIMIT,
        name="split_out_rows",
    )(grad)


def start_copies(copies, sems, first=0):
    made = [
        pltpu.make_async_copy(source, target, sems.at[first + number])
        for number, (source, target) in enumerate(copies)
    ]
    for copy in made:
        copy.start()
    return made


def to_wires(plan, copies, wires, sems, first, start):
    f = lax.axis_index("fsdp")
    for j in range(plan.n_fsdp):
        for x in range(plan.n_fsdp):

            @pl.when((f ^ j) == x)
            def _():
                for number, (holder, row, rows, source) in enumerate(copies):
                    if holder == j:
                        copy = pltpu.make_async_copy(
                            source, wires[x].at[pl.ds(row, rows)], sems.at[first + number]
                        )
                        if start:
                            copy.start()
                        else:
                            copy.wait()


def wire_second_body(plan, g_gate, g_up, g_down, *refs):
    wires, (head, halves, sems) = refs[: plan.n_fsdp], refs[plan.n_fsdp :]
    whole = second_copies(plan, g_gate, g_up, g_down, None)
    merged = halves_copies(plan, halves)
    more = [(b, a) for a, b in head_copies(plan, head, g_gate, halves)]
    to_wires(plan, whole, wires, sems, 0, True)
    for grad, begin in ((g_gate, 0), (g_up, 48)):

        def step(g, _):
            left = grad[pl.ds(aligned(32 * g, 16), 16), pl.ds(512, 64)]
            right = grad[pl.ds(aligned(32 * g + 16, 16), 16), pl.ds(512, 64)]
            halves[pl.ds(aligned(16 * (begin + g), 16), 16), :] = jnp.concatenate(
                [left, right], axis=1
            )
            return 0

        lax.fori_loop(0, 48, step, 0, unroll=8)
    to_wires(plan, merged, wires, sems, len(whole), True)
    made = start_copies(more, sems, len(whole) + len(merged))
    to_wires(plan, whole, wires, sems, 0, False)
    to_wires(plan, merged, wires, sems, len(whole), False)
    for copy in made:
        copy.wait()


def wire_second(plan, g_gate, g_up, g_down):
    many = len(second_copies(plan, *[Nowhere()] * 4)) + len(
        head_copies(plan, *[Nowhere()] * 3)
    )
    out = pl.pallas_call(
        partial(wire_second_body, plan),
        out_shape=[shape((plan.rows[2], LANE), F32)] * plan.n_fsdp
        + [shape((head_rows(plan), LANE), F32)],
        in_specs=[VMEM] * 3,
        out_specs=[ANY] * (plan.n_fsdp + 1),
        scratch_shapes=[
            pltpu.VMEM((96 * 16, LANE), F32),
            pltpu.SemaphoreType.DMA((many,)),
        ],
        compiler_params=LIMIT,
        name="wire_second",
    )(g_gate, g_up, g_down)
    return out[:-1], out[-1]


def wire_plain(plan, copies_of, rows, operands):
    many = len(copies_of(*[Nowhere()] * len(operands)))

    def body(*refs):
        *refs, sems = refs
        sources, wires = refs[: len(operands)], refs[len(operands) :]
        copies = copies_of(*sources)
        to_wires(plan, copies, wires, sems, 0, True)
        to_wires(plan, copies, wires, sems, 0, False)

    return pl.pallas_call(
        body,
        out_shape=[shape((rows, LANE), F32)] * plan.n_fsdp,
        in_specs=[VMEM] * len(operands),
        out_specs=[ANY] * plan.n_fsdp,
        scratch_shapes=[pltpu.SemaphoreType.DMA((many,))],
        compiler_params=LIMIT,
    )(*operands)


def wire_third(plan, g_down):
    return wire_plain(plan, partial(third_copies, plan), plan.rows[3], (g_down,))


def wire_middle_body(plan, head, *refs):
    pieces, refs = refs[:TP], refs[TP:]
    wires, (b_head, b_rows, sems) = refs[: plan.n_fsdp], refs[plan.n_fsdp :]
    s = lax.axis_index("seq")
    for k in range(TP):
        for n in range(2):
            unit = (s ^ k) + TP * n
            for block in range(12):
                b_rows[block, pl.ds(aligned(16 * unit, 16), 16), :] = pieces[k][
                    pl.ds(192 * n + 16 * block, 16), :
                ]
    copies = middle_copies(plan, b_rows, head)
    to_wires(plan, copies, wires, sems, 0, True)
    more = [(b, a) for a, b in b_head_copies(plan, b_head, b_rows)]
    made = start_copies(more, sems, len(copies))
    to_wires(plan, copies, wires, sems, 0, False)
    for copy in made:
        copy.wait()


def wire_middle(plan, head, pieces):
    many = len(middle_copies(plan, *[Nowhere()] * 2)) + len(
        b_head_copies(plan, *[Nowhere()] * 2)
    )
    out = pl.pallas_call(
        partial(wire_middle_body, plan),
        out_shape=[shape((plan.rows[1], LANE), F32)] * plan.n_fsdp
        + [shape((b_head_rows(plan), LANE), F32)],
        in_specs=[VMEM] * (1 + TP),
        out_specs=[ANY] * (plan.n_fsdp + 1),
        scratch_shapes=[
            pltpu.VMEM((12, 256, LANE), F32),
            pltpu.SemaphoreType.DMA((many,)),
        ],
        compiler_params=LIMIT,
        name="wire_middle",
    )(head, *pieces)
    return out[:-1], out[-1]


def split_copies(plan, copies):
    border = int(plan.offsets[1])
    return (
        [copy for copy in copies if copy[1] < border],
        [(f, row - border, rows, at) for f, row, rows, at in copies if row >= border],
    )


def wire_x(plan, g_x, b_head):
    def copies_of(g_x, b_head):
        nowhere = Nowhere()
        return split_copies(plan, first_copies(plan, nowhere, nowhere, nowhere, g_x, b_head))[1]

    return wire_plain(plan, copies_of, plan.lengths[1], (g_x, b_head))


def wire_y_body(plan, gains, vectors, gates, g_y, g_x, *refs):
    wires, (small, sems) = refs[: plan.n_fsdp], refs[plan.n_fsdp :]
    s = lax.axis_index("seq")
    small[...] = jnp.zeros_like(small)
    small[pl.ds(0, 24), :] = gains[...]
    for n in range(8):
        for part in range(2):
            small[pl.ds(24 + 16 * n + s + TP * part, 1), :] = vectors[
                pl.ds(2 * n + part, 1), :
            ]
    copies = split_copies(plan, first_copies(plan, small, gates, g_y, g_x, Nowhere()))[0]
    to_wires(plan, copies, wires, sems, 0, True)
    to_wires(plan, copies, wires, sems, 0, False)


def wire_y(plan, gains, vectors, gates, g_y, g_x):
    return pl.pallas_call(
        partial(wire_y_body, plan),
        out_shape=[shape((plan.lengths[0], LANE), F32)] * plan.n_fsdp,
        in_specs=[VMEM] * 5,
        out_specs=[ANY] * plan.n_fsdp,
        scratch_shapes=[
            pltpu.VMEM((SMALL, LANE), F32),
            pltpu.SemaphoreType.DMA((count_first(plan),)),
        ],
        compiler_params=LIMIT,
        name="wire_y",
    )(gains, vectors, gates, g_y, g_x)


def spread_body(plan, targets, *refs):
    count = len(targets)
    sums, outs, sems = refs[:count], refs[count : count + TP], refs[count + TP]
    s = lax.axis_index("seq")
    for start in (True, False):
        for summed, group in zip(sums, targets):
            for target in group:
                size = plan.lengths[target]
                at = int(plan.offsets[target] - plan.offsets[group[0]])
                for k in range(TP):

                    @pl.when((s ^ target) == k)
                    def _():
                        copy = pltpu.make_async_copy(
                            summed.at[pl.ds(at, size)],
                            outs[k].at[pl.ds(0, size)],
                            sems.at[target],
                        )
                        if start:
                            copy.start()
                        else:
                            copy.wait()


def spread(plan, targets, sums):
    rows = max(plan.lengths[s] for group in targets for s in group)
    return pl.pallas_call(
        partial(spread_body, plan, targets),
        out_shape=[shape((rows, LANE), F32)] * TP,
        in_specs=[VMEM] * len(sums),
        out_specs=[ANY] * TP,
        scratch_shapes=[pltpu.SemaphoreType.DMA((TP,))],
        compiler_params=LIMIT,
    )(*sums)


def shift_up(source, source_row, target, target_row, rows, block, amount):
    def step(j, _):
        both = pltpu.roll(source[pl.ds(source_row + j * block, block + 8), :], amount, 1)
        below = pltpu.roll(both, block + 7, 0)[:block]
        target[pl.ds(target_row + j * block, block), :] = jnp.where(
            lanes(block) < amount, both[:block], below
        )
        return 0

    lax.fori_loop(0, rows // block, step, 0, unroll=True)


def collect_body(plan, tab, *refs):
    pieces, (own, hd, hu, al, win, wire, sems) = refs[: 3 * TP], refs[3 * TP :]
    s, f = lax.axis_index("seq"), lax.axis_index("fsdp")
    me = s * plan.n_fsdp + f

    def bring(start):
        for number, (low, high) in enumerate(((0, 0), (1, 2), (3, TP - 1))):

            @pl.when((s >= low) & (s <= high))
            def _():
                for k in range(TP):
                    piece = pieces[TP * number + k]
                    copy = pltpu.make_async_copy(
                        piece, wire.at[s ^ k, pl.ds(0, piece.shape[0])], sems.at[k]
                    )
                    if start:
                        copy.start()
                    else:
                        copy.wait()

    bring(True)
    total = win.shape[0]

    def clear(j, _):
        al[pl.ds(aligned(j * 96, 8), 96), :] = jnp.zeros((96, LANE), F32)
        return 0

    lax.fori_loop(0, al.shape[0] // 96, clear, 0, unroll=4)
    bring(False)

    def columns(g, _):
        at = tab[me, 1] + g * 256
        to = tab[me, 3] + g * 16
        for block in range(16):
            row = to + 16 * tab[me, 2] * (block // TP)
            al[pl.ds(at + block, 16, stride=16), :] = wire[
                block % TP, pl.ds(aligned(row, 16), 16), :
            ]
        return 0

    lax.fori_loop(0, tab[me, 2], columns, 0)
    for slot in (4, 10):

        def grouped(j, _):
            for owner in range(TP):
                at = tab[me, slot] + j * 1536 + owner * 192
                to = tab[me, slot + 2] + j * 16
                for block in range(12):
                    row = to + 16 * tab[me, slot + 1] * block
                    al[pl.ds(at + block, 16, stride=12), :] = wire[
                        owner, pl.ds(aligned(row, 16), 16), :
                    ]
            return 0

        lax.fori_loop(0, tab[me, slot + 1], grouped, 0)

    def mixed_columns(g, _):
        at = tab[me, 7] + g * 1152
        to = tab[me, 9] + g * 32
        wide = 32 * tab[me, 8]
        last = tab[me, 9] + 4 * wide + g * 16
        for half in range(2):
            for a in range(4):
                parts = swap_lanes(
                    [
                        wire[owner, pl.ds(aligned(to + a * wide + 16 * half, 16), 16), :]
                        for owner in range(TP)
                    ]
                )
                for b in range(TP):
                    al[pl.ds(at + 576 * half + 8 * a + b, 16, stride=36), :] = parts[b]
        parts = swap_lanes(
            [wire[owner, pl.ds(aligned(last, 16), 16), :] for owner in range(TP)]
        )
        for half in range(2):
            for b in range(4):
                al[pl.ds(at + 576 * half + 32 + b, 16, stride=36), :] = parts[4 * half + b]
        return 0

    lax.fori_loop(0, tab[me, 8], mixed_columns, 0)

    @pl.when(me == 0)
    def _():
        summed = wire[0, pl.ds(0, 152), :]
        for owner in range(1, TP):
            summed = summed + wire[owner, pl.ds(0, 152), :]
        al[pl.ds(HALO, 152), :] = summed
        for kind in range(2):
            for n in range(16):
                al[pl.ds(HALO + 152 + 2048 * kind + 128 * n, 128), :] = wire[
                    n % TP, pl.ds(SMALL + 128 * (2 * kind + n // TP), 128), :
                ]

    def back(j, _):
        both = pltpu.roll(
            al[pl.ds(aligned(j * 48, 8), 56), :], lax.rem(LANE - tab[me, 0], LANE), 1
        )
        below = pltpu.roll(both, 55, 0)[:48]
        win[pl.ds(aligned(j * 48, 8), 48), :] = jnp.where(
            lanes(48) < LANE - tab[me, 0], both[:48], below
        )
        return 0

    lax.fori_loop(0, total // 48, back, 0, unroll=7)
    hd[...] = win[pl.ds(0, HALO), :]
    own[...] = win[pl.ds(HALO, plan.own_rows), :]
    shift_up(win, HALO + plan.last, hu, 0, HALO, 32, LANE - plan.part)


def collect(plan, pieces):
    total = -(-(HALO * 2 + plan.own_rows) // 672) * 672
    cleared = total + 96
    return pl.pallas_call(
        partial(collect_body, plan),
        out_shape=[
            shape((plan.own_rows, LANE), F32),
            shape((HALO, LANE), F32),
            shape((HALO, LANE), F32),
        ],
        in_specs=[SMEM] + [ANY] * (3 * TP),
        out_specs=[VMEM] * 3,
        scratch_shapes=[
            pltpu.VMEM((cleared, LANE), F32),
            pltpu.VMEM((total, LANE), F32),
            pltpu.VMEM((TP, plan.longest, LANE), F32),
            pltpu.SemaphoreType.DMA((TP,)),
        ],
        compiler_params=LIMIT,
        name="collect",
    )(jnp.asarray(plan.table), *pieces)


def tail_body(plan, value, out):
    first = (plan.last - HALO) % 8
    out[...] = jnp.zeros_like(out)
    shift_down(value, 0, out, first, HALO, 32, plan.part, True)
    z = pltpu.roll(value[pl.ds(HALO - 8, 8), :], plan.part, 1)
    row = lax.broadcasted_iota(jnp.int32, (8, LANE), 0)
    out[pl.ds(first + HALO, 8), :] = jnp.where(
        (row == 0) & (lanes(8) < plan.part), pltpu.roll(z, 1, 0), 0.0
    )


def place_tail(plan, value):
    rows = plan.own_rows - (plan.last - HALO) // 8 * 8
    return pl.pallas_call(
        partial(tail_body, plan),
        out_shape=shape((max(rows, HALO + 16), LANE), F32),
        in_specs=[VMEM],
        out_specs=VMEM,
        compiler_params=LIMIT,
        name="place_tail",
    )(value)[:rows]


def scan_body(reverse, coefficient, addend, out):
    rows, width = coefficient.shape
    at = lax.broadcasted_iota(jnp.int32, (8, width), 0)
    if reverse:
        at = 7 - at
    steps = rows // 8

    def step(j, carry):
        block = steps - 1 - j if reverse else j
        here = pl.ds(aligned(block * 8, 8), 8)
        a, b = coefficient[here, :], addend[here, :]
        for reach in (1, 2, 4):
            turn = 8 - reach if reverse else reach
            inside = at >= reach
            b = b + jnp.where(inside, a * pltpu.roll(b, turn, 0), 0.0)
            a = jnp.where(inside, a * pltpu.roll(a, turn, 0), a)
        value = b + a * carry
        out[here, :] = value
        edge = value[0:1] if reverse else value[7:8]
        return jnp.broadcast_to(edge, (8, width))

    lax.fori_loop(0, steps, step, jnp.zeros((8, width), F32), unroll=4)


def linear_scan(coefficient, addend, reverse):
    return pl.pallas_call(
        partial(scan_body, reverse),
        out_shape=shape(coefficient.shape, F32),
        in_specs=[VMEM] * 2,
        out_specs=VMEM,
        compiler_params=LIMIT,
        name="scan_back" if reverse else "scan",
    )(coefficient, addend)


def swap(value, bit):
    return lax.ppermute(value, "seq", [(i, i ^ bit) for i in range(TP)])


def exchange(pieces, targets=range(TP)):
    return [pieces[0]] + [
        lax.ppermute(pieces[k], "seq", [(i ^ k, i) for i in targets]) for k in range(1, TP)
    ]


def join_body(*refs):
    *pieces, out, sems = refs
    copies, at = [], 0
    for number, piece in enumerate(pieces):
        rows = piece.shape[0]
        copies.append(
            pltpu.make_async_copy(piece, out.at[pl.ds(at, rows)], sems.at[number])
        )
        at += rows
    for copy in copies:
        copy.start()
    for copy in copies:
        copy.wait()


def join(pieces):
    rows = sum(piece.shape[0] for piece in pieces)
    return pl.pallas_call(
        join_body,
        out_shape=shape((rows, pieces[0].shape[1]), pieces[0].dtype),
        in_specs=[ANY] * len(pieces),
        out_specs=VMEM,
        scratch_shapes=[pltpu.SemaphoreType.DMA((len(pieces),))],
        compiler_params=LIMIT,
    )(*pieces)


def gather_stream(mine):
    half = mine.shape[0] // 2

    over_x, over_y = swap(mine, 2), swap(mine, 4)
    over_xy = [swap(over_x[:half], 4), swap(over_y[half:], 2)]
    chip = [mine, over_x, over_y] + over_xy
    return join(chip + [swap(part, 1) for part in chip])


def scatter_stream(partial_sums):
    rows = partial_sums.shape[0] // TP
    half = rows // 2

    def send(value, bit):
        return swap(value.astype(BF16), bit).astype(F32)

    other = send(partial_sums[TP // 2 * rows :], 1)
    q = (partial_sums[: TP // 2 * rows] + other).reshape(4, rows, -1)
    up = send(jnp.concatenate([q[1, :half], q[3, :half]]), 2)
    down = send(jnp.concatenate([q[2, half:], q[3, half:]]), 4)
    top = send(q[2, :half] + up[half:], 4)
    low = send(q[1, half:] + down[half:], 2)
    return jnp.concatenate(
        [q[0, :half] + up[:half] + top, q[0, half:] + down[:half] + low], axis=0
    )


def to_positions(values, s):
    rows = values.shape[0] // TP
    parts = []
    for j in range(TP):
        k = s ^ j
        at = (k // 2 + 4 * (k % 2)) * rows
        parts.append(lax.dynamic_slice_in_dim(values, at, rows, 0))
    return jnp.concatenate(parts, axis=0)


def to_relative(values, s):
    rows = values.shape[0] // TP
    return jnp.concatenate(
        [lax.dynamic_slice_in_dim(values, (s ^ k) * rows, rows, 0) for k in EVEN_FIRST], axis=0
    )


def gather_line(value, count):
    def send(value, bit):
        return lax.ppermute(value, "fsdp", [(i, i ^ bit) for i in range(count)])

    opposite, near = send(value, 3), send(value, 1)
    return [value, near, send(opposite, 1), opposite]


def scatter_line(blocks):
    count = len(blocks)
    own, near, far, cross = blocks
    far = lax.ppermute(far, "fsdp", [(i, i ^ 1) for i in range(count)])
    near = lax.ppermute(near, "fsdp", [(i, i ^ 1) for i in range(count)])
    cross = lax.ppermute(cross + far, "fsdp", [(i, i ^ 3) for i in range(count)])
    return own + near + cross


def sliced(plan, *arguments):
    return sliced_step(plan, *arguments)


def sliced_step(plan, stream_in, cotangent, starts, params, momentum, average):
    n_fsdp = plan.n_fsdp
    s = lax.axis_index("seq")
    shards = TP * n_fsdp
    onward = [(i, i + 1) for i in range(shards - 1)]
    backward = [(i + 1, i) for i in range(shards - 1)]
    both = ("seq", "fsdp")
    edge = HALO * LANE
    per = plan.per

    hd, hu = lax.optimization_barrier((params[per - edge :], params[:edge]))
    hd = lax.ppermute(hd.astype(BF16), both, onward)
    hu = lax.ppermute(hu.astype(BF16), both, backward)
    own = jnp.pad(params, (0, plan.own_rows * LANE - per)).reshape(-1, LANE)
    pieces = pack(
        plan, hd.astype(F32).reshape(-1, LANE), own, hu.astype(F32).reshape(-1, LANE)
    )
    first, middle_wire, second, third = order(plan, exchange(pieces))
    stream_bf, cotangent_bf, first = lax.optimization_barrier(
        (stream_in[0], cotangent[0], first)
    )
    line = gather_line(first, n_fsdp)
    middle_wire, second, third, line = lax.optimization_barrier(
        (middle_wire, second, third, line)
    )
    small, gates, w_y, w_x, b_head = unpack_first(plan, line)
    line = gather_line(middle_wire, n_fsdp)
    *out_rows, head = unpack_middle(plan, line, b_head)
    w_out = join_out_rows(exchange(out_rows))
    line = gather_line(second, n_fsdp)
    w_gate, w_up, w_down = unpack_second(plan, line, head)
    w_down = unpack_third(plan, gather_line(third, n_fsdp), w_down)

    mine = stream_in[0].astype(F32)
    stream = gather_stream(stream_bf)
    stream = stream.astype(F32)
    grad_out = gather_stream(cotangent_bf)
    rows = stream.shape[0]

    small = small.astype(F32)
    gain_one = small[0:12].reshape(-1)
    gain_two = small[12:24].reshape(-1)

    def channels(at):
        return jnp.concatenate(
            [
                lax.dynamic_slice_in_dim(small, at + s, 1, 0),
                lax.dynamic_slice_in_dim(small, at + s + TP, 1, 0),
            ],
            axis=1,
        )[0]

    conv_bias, bias_a, bias_i, lambda_raw = (channels(24 + 16 * j) for j in range(4))
    conv_weight = jnp.stack([channels(88 + 16 * j) for j in range(KW)])

    positions = jnp.arange(rows, dtype=jnp.int32)
    ext_pos = jnp.arange(rows + KW - 1, dtype=jnp.int32) - (KW - 1)
    segment_ext = segment_ids(ext_pos, starts[0])
    starting = start_flags(positions, starts[0])[:, None]

    def gate_product(values, at):
        return jnp.concatenate(
            [matmul(values[:, :HB], gates[at : at + HB]), matmul(values[:, HB:], gates[at + HB : at + 2 * HB])],
            axis=1,
        )

    def gate_product_t(values, at):
        return jnp.concatenate(
            [matmul_t(values[:, :HB], gates[at : at + HB]), matmul_t(values[:, HB:], gates[at + HB : at + 2 * HB])],
            axis=1,
        )

    normed = rms_norm(stream, gain_one).astype(BF16)
    branch_y = matmul(normed, w_y)
    branch_x = matmul(normed, w_x).astype(BF16)
    branch_y = to_positions(branch_y, s)
    branch_x = to_positions(branch_x, s)
    extended = jnp.pad(branch_x, ((KW - 1, 0), (0, 0))).astype(F32)

    def convolve_here(extended, weight, bias):
        total = jnp.zeros((rows, bias.shape[0]), F32) + bias
        for lag in range(KW):
            source = extended[KW - 1 - lag : KW - 1 - lag + rows]
            same = segment_ext[KW - 1 - lag : KW - 1 - lag + rows] == segment_ext[KW - 1 :]
            total = total + weight[lag] * source * same.astype(F32)[:, None]
        return total

    conv_out = convolve_here(extended, conv_weight, conv_bias).astype(BF16)
    conv_val = conv_out.astype(F32)
    pre_a = gate_product(conv_out, 0) + bias_a
    pre_i = gate_product(conv_out, 2 * HB) + bias_i
    decay, drive = gate_terms(pre_a, pre_i, conv_val, lambda_raw, starting)
    state = linear_scan(decay, drive, False)
    gelu_y = jax.nn.gelu(branch_y, approximate=True)
    mixed = to_relative((state * gelu_y).astype(BF16), s)
    middle = mine + scatter_stream(matmul(mixed, w_out))
    normed_two_mine = rms_norm(middle, gain_two).astype(BF16)
    normed_two = gather_stream(normed_two_mine)
    gate = matmul(normed_two, w_gate)
    upward = matmul(normed_two, w_up)
    hidden = gelu_product(gate, upward).astype(BF16)
    g_down = t_matmul(hidden, grad_out)
    summed_three = scatter_line(wire_third(plan, g_down))
    out_sums = matmul(hidden, w_down)
    output = (middle + scatter_stream(out_sums)).astype(BF16)
    gate, upward, _ = lax.optimization_barrier((gate, upward, hidden))

    grad_hidden = matmul_t(grad_out, w_down)
    _, product_back = jax.vjp(gelu_product, gate, upward)
    grad_gate, grad_up = product_back(grad_hidden)
    grad_gate, grad_up = grad_gate.astype(BF16), grad_up.astype(BF16)
    g_gate = t_matmul(normed_two, grad_gate)
    g_up = t_matmul(normed_two, grad_up)
    grad_normed_two = scatter_stream(matmul_t(grad_gate, w_gate) + matmul_t(grad_up, w_up))
    wire_two, wire_head = wire_second(plan, g_gate, g_up, g_down)
    summed_two = scatter_line(wire_two)

    _, norm_back_two = jax.vjp(rms_norm, middle, gain_two)
    grad_middle_part, g_gain_two = norm_back_two(grad_normed_two)
    grad_middle = cotangent[0].astype(F32) + grad_middle_part
    grad_first = gather_stream(grad_middle.astype(BF16))
    g_out = t_matmul(mixed, grad_first)
    wire_mid, b_head = wire_middle(plan, wire_head, exchange(split_out_rows(g_out)))
    summed_mid = scatter_line(wire_mid)
    grad_mixed = to_positions(matmul_t(grad_first, w_out), s)
    _, gelu_back = jax.vjp(partial(jax.nn.gelu, approximate=True), branch_y)
    grad_y = gelu_back(grad_mixed * state)[0].astype(BF16)
    next_decay = jnp.concatenate([decay[1:], jnp.ones((1, decay.shape[1]), F32)], axis=0)
    adjoint = linear_scan(next_decay, grad_mixed * gelu_y, True)
    previous = jnp.concatenate([jnp.zeros((1, decay.shape[1]), F32), state[:-1]], axis=0)
    _, gates_back = jax.vjp(gate_terms, pre_a, pre_i, conv_val, lambda_raw, starting)
    grad_pre_a, grad_pre_i, grad_direct, g_lambda, _ = gates_back((adjoint * previous, adjoint))
    grad_pre_a, grad_pre_i = grad_pre_a.astype(BF16), grad_pre_i.astype(BF16)
    g_gates = jnp.concatenate(
        [
            t_matmul(conv_out[:, n : n + HB], grad[:, n : n + HB])
            for grad in (grad_pre_a, grad_pre_i)
            for n in (0, HB)
        ],
        axis=0,
    )
    g_bias_a = jnp.sum(grad_pre_a.astype(F32), axis=0)
    g_bias_i = jnp.sum(grad_pre_i.astype(F32), axis=0)
    grad_conv = grad_direct + gate_product_t(grad_pre_a, 0) + gate_product_t(grad_pre_i, 2 * HB)
    _, conv_back = jax.vjp(convolve_here, extended, conv_weight, conv_bias)
    grad_ext, g_conv_weight, g_conv_bias = conv_back(grad_conv)
    grad_x = to_relative(grad_ext[KW - 1 :].astype(BF16), s)
    grad_y = to_relative(grad_y, s)
    g_x = t_matmul(normed, grad_x)
    g_y = t_matmul(normed, grad_y)
    grad_normed = scatter_stream(matmul_t(grad_y, w_y) + matmul_t(grad_x, w_x))
    _, norm_back_one = jax.vjp(rms_norm, mine, gain_one)
    grad_stream_part, g_gain_one = norm_back_one(grad_normed)
    input_grad = grad_middle + grad_stream_part

    summed_x = scatter_line(wire_x(plan, g_x, b_head))
    gains = jnp.concatenate([g_gain_one, g_gain_two]).reshape(-1, LANE)
    vectors = jnp.stack(
        [g_conv_bias, g_bias_a, g_bias_i, g_lambda] + [g_conv_weight[k] for k in range(KW)]
    ).reshape(-1, LANE)
    summed_y = scatter_line(wire_y(plan, gains, vectors, g_gates, g_y, g_x))
    early = spread(plan, plan.groups[2:], (summed_two, summed_three))
    middle_set = spread(plan, ((1,), (2,)), (summed_x, summed_mid))
    got = exchange(spread(plan, ((0,),), (summed_y,)), (0,))
    got += exchange(middle_set, (1, 2))
    got += exchange(early)
    grad_own, grad_hd, grad_hu = collect(plan, got)
    from_next = lax.ppermute(grad_hd, both, backward)
    from_before = lax.ppermute(grad_hu, both, onward)
    tail = place_tail(plan, from_next).reshape(-1)
    whole = plan.own_rows * LANE
    summed = (
        grad_own.reshape(-1)
        + jnp.pad(from_before.reshape(-1), (0, whole - edge))
        + jnp.pad(tail, (whole - tail.shape[0], 0))
    )[:per]
    new_moment = MOMENT * momentum + summed
    new_params = params - RATE * (summed + MOMENT * new_moment)
    new_average = BLEND * average + (1.0 - BLEND) * new_params
    return (output[None], input_grad[None], new_params, new_moment, new_average)


def solution(mesh):
    n_seq, n_fsdp = mesh.shape["seq"], mesh.shape["fsdp"]
    fast = (n_seq, n_fsdp) == (TP, 4)
    body = partial(sliced, Plan(n_seq, n_fsdp)) if fast else local
    return jax.shard_map(
        body,
        mesh=mesh,
        in_specs=(
            P("fsdp", "seq", None),
            P("fsdp", "seq", None),
            P("fsdp", None),
            P(("seq", "fsdp")),
            P(("seq", "fsdp")),
            P(("seq", "fsdp")),
        ),
        out_specs=(
            P("fsdp", "seq", None),
            P("fsdp", "seq", None),
            P(("seq", "fsdp")),
            P(("seq", "fsdp")),
            P(("seq", "fsdp")),
        ),
        check_vma=False,
    )
```

```python
from functools import partial
import math

import jax
import jax.numpy as jnp
import numpy as np
from jax import lax
from jax.experimental import pallas as pl
from jax.experimental.pallas import tpu as pltpu
from jax.sharding import PartitionSpec as P


D = 1536
LRU = 2048
FF = 4608
HB = 128
KW = 4


EPS = 1e-06
RATE = 3e-05
MOMENT = 0.9
BLEND = 0.9
DECAY_SCALE = 8.0


def shifted(block, axis, distance):
    devices = range(lax.axis_size(axis))
    route = [(i - distance, i) for i in devices if i - distance in devices]
    return lax.ppermute(block, axis, route)


def carried_in(value, axis, join, neutral, backward):
    count, mine = (lax.axis_size(axis), lax.axis_index(axis))
    pieces = jax.tree.map(lambda part: lax.all_gather(part, axis), value)
    if backward:
        pieces = jax.tree.map(lambda part: part[::-1], pieces)
        mine = count - 1 - mine
    so_far = jax.tree.map(
        lambda part, zero: jnp.full_like(part, 0) + jnp.asarray(zero, part.dtype), value, neutral
    )

    def lap(position, so_far):
        longer = join(so_far, jax.tree.map(lambda part: part[position], pieces))
        return jax.tree.map(lambda new, old: jnp.where(position < mine, new, old), longer, so_far)

    return lax.fori_loop(0, count - 1, lap, so_far)


def layout():
    return [
        ("gain_one", (D,)),
        ("gain_two", (D,)),
        ("conv_bias", (LRU,)),
        ("bias_a", (LRU,)),
        ("bias_i", (LRU,)),
        ("lambda_raw", (LRU,)),
        ("conv_weight", (KW, LRU)),
        ("gate_a", (LRU // HB, HB, HB)),
        ("gate_i", (LRU // HB, HB, HB)),
        ("w_y", (D, LRU)),
        ("w_x", (D, LRU)),
        ("w_out", (LRU, D)),
        ("w_gate", (D, FF)),
        ("w_up", (D, FF)),
        ("w_down", (FF, D)),
    ]


def unpack(packed):
    result = {}
    offset = 0
    for entry_name, entry_shape in layout():
        amount = math.prod(entry_shape)
        result[entry_name] = packed[offset : offset + amount].reshape(entry_shape)
        offset += amount
    return result


def matmul(left, right):
    return jnp.dot(left, right, preferred_element_type=jnp.float32)


def matmul_t(left, right):
    return lax.dot_general(
        left, right, (((1,), (1,)), ((), ())), preferred_element_type=jnp.float32
    )


def t_matmul(left, right):
    return lax.dot_general(
        left, right, (((0,), (0,)), ((), ())), preferred_element_type=jnp.float32
    )


def blocked(values, weight):
    shaped = values.reshape(values.shape[0], LRU // HB, HB)
    return jnp.einsum("tnh,nhk->tnk", shaped, weight, preferred_element_type=jnp.float32).reshape(
        values.shape[0], LRU
    )


def blocked_t(values, weight):
    shaped = values.reshape(values.shape[0], LRU // HB, HB)
    return jnp.einsum("tnk,nhk->tnh", shaped, weight, preferred_element_type=jnp.float32).reshape(
        values.shape[0], LRU
    )


def blocked_grad(inputs, grads):
    left = inputs.reshape(inputs.shape[0], LRU // HB, HB)
    right = grads.reshape(grads.shape[0], LRU // HB, HB)
    return jnp.einsum("tnh,tnk->nhk", left, right, preferred_element_type=jnp.float32)


def rms_norm(values, gain):
    return values * lax.rsqrt(jnp.mean(values * values, axis=-1, keepdims=True) + EPS) * gain


def combine(earlier, later):
    return (earlier[0] * later[0], later[0] * earlier[1] + later[1])


def gate_terms(pre_a, pre_i, conv_val, lambda_raw, starting):
    recall = jax.nn.sigmoid(pre_a)
    admit = jax.nn.sigmoid(pre_i)
    rate = DECAY_SCALE * jax.nn.softplus(lambda_raw) * recall
    decay = (1.0 - starting) * jnp.exp(-rate)
    scale_in = starting + (1.0 - starting) * jnp.sqrt(-jnp.expm1(-2.0 * rate))
    return (decay, scale_in * admit * conv_val)


def convolve(extended, weight, bias, segment_ext, rows):
    total = jnp.zeros((rows, LRU), jnp.float32) + bias
    for lag in range(KW):
        source = extended[KW - 1 - lag : KW - 1 - lag + rows]
        same = (segment_ext[KW - 1 - lag : KW - 1 - lag + rows] == segment_ext[KW - 1 :]).astype(
            jnp.float32
        )
        total = total + weight[lag] * source * same[:, None]
    return total


def segment_ids(positions, doc_starts):
    return jnp.sum((doc_starts[None, :] <= positions[:, None]).astype(jnp.int32), axis=1)


def start_flags(positions, doc_starts):
    return jnp.max((doc_starts[None, :] == positions[:, None]).astype(jnp.float32), axis=1)


def gelu_product(left, right):
    return jax.nn.gelu(left, approximate=True) * right


def local(stream_in, cotangent, starts, params, momentum, average):
    weights = unpack(
        lax.all_gather(params.astype(jnp.bfloat16), ("seq", "fsdp"), axis=0, tiled=True)
    )
    stream = stream_in[0].astype(jnp.float32)
    incoming = cotangent[0].astype(jnp.float32)
    doc_starts = starts[0]
    rows = stream.shape[0]
    positions = lax.axis_index("seq") * rows + jnp.arange(rows, dtype=jnp.int32)
    ext_pos = positions[0] - (KW - 1) + jnp.arange(rows + KW - 1, dtype=jnp.int32)
    segment_ext = segment_ids(ext_pos, doc_starts)
    starting = start_flags(positions, doc_starts)[:, None]
    gain_one = weights["gain_one"].astype(jnp.float32)
    gain_two = weights["gain_two"].astype(jnp.float32)
    conv_weight = weights["conv_weight"].astype(jnp.float32)
    conv_bias = weights["conv_bias"].astype(jnp.float32)
    lambda_raw = weights["lambda_raw"].astype(jnp.float32)
    normed = rms_norm(stream, gain_one).astype(jnp.bfloat16)
    branch_y = matmul(normed, weights["w_y"])
    branch_x = matmul(normed, weights["w_x"]).astype(jnp.bfloat16)
    edge = shifted(branch_x[rows - (KW - 1) :], "seq", 1)
    extended = jnp.concatenate([edge, branch_x], axis=0).astype(jnp.float32)
    conv_out = convolve(extended, conv_weight, conv_bias, segment_ext, rows).astype(jnp.bfloat16)
    conv_val = conv_out.astype(jnp.float32)
    pre_a = blocked(conv_out, weights["gate_a"]) + weights["bias_a"].astype(jnp.float32)
    pre_i = blocked(conv_out, weights["gate_i"]) + weights["bias_i"].astype(jnp.float32)
    decay, drive = gate_terms(pre_a, pre_i, conv_val, lambda_raw, starting)
    prod_local, state_local = lax.associative_scan(combine, (decay, drive), axis=0)
    neutral = (jnp.ones((LRU,), jnp.float32), jnp.zeros((LRU,), jnp.float32))
    carried = carried_in((prod_local[-1], state_local[-1]), "seq", combine, neutral, False)
    carry_in = carried[1]
    state = lax.associative_scan(combine, (decay, drive.at[0].add(decay[0] * carry_in)), axis=0)[1]
    gelu_y = jax.nn.gelu(branch_y, approximate=True)
    mixed = (state * gelu_y).astype(jnp.bfloat16)
    middle = stream + matmul(mixed, weights["w_out"])
    normed_two = rms_norm(middle, gain_two).astype(jnp.bfloat16)
    gate = matmul(normed_two, weights["w_gate"])
    upward = matmul(normed_two, weights["w_up"])
    hidden = gelu_product(gate, upward).astype(jnp.bfloat16)
    output = (middle + matmul(hidden, weights["w_down"])).astype(jnp.bfloat16)
    grads = {}
    grad_out = incoming.astype(jnp.bfloat16)
    grads["w_down"] = t_matmul(hidden, grad_out)
    grad_hidden = matmul_t(grad_out, weights["w_down"])
    _, product_back = jax.vjp(gelu_product, gate, upward)
    grad_gate, grad_up = product_back(grad_hidden)
    grad_gate = grad_gate.astype(jnp.bfloat16)
    grad_up = grad_up.astype(jnp.bfloat16)
    grads["w_gate"] = t_matmul(normed_two, grad_gate)
    grads["w_up"] = t_matmul(normed_two, grad_up)
    grad_normed_two = matmul_t(grad_gate, weights["w_gate"]) + matmul_t(grad_up, weights["w_up"])
    _, norm_back_two = jax.vjp(rms_norm, middle, gain_two)
    grad_middle_part, grads["gain_two"] = norm_back_two(grad_normed_two)
    grad_middle = incoming + grad_middle_part
    grad_first = grad_middle.astype(jnp.bfloat16)
    grads["w_out"] = t_matmul(mixed, grad_first)
    grad_mixed = matmul_t(grad_first, weights["w_out"])
    _, gelu_back = jax.vjp(partial(jax.nn.gelu, approximate=True), branch_y)
    grad_y = gelu_back(grad_mixed * state)[0].astype(jnp.bfloat16)
    grad_state = grad_mixed * gelu_y
    next_decay = jnp.concatenate([decay[1:], jnp.ones((1, LRU), jnp.float32)], axis=0)
    suffix, adjoint_local = lax.associative_scan(
        combine, (next_decay, grad_state), axis=0, reverse=True
    )
    returned = carried_in(
        (prod_local[-1], decay[0] * adjoint_local[0]), "seq", combine, neutral, True
    )
    adjoint = adjoint_local + suffix * returned[1]
    previous = jnp.concatenate([carry_in[None, :], state[:-1]], axis=0)
    _, gates_back = jax.vjp(gate_terms, pre_a, pre_i, conv_val, lambda_raw, starting)
    grad_pre_a, grad_pre_i, grad_direct, grads["lambda_raw"], _ = gates_back(
        (adjoint * previous, adjoint)
    )
    grad_pre_a = grad_pre_a.astype(jnp.bfloat16)
    grad_pre_i = grad_pre_i.astype(jnp.bfloat16)
    grads["gate_a"] = blocked_grad(conv_out, grad_pre_a)
    grads["gate_i"] = blocked_grad(conv_out, grad_pre_i)
    grads["bias_a"] = jnp.sum(grad_pre_a.astype(jnp.float32), axis=0)
    grads["bias_i"] = jnp.sum(grad_pre_i.astype(jnp.float32), axis=0)
    grad_conv = (
        grad_direct
        + blocked_t(grad_pre_a, weights["gate_a"])
        + blocked_t(grad_pre_i, weights["gate_i"])
    )
    _, conv_back = jax.vjp(
        partial(convolve, segment_ext=segment_ext, rows=rows), extended, conv_weight, conv_bias
    )
    grad_ext, grads["conv_weight"], grads["conv_bias"] = conv_back(grad_conv)
    edge_back = shifted(grad_ext[: KW - 1], "seq", -1)
    grad_x = grad_ext[KW - 1 :] + jnp.concatenate(
        [jnp.zeros((rows - (KW - 1), LRU), jnp.float32), edge_back], axis=0
    )
    grad_x = grad_x.astype(jnp.bfloat16)
    grads["w_x"] = t_matmul(normed, grad_x)
    grads["w_y"] = t_matmul(normed, grad_y)
    grad_normed = matmul_t(grad_y, weights["w_y"]) + matmul_t(grad_x, weights["w_x"])
    _, norm_back_one = jax.vjp(rms_norm, stream, gain_one)
    grad_stream_part, grads["gain_one"] = norm_back_one(grad_normed)
    input_grad = grad_middle + grad_stream_part
    packed_grad = jnp.concatenate([grads[entry[0]].reshape(-1) for entry in layout()])
    summed = lax.psum_scatter(packed_grad, ("seq", "fsdp"), scatter_dimension=0, tiled=True)
    new_moment = MOMENT * momentum + summed
    new_params = params - RATE * (summed + MOMENT * new_moment)
    new_average = BLEND * average + (1.0 - BLEND) * new_params
    return (output[None], input_grad[None], new_params, new_moment, new_average)


LANE = 128
TP = 8
HALO = 544
SMALL = 160
GATES = 512
REGIONS = {
    "A": (4248, 256, 192, 32),
    "B": (53400, 1536, 16, 192),
    "C": (77976, 1152, 96, 144),
    "D": (188568, 1536, 36, 192),
}
ROWS = 243864
EVEN_FIRST = (0, 2, 4, 6, 1, 3, 5, 7)
F32 = jnp.float32
BF16 = jnp.bfloat16


class Plan:
    def __init__(self, n_seq, n_fsdp):
        self.n_fsdp = n_fsdp
        shards = n_seq * n_fsdp
        per = ROWS * LANE // shards
        self.per = per
        self.part = per % LANE
        self.own_rows = -(-per // 1024) * 8
        self.last = per // LANE
        bounds = [0]
        for i in range(1, shards):
            at = per * i / LANE
            for first, unit, count, _ in REGIONS.values():
                if first <= at < first + unit * count:
                    bounds.append(first + unit * round((at - first) / unit))
        bounds.append(ROWS)
        self.segments = []
        self.sizes = []
        self.table = np.zeros((shards, 16), np.int32)
        for i in range(shards):
            base = per * i // LANE
            self.table[i, 0] = per * i % LANE
            offset = SMALL + GATES if i == 0 else 0
            found = {}
            for slot, (name, (first, unit, count, wide)) in enumerate(REGIONS.items()):
                low = max(bounds[i], first)
                high = min(bounds[i + 1], first + unit * count)
                if high > low:
                    units = (high - low) // unit
                    found[name] = ((low - first) // unit, units, offset)
                    self.table[i, 1 + 3 * slot : 4 + 3 * slot] = (
                        low - base + HALO,
                        units,
                        offset,
                    )
                    offset += units * wide
            self.segments.append(found)
            self.sizes.append(offset)
            self.table[i, 13] = int(i == 0)
        self.lengths = [
            max(self.sizes[s * n_fsdp : (s + 1) * n_fsdp]) for s in range(n_seq)
        ]
        self.offsets = np.concatenate([[0], np.cumsum(self.lengths)]).astype(np.int32)
        self.longest = max(self.lengths)
        self.groups = ((0, 1), (2,), (3, 4, 5, 6), (7,))
        self.starts = [int(self.offsets[group[0]]) for group in self.groups]
        self.rows = [sum(self.lengths[s] for s in group) for group in self.groups]

    def pieces(self, name, groups):
        out = []
        for i, found in enumerate(self.segments):
            s, f = divmod(i, self.n_fsdp)
            if name in found and s in groups:
                first, units, offset = found[name]
                row = int(self.offsets[s] - self.offsets[groups[0]]) + offset
                out.append((f, row, first, units))
        return out


VMEM = pl.BlockSpec(memory_space=pltpu.VMEM)
ANY = pl.BlockSpec(memory_space=pl.ANY)
SMEM = pl.BlockSpec(memory_space=pltpu.SMEM)
LIMIT = pltpu.CompilerParams(vmem_limit_bytes=60 * 1024 * 1024)


def shape(dims, dtype):
    return jax.ShapeDtypeStruct(dims, dtype)


def aligned(value, multiple):
    return pl.multiple_of(value, multiple)


def lanes(rows):
    return lax.broadcasted_iota(jnp.int32, (rows, LANE), 1)


def swap_lanes(blocks):
    blocks = list(blocks)
    at = lanes(blocks[0].shape[0]) // 16
    for step in (4, 2, 1):
        low_side = (at & step) == 0
        for one in range(TP):
            if one & step == 0:
                left, right = blocks[one], blocks[one + step]
                blocks[one] = jnp.where(low_side, left, pltpu.roll(right, 16 * step, 1))
                blocks[one + step] = jnp.where(
                    low_side, pltpu.roll(left, LANE - 16 * step, 1), right
                )
    return blocks


def shift_down(source, source_row, target, target_row, rows, block, amount, unroll):
    def step(j, tail):
        z = pltpu.roll(source[pl.ds(source_row + j * block, block), :], amount, 1)
        above = pltpu.roll(jnp.concatenate([tail, z], axis=0), 1, 0)[8:]
        target[pl.ds(target_row + j * block, block), :] = jnp.where(
            lanes(block) < amount, above, z
        )
        return z[block - 8 :]

    lax.fori_loop(0, rows // block, step, jnp.zeros((8, LANE), F32), unroll=unroll)


def pack_body(plan, tab, hd, own, hu, *rest):
    outs, (win, al, wire, sems) = rest[:TP], rest[TP:]
    s, f = lax.axis_index("seq"), lax.axis_index("fsdp")
    me = s * plan.n_fsdp + f
    total = win.shape[0]
    first = pltpu.make_async_copy(hd, win.at[pl.ds(0, HALO)], sems.at[0])
    second = pltpu.make_async_copy(own, win.at[pl.ds(HALO, plan.own_rows)], sems.at[1])
    first.start()
    second.start()
    first.wait()
    second.wait()
    seam = HALO + plan.last
    kept = win[pl.ds(seam, 8), :]
    shift_down(hu, 0, win, seam, HALO, 32, plan.part, True)
    edge = lax.broadcasted_iota(jnp.int32, (8, LANE), 0) == 0
    win[pl.ds(seam, 8), :] = jnp.where(
        edge & (lanes(8) < plan.part), kept, win[pl.ds(seam, 8), :]
    )
    shift_down(win, 0, al, 0, total, 48, tab[me, 0], 7)

    def columns(g, _):
        at = tab[me, 1] + g * 256
        to = tab[me, 3] + g * 16
        for block in range(16):
            row = to + 16 * tab[me, 2] * (block // TP)
            wire[block % TP, pl.ds(aligned(row, 16), 16), :] = al[
                pl.ds(at + block, 16, stride=16), :
            ].astype(BF16)
        return 0

    lax.fori_loop(0, tab[me, 2], columns, 0)
    for slot in (4, 10):

        def grouped(j, _):
            for owner in range(TP):
                at = tab[me, slot] + j * 1536 + owner * 192
                to = tab[me, slot + 2] + j * 16
                for block in range(12):
                    row = to + 16 * tab[me, slot + 1] * block
                    wire[owner, pl.ds(aligned(row, 16), 16), :] = al[
                        pl.ds(at + block, 16, stride=12), :
                    ].astype(BF16)
            return 0

        lax.fori_loop(0, tab[me, slot + 1], grouped, 0)

    def mixed_columns(g, _):
        at = tab[me, 7] + g * 1152
        to = tab[me, 9] + g * 32
        wide = 32 * tab[me, 8]
        last = tab[me, 9] + 4 * wide + g * 16
        for half in range(2):
            for a in range(4):
                parts = swap_lanes(
                    [
                        al[pl.ds(at + 576 * half + 8 * a + b, 16, stride=36), :]
                        for b in range(TP)
                    ]
                )
                for owner in range(TP):
                    row = to + a * wide + 16 * half
                    wire[owner, pl.ds(aligned(row, 16), 16), :] = parts[owner].astype(BF16)
        parts = swap_lanes(
            [
                al[pl.ds(at + 576 * half + 32 + b, 16, stride=36), :]
                for half in range(2)
                for b in range(4)
            ]
        )
        for owner in range(TP):
            wire[owner, pl.ds(aligned(last, 16), 16), :] = parts[owner].astype(BF16)
        return 0

    lax.fori_loop(0, tab[me, 8], mixed_columns, 0)

    @pl.when(me == 0)
    def _():
        for owner in range(TP):
            wire[owner, pl.ds(0, SMALL), :] = al[pl.ds(HALO, SMALL), :].astype(BF16)
        for kind in range(2):
            for n in range(16):
                wire[n % TP, pl.ds(SMALL + 128 * (2 * kind + n // TP), 128), :] = al[
                    pl.ds(HALO + 152 + 2048 * kind + 128 * n, 128), :
                ].astype(BF16)

    copies = [
        pltpu.make_async_copy(wire.at[s ^ k], outs[k], sems.at[2 + k]) for k in range(TP)
    ]
    for copy in copies:
        copy.start()
    for copy in copies:
        copy.wait()


def pack(plan, hd, own, hu):
    total = -(-(HALO * 2 + plan.own_rows) // 672) * 672
    return pl.pallas_call(
        partial(pack_body, plan),
        out_shape=[shape((plan.longest, LANE), BF16)] * TP,
        in_specs=[SMEM, ANY, ANY, VMEM],
        out_specs=[ANY] * TP,
        scratch_shapes=[
            pltpu.VMEM((total, LANE), F32),
            pltpu.VMEM((total, LANE), F32),
            pltpu.VMEM((TP, plan.longest, LANE), BF16),
            pltpu.SemaphoreType.DMA((2 + TP,)),
        ],
        compiler_params=LIMIT,
        name="pack",
    )(jnp.asarray(plan.table), hd, own, hu)


def order_body(plan, *refs):
    pieces, outs, sems = refs[:TP], refs[TP : TP + 4], refs[TP + 4]
    s = lax.axis_index("seq")
    for start in (True, False):
        for number, group in enumerate(plan.groups):
            for source in group:
                size = plan.lengths[source]
                at = int(plan.offsets[source]) - plan.starts[number]
                for k in range(TP):

                    @pl.when((s ^ source) == k)
                    def _():
                        copy = pltpu.make_async_copy(
                            pieces[k].at[pl.ds(0, size)],
                            outs[number].at[pl.ds(at, size)],
                            sems.at[source],
                        )
                        if start:
                            copy.start()
                        else:
                            copy.wait()


def order(plan, pieces):
    return pl.pallas_call(
        partial(order_body, plan),
        out_shape=[shape((rows, LANE), BF16) for rows in plan.rows],
        in_specs=[ANY] * TP,
        out_specs=[VMEM] * 4,
        scratch_shapes=[pltpu.SemaphoreType.DMA((TP,))],
        compiler_params=LIMIT,
        name="order",
    )(*pieces)


def weight_copies(plan, number, weights, halves, b_rows):
    out = []
    for f, row, first, units in plan.pieces("A", plan.groups[number]):
        for target, begin, end in weights.get("A", ()):
            low, high = max(first, begin), min(first + units, end)
            if high > low:
                for n in range(2):
                    out.append(
                        (
                            f,
                            row + 16 * (units * n + low - first),
                            16 * (high - low),
                            target.at[pl.ds(16 * (low - begin), 16 * (high - low)), pl.ds(128 * n, 128)],
                        )
                    )
    for f, row, first, units in plan.pieces("B", plan.groups[number]):
        if b_rows is not None:
            for block in range(12):
                out.append(
                    (
                        f,
                        row + 16 * units * block,
                        16 * units,
                        b_rows.at[block, pl.ds(16 * first, 16 * units)],
                    )
                )
    for f, row, first, units in plan.pieces("C", plan.groups[number]):
        for target, begin, end in weights.get("C", ()):
            low, high = max(first, begin), min(first + units, end)
            if high > low:
                for a in range(4):
                    out.append(
                        (
                            f,
                            row + 32 * (units * a + low - first),
                            32 * (high - low),
                            target.at[pl.ds(32 * (low - begin), 32 * (high - low)), pl.ds(128 * a, 128)],
                        )
                    )
        if halves is not None:
            out.append(
                (f, row + 128 * units, 16 * units, halves.at[pl.ds(16 * first, 16 * units)])
            )
    for f, row, first, units in plan.pieces("D", plan.groups[number]):
        for target, begin, end in weights.get("D", ()):
            for n in range(12):
                out.append(
                    (
                        f,
                        row + 16 * units * n,
                        16 * units,
                        target.at[pl.ds(16 * (first - begin), 16 * units), pl.ds(128 * n, 128)],
                    )
                )
    return out


def fetch_line(plan, line, copies, sems, first=0, phases=(True, False)):
    f = lax.axis_index("fsdp")
    for start in phases:
        for source in range(plan.n_fsdp):
            for away in range(plan.n_fsdp):

                @pl.when((f ^ source) == away)
                def _():
                    for number, (holder, row, rows, target) in enumerate(copies):
                        if holder == source:
                            copy = pltpu.make_async_copy(
                                line[away].at[pl.ds(row, rows)], target, sems.at[first + number]
                            )
                            if start:
                                copy.start()
                            else:
                                copy.wait()


def first_copies(plan, small, gates, w_y, w_x, b_head):
    out = [(0, 0, SMALL, small), (0, SMALL, GATES, gates)]
    out += weight_copies(plan, 0, {"A": ((w_y, 0, 96), (w_x, 96, 192))}, None, None)
    for f, row, first, units in plan.pieces("B", plan.groups[0]):
        out.append((f, row, 192 * units, b_head.at[pl.ds(192 * first, 192 * units)]))
    return out


def first_body(plan, *refs):
    line, refs = refs[: plan.n_fsdp], refs[plan.n_fsdp :]
    *targets, sems = refs
    fetch_line(plan, line, first_copies(plan, *targets), sems)


def head_rows(plan):
    return sum(144 * p[3] for p in plan.pieces("C", plan.groups[1]))


def b_head_rows(plan):
    return sum(192 * p[3] for p in plan.pieces("B", plan.groups[0]))


class Nowhere:
    at = property(lambda self: self)

    def __getitem__(self, _):
        return self


def count_first(plan):
    return len(first_copies(plan, *[Nowhere()] * 5))


def unpack_first(plan, line):
    return pl.pallas_call(
        partial(first_body, plan),
        out_shape=[
            shape((SMALL, LANE), BF16),
            shape((GATES, LANE), BF16),
            shape((D, 256), BF16),
            shape((D, 256), BF16),
            shape((b_head_rows(plan), LANE), BF16),
        ],
        in_specs=[ANY] * len(line),
        out_specs=[VMEM] * 5,
        scratch_shapes=[pltpu.SemaphoreType.DMA((count_first(plan),))],
        compiler_params=LIMIT,
        name="unpack_first",
    )(*line)


def middle_copies(plan, b_rows, head):
    out = weight_copies(plan, 1, {}, None, b_rows)
    for f, row, first, units in plan.pieces("C", plan.groups[1]):
        out.append((f, row, 144 * units, head.at[pl.ds(144 * first, 144 * units)]))
    return out


def b_head_copies(plan, b_head, b_rows):
    out = []
    for _, _, first, units in plan.pieces("B", plan.groups[0]):
        for block in range(12):
            out.append(
                (
                    b_head.at[pl.ds(192 * first + 16 * units * block, 16 * units)],
                    b_rows.at[block, pl.ds(16 * first, 16 * units)],
                )
            )
    return out


def middle_body(plan, *refs):
    line, refs = refs[: plan.n_fsdp], refs[plan.n_fsdp :]
    b_head, outs, head, b_rows, sems, more = refs[0], refs[1 : 1 + TP], *refs[1 + TP :]
    local_copies = [
        pltpu.make_async_copy(source, target, more.at[number])
        for number, (source, target) in enumerate(b_head_copies(plan, b_head, b_rows))
    ]
    for copy in local_copies:
        copy.start()
    fetch_line(plan, line, middle_copies(plan, b_rows, head), sems)
    for copy in local_copies:
        copy.wait()
    s = lax.axis_index("seq")
    for k in range(TP):
        for n in range(2):
            unit = (s ^ k) + TP * n
            for block in range(12):
                outs[k][pl.ds(192 * n + 16 * block, 16), :] = b_rows[
                    block, pl.ds(aligned(16 * unit, 16), 16), :
                ]


def unpack_middle(plan, line, b_head):
    return pl.pallas_call(
        partial(middle_body, plan),
        out_shape=[shape((384, LANE), BF16)] * TP + [shape((head_rows(plan), LANE), BF16)],
        in_specs=[ANY] * (len(line) + 1),
        out_specs=[VMEM] * (TP + 1),
        scratch_shapes=[
            pltpu.VMEM((12, 256, LANE), BF16),
            pltpu.SemaphoreType.DMA((len(middle_copies(plan, *[Nowhere()] * 2)),)),
            pltpu.SemaphoreType.DMA((len(b_head_copies(plan, *[Nowhere()] * 2)),)),
        ],
        compiler_params=LIMIT,
        name="unpack_middle",
    )(*line, b_head)


def head_copies(plan, head, weight, halves):
    out = []
    for _, _, first, units in plan.pieces("C", plan.groups[1]):
        for a in range(4):
            out.append(
                (
                    head.at[pl.ds(144 * first + 32 * units * a, 32 * units)],
                    weight.at[pl.ds(32 * first, 32 * units), pl.ds(128 * a, 128)],
                )
            )
        out.append(
            (
                head.at[pl.ds(144 * first + 128 * units, 16 * units)],
                halves.at[pl.ds(16 * first, 16 * units)],
            )
        )
    return out


def second_copies(plan, w_gate, w_up, w_down, halves):
    return weight_copies(
        plan,
        2,
        {"C": ((w_gate, 0, 48), (w_up, 48, 96)), "D": ((w_down, 0, 16),)},
        halves,
        None,
    )


def halves_copies(plan, halves):
    return [
        (f, row + 128 * units, 16 * units, halves.at[pl.ds(16 * first, 16 * units)])
        for f, row, first, units in plan.pieces("C", plan.groups[2])
    ]


def second_body(plan, *refs):
    line, refs = refs[: plan.n_fsdp], refs[plan.n_fsdp :]
    head, w_gate, w_up, w_down, halves, sems, more = refs
    local_copies = [
        pltpu.make_async_copy(source, target, more.at[number])
        for number, (source, target) in enumerate(head_copies(plan, head, w_gate, halves))
    ]
    for copy in local_copies:
        copy.start()
    merged = halves_copies(plan, halves)
    whole = second_copies(plan, w_gate, w_up, w_down, None)
    fetch_line(plan, line, merged, sems, 0, (True,))
    fetch_line(plan, line, whole, sems, len(merged), (True,))
    fetch_line(plan, line, merged, sems, 0, (False,))
    for copy in local_copies:
        copy.wait()
    for weight, begin in ((w_gate, 0), (w_up, 48)):

        def step(g, _):
            last = halves[pl.ds(aligned(16 * (begin + g), 16), 16), :]
            weight[pl.ds(aligned(32 * g, 16), 16), pl.ds(512, 64)] = last[:, :64]
            weight[pl.ds(aligned(32 * g + 16, 16), 16), pl.ds(512, 64)] = last[:, 64:]
            return 0

        lax.fori_loop(0, 48, step, 0, unroll=8)
    fetch_line(plan, line, whole, sems, len(merged), (False,))


def unpack_second(plan, line, head):
    many = len(second_copies(plan, *[Nowhere()] * 4))
    few = len(head_copies(plan, *[Nowhere()] * 3))
    return pl.pallas_call(
        partial(second_body, plan),
        out_shape=[
            shape((D, FF // TP), BF16),
            shape((D, FF // TP), BF16),
            shape((256, D), BF16),
        ],
        in_specs=[ANY] * (len(line) + 1),
        out_specs=[VMEM] * 3,
        scratch_shapes=[
            pltpu.VMEM((96 * 16, LANE), BF16),
            pltpu.SemaphoreType.DMA((many,)),
            pltpu.SemaphoreType.DMA((few,)),
        ],
        compiler_params=LIMIT,
        name="unpack_second",
    )(*line, head)


def third_copies(plan, w_down):
    return weight_copies(plan, 3, {"D": ((w_down, 0, 36),)}, None, None)


def third_body(plan, *refs):
    line, refs = refs[: plan.n_fsdp], refs[plan.n_fsdp :]
    before, w_down, sems, one = refs
    copy = pltpu.make_async_copy(before, w_down.at[pl.ds(0, 256)], one.at[0])
    copy.start()
    fetch_line(plan, line, third_copies(plan, w_down), sems)
    copy.wait()


def unpack_third(plan, line, before):
    many = len(third_copies(plan, Nowhere()))
    return pl.pallas_call(
        partial(third_body, plan),
        out_shape=shape((FF // TP, D), BF16),
        in_specs=[ANY] * (len(line) + 1),
        out_specs=VMEM,
        scratch_shapes=[
            pltpu.SemaphoreType.DMA((many,)),
            pltpu.SemaphoreType.DMA((1,)),
        ],
        compiler_params=LIMIT,
        name="unpack_third",
    )(*line, before)


def out_rows_body(*refs):
    pieces, w_out = refs[:TP], refs[TP]
    s = lax.axis_index("seq")
    for k in range(TP):
        for n in range(2):
            to = aligned(128 * n + 16 * (s ^ k), 16)
            for block in range(12):
                w_out[pl.ds(to, 16), pl.ds(128 * block, 128)] = pieces[k][
                    pl.ds(192 * n + 16 * block, 16), :
                ]


def join_out_rows(pieces):
    return pl.pallas_call(
        out_rows_body,
        out_shape=shape((256, D), BF16),
        in_specs=[VMEM] * TP,
        out_specs=VMEM,
        compiler_params=LIMIT,
        name="join_out_rows",
    )(*pieces)


def split_rows_body(grad, *pieces):
    s = lax.axis_index("seq")
    for k in range(TP):
        for n in range(2):
            at = aligned(128 * n + 16 * (s ^ k), 16)
            for block in range(12):
                pieces[k][pl.ds(192 * n + 16 * block, 16), :] = grad[
                    pl.ds(at, 16), pl.ds(128 * block, 128)
                ]


def split_out_rows(grad):
    return pl.pallas_call(
        split_rows_body,
        out_shape=[shape((384, LANE), F32)] * TP,
        in_specs=[VMEM],
        out_specs=[VMEM] * TP,
        compiler_params=LIMIT,
        name="split_out_rows",
    )(grad)


def start_copies(copies, sems, first=0):
    made = [
        pltpu.make_async_copy(source, target, sems.at[first + number])
        for number, (source, target) in enumerate(copies)
    ]
    for copy in made:
        copy.start()
    return made


def to_wires(plan, copies, wires, sems, first, start):
    f = lax.axis_index("fsdp")
    for j in range(plan.n_fsdp):
        for x in range(plan.n_fsdp):

            @pl.when((f ^ j) == x)
            def _():
                for number, (holder, row, rows, source) in enumerate(copies):
                    if holder == j:
                        copy = pltpu.make_async_copy(
                            source, wires[x].at[pl.ds(row, rows)], sems.at[first + number]
                        )
                        if start:
                            copy.start()
                        else:
                            copy.wait()


def wire_second_body(plan, g_gate, g_up, g_down, *refs):
    wires, (head, halves, sems) = refs[: plan.n_fsdp], refs[plan.n_fsdp :]
    whole = second_copies(plan, g_gate, g_up, g_down, None)
    merged = halves_copies(plan, halves)
    more = [(b, a) for a, b in head_copies(plan, head, g_gate, halves)]
    to_wires(plan, whole, wires, sems, 0, True)
    for grad, begin in ((g_gate, 0), (g_up, 48)):

        def step(g, _):
            left = grad[pl.ds(aligned(32 * g, 16), 16), pl.ds(512, 64)]
            right = grad[pl.ds(aligned(32 * g + 16, 16), 16), pl.ds(512, 64)]
            halves[pl.ds(aligned(16 * (begin + g), 16), 16), :] = jnp.concatenate(
                [left, right], axis=1
            )
            return 0

        lax.fori_loop(0, 48, step, 0, unroll=8)
    to_wires(plan, merged, wires, sems, len(whole), True)
    made = start_copies(more, sems, len(whole) + len(merged))
    to_wires(plan, whole, wires, sems, 0, False)
    to_wires(plan, merged, wires, sems, len(whole), False)
    for copy in made:
        copy.wait()


def wire_second(plan, g_gate, g_up, g_down):
    many = len(second_copies(plan, *[Nowhere()] * 4)) + len(
        head_copies(plan, *[Nowhere()] * 3)
    )
    out = pl.pallas_call(
        partial(wire_second_body, plan),
        out_shape=[shape((plan.rows[2], LANE), F32)] * plan.n_fsdp
        + [shape((head_rows(plan), LANE), F32)],
        in_specs=[VMEM] * 3,
        out_specs=[ANY] * (plan.n_fsdp + 1),
        scratch_shapes=[
            pltpu.VMEM((96 * 16, LANE), F32),
            pltpu.SemaphoreType.DMA((many,)),
        ],
        compiler_params=LIMIT,
        name="wire_second",
    )(g_gate, g_up, g_down)
    return out[:-1], out[-1]


def wire_plain(plan, copies_of, rows, operands):
    many = len(copies_of(*[Nowhere()] * len(operands)))

    def body(*refs):
        *refs, sems = refs
        sources, wires = refs[: len(operands)], refs[len(operands) :]
        copies = copies_of(*sources)
        to_wires(plan, copies, wires, sems, 0, True)
        to_wires(plan, copies, wires, sems, 0, False)

    return pl.pallas_call(
        body,
        out_shape=[shape((rows, LANE), F32)] * plan.n_fsdp,
        in_specs=[VMEM] * len(operands),
        out_specs=[ANY] * plan.n_fsdp,
        scratch_shapes=[pltpu.SemaphoreType.DMA((many,))],
        compiler_params=LIMIT,
    )(*operands)


def wire_third(plan, g_down):
    return wire_plain(plan, partial(third_copies, plan), plan.rows[3], (g_down,))


def wire_middle_body(plan, head, *refs):
    pieces, refs = refs[:TP], refs[TP:]
    wires, (b_head, b_rows, sems) = refs[: plan.n_fsdp], refs[plan.n_fsdp :]
    s = lax.axis_index("seq")
    for k in range(TP):
        for n in range(2):
            unit = (s ^ k) + TP * n
            for block in range(12):
                b_rows[block, pl.ds(aligned(16 * unit, 16), 16), :] = pieces[k][
                    pl.ds(192 * n + 16 * block, 16), :
                ]
    copies = middle_copies(plan, b_rows, head)
    to_wires(plan, copies, wires, sems, 0, True)
    more = [(b, a) for a, b in b_head_copies(plan, b_head, b_rows)]
    made = start_copies(more, sems, len(copies))
    to_wires(plan, copies, wires, sems, 0, False)
    for copy in made:
        copy.wait()


def wire_middle(plan, head, pieces):
    many = len(middle_copies(plan, *[Nowhere()] * 2)) + len(
        b_head_copies(plan, *[Nowhere()] * 2)
    )
    out = pl.pallas_call(
        partial(wire_middle_body, plan),
        out_shape=[shape((plan.rows[1], LANE), F32)] * plan.n_fsdp
        + [shape((b_head_rows(plan), LANE), F32)],
        in_specs=[VMEM] * (1 + TP),
        out_specs=[ANY] * (plan.n_fsdp + 1),
        scratch_shapes=[
            pltpu.VMEM((12, 256, LANE), F32),
            pltpu.SemaphoreType.DMA((many,)),
        ],
        compiler_params=LIMIT,
        name="wire_middle",
    )(head, *pieces)
    return out[:-1], out[-1]


def split_copies(plan, copies):
    border = int(plan.offsets[1])
    return (
        [copy for copy in copies if copy[1] < border],
        [(f, row - border, rows, at) for f, row, rows, at in copies if row >= border],
    )


def wire_x(plan, g_x, b_head):
    def copies_of(g_x, b_head):
        nowhere = Nowhere()
        return split_copies(plan, first_copies(plan, nowhere, nowhere, nowhere, g_x, b_head))[1]

    return wire_plain(plan, copies_of, plan.lengths[1], (g_x, b_head))


def wire_y_body(plan, gains, vectors, gates, g_y, g_x, *refs):
    wires, (small, sems) = refs[: plan.n_fsdp], refs[plan.n_fsdp :]
    s = lax.axis_index("seq")
    small[...] = jnp.zeros_like(small)
    small[pl.ds(0, 24), :] = gains[...]
    for n in range(8):
        for part in range(2):
            small[pl.ds(24 + 16 * n + s + TP * part, 1), :] = vectors[
                pl.ds(2 * n + part, 1), :
            ]
    copies = split_copies(plan, first_copies(plan, small, gates, g_y, g_x, Nowhere()))[0]
    to_wires(plan, copies, wires, sems, 0, True)
    to_wires(plan, copies, wires, sems, 0, False)


def wire_y(plan, gains, vectors, gates, g_y, g_x):
    return pl.pallas_call(
        partial(wire_y_body, plan),
        out_shape=[shape((plan.lengths[0], LANE), F32)] * plan.n_fsdp,
        in_specs=[VMEM] * 5,
        out_specs=[ANY] * plan.n_fsdp,
        scratch_shapes=[
            pltpu.VMEM((SMALL, LANE), F32),
            pltpu.SemaphoreType.DMA((count_first(plan),)),
        ],
        compiler_params=LIMIT,
        name="wire_y",
    )(gains, vectors, gates, g_y, g_x)


def spread_body(plan, targets, *refs):
    count = len(targets)
    sums, outs, sems = refs[:count], refs[count : count + TP], refs[count + TP]
    s = lax.axis_index("seq")
    for start in (True, False):
        for summed, group in zip(sums, targets):
            for target in group:
                size = plan.lengths[target]
                at = int(plan.offsets[target] - plan.offsets[group[0]])
                for k in range(TP):

                    @pl.when((s ^ target) == k)
                    def _():
                        copy = pltpu.make_async_copy(
                            summed.at[pl.ds(at, size)],
                            outs[k].at[pl.ds(0, size)],
                            sems.at[target],
                        )
                        if start:
                            copy.start()
                        else:
                            copy.wait()


def spread(plan, targets, sums):
    rows = max(plan.lengths[s] for group in targets for s in group)
    return pl.pallas_call(
        partial(spread_body, plan, targets),
        out_shape=[shape((rows, LANE), F32)] * TP,
        in_specs=[VMEM] * len(sums),
        out_specs=[ANY] * TP,
        scratch_shapes=[pltpu.SemaphoreType.DMA((TP,))],
        compiler_params=LIMIT,
    )(*sums)


def shift_up(source, source_row, target, target_row, rows, block, amount):
    def step(j, _):
        both = pltpu.roll(source[pl.ds(source_row + j * block, block + 8), :], amount, 1)
        below = pltpu.roll(both, block + 7, 0)[:block]
        target[pl.ds(target_row + j * block, block), :] = jnp.where(
            lanes(block) < amount, both[:block], below
        )
        return 0

    lax.fori_loop(0, rows // block, step, 0, unroll=True)


def collect_body(plan, tab, *refs):
    pieces, (own, hd, hu, al, win, wire, sems) = refs[: 3 * TP], refs[3 * TP :]
    s, f = lax.axis_index("seq"), lax.axis_index("fsdp")
    me = s * plan.n_fsdp + f

    def bring(start):
        for number, (low, high) in enumerate(((0, 0), (1, 2), (3, TP - 1))):

            @pl.when((s >= low) & (s <= high))
            def _():
                for k in range(TP):
                    piece = pieces[TP * number + k]
                    copy = pltpu.make_async_copy(
                        piece, wire.at[s ^ k, pl.ds(0, piece.shape[0])], sems.at[k]
                    )
                    if start:
                        copy.start()
                    else:
                        copy.wait()

    bring(True)
    total = win.shape[0]

    def clear(j, _):
        al[pl.ds(aligned(j * 96, 8), 96), :] = jnp.zeros((96, LANE), F32)
        return 0

    lax.fori_loop(0, al.shape[0] // 96, clear, 0, unroll=4)
    bring(False)

    def columns(g, _):
        at = tab[me, 1] + g * 256
        to = tab[me, 3] + g * 16
        for block in range(16):
            row = to + 16 * tab[me, 2] * (block // TP)
            al[pl.ds(at + block, 16, stride=16), :] = wire[
                block % TP, pl.ds(aligned(row, 16), 16), :
            ]
        return 0

    lax.fori_loop(0, tab[me, 2], columns, 0)
    for slot in (4, 10):

        def grouped(j, _):
            for owner in range(TP):
                at = tab[me, slot] + j * 1536 + owner * 192
                to = tab[me, slot + 2] + j * 16
                for block in range(12):
                    row = to + 16 * tab[me, slot + 1] * block
                    al[pl.ds(at + block, 16, stride=12), :] = wire[
                        owner, pl.ds(aligned(row, 16), 16), :
                    ]
            return 0

        lax.fori_loop(0, tab[me, slot + 1], grouped, 0)

    def mixed_columns(g, _):
        at = tab[me, 7] + g * 1152
        to = tab[me, 9] + g * 32
        wide = 32 * tab[me, 8]
        last = tab[me, 9] + 4 * wide + g * 16
        for half in range(2):
            for a in range(4):
                parts = swap_lanes(
                    [
                        wire[owner, pl.ds(aligned(to + a * wide + 16 * half, 16), 16), :]
                        for owner in range(TP)
                    ]
                )
                for b in range(TP):
                    al[pl.ds(at + 576 * half + 8 * a + b, 16, stride=36), :] = parts[b]
        parts = swap_lanes(
            [wire[owner, pl.ds(aligned(last, 16), 16), :] for owner in range(TP)]
        )
        for half in range(2):
            for b in range(4):
                al[pl.ds(at + 576 * half + 32 + b, 16, stride=36), :] = parts[4 * half + b]
        return 0

    lax.fori_loop(0, tab[me, 8], mixed_columns, 0)

    @pl.when(me == 0)
    def _():
        summed = wire[0, pl.ds(0, 152), :]
        for owner in range(1, TP):
            summed = summed + wire[owner, pl.ds(0, 152), :]
        al[pl.ds(HALO, 152), :] = summed
        for kind in range(2):
            for n in range(16):
                al[pl.ds(HALO + 152 + 2048 * kind + 128 * n, 128), :] = wire[
                    n % TP, pl.ds(SMALL + 128 * (2 * kind + n // TP), 128), :
                ]

    def back(j, _):
        both = pltpu.roll(
            al[pl.ds(aligned(j * 48, 8), 56), :], lax.rem(LANE - tab[me, 0], LANE), 1
        )
        below = pltpu.roll(both, 55, 0)[:48]
        win[pl.ds(aligned(j * 48, 8), 48), :] = jnp.where(
            lanes(48) < LANE - tab[me, 0], both[:48], below
        )
        return 0

    lax.fori_loop(0, total // 48, back, 0, unroll=7)
    hd[...] = win[pl.ds(0, HALO), :]
    own[...] = win[pl.ds(HALO, plan.own_rows), :]
    shift_up(win, HALO + plan.last, hu, 0, HALO, 32, LANE - plan.part)


def collect(plan, pieces):
    total = -(-(HALO * 2 + plan.own_rows) // 672) * 672
    cleared = total + 96
    return pl.pallas_call(
        partial(collect_body, plan),
        out_shape=[
            shape((plan.own_rows, LANE), F32),
            shape((HALO, LANE), F32),
            shape((HALO, LANE), F32),
        ],
        in_specs=[SMEM] + [ANY] * (3 * TP),
        out_specs=[VMEM] * 3,
        scratch_shapes=[
            pltpu.VMEM((cleared, LANE), F32),
            pltpu.VMEM((total, LANE), F32),
            pltpu.VMEM((TP, plan.longest, LANE), F32),
            pltpu.SemaphoreType.DMA((TP,)),
        ],
        compiler_params=LIMIT,
        name="collect",
    )(jnp.asarray(plan.table), *pieces)


def tail_body(plan, value, out):
    first = (plan.last - HALO) % 8
    out[...] = jnp.zeros_like(out)
    shift_down(value, 0, out, first, HALO, 32, plan.part, True)
    z = pltpu.roll(value[pl.ds(HALO - 8, 8), :], plan.part, 1)
    row = lax.broadcasted_iota(jnp.int32, (8, LANE), 0)
    out[pl.ds(first + HALO, 8), :] = jnp.where(
        (row == 0) & (lanes(8) < plan.part), pltpu.roll(z, 1, 0), 0.0
    )


def place_tail(plan, value):
    rows = plan.own_rows - (plan.last - HALO) // 8 * 8
    return pl.pallas_call(
        partial(tail_body, plan),
        out_shape=shape((max(rows, HALO + 16), LANE), F32),
        in_specs=[VMEM],
        out_specs=VMEM,
        compiler_params=LIMIT,
        name="place_tail",
    )(value)[:rows]


def scan_body(reverse, coefficient, addend, out):
    rows, width = coefficient.shape
    at = lax.broadcasted_iota(jnp.int32, (8, width), 0)
    if reverse:
        at = 7 - at
    steps = rows // 8

    def step(j, carry):
        block = steps - 1 - j if reverse else j
        here = pl.ds(aligned(block * 8, 8), 8)
        a, b = coefficient[here, :], addend[here, :]
        for reach in (1, 2, 4):
            turn = 8 - reach if reverse else reach
            inside = at >= reach
            b = b + jnp.where(inside, a * pltpu.roll(b, turn, 0), 0.0)
            a = jnp.where(inside, a * pltpu.roll(a, turn, 0), a)
        value = b + a * carry
        out[here, :] = value
        edge = value[0:1] if reverse else value[7:8]
        return jnp.broadcast_to(edge, (8, width))

    lax.fori_loop(0, steps, step, jnp.zeros((8, width), F32), unroll=4)


def linear_scan(coefficient, addend, reverse):
    return pl.pallas_call(
        partial(scan_body, reverse),
        out_shape=shape(coefficient.shape, F32),
        in_specs=[VMEM] * 2,
        out_specs=VMEM,
        compiler_params=LIMIT,
        name="scan_back" if reverse else "scan",
    )(coefficient, addend)


def swap(value, bit):
    return lax.ppermute(value, "seq", [(i, i ^ bit) for i in range(TP)])


def exchange(pieces, targets=range(TP)):
    return [pieces[0]] + [
        lax.ppermute(pieces[k], "seq", [(i ^ k, i) for i in targets]) for k in range(1, TP)
    ]


def join_body(*refs):
    *pieces, out, sems = refs
    copies, at = [], 0
    for number, piece in enumerate(pieces):
        rows = piece.shape[0]
        copies.append(
            pltpu.make_async_copy(piece, out.at[pl.ds(at, rows)], sems.at[number])
        )
        at += rows
    for copy in copies:
        copy.start()
    for copy in copies:
        copy.wait()


def join(pieces):
    rows = sum(piece.shape[0] for piece in pieces)
    return pl.pallas_call(
        join_body,
        out_shape=shape((rows, pieces[0].shape[1]), pieces[0].dtype),
        in_specs=[ANY] * len(pieces),
        out_specs=VMEM,
        scratch_shapes=[pltpu.SemaphoreType.DMA((len(pieces),))],
        compiler_params=LIMIT,
    )(*pieces)


def gather_stream(mine, whole=False):
    half = mine.shape[0] // 2

    over_x, over_y = swap(mine, 2), swap(mine, 4)
    over_xy = [swap(over_x[:half], 4), swap(over_y[half:], 2)]
    chip = [mine, over_x, over_y] + over_xy
    if whole:
        chip = [join(chip)]
    return join(chip + [swap(part, 1) for part in chip])


def scatter_stream(partial_sums):
    rows = partial_sums.shape[0] // TP
    half = rows // 2

    def send(value, bit):
        return swap(value.astype(BF16), bit).astype(F32)

    other = send(partial_sums[TP // 2 * rows :], 1)
    q = (partial_sums[: TP // 2 * rows] + other).reshape(4, rows, -1)
    up = send(jnp.concatenate([q[1, :half], q[3, :half]]), 2)
    down = send(jnp.concatenate([q[2, half:], q[3, half:]]), 4)
    top = send(q[2, :half] + up[half:], 4)
    low = send(q[1, half:] + down[half:], 2)
    return jnp.concatenate(
        [q[0, :half] + up[:half] + top, q[0, half:] + down[:half] + low], axis=0
    )


def to_positions(values, s):
    rows = values.shape[0] // TP
    parts = []
    for j in range(TP):
        k = s ^ j
        at = (k // 2 + 4 * (k % 2)) * rows
        parts.append(lax.dynamic_slice_in_dim(values, at, rows, 0))
    return jnp.concatenate(parts, axis=0)


def to_relative(values, s):
    rows = values.shape[0] // TP
    return jnp.concatenate(
        [lax.dynamic_slice_in_dim(values, (s ^ k) * rows, rows, 0) for k in EVEN_FIRST], axis=0
    )


def gather_line(value, count):
    def send(value, bit):
        return lax.ppermute(value, "fsdp", [(i, i ^ bit) for i in range(count)])

    opposite, near = send(value, 3), send(value, 1)
    return [value, near, send(opposite, 1), opposite]


def scatter_line(blocks):
    count = len(blocks)
    own, near, far, cross = blocks
    far = lax.ppermute(far, "fsdp", [(i, i ^ 1) for i in range(count)])
    near = lax.ppermute(near, "fsdp", [(i, i ^ 1) for i in range(count)])
    cross = lax.ppermute(cross + far, "fsdp", [(i, i ^ 3) for i in range(count)])
    return own + near + cross


def sliced(plan, *arguments):
    return sliced_step(plan, *arguments)


def sliced_step(plan, stream_in, cotangent, starts, params, momentum, average):
    n_fsdp = plan.n_fsdp
    s = lax.axis_index("seq")
    shards = TP * n_fsdp
    onward = [(i, i + 1) for i in range(shards - 1)]
    backward = [(i + 1, i) for i in range(shards - 1)]
    both = ("seq", "fsdp")
    edge = HALO * LANE
    per = plan.per

    hd, hu = lax.optimization_barrier((params[per - edge :], params[:edge]))
    hd = lax.ppermute(hd.astype(BF16), both, onward)
    hu = lax.ppermute(hu.astype(BF16), both, backward)
    own = jnp.pad(params, (0, plan.own_rows * LANE - per)).reshape(-1, LANE)
    pieces = pack(
        plan, hd.astype(F32).reshape(-1, LANE), own, hu.astype(F32).reshape(-1, LANE)
    )
    first, middle_wire, second, third = order(plan, exchange(pieces))
    stream_bf, cotangent_bf, first = lax.optimization_barrier(
        (stream_in[0], cotangent[0], first)
    )
    line = gather_line(first, n_fsdp)
    middle_wire, second, third, line = lax.optimization_barrier(
        (middle_wire, second, third, line)
    )
    small, gates, w_y, w_x, b_head = unpack_first(plan, line)
    line = gather_line(middle_wire, n_fsdp)
    *out_rows, head = unpack_middle(plan, line, b_head)
    w_out = join_out_rows(exchange(out_rows))
    line = gather_line(second, n_fsdp)
    w_gate, w_up, w_down = unpack_second(plan, line, head)
    w_down = unpack_third(plan, gather_line(third, n_fsdp), w_down)

    mine = stream_in[0].astype(F32)
    stream = gather_stream(stream_bf)
    stream = stream.astype(F32)
    grad_out = gather_stream(cotangent_bf, True)
    rows = stream.shape[0]

    small = small.astype(F32)
    gain_one = small[0:12].reshape(-1)
    gain_two = small[12:24].reshape(-1)

    def channels(at):
        return jnp.concatenate(
            [
                lax.dynamic_slice_in_dim(small, at + s, 1, 0),
                lax.dynamic_slice_in_dim(small, at + s + TP, 1, 0),
            ],
            axis=1,
        )[0]

    conv_bias, bias_a, bias_i, lambda_raw = (channels(24 + 16 * j) for j in range(4))
    conv_weight = jnp.stack([channels(88 + 16 * j) for j in range(KW)])

    positions = jnp.arange(rows, dtype=jnp.int32)
    ext_pos = jnp.arange(rows + KW - 1, dtype=jnp.int32) - (KW - 1)
    segment_ext = segment_ids(ext_pos, starts[0])
    starting = start_flags(positions, starts[0])[:, None]

    def gate_product(values, at):
        return jnp.concatenate(
            [matmul(values[:, :HB], gates[at : at + HB]), matmul(values[:, HB:], gates[at + HB : at + 2 * HB])],
            axis=1,
        )

    def gate_product_t(values, at):
        return jnp.concatenate(
            [matmul_t(values[:, :HB], gates[at : at + HB]), matmul_t(values[:, HB:], gates[at + HB : at + 2 * HB])],
            axis=1,
        )

    normed = rms_norm(stream, gain_one).astype(BF16)
    branch_y = matmul(normed, w_y)
    branch_x = matmul(normed, w_x).astype(BF16)
    branch_y = to_positions(branch_y, s)
    branch_x = to_positions(branch_x, s)
    extended = jnp.pad(branch_x, ((KW - 1, 0), (0, 0))).astype(F32)

    def convolve_here(extended, weight, bias):
        total = jnp.zeros((rows, bias.shape[0]), F32) + bias
        for lag in range(KW):
            source = extended[KW - 1 - lag : KW - 1 - lag + rows]
            same = segment_ext[KW - 1 - lag : KW - 1 - lag + rows] == segment_ext[KW - 1 :]
            total = total + weight[lag] * source * same.astype(F32)[:, None]
        return total

    conv_out = convolve_here(extended, conv_weight, conv_bias).astype(BF16)
    conv_val = conv_out.astype(F32)
    pre_a = gate_product(conv_out, 0) + bias_a
    pre_i = gate_product(conv_out, 2 * HB) + bias_i
    decay, drive = gate_terms(pre_a, pre_i, conv_val, lambda_raw, starting)
    state = linear_scan(decay, drive, False)
    gelu_y = jax.nn.gelu(branch_y, approximate=True)
    mixed = to_relative((state * gelu_y).astype(BF16), s)
    middle = mine + scatter_stream(matmul(mixed, w_out))
    normed_two_mine = rms_norm(middle, gain_two).astype(BF16)
    normed_two = gather_stream(normed_two_mine)
    gate = matmul(normed_two, w_gate)
    upward = matmul(normed_two, w_up)
    hidden = gelu_product(gate, upward).astype(BF16)
    g_down = t_matmul(hidden, grad_out)
    summed_three = scatter_line(wire_third(plan, g_down))
    out_sums = matmul(hidden, w_down)
    output = (middle + scatter_stream(out_sums)).astype(BF16)
    gate, upward, _ = lax.optimization_barrier((gate, upward, hidden))

    grad_hidden = matmul_t(grad_out, w_down)
    _, product_back = jax.vjp(gelu_product, gate, upward)
    grad_gate, grad_up = product_back(grad_hidden)
    grad_gate, grad_up = grad_gate.astype(BF16), grad_up.astype(BF16)
    g_gate = t_matmul(normed_two, grad_gate)
    g_up = t_matmul(normed_two, grad_up)
    grad_normed_two = scatter_stream(matmul_t(grad_gate, w_gate) + matmul_t(grad_up, w_up))
    wire_two, wire_head = wire_second(plan, g_gate, g_up, g_down)
    summed_two = scatter_line(wire_two)

    _, norm_back_two = jax.vjp(rms_norm, middle, gain_two)
    grad_middle_part, g_gain_two = norm_back_two(grad_normed_two)
    grad_middle = cotangent[0].astype(F32) + grad_middle_part
    grad_first = gather_stream(grad_middle.astype(BF16))
    g_out = t_matmul(mixed, grad_first)
    wire_mid, b_head = wire_middle(plan, wire_head, exchange(split_out_rows(g_out)))
    summed_mid = scatter_line(wire_mid)
    grad_mixed = to_positions(matmul_t(grad_first, w_out), s)
    _, gelu_back = jax.vjp(partial(jax.nn.gelu, approximate=True), branch_y)
    grad_y = gelu_back(grad_mixed * state)[0].astype(BF16)
    next_decay = jnp.concatenate([decay[1:], jnp.ones((1, decay.shape[1]), F32)], axis=0)
    adjoint = linear_scan(next_decay, grad_mixed * gelu_y, True)
    previous = jnp.concatenate([jnp.zeros((1, decay.shape[1]), F32), state[:-1]], axis=0)
    _, gates_back = jax.vjp(gate_terms, pre_a, pre_i, conv_val, lambda_raw, starting)
    grad_pre_a, grad_pre_i, grad_direct, g_lambda, _ = gates_back((adjoint * previous, adjoint))
    grad_pre_a, grad_pre_i = grad_pre_a.astype(BF16), grad_pre_i.astype(BF16)
    g_gates = jnp.concatenate(
        [
            t_matmul(conv_out[:, n : n + HB], grad[:, n : n + HB])
            for grad in (grad_pre_a, grad_pre_i)
            for n in (0, HB)
        ],
        axis=0,
    )
    g_bias_a = jnp.sum(grad_pre_a.astype(F32), axis=0)
    g_bias_i = jnp.sum(grad_pre_i.astype(F32), axis=0)
    grad_conv = grad_direct + gate_product_t(grad_pre_a, 0) + gate_product_t(grad_pre_i, 2 * HB)
    _, conv_back = jax.vjp(convolve_here, extended, conv_weight, conv_bias)
    grad_ext, g_conv_weight, g_conv_bias = conv_back(grad_conv)
    grad_x = to_relative(grad_ext[KW - 1 :].astype(BF16), s)
    grad_y = to_relative(grad_y, s)
    g_x = t_matmul(normed, grad_x)
    g_y = t_matmul(normed, grad_y)
    grad_normed = scatter_stream(matmul_t(grad_y, w_y) + matmul_t(grad_x, w_x))
    _, norm_back_one = jax.vjp(rms_norm, mine, gain_one)
    grad_stream_part, g_gain_one = norm_back_one(grad_normed)
    input_grad = grad_middle + grad_stream_part

    summed_x = scatter_line(wire_x(plan, g_x, b_head))
    gains = jnp.concatenate([g_gain_one, g_gain_two]).reshape(-1, LANE)
    vectors = jnp.stack(
        [g_conv_bias, g_bias_a, g_bias_i, g_lambda] + [g_conv_weight[k] for k in range(KW)]
    ).reshape(-1, LANE)
    summed_y = scatter_line(wire_y(plan, gains, vectors, g_gates, g_y, g_x))
    early = spread(plan, plan.groups[2:], (summed_two, summed_three))
    middle_set = spread(plan, ((1,), (2,)), (summed_x, summed_mid))
    got = exchange(spread(plan, ((0,),), (summed_y,)), (0,))
    got += exchange(middle_set, (1, 2))
    got += exchange(early)
    grad_own, grad_hd, grad_hu = collect(plan, got)
    from_next = lax.ppermute(grad_hd, both, backward)
    from_before = lax.ppermute(grad_hu, both, onward)
    tail = place_tail(plan, from_next).reshape(-1)
    whole = plan.own_rows * LANE
    summed = (
        grad_own.reshape(-1)
        + jnp.pad(from_before.reshape(-1), (0, whole - edge))
        + jnp.pad(tail, (whole - tail.shape[0], 0))
    )[:per]
    new_moment = MOMENT * momentum + summed
    new_params = params - RATE * (summed + MOMENT * new_moment)
    new_average = BLEND * average + (1.0 - BLEND) * new_params
    return (output[None], input_grad[None], new_params, new_moment, new_average)


def solution(mesh):
    n_seq, n_fsdp = mesh.shape["seq"], mesh.shape["fsdp"]
    fast = (n_seq, n_fsdp) == (TP, 4)
    body = partial(sliced, Plan(n_seq, n_fsdp)) if fast else local
    return jax.shard_map(
        body,
        mesh=mesh,
        in_specs=(
            P("fsdp", "seq", None),
            P("fsdp", "seq", None),
            P("fsdp", None),
            P(("seq", "fsdp")),
            P(("seq", "fsdp")),
            P(("seq", "fsdp")),
        ),
        out_specs=(
            P("fsdp", "seq", None),
            P("fsdp", "seq", None),
            P(("seq", "fsdp")),
            P(("seq", "fsdp")),
            P(("seq", "fsdp")),
        ),
        check_vma=False,
    )
```

```python
from functools import partial
import math

import jax
import jax.numpy as jnp
import numpy as np
from jax import lax
from jax.experimental import pallas as pl
from jax.experimental.pallas import tpu as pltpu
from jax.sharding import PartitionSpec as P


D = 1536
LRU = 2048
FF = 4608
HB = 128
KW = 4


EPS = 1e-06
RATE = 3e-05
MOMENT = 0.9
BLEND = 0.9
DECAY_SCALE = 8.0


def shifted(block, axis, distance):
    devices = range(lax.axis_size(axis))
    route = [(i - distance, i) for i in devices if i - distance in devices]
    return lax.ppermute(block, axis, route)


def carried_in(value, axis, join, neutral, backward):
    count, mine = (lax.axis_size(axis), lax.axis_index(axis))
    pieces = jax.tree.map(lambda part: lax.all_gather(part, axis), value)
    if backward:
        pieces = jax.tree.map(lambda part: part[::-1], pieces)
        mine = count - 1 - mine
    so_far = jax.tree.map(
        lambda part, zero: jnp.full_like(part, 0) + jnp.asarray(zero, part.dtype), value, neutral
    )

    def lap(position, so_far):
        longer = join(so_far, jax.tree.map(lambda part: part[position], pieces))
        return jax.tree.map(lambda new, old: jnp.where(position < mine, new, old), longer, so_far)

    return lax.fori_loop(0, count - 1, lap, so_far)


def layout():
    return [
        ("gain_one", (D,)),
        ("gain_two", (D,)),
        ("conv_bias", (LRU,)),
        ("bias_a", (LRU,)),
        ("bias_i", (LRU,)),
        ("lambda_raw", (LRU,)),
        ("conv_weight", (KW, LRU)),
        ("gate_a", (LRU // HB, HB, HB)),
        ("gate_i", (LRU // HB, HB, HB)),
        ("w_y", (D, LRU)),
        ("w_x", (D, LRU)),
        ("w_out", (LRU, D)),
        ("w_gate", (D, FF)),
        ("w_up", (D, FF)),
        ("w_down", (FF, D)),
    ]


def unpack(packed):
    result = {}
    offset = 0
    for entry_name, entry_shape in layout():
        amount = math.prod(entry_shape)
        result[entry_name] = packed[offset : offset + amount].reshape(entry_shape)
        offset += amount
    return result


def matmul(left, right):
    return jnp.dot(left, right, preferred_element_type=jnp.float32)


def matmul_t(left, right):
    return lax.dot_general(
        left, right, (((1,), (1,)), ((), ())), preferred_element_type=jnp.float32
    )


def t_matmul(left, right):
    return lax.dot_general(
        left, right, (((0,), (0,)), ((), ())), preferred_element_type=jnp.float32
    )


def blocked(values, weight):
    shaped = values.reshape(values.shape[0], LRU // HB, HB)
    return jnp.einsum("tnh,nhk->tnk", shaped, weight, preferred_element_type=jnp.float32).reshape(
        values.shape[0], LRU
    )


def blocked_t(values, weight):
    shaped = values.reshape(values.shape[0], LRU // HB, HB)
    return jnp.einsum("tnk,nhk->tnh", shaped, weight, preferred_element_type=jnp.float32).reshape(
        values.shape[0], LRU
    )


def blocked_grad(inputs, grads):
    left = inputs.reshape(inputs.shape[0], LRU // HB, HB)
    right = grads.reshape(grads.shape[0], LRU // HB, HB)
    return jnp.einsum("tnh,tnk->nhk", left, right, preferred_element_type=jnp.float32)


def rms_norm(values, gain):
    return values * lax.rsqrt(jnp.mean(values * values, axis=-1, keepdims=True) + EPS) * gain


def combine(earlier, later):
    return (earlier[0] * later[0], later[0] * earlier[1] + later[1])


def gate_terms(pre_a, pre_i, conv_val, lambda_raw, starting):
    recall = jax.nn.sigmoid(pre_a)
    admit = jax.nn.sigmoid(pre_i)
    rate = DECAY_SCALE * jax.nn.softplus(lambda_raw) * recall
    decay = (1.0 - starting) * jnp.exp(-rate)
    scale_in = starting + (1.0 - starting) * jnp.sqrt(-jnp.expm1(-2.0 * rate))
    return (decay, scale_in * admit * conv_val)


def convolve(extended, weight, bias, segment_ext, rows):
    total = jnp.zeros((rows, LRU), jnp.float32) + bias
    for lag in range(KW):
        source = extended[KW - 1 - lag : KW - 1 - lag + rows]
        same = (segment_ext[KW - 1 - lag : KW - 1 - lag + rows] == segment_ext[KW - 1 :]).astype(
            jnp.float32
        )
        total = total + weight[lag] * source * same[:, None]
    return total


def segment_ids(positions, doc_starts):
    return jnp.sum((doc_starts[None, :] <= positions[:, None]).astype(jnp.int32), axis=1)


def start_flags(positions, doc_starts):
    return jnp.max((doc_starts[None, :] == positions[:, None]).astype(jnp.float32), axis=1)


def gelu_product(left, right):
    return jax.nn.gelu(left, approximate=True) * right


def local(stream_in, cotangent, starts, params, momentum, average):
    weights = unpack(
        lax.all_gather(params.astype(jnp.bfloat16), ("seq", "fsdp"), axis=0, tiled=True)
    )
    stream = stream_in[0].astype(jnp.float32)
    incoming = cotangent[0].astype(jnp.float32)
    doc_starts = starts[0]
    rows = stream.shape[0]
    positions = lax.axis_index("seq") * rows + jnp.arange(rows, dtype=jnp.int32)
    ext_pos = positions[0] - (KW - 1) + jnp.arange(rows + KW - 1, dtype=jnp.int32)
    segment_ext = segment_ids(ext_pos, doc_starts)
    starting = start_flags(positions, doc_starts)[:, None]
    gain_one = weights["gain_one"].astype(jnp.float32)
    gain_two = weights["gain_two"].astype(jnp.float32)
    conv_weight = weights["conv_weight"].astype(jnp.float32)
    conv_bias = weights["conv_bias"].astype(jnp.float32)
    lambda_raw = weights["lambda_raw"].astype(jnp.float32)
    normed = rms_norm(stream, gain_one).astype(jnp.bfloat16)
    branch_y = matmul(normed, weights["w_y"])
    branch_x = matmul(normed, weights["w_x"]).astype(jnp.bfloat16)
    edge = shifted(branch_x[rows - (KW - 1) :], "seq", 1)
    extended = jnp.concatenate([edge, branch_x], axis=0).astype(jnp.float32)
    conv_out = convolve(extended, conv_weight, conv_bias, segment_ext, rows).astype(jnp.bfloat16)
    conv_val = conv_out.astype(jnp.float32)
    pre_a = blocked(conv_out, weights["gate_a"]) + weights["bias_a"].astype(jnp.float32)
    pre_i = blocked(conv_out, weights["gate_i"]) + weights["bias_i"].astype(jnp.float32)
    decay, drive = gate_terms(pre_a, pre_i, conv_val, lambda_raw, starting)
    prod_local, state_local = lax.associative_scan(combine, (decay, drive), axis=0)
    neutral = (jnp.ones((LRU,), jnp.float32), jnp.zeros((LRU,), jnp.float32))
    carried = carried_in((prod_local[-1], state_local[-1]), "seq", combine, neutral, False)
    carry_in = carried[1]
    state = lax.associative_scan(combine, (decay, drive.at[0].add(decay[0] * carry_in)), axis=0)[1]
    gelu_y = jax.nn.gelu(branch_y, approximate=True)
    mixed = (state * gelu_y).astype(jnp.bfloat16)
    middle = stream + matmul(mixed, weights["w_out"])
    normed_two = rms_norm(middle, gain_two).astype(jnp.bfloat16)
    gate = matmul(normed_two, weights["w_gate"])
    upward = matmul(normed_two, weights["w_up"])
    hidden = gelu_product(gate, upward).astype(jnp.bfloat16)
    output = (middle + matmul(hidden, weights["w_down"])).astype(jnp.bfloat16)
    grads = {}
    grad_out = incoming.astype(jnp.bfloat16)
    grads["w_down"] = t_matmul(hidden, grad_out)
    grad_hidden = matmul_t(grad_out, weights["w_down"])
    _, product_back = jax.vjp(gelu_product, gate, upward)
    grad_gate, grad_up = product_back(grad_hidden)
    grad_gate = grad_gate.astype(jnp.bfloat16)
    grad_up = grad_up.astype(jnp.bfloat16)
    grads["w_gate"] = t_matmul(normed_two, grad_gate)
    grads["w_up"] = t_matmul(normed_two, grad_up)
    grad_normed_two = matmul_t(grad_gate, weights["w_gate"]) + matmul_t(grad_up, weights["w_up"])
    _, norm_back_two = jax.vjp(rms_norm, middle, gain_two)
    grad_middle_part, grads["gain_two"] = norm_back_two(grad_normed_two)
    grad_middle = incoming + grad_middle_part
    grad_first = grad_middle.astype(jnp.bfloat16)
    grads["w_out"] = t_matmul(mixed, grad_first)
    grad_mixed = matmul_t(grad_first, weights["w_out"])
    _, gelu_back = jax.vjp(partial(jax.nn.gelu, approximate=True), branch_y)
    grad_y = gelu_back(grad_mixed * state)[0].astype(jnp.bfloat16)
    grad_state = grad_mixed * gelu_y
    next_decay = jnp.concatenate([decay[1:], jnp.ones((1, LRU), jnp.float32)], axis=0)
    suffix, adjoint_local = lax.associative_scan(
        combine, (next_decay, grad_state), axis=0, reverse=True
    )
    returned = carried_in(
        (prod_local[-1], decay[0] * adjoint_local[0]), "seq", combine, neutral, True
    )
    adjoint = adjoint_local + suffix * returned[1]
    previous = jnp.concatenate([carry_in[None, :], state[:-1]], axis=0)
    _, gates_back = jax.vjp(gate_terms, pre_a, pre_i, conv_val, lambda_raw, starting)
    grad_pre_a, grad_pre_i, grad_direct, grads["lambda_raw"], _ = gates_back(
        (adjoint * previous, adjoint)
    )
    grad_pre_a = grad_pre_a.astype(jnp.bfloat16)
    grad_pre_i = grad_pre_i.astype(jnp.bfloat16)
    grads["gate_a"] = blocked_grad(conv_out, grad_pre_a)
    grads["gate_i"] = blocked_grad(conv_out, grad_pre_i)
    grads["bias_a"] = jnp.sum(grad_pre_a.astype(jnp.float32), axis=0)
    grads["bias_i"] = jnp.sum(grad_pre_i.astype(jnp.float32), axis=0)
    grad_conv = (
        grad_direct
        + blocked_t(grad_pre_a, weights["gate_a"])
        + blocked_t(grad_pre_i, weights["gate_i"])
    )
    _, conv_back = jax.vjp(
        partial(convolve, segment_ext=segment_ext, rows=rows), extended, conv_weight, conv_bias
    )
    grad_ext, grads["conv_weight"], grads["conv_bias"] = conv_back(grad_conv)
    edge_back = shifted(grad_ext[: KW - 1], "seq", -1)
    grad_x = grad_ext[KW - 1 :] + jnp.concatenate(
        [jnp.zeros((rows - (KW - 1), LRU), jnp.float32), edge_back], axis=0
    )
    grad_x = grad_x.astype(jnp.bfloat16)
    grads["w_x"] = t_matmul(normed, grad_x)
    grads["w_y"] = t_matmul(normed, grad_y)
    grad_normed = matmul_t(grad_y, weights["w_y"]) + matmul_t(grad_x, weights["w_x"])
    _, norm_back_one = jax.vjp(rms_norm, stream, gain_one)
    grad_stream_part, grads["gain_one"] = norm_back_one(grad_normed)
    input_grad = grad_middle + grad_stream_part
    packed_grad = jnp.concatenate([grads[entry[0]].reshape(-1) for entry in layout()])
    summed = lax.psum_scatter(packed_grad, ("seq", "fsdp"), scatter_dimension=0, tiled=True)
    new_moment = MOMENT * momentum + summed
    new_params = params - RATE * (summed + MOMENT * new_moment)
    new_average = BLEND * average + (1.0 - BLEND) * new_params
    return (output[None], input_grad[None], new_params, new_moment, new_average)


LANE = 128
TP = 8
HALO = 544
SMALL = 160
GATES = 512
REGIONS = {
    "A": (4248, 256, 192, 32),
    "B": (53400, 1536, 16, 192),
    "C": (77976, 1152, 96, 144),
    "D": (188568, 1536, 36, 192),
}
ROWS = 243864
EVEN_FIRST = (0, 2, 4, 6, 1, 3, 5, 7)
F32 = jnp.float32
BF16 = jnp.bfloat16


class Plan:
    def __init__(self, n_seq, n_fsdp):
        self.n_fsdp = n_fsdp
        shards = n_seq * n_fsdp
        per = ROWS * LANE // shards
        self.per = per
        self.part = per % LANE
        self.own_rows = -(-per // 1024) * 8
        self.last = per // LANE
        bounds = [0]
        for i in range(1, shards):
            at = per * i / LANE
            for first, unit, count, _ in REGIONS.values():
                if first <= at < first + unit * count:
                    bounds.append(first + unit * round((at - first) / unit))
        bounds.append(ROWS)
        self.segments = []
        self.sizes = []
        self.table = np.zeros((shards, 16), np.int32)
        for i in range(shards):
            base = per * i // LANE
            self.table[i, 0] = per * i % LANE
            offset = SMALL + GATES if i == 0 else 0
            found = {}
            for slot, (name, (first, unit, count, wide)) in enumerate(REGIONS.items()):
                low = max(bounds[i], first)
                high = min(bounds[i + 1], first + unit * count)
                if high > low:
                    units = (high - low) // unit
                    found[name] = ((low - first) // unit, units, offset)
                    self.table[i, 1 + 3 * slot : 4 + 3 * slot] = (
                        low - base + HALO,
                        units,
                        offset,
                    )
                    offset += units * wide
            self.segments.append(found)
            self.sizes.append(offset)
            self.table[i, 13] = int(i == 0)
        self.lengths = [
            max(self.sizes[s * n_fsdp : (s + 1) * n_fsdp]) for s in range(n_seq)
        ]
        self.offsets = np.concatenate([[0], np.cumsum(self.lengths)]).astype(np.int32)
        self.longest = max(self.lengths)
        self.groups = ((0, 1), (2,), (3, 4, 5, 6), (7,))
        self.starts = [int(self.offsets[group[0]]) for group in self.groups]
        self.rows = [sum(self.lengths[s] for s in group) for group in self.groups]

    def pieces(self, name, groups):
        out = []
        for i, found in enumerate(self.segments):
            s, f = divmod(i, self.n_fsdp)
            if name in found and s in groups:
                first, units, offset = found[name]
                row = int(self.offsets[s] - self.offsets[groups[0]]) + offset
                out.append((f, row, first, units))
        return out


VMEM = pl.BlockSpec(memory_space=pltpu.VMEM)
ANY = pl.BlockSpec(memory_space=pl.ANY)
SMEM = pl.BlockSpec(memory_space=pltpu.SMEM)
LIMIT = pltpu.CompilerParams(vmem_limit_bytes=60 * 1024 * 1024)


def shape(dims, dtype):
    return jax.ShapeDtypeStruct(dims, dtype)


def aligned(value, multiple):
    return pl.multiple_of(value, multiple)


def lanes(rows):
    return lax.broadcasted_iota(jnp.int32, (rows, LANE), 1)


def swap_lanes(blocks):
    blocks = list(blocks)
    at = lanes(blocks[0].shape[0]) // 16
    for step in (4, 2, 1):
        low_side = (at & step) == 0
        for one in range(TP):
            if one & step == 0:
                left, right = blocks[one], blocks[one + step]
                blocks[one] = jnp.where(low_side, left, pltpu.roll(right, 16 * step, 1))
                blocks[one + step] = jnp.where(
                    low_side, pltpu.roll(left, LANE - 16 * step, 1), right
                )
    return blocks


def shift_down(source, source_row, target, target_row, rows, block, amount, unroll):
    def step(j, tail):
        z = pltpu.roll(source[pl.ds(source_row + j * block, block), :], amount, 1)
        above = pltpu.roll(jnp.concatenate([tail, z], axis=0), 1, 0)[8:]
        target[pl.ds(target_row + j * block, block), :] = jnp.where(
            lanes(block) < amount, above, z
        )
        return z[block - 8 :]

    lax.fori_loop(0, rows // block, step, jnp.zeros((8, LANE), F32), unroll=unroll)


def pack_body(plan, tab, hd, own, hu, *rest):
    outs, (win, al, wire, sems) = rest[:TP], rest[TP:]
    s, f = lax.axis_index("seq"), lax.axis_index("fsdp")
    me = s * plan.n_fsdp + f
    total = win.shape[0]
    first = pltpu.make_async_copy(hd, win.at[pl.ds(0, HALO)], sems.at[0])
    second = pltpu.make_async_copy(own, win.at[pl.ds(HALO, plan.own_rows)], sems.at[1])
    first.start()
    second.start()
    first.wait()
    second.wait()
    seam = HALO + plan.last
    kept = win[pl.ds(seam, 8), :]
    shift_down(hu, 0, win, seam, HALO, 32, plan.part, True)
    edge = lax.broadcasted_iota(jnp.int32, (8, LANE), 0) == 0
    win[pl.ds(seam, 8), :] = jnp.where(
        edge & (lanes(8) < plan.part), kept, win[pl.ds(seam, 8), :]
    )
    shift_down(win, 0, al, 0, total, 48, tab[me, 0], 7)

    def columns(g, _):
        at = tab[me, 1] + g * 256
        to = tab[me, 3] + g * 16
        for block in range(16):
            row = to + 16 * tab[me, 2] * (block // TP)
            wire[block % TP, pl.ds(aligned(row, 16), 16), :] = al[
                pl.ds(at + block, 16, stride=16), :
            ].astype(BF16)
        return 0

    lax.fori_loop(0, tab[me, 2], columns, 0)
    for slot in (4, 10):

        def grouped(j, _):
            for owner in range(TP):
                at = tab[me, slot] + j * 1536 + owner * 192
                to = tab[me, slot + 2] + j * 16
                for block in range(12):
                    row = to + 16 * tab[me, slot + 1] * block
                    wire[owner, pl.ds(aligned(row, 16), 16), :] = al[
                        pl.ds(at + block, 16, stride=12), :
                    ].astype(BF16)
            return 0

        lax.fori_loop(0, tab[me, slot + 1], grouped, 0)

    def mixed_columns(g, _):
        at = tab[me, 7] + g * 1152
        to = tab[me, 9] + g * 32
        wide = 32 * tab[me, 8]
        last = tab[me, 9] + 4 * wide + g * 16
        for half in range(2):
            for a in range(4):
                parts = swap_lanes(
                    [
                        al[pl.ds(at + 576 * half + 8 * a + b, 16, stride=36), :]
                        for b in range(TP)
                    ]
                )
                for owner in range(TP):
                    row = to + a * wide + 16 * half
                    wire[owner, pl.ds(aligned(row, 16), 16), :] = parts[owner].astype(BF16)
        parts = swap_lanes(
            [
                al[pl.ds(at + 576 * half + 32 + b, 16, stride=36), :]
                for half in range(2)
                for b in range(4)
            ]
        )
        for owner in range(TP):
            wire[owner, pl.ds(aligned(last, 16), 16), :] = parts[owner].astype(BF16)
        return 0

    lax.fori_loop(0, tab[me, 8], mixed_columns, 0)

    @pl.when(me == 0)
    def _():
        for owner in range(TP):
            wire[owner, pl.ds(0, SMALL), :] = al[pl.ds(HALO, SMALL), :].astype(BF16)
        for kind in range(2):
            for n in range(16):
                wire[n % TP, pl.ds(SMALL + 128 * (2 * kind + n // TP), 128), :] = al[
                    pl.ds(HALO + 152 + 2048 * kind + 128 * n, 128), :
                ].astype(BF16)

    copies = [
        pltpu.make_async_copy(wire.at[s ^ k], outs[k], sems.at[2 + k]) for k in range(TP)
    ]
    for copy in copies:
        copy.start()
    for copy in copies:
        copy.wait()


def pack(plan, hd, own, hu):
    total = -(-(HALO * 2 + plan.own_rows) // 672) * 672
    return pl.pallas_call(
        partial(pack_body, plan),
        out_shape=[shape((plan.longest, LANE), BF16)] * TP,
        in_specs=[SMEM, ANY, ANY, VMEM],
        out_specs=[ANY] * TP,
        scratch_shapes=[
            pltpu.VMEM((total, LANE), F32),
            pltpu.VMEM((total, LANE), F32),
            pltpu.VMEM((TP, plan.longest, LANE), BF16),
            pltpu.SemaphoreType.DMA((2 + TP,)),
        ],
        compiler_params=LIMIT,
        name="pack",
    )(jnp.asarray(plan.table), hd, own, hu)


def order_body(plan, *refs):
    pieces, outs, sems = refs[:TP], refs[TP : TP + 4], refs[TP + 4]
    s = lax.axis_index("seq")
    for start in (True, False):
        for number, group in enumerate(plan.groups):
            for source in group:
                size = plan.lengths[source]
                at = int(plan.offsets[source]) - plan.starts[number]
                for k in range(TP):

                    @pl.when((s ^ source) == k)
                    def _():
                        copy = pltpu.make_async_copy(
                            pieces[k].at[pl.ds(0, size)],
                            outs[number].at[pl.ds(at, size)],
                            sems.at[source],
                        )
                        if start:
                            copy.start()
                        else:
                            copy.wait()


def order(plan, pieces):
    return pl.pallas_call(
        partial(order_body, plan),
        out_shape=[shape((rows, LANE), BF16) for rows in plan.rows],
        in_specs=[ANY] * TP,
        out_specs=[VMEM] * 4,
        scratch_shapes=[pltpu.SemaphoreType.DMA((TP,))],
        compiler_params=LIMIT,
        name="order",
    )(*pieces)


def weight_copies(plan, number, weights, halves, b_rows):
    out = []
    for f, row, first, units in plan.pieces("A", plan.groups[number]):
        for target, begin, end in weights.get("A", ()):
            low, high = max(first, begin), min(first + units, end)
            if high > low:
                for n in range(2):
                    out.append(
                        (
                            f,
                            row + 16 * (units * n + low - first),
                            16 * (high - low),
                            target.at[pl.ds(16 * (low - begin), 16 * (high - low)), pl.ds(128 * n, 128)],
                        )
                    )
    for f, row, first, units in plan.pieces("B", plan.groups[number]):
        if b_rows is not None:
            for block in range(12):
                out.append(
                    (
                        f,
                        row + 16 * units * block,
                        16 * units,
                        b_rows.at[block, pl.ds(16 * first, 16 * units)],
                    )
                )
    for f, row, first, units in plan.pieces("C", plan.groups[number]):
        for target, begin, end in weights.get("C", ()):
            low, high = max(first, begin), min(first + units, end)
            if high > low:
                for a in range(4):
                    out.append(
                        (
                            f,
                            row + 32 * (units * a + low - first),
                            32 * (high - low),
                            target.at[pl.ds(32 * (low - begin), 32 * (high - low)), pl.ds(128 * a, 128)],
                        )
                    )
        if halves is not None:
            out.append(
                (f, row + 128 * units, 16 * units, halves.at[pl.ds(16 * first, 16 * units)])
            )
    for f, row, first, units in plan.pieces("D", plan.groups[number]):
        for target, begin, end in weights.get("D", ()):
            for n in range(12):
                out.append(
                    (
                        f,
                        row + 16 * units * n,
                        16 * units,
                        target.at[pl.ds(16 * (first - begin), 16 * units), pl.ds(128 * n, 128)],
                    )
                )
    return out


def fetch_line(plan, line, copies, sems, first=0, phases=(True, False)):
    f = lax.axis_index("fsdp")
    for start in phases:
        for source in range(plan.n_fsdp):
            for away in range(plan.n_fsdp):

                @pl.when((f ^ source) == away)
                def _():
                    for number, (holder, row, rows, target) in enumerate(copies):
                        if holder == source:
                            copy = pltpu.make_async_copy(
                                line[away].at[pl.ds(row, rows)], target, sems.at[first + number]
                            )
                            if start:
                                copy.start()
                            else:
                                copy.wait()


def first_copies(plan, small, gates, w_y, w_x, b_head):
    out = [(0, 0, SMALL, small), (0, SMALL, GATES, gates)]
    out += weight_copies(plan, 0, {"A": ((w_y, 0, 96), (w_x, 96, 192))}, None, None)
    for f, row, first, units in plan.pieces("B", plan.groups[0]):
        out.append((f, row, 192 * units, b_head.at[pl.ds(192 * first, 192 * units)]))
    return out


def first_body(plan, *refs):
    line, refs = refs[: plan.n_fsdp], refs[plan.n_fsdp :]
    *targets, sems = refs
    fetch_line(plan, line, first_copies(plan, *targets), sems)


def head_rows(plan):
    return sum(144 * p[3] for p in plan.pieces("C", plan.groups[1]))


def b_head_rows(plan):
    return sum(192 * p[3] for p in plan.pieces("B", plan.groups[0]))


class Nowhere:
    at = property(lambda self: self)

    def __getitem__(self, _):
        return self


def count_first(plan):
    return len(first_copies(plan, *[Nowhere()] * 5))


def unpack_first(plan, line):
    return pl.pallas_call(
        partial(first_body, plan),
        out_shape=[
            shape((SMALL, LANE), BF16),
            shape((GATES, LANE), BF16),
            shape((D, 256), BF16),
            shape((D, 256), BF16),
            shape((b_head_rows(plan), LANE), BF16),
        ],
        in_specs=[ANY] * len(line),
        out_specs=[VMEM] * 5,
        scratch_shapes=[pltpu.SemaphoreType.DMA((count_first(plan),))],
        compiler_params=LIMIT,
        name="unpack_first",
    )(*line)


def middle_copies(plan, b_rows, head):
    out = weight_copies(plan, 1, {}, None, b_rows)
    for f, row, first, units in plan.pieces("C", plan.groups[1]):
        out.append((f, row, 144 * units, head.at[pl.ds(144 * first, 144 * units)]))
    return out


def b_head_copies(plan, b_head, b_rows):
    out = []
    for _, _, first, units in plan.pieces("B", plan.groups[0]):
        for block in range(12):
            out.append(
                (
                    b_head.at[pl.ds(192 * first + 16 * units * block, 16 * units)],
                    b_rows.at[block, pl.ds(16 * first, 16 * units)],
                )
            )
    return out


def middle_body(plan, *refs):
    line, refs = refs[: plan.n_fsdp], refs[plan.n_fsdp :]
    b_head, outs, head, b_rows, sems, more = refs[0], refs[1 : 1 + TP], *refs[1 + TP :]
    local_copies = [
        pltpu.make_async_copy(source, target, more.at[number])
        for number, (source, target) in enumerate(b_head_copies(plan, b_head, b_rows))
    ]
    for copy in local_copies:
        copy.start()
    fetch_line(plan, line, middle_copies(plan, b_rows, head), sems)
    for copy in local_copies:
        copy.wait()
    s = lax.axis_index("seq")
    for k in range(TP):
        for n in range(2):
            unit = (s ^ k) + TP * n
            for block in range(12):
                outs[k][pl.ds(192 * n + 16 * block, 16), :] = b_rows[
                    block, pl.ds(aligned(16 * unit, 16), 16), :
                ]


def unpack_middle(plan, line, b_head):
    return pl.pallas_call(
        partial(middle_body, plan),
        out_shape=[shape((384, LANE), BF16)] * TP + [shape((head_rows(plan), LANE), BF16)],
        in_specs=[ANY] * (len(line) + 1),
        out_specs=[VMEM] * (TP + 1),
        scratch_shapes=[
            pltpu.VMEM((12, 256, LANE), BF16),
            pltpu.SemaphoreType.DMA((len(middle_copies(plan, *[Nowhere()] * 2)),)),
            pltpu.SemaphoreType.DMA((len(b_head_copies(plan, *[Nowhere()] * 2)),)),
        ],
        compiler_params=LIMIT,
        name="unpack_middle",
    )(*line, b_head)


def head_copies(plan, head, weight, halves):
    out = []
    for _, _, first, units in plan.pieces("C", plan.groups[1]):
        for a in range(4):
            out.append(
                (
                    head.at[pl.ds(144 * first + 32 * units * a, 32 * units)],
                    weight.at[pl.ds(32 * first, 32 * units), pl.ds(128 * a, 128)],
                )
            )
        out.append(
            (
                head.at[pl.ds(144 * first + 128 * units, 16 * units)],
                halves.at[pl.ds(16 * first, 16 * units)],
            )
        )
    return out


def second_copies(plan, w_gate, w_up, w_down, halves):
    return weight_copies(
        plan,
        2,
        {"C": ((w_gate, 0, 48), (w_up, 48, 96)), "D": ((w_down, 0, 16),)},
        halves,
        None,
    )


def halves_copies(plan, halves):
    return [
        (f, row + 128 * units, 16 * units, halves.at[pl.ds(16 * first, 16 * units)])
        for f, row, first, units in plan.pieces("C", plan.groups[2])
    ]


def second_body(plan, *refs):
    line, refs = refs[: plan.n_fsdp], refs[plan.n_fsdp :]
    head, w_gate, w_up, w_down, halves, sems, more = refs
    local_copies = [
        pltpu.make_async_copy(source, target, more.at[number])
        for number, (source, target) in enumerate(head_copies(plan, head, w_gate, halves))
    ]
    for copy in local_copies:
        copy.start()
    merged = halves_copies(plan, halves)
    whole = second_copies(plan, w_gate, w_up, w_down, None)
    fetch_line(plan, line, merged, sems, 0, (True,))
    fetch_line(plan, line, whole, sems, len(merged), (True,))
    fetch_line(plan, line, merged, sems, 0, (False,))
    for copy in local_copies:
        copy.wait()
    for weight, begin in ((w_gate, 0), (w_up, 48)):

        def step(g, _):
            last = halves[pl.ds(aligned(16 * (begin + g), 16), 16), :]
            weight[pl.ds(aligned(32 * g, 16), 16), pl.ds(512, 64)] = last[:, :64]
            weight[pl.ds(aligned(32 * g + 16, 16), 16), pl.ds(512, 64)] = last[:, 64:]
            return 0

        lax.fori_loop(0, 48, step, 0, unroll=8)
    fetch_line(plan, line, whole, sems, len(merged), (False,))


def unpack_second(plan, line, head):
    many = len(second_copies(plan, *[Nowhere()] * 4))
    few = len(head_copies(plan, *[Nowhere()] * 3))
    return pl.pallas_call(
        partial(second_body, plan),
        out_shape=[
            shape((D, FF // TP), BF16),
            shape((D, FF // TP), BF16),
            shape((256, D), BF16),
        ],
        in_specs=[ANY] * (len(line) + 1),
        out_specs=[VMEM] * 3,
        scratch_shapes=[
            pltpu.VMEM((96 * 16, LANE), BF16),
            pltpu.SemaphoreType.DMA((many,)),
            pltpu.SemaphoreType.DMA((few,)),
        ],
        compiler_params=LIMIT,
        name="unpack_second",
    )(*line, head)


def third_copies(plan, w_down):
    return weight_copies(plan, 3, {"D": ((w_down, 0, 36),)}, None, None)


def third_body(plan, *refs):
    line, refs = refs[: plan.n_fsdp], refs[plan.n_fsdp :]
    before, w_down, sems, one = refs
    copy = pltpu.make_async_copy(before, w_down.at[pl.ds(0, 256)], one.at[0])
    copy.start()
    fetch_line(plan, line, third_copies(plan, w_down), sems)
    copy.wait()


def unpack_third(plan, line, before):
    many = len(third_copies(plan, Nowhere()))
    return pl.pallas_call(
        partial(third_body, plan),
        out_shape=shape((FF // TP, D), BF16),
        in_specs=[ANY] * (len(line) + 1),
        out_specs=VMEM,
        scratch_shapes=[
            pltpu.SemaphoreType.DMA((many,)),
            pltpu.SemaphoreType.DMA((1,)),
        ],
        compiler_params=LIMIT,
        name="unpack_third",
    )(*line, before)


def out_rows_body(*refs):
    pieces, w_out = refs[:TP], refs[TP]
    s = lax.axis_index("seq")
    for k in range(TP):
        for n in range(2):
            to = aligned(128 * n + 16 * (s ^ k), 16)
            for block in range(12):
                w_out[pl.ds(to, 16), pl.ds(128 * block, 128)] = pieces[k][
                    pl.ds(192 * n + 16 * block, 16), :
                ]


def join_out_rows(pieces):
    return pl.pallas_call(
        out_rows_body,
        out_shape=shape((256, D), BF16),
        in_specs=[VMEM] * TP,
        out_specs=VMEM,
        compiler_params=LIMIT,
        name="join_out_rows",
    )(*pieces)


def split_rows_body(grad, *pieces):
    s = lax.axis_index("seq")
    for k in range(TP):
        for n in range(2):
            at = aligned(128 * n + 16 * (s ^ k), 16)
            for block in range(12):
                pieces[k][pl.ds(192 * n + 16 * block, 16), :] = grad[
                    pl.ds(at, 16), pl.ds(128 * block, 128)
                ]


def split_out_rows(grad):
    return pl.pallas_call(
        split_rows_body,
        out_shape=[shape((384, LANE), F32)] * TP,
        in_specs=[VMEM],
        out_specs=[VMEM] * TP,
        compiler_params=LIMIT,
        name="split_out_rows",
    )(grad)


def start_copies(copies, sems, first=0):
    made = [
        pltpu.make_async_copy(source, target, sems.at[first + number])
        for number, (source, target) in enumerate(copies)
    ]
    for copy in made:
        copy.start()
    return made


def to_wires(plan, copies, wires, sems, first, start):
    f = lax.axis_index("fsdp")
    for j in range(plan.n_fsdp):
        for x in range(plan.n_fsdp):

            @pl.when((f ^ j) == x)
            def _():
                for number, (holder, row, rows, source) in enumerate(copies):
                    if holder == j:
                        copy = pltpu.make_async_copy(
                            source, wires[x].at[pl.ds(row, rows)], sems.at[first + number]
                        )
                        if start:
                            copy.start()
                        else:
                            copy.wait()


def wire_second_body(plan, g_gate, g_up, g_down, *refs):
    wires, (head, halves, sems) = refs[: plan.n_fsdp], refs[plan.n_fsdp :]
    whole = second_copies(plan, g_gate, g_up, g_down, None)
    merged = halves_copies(plan, halves)
    more = [(b, a) for a, b in head_copies(plan, head, g_gate, halves)]
    to_wires(plan, whole, wires, sems, 0, True)
    for grad, begin in ((g_gate, 0), (g_up, 48)):

        def step(g, _):
            left = grad[pl.ds(aligned(32 * g, 16), 16), pl.ds(512, 64)]
            right = grad[pl.ds(aligned(32 * g + 16, 16), 16), pl.ds(512, 64)]
            halves[pl.ds(aligned(16 * (begin + g), 16), 16), :] = jnp.concatenate(
                [left, right], axis=1
            )
            return 0

        lax.fori_loop(0, 48, step, 0, unroll=8)
    to_wires(plan, merged, wires, sems, len(whole), True)
    made = start_copies(more, sems, len(whole) + len(merged))
    to_wires(plan, whole, wires, sems, 0, False)
    to_wires(plan, merged, wires, sems, len(whole), False)
    for copy in made:
        copy.wait()


def wire_second(plan, g_gate, g_up, g_down):
    many = len(second_copies(plan, *[Nowhere()] * 4)) + len(
        head_copies(plan, *[Nowhere()] * 3)
    )
    out = pl.pallas_call(
        partial(wire_second_body, plan),
        out_shape=[shape((plan.rows[2], LANE), F32)] * plan.n_fsdp
        + [shape((head_rows(plan), LANE), F32)],
        in_specs=[VMEM] * 3,
        out_specs=[ANY] * (plan.n_fsdp + 1),
        scratch_shapes=[
            pltpu.VMEM((96 * 16, LANE), F32),
            pltpu.SemaphoreType.DMA((many,)),
        ],
        compiler_params=LIMIT,
        name="wire_second",
    )(g_gate, g_up, g_down)
    return out[:-1], out[-1]


def wire_plain(plan, copies_of, rows, operands):
    many = len(copies_of(*[Nowhere()] * len(operands)))

    def body(*refs):
        *refs, sems = refs
        sources, wires = refs[: len(operands)], refs[len(operands) :]
        copies = copies_of(*sources)
        to_wires(plan, copies, wires, sems, 0, True)
        to_wires(plan, copies, wires, sems, 0, False)

    return pl.pallas_call(
        body,
        out_shape=[shape((rows, LANE), F32)] * plan.n_fsdp,
        in_specs=[VMEM] * len(operands),
        out_specs=[ANY] * plan.n_fsdp,
        scratch_shapes=[pltpu.SemaphoreType.DMA((many,))],
        compiler_params=LIMIT,
    )(*operands)


def wire_third(plan, g_down):
    return wire_plain(plan, partial(third_copies, plan), plan.rows[3], (g_down,))


def wire_middle_body(plan, head, *refs):
    pieces, refs = refs[:TP], refs[TP:]
    wires, (b_head, b_rows, sems) = refs[: plan.n_fsdp], refs[plan.n_fsdp :]
    s = lax.axis_index("seq")
    for k in range(TP):
        for n in range(2):
            unit = (s ^ k) + TP * n
            for block in range(12):
                b_rows[block, pl.ds(aligned(16 * unit, 16), 16), :] = pieces[k][
                    pl.ds(192 * n + 16 * block, 16), :
                ]
    copies = middle_copies(plan, b_rows, head)
    to_wires(plan, copies, wires, sems, 0, True)
    more = [(b, a) for a, b in b_head_copies(plan, b_head, b_rows)]
    made = start_copies(more, sems, len(copies))
    to_wires(plan, copies, wires, sems, 0, False)
    for copy in made:
        copy.wait()


def wire_middle(plan, head, pieces):
    many = len(middle_copies(plan, *[Nowhere()] * 2)) + len(
        b_head_copies(plan, *[Nowhere()] * 2)
    )
    out = pl.pallas_call(
        partial(wire_middle_body, plan),
        out_shape=[shape((plan.rows[1], LANE), F32)] * plan.n_fsdp
        + [shape((b_head_rows(plan), LANE), F32)],
        in_specs=[VMEM] * (1 + TP),
        out_specs=[ANY] * (plan.n_fsdp + 1),
        scratch_shapes=[
            pltpu.VMEM((12, 256, LANE), F32),
            pltpu.SemaphoreType.DMA((many,)),
        ],
        compiler_params=LIMIT,
        name="wire_middle",
    )(head, *pieces)
    return out[:-1], out[-1]


def split_copies(plan, copies):
    border = int(plan.offsets[1])
    return (
        [copy for copy in copies if copy[1] < border],
        [(f, row - border, rows, at) for f, row, rows, at in copies if row >= border],
    )


def wire_x(plan, g_x, b_head):
    def copies_of(g_x, b_head):
        nowhere = Nowhere()
        return split_copies(plan, first_copies(plan, nowhere, nowhere, nowhere, g_x, b_head))[1]

    return wire_plain(plan, copies_of, plan.lengths[1], (g_x, b_head))


def wire_y_body(plan, gains, vectors, gates, g_y, g_x, *refs):
    wires, (small, sems) = refs[: plan.n_fsdp], refs[plan.n_fsdp :]
    s = lax.axis_index("seq")
    small[...] = jnp.zeros_like(small)
    small[pl.ds(0, 24), :] = gains[...]
    for n in range(8):
        for part in range(2):
            small[pl.ds(24 + 16 * n + s + TP * part, 1), :] = vectors[
                pl.ds(2 * n + part, 1), :
            ]
    copies = split_copies(plan, first_copies(plan, small, gates, g_y, g_x, Nowhere()))[0]
    to_wires(plan, copies, wires, sems, 0, True)
    to_wires(plan, copies, wires, sems, 0, False)


def wire_y(plan, gains, vectors, gates, g_y, g_x):
    return pl.pallas_call(
        partial(wire_y_body, plan),
        out_shape=[shape((plan.lengths[0], LANE), F32)] * plan.n_fsdp,
        in_specs=[VMEM] * 5,
        out_specs=[ANY] * plan.n_fsdp,
        scratch_shapes=[
            pltpu.VMEM((SMALL, LANE), F32),
            pltpu.SemaphoreType.DMA((count_first(plan),)),
        ],
        compiler_params=LIMIT,
        name="wire_y",
    )(gains, vectors, gates, g_y, g_x)


def spread_body(plan, targets, *refs):
    count = len(targets)
    sums, outs, sems = refs[:count], refs[count : count + TP], refs[count + TP]
    s = lax.axis_index("seq")
    for start in (True, False):
        for summed, group in zip(sums, targets):
            for target in group:
                size = plan.lengths[target]
                at = int(plan.offsets[target] - plan.offsets[group[0]])
                for k in range(TP):

                    @pl.when((s ^ target) == k)
                    def _():
                        copy = pltpu.make_async_copy(
                            summed.at[pl.ds(at, size)],
                            outs[k].at[pl.ds(0, size)],
                            sems.at[target],
                        )
                        if start:
                            copy.start()
                        else:
                            copy.wait()


def spread(plan, targets, sums):
    rows = max(plan.lengths[s] for group in targets for s in group)
    return pl.pallas_call(
        partial(spread_body, plan, targets),
        out_shape=[shape((rows, LANE), F32)] * TP,
        in_specs=[VMEM] * len(sums),
        out_specs=[ANY] * TP,
        scratch_shapes=[pltpu.SemaphoreType.DMA((TP,))],
        compiler_params=LIMIT,
    )(*sums)


def shift_up(source, source_row, target, target_row, rows, block, amount):
    def step(j, _):
        both = pltpu.roll(source[pl.ds(source_row + j * block, block + 8), :], amount, 1)
        below = pltpu.roll(both, block + 7, 0)[:block]
        target[pl.ds(target_row + j * block, block), :] = jnp.where(
            lanes(block) < amount, both[:block], below
        )
        return 0

    lax.fori_loop(0, rows // block, step, 0, unroll=True)


def collect_body(plan, tab, *refs):
    pieces, (own, hd, hu, al, win, wire, sems) = refs[: 3 * TP], refs[3 * TP :]
    s, f = lax.axis_index("seq"), lax.axis_index("fsdp")
    me = s * plan.n_fsdp + f

    def bring(start):
        for number, (low, high) in enumerate(((0, 0), (1, 2), (3, TP - 1))):

            @pl.when((s >= low) & (s <= high))
            def _():
                for k in range(TP):
                    piece = pieces[TP * number + k]
                    copy = pltpu.make_async_copy(
                        piece, wire.at[s ^ k, pl.ds(0, piece.shape[0])], sems.at[k]
                    )
                    if start:
                        copy.start()
                    else:
                        copy.wait()

    bring(True)
    total = win.shape[0]

    def clear(j, _):
        al[pl.ds(aligned(j * 96, 8), 96), :] = jnp.zeros((96, LANE), F32)
        return 0

    lax.fori_loop(0, al.shape[0] // 96, clear, 0, unroll=4)
    bring(False)

    def columns(g, _):
        at = tab[me, 1] + g * 256
        to = tab[me, 3] + g * 16
        for block in range(16):
            row = to + 16 * tab[me, 2] * (block // TP)
            al[pl.ds(at + block, 16, stride=16), :] = wire[
                block % TP, pl.ds(aligned(row, 16), 16), :
            ]
        return 0

    lax.fori_loop(0, tab[me, 2], columns, 0)
    for slot in (4, 10):

        def grouped(j, _):
            for owner in range(TP):
                at = tab[me, slot] + j * 1536 + owner * 192
                to = tab[me, slot + 2] + j * 16
                for block in range(12):
                    row = to + 16 * tab[me, slot + 1] * block
                    al[pl.ds(at + block, 16, stride=12), :] = wire[
                        owner, pl.ds(aligned(row, 16), 16), :
                    ]
            return 0

        lax.fori_loop(0, tab[me, slot + 1], grouped, 0)

    def mixed_columns(g, _):
        at = tab[me, 7] + g * 1152
        to = tab[me, 9] + g * 32
        wide = 32 * tab[me, 8]
        last = tab[me, 9] + 4 * wide + g * 16
        for half in range(2):
            for a in range(4):
                parts = swap_lanes(
                    [
                        wire[owner, pl.ds(aligned(to + a * wide + 16 * half, 16), 16), :]
                        for owner in range(TP)
                    ]
                )
                for b in range(TP):
                    al[pl.ds(at + 576 * half + 8 * a + b, 16, stride=36), :] = parts[b]
        parts = swap_lanes(
            [wire[owner, pl.ds(aligned(last, 16), 16), :] for owner in range(TP)]
        )
        for half in range(2):
            for b in range(4):
                al[pl.ds(at + 576 * half + 32 + b, 16, stride=36), :] = parts[4 * half + b]
        return 0

    lax.fori_loop(0, tab[me, 8], mixed_columns, 0)

    @pl.when(me == 0)
    def _():
        summed = wire[0, pl.ds(0, 152), :]
        for owner in range(1, TP):
            summed = summed + wire[owner, pl.ds(0, 152), :]
        al[pl.ds(HALO, 152), :] = summed
        for kind in range(2):
            for n in range(16):
                al[pl.ds(HALO + 152 + 2048 * kind + 128 * n, 128), :] = wire[
                    n % TP, pl.ds(SMALL + 128 * (2 * kind + n // TP), 128), :
                ]

    def back(j, _):
        both = pltpu.roll(
            al[pl.ds(aligned(j * 48, 8), 56), :], lax.rem(LANE - tab[me, 0], LANE), 1
        )
        below = pltpu.roll(both, 55, 0)[:48]
        win[pl.ds(aligned(j * 48, 8), 48), :] = jnp.where(
            lanes(48) < LANE - tab[me, 0], both[:48], below
        )
        return 0

    lax.fori_loop(0, total // 48, back, 0, unroll=7)
    made = start_copies(
        [
            (win.at[pl.ds(HALO, plan.own_rows)], own),
            (win.at[pl.ds(0, HALO)], hd),
        ],
        sems,
    )
    shift_up(win, HALO + plan.last, hu, 0, HALO, 32, LANE - plan.part)
    for copy in made:
        copy.wait()


def collect(plan, pieces):
    total = -(-(HALO * 2 + plan.own_rows) // 672) * 672
    cleared = total + 96
    return pl.pallas_call(
        partial(collect_body, plan),
        out_shape=[
            shape((plan.own_rows, LANE), F32),
            shape((HALO, LANE), F32),
            shape((HALO, LANE), F32),
        ],
        in_specs=[SMEM] + [ANY] * (3 * TP),
        out_specs=[ANY, ANY, VMEM],
        scratch_shapes=[
            pltpu.VMEM((cleared, LANE), F32),
            pltpu.VMEM((total, LANE), F32),
            pltpu.VMEM((TP, plan.longest, LANE), F32),
            pltpu.SemaphoreType.DMA((TP,)),
        ],
        compiler_params=LIMIT,
        name="collect",
    )(jnp.asarray(plan.table), *pieces)


def tail_body(plan, value, out):
    first = (plan.last - HALO) % 8
    out[...] = jnp.zeros_like(out)
    shift_down(value, 0, out, first, HALO, 32, plan.part, True)
    z = pltpu.roll(value[pl.ds(HALO - 8, 8), :], plan.part, 1)
    row = lax.broadcasted_iota(jnp.int32, (8, LANE), 0)
    out[pl.ds(first + HALO, 8), :] = jnp.where(
        (row == 0) & (lanes(8) < plan.part), pltpu.roll(z, 1, 0), 0.0
    )


def place_tail(plan, value):
    rows = plan.own_rows - (plan.last - HALO) // 8 * 8
    return pl.pallas_call(
        partial(tail_body, plan),
        out_shape=shape((max(rows, HALO + 16), LANE), F32),
        in_specs=[VMEM],
        out_specs=VMEM,
        compiler_params=LIMIT,
        name="place_tail",
    )(value)[:rows]


def scan_body(reverse, coefficient, addend, out):
    rows, width = coefficient.shape
    at = lax.broadcasted_iota(jnp.int32, (8, width), 0)
    if reverse:
        at = 7 - at
    steps = rows // 8

    def step(j, carry):
        block = steps - 1 - j if reverse else j
        here = pl.ds(aligned(block * 8, 8), 8)
        a, b = coefficient[here, :], addend[here, :]
        for reach in (1, 2, 4):
            turn = 8 - reach if reverse else reach
            inside = at >= reach
            b = b + jnp.where(inside, a * pltpu.roll(b, turn, 0), 0.0)
            a = jnp.where(inside, a * pltpu.roll(a, turn, 0), a)
        value = b + a * carry
        out[here, :] = value
        edge = value[0:1] if reverse else value[7:8]
        return jnp.broadcast_to(edge, (8, width))

    lax.fori_loop(0, steps, step, jnp.zeros((8, width), F32), unroll=4)


def linear_scan(coefficient, addend, reverse):
    return pl.pallas_call(
        partial(scan_body, reverse),
        out_shape=shape(coefficient.shape, F32),
        in_specs=[VMEM] * 2,
        out_specs=VMEM,
        compiler_params=LIMIT,
        name="scan_back" if reverse else "scan",
    )(coefficient, addend)


def swap(value, bit):
    return lax.ppermute(value, "seq", [(i, i ^ bit) for i in range(TP)])


def exchange(pieces, targets=range(TP)):
    return [pieces[0]] + [
        lax.ppermute(pieces[k], "seq", [(i ^ k, i) for i in targets]) for k in range(1, TP)
    ]


def join_body(*refs):
    *pieces, out, sems = refs
    copies, at = [], 0
    for number, piece in enumerate(pieces):
        rows = piece.shape[0]
        copies.append(
            pltpu.make_async_copy(piece, out.at[pl.ds(at, rows)], sems.at[number])
        )
        at += rows
    for copy in copies:
        copy.start()
    for copy in copies:
        copy.wait()


def join(pieces):
    rows = sum(piece.shape[0] for piece in pieces)
    return pl.pallas_call(
        join_body,
        out_shape=shape((rows, pieces[0].shape[1]), pieces[0].dtype),
        in_specs=[ANY] * len(pieces),
        out_specs=VMEM,
        scratch_shapes=[pltpu.SemaphoreType.DMA((len(pieces),))],
        compiler_params=LIMIT,
    )(*pieces)


def gather_stream(mine, whole=False):
    half = mine.shape[0] // 2

    over_x, over_y = swap(mine, 2), swap(mine, 4)
    over_xy = [swap(over_x[:half], 4), swap(over_y[half:], 2)]
    chip = [mine, over_x, over_y] + over_xy
    if whole:
        chip = [join(chip)]
    return join(chip + [swap(part, 1) for part in chip])


def scatter_stream(partial_sums):
    rows = partial_sums.shape[0] // TP
    half = rows // 2

    def send(value, bit):
        return swap(value.astype(BF16), bit).astype(F32)

    other = send(partial_sums[TP // 2 * rows :], 1)
    q = (partial_sums[: TP // 2 * rows] + other).reshape(4, rows, -1)
    up = send(jnp.concatenate([q[1, :half], q[3, :half]]), 2)
    down = send(jnp.concatenate([q[2, half:], q[3, half:]]), 4)
    top = send(q[2, :half] + up[half:], 4)
    low = send(q[1, half:] + down[half:], 2)
    return jnp.concatenate(
        [q[0, :half] + up[:half] + top, q[0, half:] + down[:half] + low], axis=0
    )


def to_positions(values, s):
    rows = values.shape[0] // TP
    parts = []
    for j in range(TP):
        k = s ^ j
        at = (k // 2 + 4 * (k % 2)) * rows
        parts.append(lax.dynamic_slice_in_dim(values, at, rows, 0))
    return jnp.concatenate(parts, axis=0)


def to_relative(values, s):
    rows = values.shape[0] // TP
    return jnp.concatenate(
        [lax.dynamic_slice_in_dim(values, (s ^ k) * rows, rows, 0) for k in EVEN_FIRST], axis=0
    )


def gather_line(value, count):
    def send(value, bit):
        return lax.ppermute(value, "fsdp", [(i, i ^ bit) for i in range(count)])

    opposite, near = send(value, 3), send(value, 1)
    return [value, near, send(opposite, 1), opposite]


def scatter_line(blocks):
    count = len(blocks)
    own, near, far, cross = blocks
    far = lax.ppermute(far, "fsdp", [(i, i ^ 1) for i in range(count)])
    near = lax.ppermute(near, "fsdp", [(i, i ^ 1) for i in range(count)])
    cross = lax.ppermute(cross + far, "fsdp", [(i, i ^ 3) for i in range(count)])
    return own + near + cross


def sliced(plan, *arguments):
    return sliced_step(plan, *arguments)


def sliced_step(plan, stream_in, cotangent, starts, params, momentum, average):
    n_fsdp = plan.n_fsdp
    s = lax.axis_index("seq")
    shards = TP * n_fsdp
    onward = [(i, i + 1) for i in range(shards - 1)]
    backward = [(i + 1, i) for i in range(shards - 1)]
    both = ("seq", "fsdp")
    edge = HALO * LANE
    per = plan.per

    hd, hu = lax.optimization_barrier((params[per - edge :], params[:edge]))
    hd = lax.ppermute(hd.astype(BF16), both, onward)
    hu = lax.ppermute(hu.astype(BF16), both, backward)
    own = jnp.pad(params, (0, plan.own_rows * LANE - per)).reshape(-1, LANE)
    pieces = pack(
        plan, hd.astype(F32).reshape(-1, LANE), own, hu.astype(F32).reshape(-1, LANE)
    )
    first, middle_wire, second, third = order(plan, exchange(pieces))
    stream_bf, cotangent_bf, first = lax.optimization_barrier(
        (stream_in[0], cotangent[0], first)
    )
    line = gather_line(first, n_fsdp)
    middle_wire, second, third, line = lax.optimization_barrier(
        (middle_wire, second, third, line)
    )
    small, gates, w_y, w_x, b_head = unpack_first(plan, line)
    line = gather_line(middle_wire, n_fsdp)
    *out_rows, head = unpack_middle(plan, line, b_head)
    w_out = join_out_rows(exchange(out_rows))
    line = gather_line(second, n_fsdp)
    w_gate, w_up, w_down = unpack_second(plan, line, head)
    w_down = unpack_third(plan, gather_line(third, n_fsdp), w_down)

    mine = stream_in[0].astype(F32)
    stream = gather_stream(stream_bf)
    stream = stream.astype(F32)
    grad_out = gather_stream(cotangent_bf, True)
    rows = stream.shape[0]

    small = small.astype(F32)
    gain_one = small[0:12].reshape(-1)
    gain_two = small[12:24].reshape(-1)

    def channels(at):
        return jnp.concatenate(
            [
                lax.dynamic_slice_in_dim(small, at + s, 1, 0),
                lax.dynamic_slice_in_dim(small, at + s + TP, 1, 0),
            ],
            axis=1,
        )[0]

    conv_bias, bias_a, bias_i, lambda_raw = (channels(24 + 16 * j) for j in range(4))
    conv_weight = jnp.stack([channels(88 + 16 * j) for j in range(KW)])

    positions = jnp.arange(rows, dtype=jnp.int32)
    ext_pos = jnp.arange(rows + KW - 1, dtype=jnp.int32) - (KW - 1)
    segment_ext = segment_ids(ext_pos, starts[0])
    starting = start_flags(positions, starts[0])[:, None]

    def gate_product(values, at):
        return jnp.concatenate(
            [matmul(values[:, :HB], gates[at : at + HB]), matmul(values[:, HB:], gates[at + HB : at + 2 * HB])],
            axis=1,
        )

    def gate_product_t(values, at):
        return jnp.concatenate(
            [matmul_t(values[:, :HB], gates[at : at + HB]), matmul_t(values[:, HB:], gates[at + HB : at + 2 * HB])],
            axis=1,
        )

    normed = rms_norm(stream, gain_one).astype(BF16)
    branch_y = matmul(normed, w_y)
    branch_x = matmul(normed, w_x).astype(BF16)
    branch_y = to_positions(branch_y, s)
    branch_x = to_positions(branch_x, s)
    extended = jnp.pad(branch_x, ((KW - 1, 0), (0, 0))).astype(F32)

    def convolve_here(extended, weight, bias):
        total = jnp.zeros((rows, bias.shape[0]), F32) + bias
        for lag in range(KW):
            source = extended[KW - 1 - lag : KW - 1 - lag + rows]
            same = segment_ext[KW - 1 - lag : KW - 1 - lag + rows] == segment_ext[KW - 1 :]
            total = total + weight[lag] * source * same.astype(F32)[:, None]
        return total

    conv_out = convolve_here(extended, conv_weight, conv_bias).astype(BF16)
    conv_val = conv_out.astype(F32)
    pre_a = gate_product(conv_out, 0) + bias_a
    pre_i = gate_product(conv_out, 2 * HB) + bias_i
    decay, drive = gate_terms(pre_a, pre_i, conv_val, lambda_raw, starting)
    state = linear_scan(decay, drive, False)
    gelu_y = jax.nn.gelu(branch_y, approximate=True)
    mixed = to_relative((state * gelu_y).astype(BF16), s)
    middle = mine + scatter_stream(matmul(mixed, w_out))
    normed_two_mine = rms_norm(middle, gain_two).astype(BF16)
    normed_two = gather_stream(normed_two_mine)
    gate = matmul(normed_two, w_gate)
    upward = matmul(normed_two, w_up)
    hidden = gelu_product(gate, upward).astype(BF16)
    g_down = t_matmul(hidden, grad_out)
    summed_three = scatter_line(wire_third(plan, g_down))
    out_sums = matmul(hidden, w_down)
    output = (middle + scatter_stream(out_sums)).astype(BF16)
    gate, upward, _ = lax.optimization_barrier((gate, upward, hidden))

    grad_hidden = matmul_t(grad_out, w_down)
    _, product_back = jax.vjp(gelu_product, gate, upward)
    grad_gate, grad_up = product_back(grad_hidden)
    grad_gate, grad_up = grad_gate.astype(BF16), grad_up.astype(BF16)
    g_gate = t_matmul(normed_two, grad_gate)
    g_up = t_matmul(normed_two, grad_up)
    in_sums = matmul_t(grad_gate, w_gate) + matmul_t(grad_up, w_up)
    grad_normed_two = scatter_stream(in_sums)
    wire_two, wire_head = wire_second(plan, g_gate, g_up, g_down)
    summed_two = scatter_line(wire_two)

    _, norm_back_two = jax.vjp(rms_norm, middle, gain_two)
    grad_middle_part, g_gain_two = norm_back_two(grad_normed_two)
    grad_middle = cotangent[0].astype(F32) + grad_middle_part
    grad_first = gather_stream(grad_middle.astype(BF16))
    g_out = t_matmul(mixed, grad_first)
    wire_mid, b_head = wire_middle(plan, wire_head, exchange(split_out_rows(g_out)))
    summed_mid = scatter_line(wire_mid)
    grad_mixed = to_positions(matmul_t(grad_first, w_out), s)
    _, gelu_back = jax.vjp(partial(jax.nn.gelu, approximate=True), branch_y)
    grad_y = gelu_back(grad_mixed * state)[0].astype(BF16)
    next_decay = jnp.concatenate([decay[1:], jnp.ones((1, decay.shape[1]), F32)], axis=0)
    adjoint = linear_scan(next_decay, grad_mixed * gelu_y, True)
    previous = jnp.concatenate([jnp.zeros((1, decay.shape[1]), F32), state[:-1]], axis=0)
    _, gates_back = jax.vjp(gate_terms, pre_a, pre_i, conv_val, lambda_raw, starting)
    grad_pre_a, grad_pre_i, grad_direct, g_lambda, _ = gates_back((adjoint * previous, adjoint))
    grad_pre_a, grad_pre_i = grad_pre_a.astype(BF16), grad_pre_i.astype(BF16)
    g_gates = jnp.concatenate(
        [
            t_matmul(conv_out[:, n : n + HB], grad[:, n : n + HB])
            for grad in (grad_pre_a, grad_pre_i)
            for n in (0, HB)
        ],
        axis=0,
    )
    g_bias_a = jnp.sum(grad_pre_a.astype(F32), axis=0)
    g_bias_i = jnp.sum(grad_pre_i.astype(F32), axis=0)
    grad_conv = grad_direct + gate_product_t(grad_pre_a, 0) + gate_product_t(grad_pre_i, 2 * HB)
    _, conv_back = jax.vjp(convolve_here, extended, conv_weight, conv_bias)
    grad_ext, g_conv_weight, g_conv_bias = conv_back(grad_conv)
    grad_x = to_relative(grad_ext[KW - 1 :].astype(BF16), s)
    grad_y = to_relative(grad_y, s)
    g_x = t_matmul(normed, grad_x)
    g_y = t_matmul(normed, grad_y)
    grad_normed = scatter_stream(matmul_t(grad_y, w_y) + matmul_t(grad_x, w_x))
    _, norm_back_one = jax.vjp(rms_norm, mine, gain_one)
    grad_stream_part, g_gain_one = norm_back_one(grad_normed)
    input_grad = grad_middle + grad_stream_part

    summed_x = scatter_line(wire_x(plan, g_x, b_head))
    gains = jnp.concatenate([g_gain_one, g_gain_two]).reshape(-1, LANE)
    vectors = jnp.stack(
        [g_conv_bias, g_bias_a, g_bias_i, g_lambda] + [g_conv_weight[k] for k in range(KW)]
    ).reshape(-1, LANE)
    summed_y = scatter_line(wire_y(plan, gains, vectors, g_gates, g_y, g_x))
    early = spread(plan, plan.groups[2:], (summed_two, summed_three))
    middle_set = spread(plan, ((1,), (2,)), (summed_x, summed_mid))
    got = exchange(spread(plan, ((0,),), (summed_y,)), (0,))
    got += exchange(middle_set, (1, 2))
    got += exchange(early)
    grad_own, grad_hd, grad_hu = collect(plan, got)
    from_next = lax.ppermute(grad_hd, both, backward)
    from_before = lax.ppermute(grad_hu, both, onward)
    tail = place_tail(plan, from_next).reshape(-1)
    whole = plan.own_rows * LANE
    summed = (
        grad_own.reshape(-1)
        + jnp.pad(from_before.reshape(-1), (0, whole - edge))
        + jnp.pad(tail, (whole - tail.shape[0], 0))
    )[:per]
    new_moment = MOMENT * momentum + summed
    new_params = params - RATE * (summed + MOMENT * new_moment)
    new_average = BLEND * average + (1.0 - BLEND) * new_params
    return (output[None], input_grad[None], new_params, new_moment, new_average)


def solution(mesh):
    n_seq, n_fsdp = mesh.shape["seq"], mesh.shape["fsdp"]
    fast = (n_seq, n_fsdp) == (TP, 4)
    body = partial(sliced, Plan(n_seq, n_fsdp)) if fast else local
    return jax.shard_map(
        body,
        mesh=mesh,
        in_specs=(
            P("fsdp", "seq", None),
            P("fsdp", "seq", None),
            P("fsdp", None),
            P(("seq", "fsdp")),
            P(("seq", "fsdp")),
            P(("seq", "fsdp")),
        ),
        out_specs=(
            P("fsdp", "seq", None),
            P("fsdp", "seq", None),
            P(("seq", "fsdp")),
            P(("seq", "fsdp")),
            P(("seq", "fsdp")),
        ),
        check_vma=False,
    )
```
